32 devices in a mesh: batch: 4 (over y, x), seq: 8 (over z, core).
Axes of the slice: x: 2, y: 2, z: 4, core: 2. Of those that a mesh axis runs over, the one named last changes fastest.
Arguments:
- inputs: bfloat16 [2, 4, 1024, 1024], P(None, 'batch', 'seq'), may hold values from -6 to 6
- w_query: bfloat16 [1024, 1024], P('seq'), may hold values from -0.1875 to 0.1875
- w_key: bfloat16 [1024, 1024], P('seq'), may hold values from -0.1875 to 0.1875
- w_value: bfloat16 [1024, 1024], P('seq'), may hold values from -0.1875 to 0.1875
- w_output: bfloat16 [1024, 1024], P('seq'), may hold values from -0.75 to 0.75
- gain_attention: bfloat16 [1024], P('seq'), may hold values from 0.25 to 1.75
- w_gate: bfloat16 [1024, 4096], P('seq'), may hold values from -0.1875 to 0.1875
- w_up: bfloat16 [1024, 4096], P('seq'), may hold values from -0.1875 to 0.1875
- w_down: bfloat16 [4096, 1024], P('seq'), may hold values from -0.1875 to 0.1875
- gain_feed: bfloat16 [1024], P('seq'), may hold values from 0.25 to 1.75
- variate_bias: float32 [2, 16], replicated, may hold values from -1 to 1
- segment_ids: int32 [2, 4, 1024], P(None, 'batch', 'seq'), may hold values from 0 to 1, never falling along the last dimension, each value on 1 to 768 neighbouring positions
- variate_ids: int32 [2, 4, 1024], P(None, 'batch', 'seq'), may hold values from 0 to 3
- positions: int32 [2, 4, 1024], P(None, 'batch', 'seq'), may hold values from 0 to 1023
- grad_output: bfloat16 [2, 4, 1024, 1024], P(None, 'batch', 'seq'), may hold values from -6 to 6
Outputs:
- block_output: bfloat16 [2, 4, 1024, 1024], P(None, 'batch', 'seq')
- grad_inputs: float32 [2, 4, 1024, 1024], P(None, 'batch', 'seq')
- grad_w_query: float32 [1024, 1024], P('seq')
- grad_w_key: float32 [1024, 1024], P('seq')
- grad_w_value: float32 [1024, 1024], P('seq')
- grad_w_output: float32 [1024, 1024], P('seq')
- grad_gain_attention: float32 [1024], P('seq')
- grad_w_gate: float32 [1024, 4096], P('seq')
- grad_w_up: float32 [1024, 4096], P('seq')
- grad_w_down: float32 [4096, 1024], P('seq')
- grad_gain_feed: float32 [1024], P('seq')
- grad_variate_bias: float32 [2, 16], replicated
The draws below stay inside these ranges and needn't reach their ends.
Inputs may be any that keep to these rules, and one draw needn't show every extreme that they name: `segment_ids`: segment numbers never fall along a sequence; a document has 1 to 768 tokens.
All inputs are finite; a program needn't handle non-finite values.
Results may differ from the reference program's by a relative error of at most 0.038.
Values may be sent and summed in bfloat16 or wider, within the bound.
No kernel may reach another device: no remote copies, remote signals or barrier semaphores. Data moves between devices by JAX's collectives and lax.ppermute only.
A program may use at most 320 MiB of HBM per device.

```python
import math
import jax
import jax.numpy as jnp
import numpy as np
from jax import lax

D = 1024
H = 16
HD = 64
FF = 4096
MB = 2
SEQ_LEN = 1024
DOC_MOST = 768
DOCS = 2
N_BATCH = 4


def place_ends(drawn, own_key, least, high):
    longest = drawn.shape.index(max(drawn.shape))
    spots = []
    for shift in (0, 1):
        where = [jax.random.randint(jax.random.fold_in(own_key, axis), (), 0, length) for axis, length in enumerate(drawn.shape)]
        where[longest] = (where[longest] + shift) % drawn.shape[longest]
        spots.append(tuple(where))
    return drawn.at[spots[0]].set(least).at[spots[1]].set(high)


def shard_levels(stream_key, dims, shards, smallest, top_value):
    def one(axis_at, blocks):
        heights = jax.random.uniform(jax.random.fold_in(jax.random.fold_in(stream_key, 6), axis_at), (blocks,), jnp.float32, smallest / len(shards), top_value / len(shards))
        return jnp.repeat(jnp.exp(heights), dims[axis_at] // blocks).reshape((-1,) + (1,) * (len(dims) - axis_at - 1))

    factor_of = one(*shards[0])
    for cut in shards[1:]:
        factor_of = factor_of * one(*cut)
    return factor_of


def split_up(count, total, reach, skew):
    loads = [(1 << 20) // math.isqrt(grade ** skew) + 1 for grade in range(2, count + 1)]
    spare, given = total - reach - (count - 1), [1] * (count - 1)
    while spare > 0:
        candidates = [i for i in range(count - 1) if given[i] < reach]
        whole, left = sum([loads[i] for i in candidates]), spare
        for i in candidates:
            extra = min(reach - given[i], max(1, left * loads[i] // whole), spare)
            given[i] = given[i] + extra
            spare = spare - extra
    return np.array([reach] + given)


def ragged_sizes(rng, count, total, reach, skew):
    if count == 2:
        one = jax.random.randint(rng, (), max(1, total - reach), min(reach, total - 1) + 1)
        return jnp.stack([one, total - one])
    lengths = jnp.asarray(split_up(count, total, reach, skew), jnp.int32)
    couples = (count - 1) // 2
    giver, taker = lengths[1:1 + 2 * couples:2], lengths[2:2 + 2 * couples:2]
    slack = jnp.minimum(giver - 1, reach - taker)
    shifted = jax.random.randint(jax.random.fold_in(rng, 1), (couples,), 0, 1 << 20) % (slack + 1)
    lengths = lengths.at[1:1 + 2 * couples:2].set(giver - shifted).at[2:2 + 2 * couples:2].set(taker + shifted)
    return lengths[jax.random.permutation(jax.random.fold_in(rng, 2), count)]


def scatter_about(rng, dims, deviation, reach, pieces=(), held_as=jnp.bfloat16):
    factor_of = shard_levels(rng, dims, pieces, -0.22, 0.18) if pieces else 1.0
    entries = jax.random.normal(rng, dims, jnp.float32) * deviation * factor_of
    return jnp.minimum(jnp.maximum(entries, -reach), reach).astype(held_as)


def setup_inputs(seed: int = 0) -> dict:
    key_list = jax.random.split(jax.random.key(seed), 16)
    inputs = scatter_about(key_list[0], (MB, N_BATCH, SEQ_LEN, D), 1.0, 6.0, ((1, 4), (2, 8)))
    w_query = scatter_about(key_list[1], (D, D), D ** -0.5, 0.1875, ((0, 8),))
    w_key = scatter_about(key_list[2], (D, D), D ** -0.5, 0.1875, ((0, 8),))
    w_value = scatter_about(key_list[3], (D, D), D ** -0.5, 0.1875, ((0, 8),))
    w_output = scatter_about(key_list[4], (D, D), (D // 16) ** -0.5, 0.75, ((0, 8),))
    gain_attention = jnp.clip(1.0 + 0.15 * jax.random.normal(key_list[5], (D,), jnp.float32), 0.25, 1.75).astype(jnp.bfloat16)
    w_gate = scatter_about(key_list[6], (D, FF), D ** -0.5, 0.1875, ((0, 8),))
    w_up = scatter_about(key_list[7], (D, FF), D ** -0.5, 0.1875, ((0, 8),))
    w_down = scatter_about(key_list[8], (FF, D), (FF // 4) ** -0.5, 0.1875, ((0, 8),))
    gain_feed = jnp.clip(1.0 + 0.15 * jax.random.normal(key_list[9], (D,), jnp.float32), 0.25, 1.75).astype(jnp.bfloat16)
    variate_bias = jnp.clip(jax.random.uniform(key_list[10], (2, H), jnp.float32, -1.0, 1.0), -1.0, 1.0)
    segment_ids = jax.vmap(lambda own: jnp.searchsorted(jnp.cumsum(ragged_sizes(own, DOCS, SEQ_LEN, DOC_MOST, 2)), jnp.arange(SEQ_LEN), side="right"))(jax.random.split(key_list[11], MB * N_BATCH)).reshape((MB, N_BATCH, SEQ_LEN)).astype(jnp.int32)
    variate_ids = place_ends(jax.random.randint(key_list[12], (MB, N_BATCH, SEQ_LEN), 0, 4), jax.random.fold_in(key_list[12], 1), 0, 3).astype(jnp.int32)
    positions = place_ends(jax.random.randint(key_list[13], (MB, N_BATCH, SEQ_LEN), 0, 1024), jax.random.fold_in(key_list[13], 1), 0, 1023).astype(jnp.int32)
    grad_output = scatter_about(key_list[14], (MB, N_BATCH, SEQ_LEN, D), 1.0, 6.0, ((1, 4), (2, 8)))
    return {"inputs": inputs, "w_query": w_query, "w_key": w_key, "w_value": w_value, "w_output": w_output, "gain_attention": gain_attention, "w_gate": w_gate, "w_up": w_up, "w_down": w_down, "gain_feed": gain_feed, "variate_bias": variate_bias, "segment_ids": segment_ids, "variate_ids": variate_ids, "positions": positions, "grad_output": grad_output}


EPSILON = 1e-05
SCORE_SCALE = 0.125
MASKED = -1e+30

@jax.custom_vjp
def low(v):
    return lax.optimization_barrier(v.astype(jnp.bfloat16)).astype(jnp.float32)

@jax.custom_vjp
def low_back(v):
    return v

def low_keep(v):
    return (low(v), None)

def low_pass(kept, grad):
    return (grad,)

def back_keep(v):
    return (v, None)

def back_low(kept, grad):
    return (low(grad),)
low.defvjp(low_keep, low_pass)
low_back.defvjp(back_keep, back_low)

def rotary(values_in, positions_in):
    row_count = values_in.shape[0]
    halfway = HD // 2
    freqs = jnp.exp(jnp.arange(halfway, dtype=jnp.float32) * (-2.0 * math.log(10000.0) / HD))
    angles = positions_in.astype(jnp.float32)[:, None] * freqs[None, :]
    cosine = jnp.cos(angles)[:, None, :]
    sine = jnp.sin(angles)[:, None, :]
    shaped = values_in.reshape(row_count, H, HD)
    first_half = shaped[..., :halfway]
    second_half = shaped[..., halfway:]
    return jnp.concatenate([first_half * cosine - second_half * sine, first_half * sine + second_half * cosine], -1)

def attend_sequence(query_heads, key_heads, value_heads, segments, variates, bias_table):
    seq_length = query_heads.shape[0]
    block_rows = min(512, seq_length)
    block_count = seq_length // block_rows

    def one_block(block_item):
        query_block, segment_block, variate_block = block_item
        logits = jnp.einsum('qhd,khd->hqk', query_block, key_heads, precision=lax.Precision.HIGHEST) * SCORE_SCALE
        same_variate = (variate_block[:, None] == variates[None, :])[None]
        logits = logits + jnp.where(same_variate, bias_table[0][:, None, None], bias_table[1][:, None, None])
        logits = low_back(logits)
        live = (segment_block[:, None] == segments[None, :])[None]
        weights = jax.nn.softmax(jnp.where(live, logits, MASKED), axis=-1)
        return jnp.einsum('hqk,khd->qhd', low(weights), value_heads, precision=lax.Precision.HIGHEST)
    blocks = (query_heads.reshape(block_count, block_rows, H, HD), segments.reshape(block_count, block_rows), variates.reshape(block_count, block_rows))
    mixed = lax.map(jax.checkpoint(one_block), blocks)
    return mixed.reshape(seq_length, H * HD)

def layer_forward(seq_in, w_query, w_key, w_value, w_output, gain_attention, w_gate, w_up, w_down, gain_feed, variate_bias, segments, variates, seq_positions):
    highest = lax.Precision.HIGHEST
    scale_first = lax.rsqrt(lax.optimization_barrier(jnp.mean(seq_in * seq_in, -1, keepdims=True)) + EPSILON)
    mixed_first = low(seq_in * scale_first * gain_attention)
    query_heads = low(rotary(low_back(jnp.dot(mixed_first, w_query, precision=highest)), seq_positions))
    key_heads = low(rotary(low_back(jnp.dot(mixed_first, w_key, precision=highest)), seq_positions))
    value_rows = low(low_back(jnp.dot(mixed_first, w_value, precision=highest)))
    value_heads = value_rows.reshape(value_rows.shape[0], H, HD)
    attended = attend_sequence(query_heads, key_heads, value_heads, segments, variates, variate_bias)
    attended_low = low(low_back(attended))
    middle = seq_in + low_back(jnp.dot(attended_low, w_output, precision=highest))
    scale_second = lax.rsqrt(lax.optimization_barrier(jnp.mean(middle * middle, -1, keepdims=True)) + EPSILON)
    mixed_second = low(middle * scale_second * gain_feed)
    gate_proj = low_back(jnp.dot(mixed_second, w_gate, precision=highest))
    up_proj = low_back(jnp.dot(mixed_second, w_up, precision=highest))
    hidden_rows = low(jax.nn.silu(gate_proj) * up_proj)
    return middle + low_back(jnp.dot(hidden_rows, w_down, precision=highest))

def reference(inputs, w_query, w_key, w_value, w_output, gain_attention, w_gate, w_up, w_down, gain_feed, variate_bias, segment_ids, variate_ids, positions, grad_output):
    weights_all = tuple((weight.astype(jnp.float32) for weight in (w_query, w_key, w_value, w_output, gain_attention, w_gate, w_up, w_down, gain_feed, variate_bias)))
    seq_total = inputs.shape[0] * inputs.shape[1]
    seq_length = inputs.shape[2]
    stacked_in = inputs.reshape(seq_total, seq_length, D).astype(jnp.float32)
    stacked_cot = grad_output.reshape(seq_total, seq_length, D).astype(jnp.float32)
    stacked_seg = segment_ids.reshape(seq_total, seq_length).astype(jnp.int32)
    stacked_var = variate_ids.reshape(seq_total, seq_length).astype(jnp.int32)
    stacked_pos = positions.reshape(seq_total, seq_length).astype(jnp.int32)

    def one_sequence(running, seq_item):
        seq_in, seq_segments, seq_variates, seq_positions, seq_cotangent = seq_item

        def forward(values_in, *params):
            return layer_forward(values_in, *params, seq_segments, seq_variates, seq_positions)
        result, pullback = jax.vjp(forward, seq_in, *weights_all)
        gradients = pullback(seq_cotangent)
        running = tuple((accum + gradient for accum, gradient in zip(running, gradients[1:])))
        return (running, (result.astype(jnp.bfloat16), gradients[0]))
    start_sums = tuple((jnp.zeros(weight.shape, jnp.float32) for weight in weights_all))
    totals, (results, grad_rows) = lax.scan(one_sequence, start_sums, (stacked_in, stacked_seg, stacked_var, stacked_pos, stacked_cot))
    block_output = results.reshape(inputs.shape)
    grad_inputs = grad_rows.reshape(inputs.shape)
    return (block_output, grad_inputs, totals[0], totals[1], totals[2], totals[3], totals[4], totals[5], totals[6], totals[7], totals[8], totals[9])
```

```python
import math

import jax
import jax.numpy as jnp
from jax import lax
from jax.experimental import pallas as pl
from jax.experimental.pallas import tpu as pltpu
from jax.sharding import PartitionSpec as P

D = 1024
H = 16
HD = 64
REACH = 6


EPSILON = 1e-05
SCORE_SCALE = 0.125
MASKED = -1e30


def from_behind(value, axis, by):
    length = lax.axis_size(axis)
    pairs = [(i, i + by) for i in range(length) if 0 <= i + by < length]
    return lax.ppermute(value, axis, pairs)


def step_offset(step):
    distance = step // 2 + 1
    return distance if step % 2 == 0 else -distance


def rotary(values_in, positions_in, turn):
    row_count = values_in.shape[0]
    halfway = HD // 2
    freqs = jnp.exp(jnp.arange(halfway, dtype=jnp.float32) * (-2.0 * math.log(10000.0) / HD))
    angles = positions_in.astype(jnp.float32)[:, None] * freqs[None, :]
    cosine = jnp.cos(angles)[:, None, :]
    sine = turn * jnp.sin(angles)[:, None, :]
    shaped = values_in.reshape(row_count, H, HD)
    first_half = shaped[..., :halfway]
    second_half = shaped[..., halfway:]
    turned = jnp.concatenate(
        [first_half * cosine - second_half * sine, first_half * sine + second_half * cosine], -1
    )
    return turned.reshape(row_count, H * HD)


def head_scores(query_heads, key_heads, query_variates, key_variates, bias_table):
    raw = jnp.einsum("qhd,khd->hqk", query_heads, key_heads, preferred_element_type=jnp.float32)
    same_variate = (query_variates[:, None] == key_variates[None, :])[None]
    return raw * SCORE_SCALE + jnp.where(
        same_variate, bias_table[0][:, None, None], bias_table[1][:, None, None]
    )


def attend_forward(query_rows, own_keys, own_values, own_segments, own_variates, bias_table):
    tok_count = query_rows.shape[0]
    query_heads = query_rows.reshape(tok_count, H, HD)
    shifted_segments = own_segments + 1

    def fold_keys(carried, piece_rows):
        key_part, value_part, segment_part, variate_part = piece_rows
        part_count = key_part.shape[0]
        live = shifted_segments[:, None] == segment_part[None, :]

        def update(state):
            running_max, running_total, running_sum = state
            logits = head_scores(
                query_heads,
                key_part.reshape(part_count, H, HD),
                own_variates,
                variate_part,
                bias_table,
            )
            logits = jnp.where(live[None], logits, MASKED)
            new_max = jnp.maximum(running_max, jnp.max(logits, -1))
            rescale = jnp.exp(running_max - new_max)
            weights = jnp.where(live[None], jnp.exp(logits - new_max[..., None]), 0.0)
            new_total = running_total * rescale + jnp.sum(weights, -1)
            mixed = jnp.einsum(
                "hqk,khd->qhd",
                weights.astype(jnp.bfloat16),
                value_part.reshape(part_count, H, HD),
                preferred_element_type=jnp.float32,
            )
            new_sum = running_sum * jnp.transpose(rescale)[:, :, None] + mixed
            return (new_max, new_total, new_sum)

        return lax.cond(jnp.any(live), update, lambda state: state, carried)

    near_rows = (own_keys, own_values, shifted_segments, own_variates)
    state = (
        jnp.full((H, tok_count), MASKED, jnp.float32),
        jnp.zeros((H, tok_count), jnp.float32),
        jnp.zeros((tok_count, H, HD), jnp.float32),
    )
    state = fold_keys(state, near_rows)
    for step in range(2 * REACH):
        arrived = from_behind(
            (own_keys, own_values, shifted_segments, own_variates), "seq", step_offset(step)
        )
        state = fold_keys(state, arrived)
    final_max, final_total, final_sum = state
    attended = final_sum / jnp.transpose(final_total)[:, :, None]
    log_rows = jnp.transpose(final_max + jnp.log(final_total))
    return (attended.reshape(tok_count, H * HD), log_rows)


def attend_queries_back(
    query_rows,
    grad_rows,
    log_rows,
    delta_rows,
    own_keys,
    own_values,
    own_segments,
    own_variates,
    bias_table,
):
    tok_count = query_rows.shape[0]
    query_heads = query_rows.reshape(tok_count, H, HD)
    grad_heads = grad_rows.reshape(tok_count, H, HD)
    log_heads = jnp.transpose(log_rows)
    delta_heads = jnp.transpose(delta_rows)
    shifted_segments = own_segments + 1

    def fold_keys_back(carried, piece_rows):
        key_part, value_part, segment_part, variate_part = piece_rows
        part_count = key_part.shape[0]
        live = shifted_segments[:, None] == segment_part[None, :]

        def update(state):
            grad_query, grad_bias = state
            key_heads = key_part.reshape(part_count, H, HD)
            logits = head_scores(query_heads, key_heads, own_variates, variate_part, bias_table)
            weights = jnp.where(live[None], jnp.exp(logits - log_heads[..., None]), 0.0)
            grad_weights = jnp.einsum(
                "qhd,khd->hqk",
                grad_heads,
                value_part.reshape(part_count, H, HD),
                preferred_element_type=jnp.float32,
            )
            grad_logits = (weights * (grad_weights - delta_heads[..., None])).astype(jnp.bfloat16)
            grad_query = grad_query + SCORE_SCALE * jnp.einsum(
                "hqk,khd->qhd", grad_logits, key_heads, preferred_element_type=jnp.float32
            )
            same_variate = (own_variates[:, None] == variate_part[None, :])[None]
            logit_values = grad_logits.astype(jnp.float32)
            same_total = jnp.sum(jnp.where(same_variate, logit_values, 0.0), axis=(1, 2))
            other_total = jnp.sum(jnp.where(same_variate, 0.0, logit_values), axis=(1, 2))
            return (grad_query, grad_bias + jnp.stack([same_total, other_total]))

        return lax.cond(jnp.any(live), update, lambda state: state, carried)

    state = (jnp.zeros((tok_count, H, HD), jnp.float32), jnp.zeros((2, H), jnp.float32))
    state = fold_keys_back(state, (own_keys, own_values, shifted_segments, own_variates))
    for step in range(2 * REACH):
        arrived = from_behind(
            (own_keys, own_values, shifted_segments, own_variates), "seq", step_offset(step)
        )
        state = fold_keys_back(state, arrived)
    grad_query, grad_bias = state
    return (grad_query.reshape(tok_count, H * HD), grad_bias)


def attend_keys_back(
    query_rows,
    grad_rows,
    log_rows,
    delta_rows,
    own_keys,
    own_values,
    own_segments,
    own_variates,
    bias_table,
):
    tok_count = own_keys.shape[0]
    key_heads = own_keys.reshape(tok_count, H, HD)
    value_heads = own_values.reshape(tok_count, H, HD)
    shifted_segments = own_segments + 1

    def fold_queries(carried, piece_rows):
        query_part, grad_part, log_part, delta_part, segment_part, variate_part = piece_rows
        part_count = query_part.shape[0]
        live = segment_part[:, None] == shifted_segments[None, :]

        def update(state):
            grad_key, grad_value = state
            query_heads = query_part.reshape(part_count, H, HD)
            grad_heads = grad_part.reshape(part_count, H, HD)
            logits = head_scores(query_heads, key_heads, variate_part, own_variates, bias_table)
            weights = jnp.where(
                live[None], jnp.exp(logits - jnp.transpose(log_part)[..., None]), 0.0
            )
            grad_value = grad_value + jnp.einsum(
                "hqk,qhd->khd",
                weights.astype(jnp.bfloat16),
                grad_heads,
                preferred_element_type=jnp.float32,
            )
            grad_weights = jnp.einsum(
                "qhd,khd->hqk", grad_heads, value_heads, preferred_element_type=jnp.float32
            )
            grad_logits = (weights * (grad_weights - jnp.transpose(delta_part)[..., None])).astype(
                jnp.bfloat16
            )
            grad_key = grad_key + SCORE_SCALE * jnp.einsum(
                "hqk,qhd->khd", grad_logits, query_heads, preferred_element_type=jnp.float32
            )
            return (grad_key, grad_value)

        return lax.cond(jnp.any(live), update, lambda state: state, carried)

    state = (jnp.zeros((tok_count, H, HD), jnp.float32), jnp.zeros((tok_count, H, HD), jnp.float32))
    state = fold_queries(
        state, (query_rows, grad_rows, log_rows, delta_rows, shifted_segments, own_variates)
    )
    for step in range(2 * REACH):
        arrived = (
            from_behind(query_rows, "seq", step_offset(step)),
            from_behind(grad_rows, "seq", step_offset(step)),
            from_behind(log_rows.astype(jnp.bfloat16), "seq", step_offset(step)).astype(
                log_rows.dtype
            ),
            from_behind(delta_rows.astype(jnp.bfloat16), "seq", step_offset(step)).astype(
                delta_rows.dtype
            ),
            from_behind(shifted_segments, "seq", step_offset(step)),
            from_behind(own_variates, "seq", step_offset(step)),
        )
        state = fold_queries(state, arrived)
    grad_key, grad_value = state
    return (grad_key.reshape(tok_count, H * HD), grad_value.reshape(tok_count, H * HD))


def norm_back(grad_normed, normed, scale_rows):
    return scale_rows * (grad_normed - normed * jnp.mean(grad_normed * normed, -1, keepdims=True))


def on_device(
    inputs,
    w_query,
    w_key,
    w_value,
    w_output,
    gain_attention,
    w_gate,
    w_up,
    w_down,
    gain_feed,
    variate_bias,
    segment_ids,
    variate_ids,
    positions,
    grad_output,
):
    micro_count = inputs.shape[0]
    tok_count = inputs.shape[2]
    row_count = micro_count * tok_count
    residual_in = inputs.reshape(row_count, D).astype(jnp.float32)
    cotangent = grad_output.reshape(row_count, D).astype(jnp.float32)
    segment_rows = segment_ids.reshape(micro_count, tok_count)
    variate_rows = variate_ids.reshape(micro_count, tok_count)
    position_rows = positions.reshape(row_count)
    full_query, full_key, full_value, full_output, full_gain_first = (
        lax.all_gather(w_query, "seq", axis=0, tiled=True),
        lax.all_gather(w_key, "seq", axis=0, tiled=True),
        lax.all_gather(w_value, "seq", axis=0, tiled=True),
        lax.all_gather(w_output, "seq", axis=0, tiled=True),
        lax.all_gather(gain_attention, "seq", axis=0, tiled=True),
    )
    full_gate, full_up, full_down, full_gain_second = (
        lax.all_gather(w_gate, "seq", axis=0, tiled=True),
        lax.all_gather(w_up, "seq", axis=0, tiled=True),
        lax.all_gather(w_down, "seq", axis=0, tiled=True),
        lax.all_gather(gain_feed, "seq", axis=0, tiled=True),
    )
    scale_first = lax.rsqrt(jnp.mean(residual_in * residual_in, -1, keepdims=True) + EPSILON)
    normed_first = residual_in * scale_first
    mixed_first = (normed_first * full_gain_first.astype(jnp.float32)).astype(jnp.bfloat16)
    query_proj = jnp.dot(mixed_first, full_query, preferred_element_type=jnp.float32)
    key_proj = jnp.dot(mixed_first, full_key, preferred_element_type=jnp.float32)
    value_proj = jnp.dot(mixed_first, full_value, preferred_element_type=jnp.float32)
    query_rows = rotary(query_proj, position_rows, 1.0).astype(jnp.bfloat16)
    key_rows = rotary(key_proj, position_rows, 1.0).astype(jnp.bfloat16)
    value_rows = value_proj.astype(jnp.bfloat16)
    attended_parts = []
    log_parts = []
    for micro_index in range(micro_count):
        lower_row = micro_index * tok_count
        upper_row = lower_row + tok_count
        attended_part, log_part = attend_forward(
            query_rows[lower_row:upper_row],
            key_rows[lower_row:upper_row],
            value_rows[lower_row:upper_row],
            segment_rows[micro_index],
            variate_rows[micro_index],
            variate_bias,
        )
        attended_parts.append(attended_part)
        log_parts.append(log_part)
    attended_all = jnp.concatenate(attended_parts, 0)
    attended_low = attended_all.astype(jnp.bfloat16)
    middle = residual_in + jnp.dot(attended_low, full_output, preferred_element_type=jnp.float32)
    scale_second = lax.rsqrt(jnp.mean(middle * middle, -1, keepdims=True) + EPSILON)
    normed_second = middle * scale_second
    mixed_second = (normed_second * full_gain_second.astype(jnp.float32)).astype(jnp.bfloat16)
    gate_proj = jnp.dot(mixed_second, full_gate, preferred_element_type=jnp.float32)
    up_proj = jnp.dot(mixed_second, full_up, preferred_element_type=jnp.float32)
    sigmoid_gate = jax.nn.sigmoid(gate_proj)
    silu_gate = gate_proj * sigmoid_gate
    hidden_rows = (silu_gate * up_proj).astype(jnp.bfloat16)
    block_rows = middle + jnp.dot(hidden_rows, full_down, preferred_element_type=jnp.float32)
    block_output = block_rows.astype(jnp.bfloat16).reshape(inputs.shape)
    full_query, full_key, full_value, full_output, full_gain_first = (
        lax.all_gather(w_query, "seq", axis=0, tiled=True),
        lax.all_gather(w_key, "seq", axis=0, tiled=True),
        lax.all_gather(w_value, "seq", axis=0, tiled=True),
        lax.all_gather(w_output, "seq", axis=0, tiled=True),
        lax.all_gather(gain_attention, "seq", axis=0, tiled=True),
    )
    full_gate, full_up, full_down, full_gain_second = (
        lax.all_gather(w_gate, "seq", axis=0, tiled=True),
        lax.all_gather(w_up, "seq", axis=0, tiled=True),
        lax.all_gather(w_down, "seq", axis=0, tiled=True),
        lax.all_gather(gain_feed, "seq", axis=0, tiled=True),
    )
    grad_branch_second = cotangent.astype(jnp.bfloat16)
    grad_down = jnp.einsum(
        "rf,rd->fd", hidden_rows, grad_branch_second, preferred_element_type=jnp.float32
    )
    grad_hidden = jnp.einsum(
        "rd,fd->rf", grad_branch_second, full_down, preferred_element_type=jnp.float32
    )
    silu_slope = sigmoid_gate * (1.0 + gate_proj * (1.0 - sigmoid_gate))
    grad_gate_rows = (grad_hidden * up_proj * silu_slope).astype(jnp.bfloat16)
    grad_up_rows = (grad_hidden * silu_gate).astype(jnp.bfloat16)
    grad_gate = jnp.einsum(
        "rd,rf->df", mixed_second, grad_gate_rows, preferred_element_type=jnp.float32
    )
    grad_up = jnp.einsum(
        "rd,rf->df", mixed_second, grad_up_rows, preferred_element_type=jnp.float32
    )
    grad_mixed_second = jnp.einsum(
        "rf,df->rd", grad_gate_rows, full_gate, preferred_element_type=jnp.float32
    ) + jnp.einsum("rf,df->rd", grad_up_rows, full_up, preferred_element_type=jnp.float32)
    grad_gain_second = jnp.sum(grad_mixed_second * normed_second, 0)
    grad_middle = cotangent + norm_back(
        grad_mixed_second * full_gain_second.astype(jnp.float32), normed_second, scale_second
    )
    grad_branch_first = grad_middle.astype(jnp.bfloat16)
    grad_out_proj = jnp.einsum(
        "rd,re->de", attended_low, grad_branch_first, preferred_element_type=jnp.float32
    )
    grad_attended = jnp.einsum(
        "re,de->rd", grad_branch_first, full_output, preferred_element_type=jnp.float32
    ).astype(jnp.bfloat16)
    delta_all = jnp.einsum(
        "rhd,rhd->rh",
        grad_attended.astype(jnp.float32).reshape(row_count, H, HD),
        attended_all.reshape(row_count, H, HD),
    )
    grad_bias_local = jnp.zeros((2, H), jnp.float32)
    query_grad_parts = []
    key_grad_parts = []
    value_grad_parts = []
    for micro_index in range(micro_count):
        lower_row = micro_index * tok_count
        upper_row = lower_row + tok_count
        query_grad_part, bias_part = attend_queries_back(
            query_rows[lower_row:upper_row],
            grad_attended[lower_row:upper_row],
            log_parts[micro_index],
            delta_all[lower_row:upper_row],
            key_rows[lower_row:upper_row],
            value_rows[lower_row:upper_row],
            segment_rows[micro_index],
            variate_rows[micro_index],
            variate_bias,
        )
        key_grad_part, value_grad_part = attend_keys_back(
            query_rows[lower_row:upper_row],
            grad_attended[lower_row:upper_row],
            log_parts[micro_index],
            delta_all[lower_row:upper_row],
            key_rows[lower_row:upper_row],
            value_rows[lower_row:upper_row],
            segment_rows[micro_index],
            variate_rows[micro_index],
            variate_bias,
        )
        grad_bias_local = grad_bias_local + bias_part
        query_grad_parts.append(query_grad_part)
        key_grad_parts.append(key_grad_part)
        value_grad_parts.append(value_grad_part)
    grad_query_rows = rotary(jnp.concatenate(query_grad_parts, 0), position_rows, -1.0).astype(
        jnp.bfloat16
    )
    grad_key_rows = rotary(jnp.concatenate(key_grad_parts, 0), position_rows, -1.0).astype(
        jnp.bfloat16
    )
    grad_value_rows = jnp.concatenate(value_grad_parts, 0).astype(jnp.bfloat16)
    grad_query = jnp.einsum(
        "rd,re->de", mixed_first, grad_query_rows, preferred_element_type=jnp.float32
    )
    grad_key = jnp.einsum(
        "rd,re->de", mixed_first, grad_key_rows, preferred_element_type=jnp.float32
    )
    grad_value = jnp.einsum(
        "rd,re->de", mixed_first, grad_value_rows, preferred_element_type=jnp.float32
    )
    grad_mixed_first = (
        jnp.einsum("re,de->rd", grad_query_rows, full_query, preferred_element_type=jnp.float32)
        + jnp.einsum("re,de->rd", grad_key_rows, full_key, preferred_element_type=jnp.float32)
        + jnp.einsum("re,de->rd", grad_value_rows, full_value, preferred_element_type=jnp.float32)
    )
    grad_gain_first = jnp.sum(grad_mixed_first * normed_first, 0)
    grad_input_rows = grad_middle + norm_back(
        grad_mixed_first * full_gain_first.astype(jnp.float32), normed_first, scale_first
    )
    grad_inputs = grad_input_rows.reshape(inputs.shape)
    (
        shard_query,
        shard_key,
        shard_value,
        shard_output,
        shard_gain_first,
        shard_gate,
        shard_up,
        shard_down,
        shard_gain_second,
    ) = (
        lax.psum_scatter(grad_query, "seq", scatter_dimension=0, tiled=True),
        lax.psum_scatter(grad_key, "seq", scatter_dimension=0, tiled=True),
        lax.psum_scatter(grad_value, "seq", scatter_dimension=0, tiled=True),
        lax.psum_scatter(grad_out_proj, "seq", scatter_dimension=0, tiled=True),
        lax.psum_scatter(grad_gain_first, "seq", scatter_dimension=0, tiled=True),
        lax.psum_scatter(grad_gate, "seq", scatter_dimension=0, tiled=True),
        lax.psum_scatter(grad_up, "seq", scatter_dimension=0, tiled=True),
        lax.psum_scatter(grad_down, "seq", scatter_dimension=0, tiled=True),
        lax.psum_scatter(grad_gain_second, "seq", scatter_dimension=0, tiled=True),
    )
    summed = (
        lax.psum(shard_query.astype(jnp.bfloat16), "batch").astype(jnp.float32),
        lax.psum(shard_key.astype(jnp.bfloat16), "batch").astype(jnp.float32),
        lax.psum(shard_value.astype(jnp.bfloat16), "batch").astype(jnp.float32),
        lax.psum(shard_output.astype(jnp.bfloat16), "batch").astype(jnp.float32),
        lax.psum(shard_gain_first.astype(jnp.bfloat16), "batch").astype(jnp.float32),
        lax.psum(shard_gate.astype(jnp.bfloat16), "batch").astype(jnp.float32),
        lax.psum(shard_up.astype(jnp.bfloat16), "batch").astype(jnp.float32),
        lax.psum(shard_down.astype(jnp.bfloat16), "batch").astype(jnp.float32),
        lax.psum(shard_gain_second.astype(jnp.bfloat16), "batch").astype(jnp.float32),
    )
    grad_bias_total = lax.psum(grad_bias_local, ("batch", "seq"))
    return (
        block_output,
        grad_inputs,
        summed[0],
        summed[1],
        summed[2],
        summed[3],
        summed[4],
        summed[5],
        summed[6],
        summed[7],
        summed[8],
        grad_bias_total,
    )


ORDER_A = (0, 1, 2, 3)
ORDER_B = (0, 2, 1, 3)
FEATURES = 128
LSE_AT = 64


def swap(value, bit):
    return lax.ppermute(value, "batch", [(i, i ^ bit) for i in range(4)])


def gather_plane(own):
    half = own.shape[0] // 2
    lower, upper = own[:half], own[half:]
    lower_pair = jnp.concatenate([lower, swap(lower, 1)], 0)
    upper_pair = jnp.concatenate([upper, swap(upper, 2)], 0)
    return lower_pair, swap(lower_pair, 2), upper_pair, swap(upper_pair, 1)


def scatter_plane(partial):
    quarter = partial.shape[0] // 4
    half = quarter // 2
    lower = partial[:quarter] + swap(partial[quarter : 2 * quarter], 2)
    upper = partial[2 * quarter : 3 * quarter] + swap(partial[3 * quarter :], 1)
    return jnp.concatenate(
        [lower[:half] + swap(lower[half:], 1), upper[:half] + swap(upper[half:], 2)], 0
    )


def by_rank(stacked, rank):
    return jnp.stack([lax.dynamic_index_in_dim(stacked, rank ^ a, 0, False) for a in range(4)])


def reorder(rows, order, mask):
    blocks = rows.reshape(4, rows.shape[0] // 4, rows.shape[1])
    return jnp.concatenate([blocks[order.index(r ^ mask)] for r in order], 0)


def gather_heads(own):
    half = own.shape[0] // 2
    lower, upper = own[:half], own[half:]
    lower_x = reorder(swap(lower, 1), ORDER_A, 1)
    upper_y = reorder(swap(upper, 2), ORDER_B, 2)
    lower_far = swap(jnp.concatenate([lower, lower_x], 1), 2)
    upper_far = swap(jnp.concatenate([upper, upper_y], 1), 1)
    lower_far = reorder(lower_far, ORDER_A, 2)
    upper_far = reorder(upper_far, ORDER_B, 1)
    width = own.shape[1]
    return jnp.concatenate(
        [
            jnp.concatenate([lower, lower_x, lower_far], 1),
            jnp.concatenate([upper, upper_far[:, :width], upper_y, upper_far[:, width:]], 1),
        ],
        0,
    )


def to_sequence(rows):
    micro, tokens, width = rows.shape
    quarter = tokens // 4
    pieces = jnp.transpose(rows.reshape(micro, 4, quarter, width), (1, 0, 2, 3))
    pieces = lax.all_to_all(pieces, "batch", 0, 0, tiled=True)
    pieces = pieces.reshape(4 * micro, quarter, width)
    pieces = lax.all_to_all(pieces, "seq", 0, 0, tiled=True)
    return pieces.reshape(4 * micro * quarter, width)


def from_sequence(rows, micro):
    width = rows.shape[1]
    quarter = rows.shape[0] // (4 * micro)
    pieces = rows.reshape(4 * micro, quarter, width)
    pieces = lax.all_to_all(pieces, "seq", 0, 0, tiled=True)
    pieces = pieces.reshape(4, micro, quarter, width)
    pieces = lax.all_to_all(pieces, "batch", 0, 0, tiled=True)
    return jnp.transpose(pieces, (1, 0, 2, 3)).reshape(micro, 4 * quarter, width)


def three_parts(value):
    high = value.astype(jnp.bfloat16)
    rest = value - high.astype(jnp.float32)
    middle = rest.astype(jnp.bfloat16)
    low = (rest - middle.astype(jnp.float32)).astype(jnp.bfloat16)
    return high, middle, low


def token_features(segments, variates):
    lane = lax.broadcasted_iota(jnp.int32, (1, FEATURES), 1)
    variate_hot = (lane < 12) & (lane % 4 == variates)
    ones = (lane >= 12) & (lane < 15)
    segment_lane = (lane >= 16) & (lane < LSE_AT)
    segment_hot = segment_lane & (lane - 16 == segments)
    query_side = variate_hot | ones | segment_hot
    key_side = (
        variate_hot
        | ones
        | (segment_lane & ~segment_hot)
        | ((lane >= LSE_AT) & (lane < LSE_AT + 3))
    )
    return query_side.astype(jnp.bfloat16), key_side.astype(jnp.bfloat16)


def head_weights(same_bias, other_bias):
    gap = [part[:, None] for part in three_parts(same_bias - other_bias)]
    base = [part[:, None] for part in three_parts(other_bias)]
    heads = same_bias.shape[0]
    columns = [jnp.broadcast_to(part, (heads, 4)) for part in gap] + base
    columns.append(jnp.zeros((heads, 1), jnp.bfloat16))
    columns.append(jnp.full((heads, LSE_AT - 16), MASKED, jnp.bfloat16))
    columns.append(jnp.zeros((heads, FEATURES - LSE_AT), jnp.bfloat16))
    return jnp.concatenate(columns, 1)


def turn_pair(pair, cosine, sine):
    lane = lax.broadcasted_iota(jnp.int32, pair.shape, 1)
    crossed = jnp.where(lane % 64 < 32, pltpu.roll(pair, 96, 1), pltpu.roll(pair, 32, 1))
    return pair * cosine + crossed * sine


def dot_rows(left, right):
    return lax.dot_general(left, right, (((1,), (1,)), ((), ())), preferred_element_type=jnp.float32)


def dot_first(left, right):
    return lax.dot_general(left, right, (((0,), (0,)), ((), ())), preferred_element_type=jnp.float32)


def attend_kernel(
    proj_ref,
    cos_ref,
    sin_ref,
    query_side_ref,
    key_side_ref,
    weights_ref,
    turned_ref,
    wide_ref,
    low_ref,
    log_ref,
    keys_ref,
    values_ref,
):
    length = proj_ref.shape[0]
    rows_at_once = 256
    ones_lane = lax.broadcasted_iota(jnp.int32, (length, 128), 1) == 0
    for pair in range(2):
        at = 128 * pair
        turned = turn_pair(
            proj_ref[:, 256 + at : 384 + at], cos_ref[...], sin_ref[...]
        ).astype(jnp.bfloat16)
        turned_ref[:, 256 + at : 384 + at] = turned
        keys_ref[pair, :, :128] = turned
        keys_ref[pair, :, 128:] = key_side_ref[...]
        value = proj_ref[:, 512 + at : 640 + at].astype(jnp.bfloat16)
        turned_ref[:, 512 + at : 640 + at] = value
        values_ref[pair, :, :128] = value
        values_ref[pair, :, 128:] = ones_lane.astype(jnp.bfloat16)
    half_lane = lax.broadcasted_iota(jnp.int32, (rows_at_once, 128), 1) // 64
    lane = lax.broadcasted_iota(jnp.int32, (rows_at_once, 128), 1)

    def one_block(index, carry):
        rows = pl.ds(pl.multiple_of(index * rows_at_once, rows_at_once), rows_at_once)
        cosine = cos_ref[rows, :]
        sine = sin_ref[rows, :]
        side = query_side_ref[rows, :]
        logs = jnp.zeros((rows_at_once, 128), jnp.float32)
        for pair in range(2):
            at = 128 * pair
            turned = turn_pair(proj_ref[rows, at : at + 128], cosine, sine).astype(jnp.bfloat16)
            turned_ref[rows, at : at + 128] = turned
            scaled = turned * jnp.bfloat16(SCORE_SCALE)
            mixed = jnp.zeros((rows_at_once, 128), jnp.float32)
            for half in range(2):
                head = 2 * pair + half
                query = jnp.concatenate(
                    [
                        jnp.where(half_lane == half, scaled, jnp.bfloat16(0)),
                        side * weights_ref[head : head + 1, :],
                    ],
                    1,
                )
                scores = dot_rows(query, keys_ref[pair])
                top = jnp.max(scores, 1, keepdims=True)
                powers = jnp.exp(scores - top).astype(jnp.bfloat16)
                summed = jnp.dot(powers, values_ref[pair], preferred_element_type=jnp.float32)
                total = summed[:, 128:129]
                mixed = jnp.where(half_lane == half, summed[:, :128] / total, mixed)
                logs = jnp.where(lane == head, top + jnp.log(total), logs)
            wide_ref[rows, at : at + 128] = mixed
            low_ref[rows, at : at + 128] = mixed.astype(jnp.bfloat16)
        log_ref[rows, :] = logs
        return carry

    lax.fori_loop(0, length // rows_at_once, one_block, 0)


def attend_sequence(proj, cosine, sine, query_side, key_side, weights):
    length = proj.shape[0]
    return pl.pallas_call(
        attend_kernel,
        out_shape=(
            jax.ShapeDtypeStruct((length, 768), jnp.bfloat16),
            jax.ShapeDtypeStruct((length, 256), jnp.float32),
            jax.ShapeDtypeStruct((length, 256), jnp.bfloat16),
            jax.ShapeDtypeStruct((length, 128), jnp.float32),
        ),
        scratch_shapes=[
            pltpu.VMEM((2, length, 256), jnp.bfloat16),
            pltpu.VMEM((2, length, 256), jnp.bfloat16),
        ],
        cost_estimate=pl.CostEstimate(
            flops=16 * length * length * 256, bytes_accessed=8 * 2**20, transcendentals=0
        ),
        name="attend",
    )(proj, cosine, sine, query_side, key_side, weights)


def attend_back_kernel(
    turned_ref,
    wide_ref,
    log_ref,
    grad_ref,
    cos_ref,
    sin_ref,
    query_side_ref,
    key_side_ref,
    weights_ref,
    out_ref,
    bias_ref,
    queries_ref,
    grads_ref,
    total_ref,
):
    length = turned_ref.shape[0]
    rows_at_once = 256
    half_lane = lax.broadcasted_iota(jnp.int32, (length, 128), 1) // 64
    lane = lax.broadcasted_iota(jnp.int32, (length, 128), 1)
    for pair in range(2):
        at = 128 * pair
        scaled = turned_ref[:, at : at + 128] * jnp.bfloat16(SCORE_SCALE)
        grad = grad_ref[:, at : at + 128]
        product = grad.astype(jnp.float32) * wide_ref[:, at : at + 128]
        for half in range(2):
            head = 2 * pair + half
            side = query_side_ref[...] * weights_ref[head : head + 1, :]
            for place, part in enumerate(three_parts(-log_ref[:, head : head + 1])):
                side = jnp.where(lane == LSE_AT + place, part, side)
            queries_ref[head, :, :128] = jnp.where(half_lane == half, scaled, jnp.bfloat16(0))
            queries_ref[head, :, 128:] = side
            delta = jnp.sum(jnp.where(half_lane == half, product, 0.0), 1, keepdims=True)
            extra = jnp.zeros((length, 128), jnp.bfloat16)
            for place, part in enumerate(three_parts(-delta)):
                extra = jnp.where(lane == place, part, extra)
            grads_ref[head, :, :128] = grad
            grads_ref[head, :, 128:] = extra
    total_ref[...] = jnp.zeros_like(total_ref)
    half_short = half_lane[:rows_at_once]
    lane_short = lane[:rows_at_once]
    three_ones = (lane_short < 3).astype(jnp.bfloat16)

    def one_block(index, carry):
        rows = pl.ds(pl.multiple_of(index * rows_at_once, rows_at_once), rows_at_once)
        cosine = cos_ref[rows, :]
        sine = -sin_ref[rows, :]
        key_side = key_side_ref[rows, :]
        first_four = jnp.where(lane_short < 4, key_side.astype(jnp.float32), 0.0)
        sums = list(carry)
        for pair in range(2):
            at = 128 * pair
            keys = turned_ref[rows, 256 + at : 384 + at]
            values = turned_ref[rows, 512 + at : 640 + at]
            grad_keys = jnp.zeros((rows_at_once, 128), jnp.float32)
            grad_values = jnp.zeros((rows_at_once, 128), jnp.float32)
            for half in range(2):
                head = 2 * pair + half
                scores = dot_rows(jnp.concatenate([keys, key_side], 1), queries_ref[head])
                weights = jnp.exp(scores)
                grad_weights = dot_rows(
                    jnp.concatenate(
                        [jnp.where(half_short == half, values, jnp.bfloat16(0)), three_ones], 1
                    ),
                    grads_ref[head],
                )
                grad_values = jnp.where(
                    half_short == half,
                    jnp.dot(
                        weights.astype(jnp.bfloat16),
                        grads_ref[head, :, :128],
                        preferred_element_type=jnp.float32,
                    ),
                    grad_values,
                )
                grad_scores = (weights * grad_weights).astype(jnp.bfloat16)
                both = jnp.dot(
                    grad_scores,
                    jnp.concatenate([queries_ref[head, :, :128], query_side_ref[...]], 1),
                    preferred_element_type=jnp.float32,
                )
                grad_keys = grad_keys + both[:, :128]
                counted = both[:, 128:]
                same = jnp.sum(counted * first_four, 0, keepdims=True)
                every = jnp.sum(jnp.where(lane_short < 4, counted, 0.0), 0, keepdims=True)
                sums[head] = sums[head] + same
                sums[4 + head] = sums[4 + head] + (every - same)
                total_ref[:, at : at + 128] += dot_first(
                    grad_scores, jnp.where(half_short == half, keys, jnp.bfloat16(0))
                )
            out_ref[rows, 256 + at : 384 + at] = turn_pair(grad_keys, cosine, sine).astype(
                jnp.bfloat16
            )
            out_ref[rows, 512 + at : 640 + at] = grad_values.astype(jnp.bfloat16)
        return tuple(sums)

    start = tuple(jnp.zeros((1, 128), jnp.float32) for _ in range(8))
    sums = lax.fori_loop(0, length // rows_at_once, one_block, start)
    for place in range(8):
        bias_ref[place : place + 1, :] = sums[place]
    for pair in range(2):
        at = 128 * pair
        out_ref[:, at : at + 128] = turn_pair(
            total_ref[:, at : at + 128] * SCORE_SCALE, cos_ref[...], -sin_ref[...]
        ).astype(jnp.bfloat16)


def attend_sequence_back(turned, wide, logs, grads, cosine, sine, query_side, key_side, weights):
    length = turned.shape[0]
    return pl.pallas_call(
        attend_back_kernel,
        out_shape=(
            jax.ShapeDtypeStruct((length, 768), jnp.bfloat16),
            jax.ShapeDtypeStruct((8, 128), jnp.float32),
        ),
        scratch_shapes=[
            pltpu.VMEM((4, length, 256), jnp.bfloat16),
            pltpu.VMEM((4, length, 256), jnp.bfloat16),
            pltpu.VMEM((length, 256), jnp.float32),
        ],
        cost_estimate=pl.CostEstimate(
            flops=40 * length * length * 256, bytes_accessed=8 * 2**20, transcendentals=0
        ),
        name="attend_back",
    )(turned, wide, logs, grads, cosine, sine, query_side, key_side, weights)


def on_plane(
    inputs,
    w_query,
    w_key,
    w_value,
    w_output,
    gain_attention,
    w_gate,
    w_up,
    w_down,
    gain_feed,
    variate_bias,
    segment_ids,
    variate_ids,
    positions,
    grad_output,
):
    low, wide = jnp.bfloat16, jnp.float32
    rank = lax.axis_index("batch")
    micro, tokens = inputs.shape[0], inputs.shape[2]
    n_seq = lax.axis_size("seq")
    shard = w_query.shape[0]
    per = D // 4
    ff = w_gate.shape[1]
    ff_per = ff // 4
    ff_piece = ff_per // n_seq
    rows_in = inputs.reshape(micro, tokens, D)

    def columns(weight):
        return lax.dynamic_slice_in_dim(weight, rank * per, per, 1)

    gain_columns = jnp.concatenate(
        [gain_attention[:, None], gain_feed[:, None], jnp.zeros((shard, 126), low)], 1
    )
    first_shard = jnp.concatenate(
        [columns(w_query), columns(w_key), columns(w_value), w_output, gain_columns], 1
    )

    def ff_columns(weight):
        cut = weight.reshape(shard, n_seq, 4 * ff_piece)
        return lax.dynamic_slice_in_dim(cut, rank * ff_piece, ff_piece, 2).reshape(shard, ff_per)

    down_rows = lax.dynamic_slice_in_dim(w_down, rank * ff_piece, ff_piece, 0)
    first_weights = lax.all_gather(first_shard, "seq", axis=0, tiled=True)
    second_shard = jnp.concatenate([ff_columns(w_gate), ff_columns(w_up)], 1)
    second_weights = lax.all_gather(second_shard, "seq", axis=0, tiled=True)
    down_weights = lax.all_gather(down_rows, "seq", axis=0, tiled=True)
    gains = jnp.transpose(first_weights[:, 3 * per + D : 3 * per + D + 2]).astype(wide)
    gain_first, gain_second = gains[0:1], gains[1:2]
    qkv_weights = first_weights[:, : 3 * per]
    out_weights = by_rank(
        first_weights[:, 3 * per : 3 * per + D].reshape(4, per, D), rank
    ).reshape(D, D)

    numbers = jnp.stack(
        [segment_ids, variate_ids, positions // 32, positions % 32], -1
    ).reshape(micro, tokens, 4)
    numbers = jnp.pad(numbers.astype(low), ((0, 0), (0, 0), (0, 124)))
    mine = to_sequence(jnp.concatenate([rows_in, numbers], 2))
    cot_mine = to_sequence(grad_output.reshape(micro, tokens, D))
    whole = jnp.concatenate(gather_plane(mine), 0)
    cot_low = jnp.concatenate(gather_plane(cot_mine), 0)
    length = whole.shape[0]
    quarter = length // 4
    eighth = quarter // 2

    def own(rows):
        return jnp.concatenate([rows[:eighth], rows[2 * quarter : 2 * quarter + eighth]], 0)

    numbers = whole[:, D : D + 4].astype(jnp.int32)
    segments, variates = numbers[:, 0:1], numbers[:, 1:2]
    places = (numbers[:, 2:3] * 32 + numbers[:, 3:4]).astype(wide)
    lane = jnp.arange(128)
    freqs = jnp.exp((lane % 32).astype(wide) * (-2.0 * math.log(10000.0) / HD))
    angles = places * freqs[None, :]
    cosine = jnp.cos(angles)
    sine = jnp.where((lane % 64 < 32)[None, :], -jnp.sin(angles), jnp.sin(angles))
    query_side, key_side = token_features(segments, variates)
    my_bias = lax.dynamic_slice_in_dim(variate_bias, rank * 4, 4, 1)
    weights = jnp.pad(head_weights(my_bias[0], my_bias[1]), ((0, 4), (0, 0)))

    residual = whole[:, :D].astype(wide)
    scale_first = lax.rsqrt(jnp.mean(residual * residual, -1, keepdims=True) + EPSILON)
    mixed_first = (residual * scale_first * gain_first).astype(low)
    proj = jnp.dot(mixed_first, qkv_weights, preferred_element_type=wide)
    turned, attended_wide, attended_low, logs = attend_sequence(
        proj, cosine, sine, query_side, key_side, weights
    )
    attended = gather_heads(attended_low)
    middle = residual + jnp.dot(attended, out_weights, preferred_element_type=wide)
    scale_second = lax.rsqrt(jnp.mean(middle * middle, -1, keepdims=True) + EPSILON)
    mixed_second = (middle * scale_second * gain_second).astype(low)
    gate_up = jnp.dot(mixed_second, second_weights, preferred_element_type=wide)
    gate_proj, up_proj = gate_up[:, :ff_per], gate_up[:, ff_per:]
    sigmoid_gate = jax.nn.sigmoid(gate_proj)
    silu_gate = gate_proj * sigmoid_gate
    hidden = (silu_gate * up_proj).astype(low)

    grad_hidden = dot_rows(cot_low, down_weights)
    silu_slope = sigmoid_gate * (1.0 + gate_proj * (1.0 - sigmoid_gate))
    grad_gate_up = jnp.concatenate(
        [(grad_hidden * up_proj * silu_slope).astype(low), (grad_hidden * silu_gate).astype(low)],
        1,
    )
    grad_mixed_part = dot_rows(grad_gate_up, second_weights).astype(low)
    grad_mixed_second = scatter_plane(grad_mixed_part).astype(wide)
    out_part = jnp.dot(hidden, down_weights, preferred_element_type=wide).astype(low)
    block_rows = (own(middle) + scatter_plane(out_part).astype(wide)).astype(low)
    block_output = from_sequence(block_rows, micro).reshape(inputs.shape)
    grad_down = dot_first(hidden, cot_low).astype(low)
    grad_gate_up_weights = dot_first(mixed_second, grad_gate_up).astype(low)
    shard_down = lax.psum_scatter(grad_down, "seq", scatter_dimension=0, tiled=True)
    shard_gate_up = lax.psum_scatter(grad_gate_up_weights, "seq", scatter_dimension=0, tiled=True)

    own_scale_second = own(scale_second)
    grad_middle = cot_mine.astype(wide) + norm_back(
        grad_mixed_second * gain_second, own(middle) * own_scale_second, own_scale_second
    )
    grad_branch = grad_middle.astype(low)
    grad_attended = dot_rows(grad_branch, out_weights).astype(low)
    branch_columns = by_rank(
        jnp.transpose(grad_branch.reshape(quarter, 4, per), (1, 0, 2)), rank
    )
    parcels = [
        jnp.concatenate([grad_attended[:, r * per : (r + 1) * per], branch_columns[r]], 1)
        for r in range(4)
    ]
    parcels = [parcels[0]] + [swap(parcels[r], r) for r in range(1, 4)]
    arrived = jnp.concatenate(
        [parcels[r][:eighth] for r in ORDER_A] + [parcels[r][eighth:] for r in ORDER_B], 0
    )
    grad_heads, branch_mine = arrived[:, :per], arrived[:, per:]
    grad_proj, bias_sums = attend_sequence_back(
        turned,
        attended_wide,
        logs,
        grad_heads,
        cosine,
        sine,
        query_side,
        key_side,
        weights,
    )
    grad_first_part = dot_rows(grad_proj, qkv_weights).astype(low)
    grad_mixed_first = scatter_plane(grad_first_part).astype(wide)
    own_scale_first = own(scale_first)
    grad_rows = grad_middle + norm_back(
        grad_mixed_first * gain_first,
        mine[:, :D].astype(wide) * own_scale_first,
        own_scale_first,
    )
    grad_inputs = from_sequence(grad_rows.astype(low), micro).astype(wide).reshape(inputs.shape)

    grad_out = dot_first(attended, branch_mine)
    grad_out = by_rank(grad_out.reshape(4, per, per), rank).reshape(D, per)
    grad_first_weights = jnp.concatenate([dot_first(mixed_first, grad_proj), grad_out], 1)
    shard_first = lax.psum_scatter(
        grad_first_weights.astype(low), "seq", scatter_dimension=0, tiled=True
    )

    def all_ranks(rows):
        lower, lower_far, upper, upper_far = gather_plane(rows)
        half = rows.shape[0] // 2
        blocks = [
            (lower[:half], upper[:half]),
            (lower[half:], upper_far[:half]),
            (lower_far[:half], upper[half:]),
            (lower_far[half:], upper_far[half:]),
        ]
        return by_rank(jnp.stack([jnp.concatenate(pair, 0) for pair in blocks]), rank)

    full_gate_up = all_ranks(shard_gate_up).astype(wide)
    full_down = all_ranks(shard_down).astype(wide)

    def ff_whole(blocks):
        cut = blocks.reshape(4, shard, n_seq, ff_piece)
        return jnp.transpose(cut, (1, 2, 0, 3)).reshape(shard, ff)

    grad_gate = ff_whole(full_gate_up[:, :, :ff_per])
    grad_up = ff_whole(full_gate_up[:, :, ff_per:])
    grad_down = full_down.reshape(4 * ff_piece, D)
    full_first = all_ranks(shard_first).astype(wide)
    grad_query, grad_key, grad_value, grad_output_weights = [
        jnp.transpose(full_first[:, :, i * per : (i + 1) * per], (1, 0, 2)).reshape(shard, D)
        for i in range(4)
    ]

    def gain_grad(pairs, gain):
        total = sum(jnp.sum(weight.astype(wide) * grad, 1) for weight, grad in pairs)
        return total / gain.astype(wide)

    grad_gain_first = gain_grad(
        [(w_query, grad_query), (w_key, grad_key), (w_value, grad_value)], gain_attention
    )
    grad_gain_second = gain_grad([(w_gate, grad_gate), (w_up, grad_up)], gain_feed)
    bias_part = jnp.sum(bias_sums, 1).reshape(2, 4)
    bias_part = lax.dynamic_update_slice(jnp.zeros((2, H), wide), bias_part, (0, rank * 4))
    grad_bias = lax.psum(bias_part, ("batch", "seq"))
    return (
        block_output,
        grad_inputs,
        grad_query,
        grad_key,
        grad_value,
        grad_output_weights,
        grad_gain_first,
        grad_gate,
        grad_up,
        grad_down,
        grad_gain_second,
        grad_bias,
    )


def solution(mesh):
    n_batch, n_seq = mesh.shape["batch"], mesh.shape["seq"]
    step = on_plane if n_batch == 4 and n_seq == 8 else on_device
    return jax.shard_map(
        step,
        mesh=mesh,
        in_specs=(
            P(None, "batch", "seq", None),
            P("seq", None),
            P("seq", None),
            P("seq", None),
            P("seq", None),
            P("seq"),
            P("seq", None),
            P("seq", None),
            P("seq", None),
            P("seq"),
            P(),
            P(None, "batch", "seq"),
            P(None, "batch", "seq"),
            P(None, "batch", "seq"),
            P(None, "batch", "seq", None),
        ),
        out_specs=(
            P(None, "batch", "seq", None),
            P(None, "batch", "seq", None),
            P("seq", None),
            P("seq", None),
            P("seq", None),
            P("seq", None),
            P("seq"),
            P("seq", None),
            P("seq", None),
            P("seq", None),
            P("seq"),
            P(),
        ),
        check_vma=False,
    )
```

```python
import functools
import math

import jax
import jax.numpy as jnp
from jax import lax
from jax.experimental import pallas as pl
from jax.experimental.pallas import tpu as pltpu
from jax.sharding import PartitionSpec as P

D = 1024
H = 16
HD = 64
REACH = 6


EPSILON = 1e-05
SCORE_SCALE = 0.125
MASKED = -1e30


def from_behind(value, axis, by):
    length = lax.axis_size(axis)
    pairs = [(i, i + by) for i in range(length) if 0 <= i + by < length]
    return lax.ppermute(value, axis, pairs)


def step_offset(step):
    distance = step // 2 + 1
    return distance if step % 2 == 0 else -distance


def rotary(values_in, positions_in, turn):
    row_count = values_in.shape[0]
    halfway = HD // 2
    freqs = jnp.exp(jnp.arange(halfway, dtype=jnp.float32) * (-2.0 * math.log(10000.0) / HD))
    angles = positions_in.astype(jnp.float32)[:, None] * freqs[None, :]
    cosine = jnp.cos(angles)[:, None, :]
    sine = turn * jnp.sin(angles)[:, None, :]
    shaped = values_in.reshape(row_count, H, HD)
    first_half = shaped[..., :halfway]
    second_half = shaped[..., halfway:]
    turned = jnp.concatenate(
        [first_half * cosine - second_half * sine, first_half * sine + second_half * cosine], -1
    )
    return turned.reshape(row_count, H * HD)


def head_scores(query_heads, key_heads, query_variates, key_variates, bias_table):
    raw = jnp.einsum("qhd,khd->hqk", query_heads, key_heads, preferred_element_type=jnp.float32)
    same_variate = (query_variates[:, None] == key_variates[None, :])[None]
    return raw * SCORE_SCALE + jnp.where(
        same_variate, bias_table[0][:, None, None], bias_table[1][:, None, None]
    )


def attend_forward(query_rows, own_keys, own_values, own_segments, own_variates, bias_table):
    tok_count = query_rows.shape[0]
    query_heads = query_rows.reshape(tok_count, H, HD)
    shifted_segments = own_segments + 1

    def fold_keys(carried, piece_rows):
        key_part, value_part, segment_part, variate_part = piece_rows
        part_count = key_part.shape[0]
        live = shifted_segments[:, None] == segment_part[None, :]

        def update(state):
            running_max, running_total, running_sum = state
            logits = head_scores(
                query_heads,
                key_part.reshape(part_count, H, HD),
                own_variates,
                variate_part,
                bias_table,
            )
            logits = jnp.where(live[None], logits, MASKED)
            new_max = jnp.maximum(running_max, jnp.max(logits, -1))
            rescale = jnp.exp(running_max - new_max)
            weights = jnp.where(live[None], jnp.exp(logits - new_max[..., None]), 0.0)
            new_total = running_total * rescale + jnp.sum(weights, -1)
            mixed = jnp.einsum(
                "hqk,khd->qhd",
                weights.astype(jnp.bfloat16),
                value_part.reshape(part_count, H, HD),
                preferred_element_type=jnp.float32,
            )
            new_sum = running_sum * jnp.transpose(rescale)[:, :, None] + mixed
            return (new_max, new_total, new_sum)

        return lax.cond(jnp.any(live), update, lambda state: state, carried)

    near_rows = (own_keys, own_values, shifted_segments, own_variates)
    state = (
        jnp.full((H, tok_count), MASKED, jnp.float32),
        jnp.zeros((H, tok_count), jnp.float32),
        jnp.zeros((tok_count, H, HD), jnp.float32),
    )
    state = fold_keys(state, near_rows)
    for step in range(2 * REACH):
        arrived = from_behind(
            (own_keys, own_values, shifted_segments, own_variates), "seq", step_offset(step)
        )
        state = fold_keys(state, arrived)
    final_max, final_total, final_sum = state
    attended = final_sum / jnp.transpose(final_total)[:, :, None]
    log_rows = jnp.transpose(final_max + jnp.log(final_total))
    return (attended.reshape(tok_count, H * HD), log_rows)


def attend_queries_back(
    query_rows,
    grad_rows,
    log_rows,
    delta_rows,
    own_keys,
    own_values,
    own_segments,
    own_variates,
    bias_table,
):
    tok_count = query_rows.shape[0]
    query_heads = query_rows.reshape(tok_count, H, HD)
    grad_heads = grad_rows.reshape(tok_count, H, HD)
    log_heads = jnp.transpose(log_rows)
    delta_heads = jnp.transpose(delta_rows)
    shifted_segments = own_segments + 1

    def fold_keys_back(carried, piece_rows):
        key_part, value_part, segment_part, variate_part = piece_rows
        part_count = key_part.shape[0]
        live = shifted_segments[:, None] == segment_part[None, :]

        def update(state):
            grad_query, grad_bias = state
            key_heads = key_part.reshape(part_count, H, HD)
            logits = head_scores(query_heads, key_heads, own_variates, variate_part, bias_table)
            weights = jnp.where(live[None], jnp.exp(logits - log_heads[..., None]), 0.0)
            grad_weights = jnp.einsum(
                "qhd,khd->hqk",
                grad_heads,
                value_part.reshape(part_count, H, HD),
                preferred_element_type=jnp.float32,
            )
            grad_logits = (weights * (grad_weights - delta_heads[..., None])).astype(jnp.bfloat16)
            grad_query = grad_query + SCORE_SCALE * jnp.einsum(
                "hqk,khd->qhd", grad_logits, key_heads, preferred_element_type=jnp.float32
            )
            same_variate = (own_variates[:, None] == variate_part[None, :])[None]
            logit_values = grad_logits.astype(jnp.float32)
            same_total = jnp.sum(jnp.where(same_variate, logit_values, 0.0), axis=(1, 2))
            other_total = jnp.sum(jnp.where(same_variate, 0.0, logit_values), axis=(1, 2))
            return (grad_query, grad_bias + jnp.stack([same_total, other_total]))

        return lax.cond(jnp.any(live), update, lambda state: state, carried)

    state = (jnp.zeros((tok_count, H, HD), jnp.float32), jnp.zeros((2, H), jnp.float32))
    state = fold_keys_back(state, (own_keys, own_values, shifted_segments, own_variates))
    for step in range(2 * REACH):
        arrived = from_behind(
            (own_keys, own_values, shifted_segments, own_variates), "seq", step_offset(step)
        )
        state = fold_keys_back(state, arrived)
    grad_query, grad_bias = state
    return (grad_query.reshape(tok_count, H * HD), grad_bias)


def attend_keys_back(
    query_rows,
    grad_rows,
    log_rows,
    delta_rows,
    own_keys,
    own_values,
    own_segments,
    own_variates,
    bias_table,
):
    tok_count = own_keys.shape[0]
    key_heads = own_keys.reshape(tok_count, H, HD)
    value_heads = own_values.reshape(tok_count, H, HD)
    shifted_segments = own_segments + 1

    def fold_queries(carried, piece_rows):
        query_part, grad_part, log_part, delta_part, segment_part, variate_part = piece_rows
        part_count = query_part.shape[0]
        live = segment_part[:, None] == shifted_segments[None, :]

        def update(state):
            grad_key, grad_value = state
            query_heads = query_part.reshape(part_count, H, HD)
            grad_heads = grad_part.reshape(part_count, H, HD)
            logits = head_scores(query_heads, key_heads, variate_part, own_variates, bias_table)
            weights = jnp.where(
                live[None], jnp.exp(logits - jnp.transpose(log_part)[..., None]), 0.0
            )
            grad_value = grad_value + jnp.einsum(
                "hqk,qhd->khd",
                weights.astype(jnp.bfloat16),
                grad_heads,
                preferred_element_type=jnp.float32,
            )
            grad_weights = jnp.einsum(
                "qhd,khd->hqk", grad_heads, value_heads, preferred_element_type=jnp.float32
            )
            grad_logits = (weights * (grad_weights - jnp.transpose(delta_part)[..., None])).astype(
                jnp.bfloat16
            )
            grad_key = grad_key + SCORE_SCALE * jnp.einsum(
                "hqk,qhd->khd", grad_logits, query_heads, preferred_element_type=jnp.float32
            )
            return (grad_key, grad_value)

        return lax.cond(jnp.any(live), update, lambda state: state, carried)

    state = (jnp.zeros((tok_count, H, HD), jnp.float32), jnp.zeros((tok_count, H, HD), jnp.float32))
    state = fold_queries(
        state, (query_rows, grad_rows, log_rows, delta_rows, shifted_segments, own_variates)
    )
    for step in range(2 * REACH):
        arrived = (
            from_behind(query_rows, "seq", step_offset(step)),
            from_behind(grad_rows, "seq", step_offset(step)),
            from_behind(log_rows.astype(jnp.bfloat16), "seq", step_offset(step)).astype(
                log_rows.dtype
            ),
            from_behind(delta_rows.astype(jnp.bfloat16), "seq", step_offset(step)).astype(
                delta_rows.dtype
            ),
            from_behind(shifted_segments, "seq", step_offset(step)),
            from_behind(own_variates, "seq", step_offset(step)),
        )
        state = fold_queries(state, arrived)
    grad_key, grad_value = state
    return (grad_key.reshape(tok_count, H * HD), grad_value.reshape(tok_count, H * HD))


def norm_back(grad_normed, normed, scale_rows):
    return scale_rows * (grad_normed - normed * jnp.mean(grad_normed * normed, -1, keepdims=True))


def on_device(
    inputs,
    w_query,
    w_key,
    w_value,
    w_output,
    gain_attention,
    w_gate,
    w_up,
    w_down,
    gain_feed,
    variate_bias,
    segment_ids,
    variate_ids,
    positions,
    grad_output,
):
    micro_count = inputs.shape[0]
    tok_count = inputs.shape[2]
    row_count = micro_count * tok_count
    residual_in = inputs.reshape(row_count, D).astype(jnp.float32)
    cotangent = grad_output.reshape(row_count, D).astype(jnp.float32)
    segment_rows = segment_ids.reshape(micro_count, tok_count)
    variate_rows = variate_ids.reshape(micro_count, tok_count)
    position_rows = positions.reshape(row_count)
    full_query, full_key, full_value, full_output, full_gain_first = (
        lax.all_gather(w_query, "seq", axis=0, tiled=True),
        lax.all_gather(w_key, "seq", axis=0, tiled=True),
        lax.all_gather(w_value, "seq", axis=0, tiled=True),
        lax.all_gather(w_output, "seq", axis=0, tiled=True),
        lax.all_gather(gain_attention, "seq", axis=0, tiled=True),
    )
    full_gate, full_up, full_down, full_gain_second = (
        lax.all_gather(w_gate, "seq", axis=0, tiled=True),
        lax.all_gather(w_up, "seq", axis=0, tiled=True),
        lax.all_gather(w_down, "seq", axis=0, tiled=True),
        lax.all_gather(gain_feed, "seq", axis=0, tiled=True),
    )
    scale_first = lax.rsqrt(jnp.mean(residual_in * residual_in, -1, keepdims=True) + EPSILON)
    normed_first = residual_in * scale_first
    mixed_first = (normed_first * full_gain_first.astype(jnp.float32)).astype(jnp.bfloat16)
    query_proj = jnp.dot(mixed_first, full_query, preferred_element_type=jnp.float32)
    key_proj = jnp.dot(mixed_first, full_key, preferred_element_type=jnp.float32)
    value_proj = jnp.dot(mixed_first, full_value, preferred_element_type=jnp.float32)
    query_rows = rotary(query_proj, position_rows, 1.0).astype(jnp.bfloat16)
    key_rows = rotary(key_proj, position_rows, 1.0).astype(jnp.bfloat16)
    value_rows = value_proj.astype(jnp.bfloat16)
    attended_parts = []
    log_parts = []
    for micro_index in range(micro_count):
        lower_row = micro_index * tok_count
        upper_row = lower_row + tok_count
        attended_part, log_part = attend_forward(
            query_rows[lower_row:upper_row],
            key_rows[lower_row:upper_row],
            value_rows[lower_row:upper_row],
            segment_rows[micro_index],
            variate_rows[micro_index],
            variate_bias,
        )
        attended_parts.append(attended_part)
        log_parts.append(log_part)
    attended_all = jnp.concatenate(attended_parts, 0)
    attended_low = attended_all.astype(jnp.bfloat16)
    middle = residual_in + jnp.dot(attended_low, full_output, preferred_element_type=jnp.float32)
    scale_second = lax.rsqrt(jnp.mean(middle * middle, -1, keepdims=True) + EPSILON)
    normed_second = middle * scale_second
    mixed_second = (normed_second * full_gain_second.astype(jnp.float32)).astype(jnp.bfloat16)
    gate_proj = jnp.dot(mixed_second, full_gate, preferred_element_type=jnp.float32)
    up_proj = jnp.dot(mixed_second, full_up, preferred_element_type=jnp.float32)
    sigmoid_gate = jax.nn.sigmoid(gate_proj)
    silu_gate = gate_proj * sigmoid_gate
    hidden_rows = (silu_gate * up_proj).astype(jnp.bfloat16)
    block_rows = middle + jnp.dot(hidden_rows, full_down, preferred_element_type=jnp.float32)
    block_output = block_rows.astype(jnp.bfloat16).reshape(inputs.shape)
    full_query, full_key, full_value, full_output, full_gain_first = (
        lax.all_gather(w_query, "seq", axis=0, tiled=True),
        lax.all_gather(w_key, "seq", axis=0, tiled=True),
        lax.all_gather(w_value, "seq", axis=0, tiled=True),
        lax.all_gather(w_output, "seq", axis=0, tiled=True),
        lax.all_gather(gain_attention, "seq", axis=0, tiled=True),
    )
    full_gate, full_up, full_down, full_gain_second = (
        lax.all_gather(w_gate, "seq", axis=0, tiled=True),
        lax.all_gather(w_up, "seq", axis=0, tiled=True),
        lax.all_gather(w_down, "seq", axis=0, tiled=True),
        lax.all_gather(gain_feed, "seq", axis=0, tiled=True),
    )
    grad_branch_second = cotangent.astype(jnp.bfloat16)
    grad_down = jnp.einsum(
        "rf,rd->fd", hidden_rows, grad_branch_second, preferred_element_type=jnp.float32
    )
    grad_hidden = jnp.einsum(
        "rd,fd->rf", grad_branch_second, full_down, preferred_element_type=jnp.float32
    )
    silu_slope = sigmoid_gate * (1.0 + gate_proj * (1.0 - sigmoid_gate))
    grad_gate_rows = (grad_hidden * up_proj * silu_slope).astype(jnp.bfloat16)
    grad_up_rows = (grad_hidden * silu_gate).astype(jnp.bfloat16)
    grad_gate = jnp.einsum(
        "rd,rf->df", mixed_second, grad_gate_rows, preferred_element_type=jnp.float32
    )
    grad_up = jnp.einsum(
        "rd,rf->df", mixed_second, grad_up_rows, preferred_element_type=jnp.float32
    )
    grad_mixed_second = jnp.einsum(
        "rf,df->rd", grad_gate_rows, full_gate, preferred_element_type=jnp.float32
    ) + jnp.einsum("rf,df->rd", grad_up_rows, full_up, preferred_element_type=jnp.float32)
    grad_gain_second = jnp.sum(grad_mixed_second * normed_second, 0)
    grad_middle = cotangent + norm_back(
        grad_mixed_second * full_gain_second.astype(jnp.float32), normed_second, scale_second
    )
    grad_branch_first = grad_middle.astype(jnp.bfloat16)
    grad_out_proj = jnp.einsum(
        "rd,re->de", attended_low, grad_branch_first, preferred_element_type=jnp.float32
    )
    grad_attended = jnp.einsum(
        "re,de->rd", grad_branch_first, full_output, preferred_element_type=jnp.float32
    ).astype(jnp.bfloat16)
    delta_all = jnp.einsum(
        "rhd,rhd->rh",
        grad_attended.astype(jnp.float32).reshape(row_count, H, HD),
        attended_all.reshape(row_count, H, HD),
    )
    grad_bias_local = jnp.zeros((2, H), jnp.float32)
    query_grad_parts = []
    key_grad_parts = []
    value_grad_parts = []
    for micro_index in range(micro_count):
        lower_row = micro_index * tok_count
        upper_row = lower_row + tok_count
        query_grad_part, bias_part = attend_queries_back(
            query_rows[lower_row:upper_row],
            grad_attended[lower_row:upper_row],
            log_parts[micro_index],
            delta_all[lower_row:upper_row],
            key_rows[lower_row:upper_row],
            value_rows[lower_row:upper_row],
            segment_rows[micro_index],
            variate_rows[micro_index],
            variate_bias,
        )
        key_grad_part, value_grad_part = attend_keys_back(
            query_rows[lower_row:upper_row],
            grad_attended[lower_row:upper_row],
            log_parts[micro_index],
            delta_all[lower_row:upper_row],
            key_rows[lower_row:upper_row],
            value_rows[lower_row:upper_row],
            segment_rows[micro_index],
            variate_rows[micro_index],
            variate_bias,
        )
        grad_bias_local = grad_bias_local + bias_part
        query_grad_parts.append(query_grad_part)
        key_grad_parts.append(key_grad_part)
        value_grad_parts.append(value_grad_part)
    grad_query_rows = rotary(jnp.concatenate(query_grad_parts, 0), position_rows, -1.0).astype(
        jnp.bfloat16
    )
    grad_key_rows = rotary(jnp.concatenate(key_grad_parts, 0), position_rows, -1.0).astype(
        jnp.bfloat16
    )
    grad_value_rows = jnp.concatenate(value_grad_parts, 0).astype(jnp.bfloat16)
    grad_query = jnp.einsum(
        "rd,re->de", mixed_first, grad_query_rows, preferred_element_type=jnp.float32
    )
    grad_key = jnp.einsum(
        "rd,re->de", mixed_first, grad_key_rows, preferred_element_type=jnp.float32
    )
    grad_value = jnp.einsum(
        "rd,re->de", mixed_first, grad_value_rows, preferred_element_type=jnp.float32
    )
    grad_mixed_first = (
        jnp.einsum("re,de->rd", grad_query_rows, full_query, preferred_element_type=jnp.float32)
        + jnp.einsum("re,de->rd", grad_key_rows, full_key, preferred_element_type=jnp.float32)
        + jnp.einsum("re,de->rd", grad_value_rows, full_value, preferred_element_type=jnp.float32)
    )
    grad_gain_first = jnp.sum(grad_mixed_first * normed_first, 0)
    grad_input_rows = grad_middle + norm_back(
        grad_mixed_first * full_gain_first.astype(jnp.float32), normed_first, scale_first
    )
    grad_inputs = grad_input_rows.reshape(inputs.shape)
    (
        shard_query,
        shard_key,
        shard_value,
        shard_output,
        shard_gain_first,
        shard_gate,
        shard_up,
        shard_down,
        shard_gain_second,
    ) = (
        lax.psum_scatter(grad_query, "seq", scatter_dimension=0, tiled=True),
        lax.psum_scatter(grad_key, "seq", scatter_dimension=0, tiled=True),
        lax.psum_scatter(grad_value, "seq", scatter_dimension=0, tiled=True),
        lax.psum_scatter(grad_out_proj, "seq", scatter_dimension=0, tiled=True),
        lax.psum_scatter(grad_gain_first, "seq", scatter_dimension=0, tiled=True),
        lax.psum_scatter(grad_gate, "seq", scatter_dimension=0, tiled=True),
        lax.psum_scatter(grad_up, "seq", scatter_dimension=0, tiled=True),
        lax.psum_scatter(grad_down, "seq", scatter_dimension=0, tiled=True),
        lax.psum_scatter(grad_gain_second, "seq", scatter_dimension=0, tiled=True),
    )
    summed = (
        lax.psum(shard_query.astype(jnp.bfloat16), "batch").astype(jnp.float32),
        lax.psum(shard_key.astype(jnp.bfloat16), "batch").astype(jnp.float32),
        lax.psum(shard_value.astype(jnp.bfloat16), "batch").astype(jnp.float32),
        lax.psum(shard_output.astype(jnp.bfloat16), "batch").astype(jnp.float32),
        lax.psum(shard_gain_first.astype(jnp.bfloat16), "batch").astype(jnp.float32),
        lax.psum(shard_gate.astype(jnp.bfloat16), "batch").astype(jnp.float32),
        lax.psum(shard_up.astype(jnp.bfloat16), "batch").astype(jnp.float32),
        lax.psum(shard_down.astype(jnp.bfloat16), "batch").astype(jnp.float32),
        lax.psum(shard_gain_second.astype(jnp.bfloat16), "batch").astype(jnp.float32),
    )
    grad_bias_total = lax.psum(grad_bias_local, ("batch", "seq"))
    return (
        block_output,
        grad_inputs,
        summed[0],
        summed[1],
        summed[2],
        summed[3],
        summed[4],
        summed[5],
        summed[6],
        summed[7],
        summed[8],
        grad_bias_total,
    )


ORDER_A = (0, 1, 2, 3)
ORDER_B = (0, 2, 1, 3)
FEATURES = 128
LSE_AT = 64
LOW = jnp.bfloat16
WIDE = jnp.float32


def swap(value, bit):
    return lax.ppermute(value, "batch", [(i, i ^ bit) for i in range(4)])


def after(value, *others):
    return lax.optimization_barrier((value, *others))[0]


def gather_plane(own):
    half = own.shape[0] // 2
    lower, upper = own[:half], own[half:]
    lower_pair = jnp.concatenate([lower, swap(lower, 1)], 0)
    upper_pair = jnp.concatenate([upper, swap(upper, 2)], 0)
    return lower_pair, swap(lower_pair, 2), upper_pair, swap(upper_pair, 1)


def scatter_first(chunks):
    return swap(chunks[1], 2), swap(chunks[3], 1)


def scatter_second(chunks, got):
    near_lower, _, near_upper, _ = chunks
    got_lower, got_upper = got
    half = near_lower.shape[0] // 2
    last_lower = swap(near_lower[half:] + got_lower[half:], 1)
    last_upper = swap(near_upper[half:] + got_upper[half:], 2)
    return (near_lower, got_lower, last_lower, near_upper, got_upper, last_upper)


def swap_pairs(own):
    half = own.shape[0] // 2
    return swap(own[:half], 1), swap(own[half:], 2)


def far_pairs(own, got):
    half = own.shape[0] // 2
    lower_pair = jnp.concatenate([own[:half], got[0]], 0)
    upper_pair = jnp.concatenate([own[half:], got[1]], 0)
    return lower_pair, swap(lower_pair, 2), upper_pair, swap(upper_pair, 1)


def over_seq(pieces):
    count, quarter, width = pieces.shape
    return lax.all_to_all(pieces, "seq", 0, 0, tiled=True).reshape(count * quarter, width)


def three_parts(value):
    high = value.astype(LOW)
    rest = value - high.astype(WIDE)
    middle = rest.astype(LOW)
    low = (rest - middle.astype(WIDE)).astype(LOW)
    return high, middle, low


def token_features(segments, variates):
    lane = lax.broadcasted_iota(jnp.int32, (segments.shape[0], FEATURES), 1)
    variate_hot = (lane < 12) & (lane % 4 == variates)
    ones = (lane >= 12) & (lane < 15)
    segment_lane = (lane >= 16) & (lane < LSE_AT)
    segment_hot = segment_lane & (lane - 16 == segments)
    segment_cold = segment_lane & (lane - 16 != segments)
    query_side = variate_hot | ones | segment_hot
    key_side = variate_hot | ones | segment_cold | ((lane >= LSE_AT) & (lane < LSE_AT + 3))
    return jnp.where(query_side, 1.0, 0.0).astype(LOW), jnp.where(key_side, 1.0, 0.0).astype(LOW)


def head_weights(same_bias, other_bias):
    gap = [part[:, None] for part in three_parts(same_bias - other_bias)]
    base = [part[:, None] for part in three_parts(other_bias)]
    heads = same_bias.shape[0]
    columns = [jnp.broadcast_to(part, (heads, 4)) for part in gap] + base
    columns.append(jnp.zeros((heads, 1), LOW))
    columns.append(jnp.full((heads, LSE_AT - 16), MASKED, LOW))
    columns.append(jnp.zeros((heads, FEATURES - LSE_AT), LOW))
    return jnp.concatenate(columns, 1)


def turn_pair(pair, cosine, sine):
    lane = lax.broadcasted_iota(jnp.int32, pair.shape, 1)
    crossed = jnp.where(lane % 64 < 32, pltpu.roll(pair, 96, 1), pltpu.roll(pair, 32, 1))
    return pair * cosine + crossed * sine


def dot_plain(left, right):
    return jnp.dot(left, right, preferred_element_type=WIDE)


def dot_rows(left, right):
    return lax.dot_general(left, right, (((1,), (1,)), ((), ())), preferred_element_type=WIDE)


def dot_first(left, right):
    return lax.dot_general(left, right, (((0,), (0,)), ((), ())), preferred_element_type=WIDE)


def whole_block():
    return pl.BlockSpec(memory_space=pltpu.VMEM)


def column_block(rows, columns, place):
    return pl.BlockSpec((rows, columns), lambda i, place=place: (0, place))


def call(kernel, name, outs, specs, flops, moved, args, scratch=()):
    return pl.pallas_call(
        kernel,
        grid=(1,),
        out_shape=[jax.ShapeDtypeStruct(shape, dtype) for shape, dtype in outs],
        in_specs=specs,
        out_specs=[pl.BlockSpec(memory_space=pltpu.VMEM) for _ in outs],
        scratch_shapes=list(scratch),
        cost_estimate=pl.CostEstimate(flops=flops, bytes_accessed=moved, transcendentals=0),
        compiler_params=pltpu.CompilerParams(vmem_limit_bytes=56 * 2**20),
        name=name,
    )(*args)


def unit_rows(rows):
    return lax.rsqrt(jnp.mean(rows * rows, -1, keepdims=True) + EPSILON)


def pack_first_kernel(
    rank_ref, x_ref, cot_ref, segment_ref, variate_ref, position_ref, wq_ref, wk_ref, wv_ref, wo_ref,
    gain_first_ref, gain_second_ref, rows_ref, shard_ref,
):
    rank = rank_ref[0]
    micro, tokens, _ = x_ref.shape
    quarter = tokens // 4
    columns = pl.ds(pl.multiple_of(rank * 256, 256), 256)
    shard_ref[:, :D] = wo_ref[...]
    shard_ref[:, D : D + 256] = wq_ref[:, columns]
    shard_ref[:, D + 256 : D + 512] = wk_ref[:, columns]
    shard_ref[:, D + 512 : D + 768] = wv_ref[:, columns]
    lane = lax.broadcasted_iota(jnp.int32, (tokens, 128), 1)
    on_line = lax.broadcasted_iota(jnp.int32, (tokens, 128), 0) == lane

    def upright(row):
        return jnp.sum(jnp.where(on_line, row, 0.0), 1, keepdims=True)

    gains = jnp.where(
        lane == 0,
        upright(gain_first_ref[...].astype(WIDE)),
        jnp.where(lane == 1, upright(gain_second_ref[...].astype(WIDE)), 0.0),
    )
    shard_ref[:, D + 768 :] = gains.astype(LOW)
    for m in range(micro):
        places = position_ref[m : m + 1, :]
        numbers = jnp.zeros((tokens, 128), WIDE)
        for place, row in enumerate(
            (
                segment_ref[m : m + 1, :],
                variate_ref[m : m + 1, :],
                lax.shift_right_logical(places, 5),
                places & 31,
            )
        ):
            numbers = jnp.where(lane == place, upright(row.astype(WIDE)), numbers)
        numbers = numbers.astype(LOW)
        for r in range(4):
            rows = slice(r * quarter, (r + 1) * quarter)
            rows_ref[r, 0, m, :, :D] = x_ref[m, rows, :]
            rows_ref[r, 0, m, :, D:] = numbers[rows, :]
            rows_ref[r, 1, m, :, :D] = cot_ref[m, rows, :]
            rows_ref[r, 1, m, :, D:] = jnp.zeros((quarter, 128), LOW)


def pack_first(rank, x, cot, segments, variates, positions, shards, gains):
    micro, tokens, _ = x.shape
    return call(
        pack_first_kernel,
        "pack_first",
        [((4, 2, micro, tokens // 4, D + 128), LOW), ((shards[0].shape[0], D + 896), LOW)],
        [pl.BlockSpec(memory_space=pltpu.SMEM)] + [whole_block()] * 11,
        x.size,
        3 * 2**20,
        (rank, x, cot, segments, variates, positions, *shards, *gains),
    )


def pack_feed_kernel(rank_ref, gate_ref, up_ref, down_ref, gate_up_ref, out_ref):
    rank = rank_ref[0]
    piece = out_ref.shape[0]
    per = gate_up_ref.shape[1] // 2
    for s in range(per // piece):
        source = pl.ds(pl.multiple_of((4 * s + rank) * piece, piece), piece)
        gate_up_ref[:, s * piece : (s + 1) * piece] = gate_ref[:, source]
        gate_up_ref[:, per + s * piece : per + (s + 1) * piece] = up_ref[:, source]
    out_ref[...] = down_ref[pl.ds(pl.multiple_of(rank * piece, piece), piece), :]


def pack_feed(rank, w_gate, w_up, w_down):
    shard, ff = w_gate.shape
    return call(
        pack_feed_kernel,
        "pack_feed",
        [((shard, ff // 2), LOW), ((w_down.shape[0] // 4, D), LOW)],
        [pl.BlockSpec(memory_space=pltpu.SMEM)] + [whole_block()] * 3,
        shard * ff,
        4 * 2**20,
        (rank, w_gate, w_up, w_down),
    )


def attend_kernel(
    x0, x1, x2, x3, wq_ref, wk_ref, wv_ref, gains_ref, freqs_ref, weights_ref,
    gain_ref, mixed_ref, turned_ref, wide_ref, lower_ref, upper_ref, log_ref, cos_ref, sin_ref,
    query_side_ref, key_side_ref, keys_ref, values_ref,
):
    chunk = x0.shape[0]
    lane = lax.broadcasted_iota(jnp.int32, (chunk, 128), 1)
    half_lane = lane // 64
    pick = lax.broadcasted_iota(jnp.int32, (16, 128), 0) == lax.broadcasted_iota(
        jnp.int32, (16, 128), 1
    )
    gain_ref[...] = dot_rows(jnp.where(pick, 1.0, 0.0).astype(LOW), gains_ref[...])
    for place, x_ref in enumerate((x0, x1, x2, x3)):
        rows = slice(place * chunk, (place + 1) * chunk)
        x = x_ref[:, :D].astype(WIDE)
        mixed = (x * unit_rows(x) * gain_ref[0:1, :]).astype(LOW)
        mixed_ref[rows, :] = mixed
        numbers = x_ref[:, D : D + 128].astype(WIDE)
        angles = (numbers[:, 2:3] * 32.0 + numbers[:, 3:4]) * freqs_ref[...]
        cosine = jnp.cos(angles)
        sine = jnp.sin(angles)
        sine = jnp.where(lane % 64 < 32, -sine, sine)
        cos_ref[rows, :] = cosine
        sin_ref[rows, :] = sine
        numbers = numbers.astype(jnp.int32)
        query_side, key_side = token_features(numbers[:, 0:1], numbers[:, 1:2])
        query_side_ref[rows, :] = query_side
        key_side_ref[rows, :] = key_side
        queries = dot_plain(mixed, wq_ref[...])
        keys = dot_plain(mixed, wk_ref[...])
        values = dot_plain(mixed, wv_ref[...]).astype(LOW)
        turned_ref[rows, 512:768] = values
        for pair in range(2):
            at = 128 * pair
            turned_ref[rows, at : at + 128] = turn_pair(
                queries[:, at : at + 128], cosine, sine
            ).astype(LOW)
            turned = turn_pair(keys[:, at : at + 128], cosine, sine).astype(LOW)
            turned_ref[rows, 256 + at : 384 + at] = turned
            keys_ref[pair, rows, :128] = turned
            keys_ref[pair, rows, 128:] = key_side
            values_ref[pair, rows, :128] = values[:, at : at + 128]
            values_ref[pair, rows, 128:] = jnp.where(lane == 0, 1.0, 0.0).astype(LOW)

    for part, low_ref in enumerate((lower_ref, upper_ref)):

        def one_block(index, carry, part=part, low_ref=low_ref):
            here = pl.ds(pl.multiple_of(index * chunk, chunk), chunk)
            rows = pl.ds(pl.multiple_of((2 * part + index) * chunk, chunk), chunk)
            side = query_side_ref[rows, :]
            logs = jnp.zeros((chunk, 128), WIDE)
            for pair in range(2):
                at = 128 * pair
                scaled = turned_ref[rows, at : at + 128] * LOW(SCORE_SCALE)
                mixed = jnp.zeros((chunk, 128), WIDE)
                for half in range(2):
                    head = 2 * pair + half
                    query = jnp.concatenate(
                        [
                            jnp.where(half_lane == half, scaled, LOW(0)),
                            side * weights_ref[head : head + 1, :],
                        ],
                        1,
                    )
                    scores = dot_rows(query, keys_ref[pair])
                    top = jnp.max(scores, 1, keepdims=True)
                    powers = jnp.exp(scores - top).astype(LOW)
                    summed = dot_plain(powers, values_ref[pair])
                    total = summed[:, 128:129]
                    mixed = jnp.where(half_lane == half, summed[:, :128] / total, mixed)
                    logs = jnp.where(lane == head, top + jnp.log(total), logs)
                wide_ref[rows, at : at + 128] = mixed
                low_ref[here, at : at + 128] = mixed.astype(LOW)
            log_ref[rows, :] = logs
            return carry

        lax.fori_loop(0, 2, one_block, 0)


def attend(chunks, first_weights, freqs, weights):
    chunk = chunks[0].shape[0]
    length = 4 * chunk
    return call(
        attend_kernel,
        "attend",
        [
            ((16, D), WIDE),
            ((length, D), LOW),
            ((length, 768), LOW),
            ((length, 256), WIDE),
            ((length // 2, 256), LOW),
            ((length // 2, 256), LOW),
            ((length, 128), WIDE),
            ((length, 128), WIDE),
            ((length, 128), WIDE),
            ((length, FEATURES), LOW),
            ((length, FEATURES), LOW),
        ],
        [whole_block()] * 4
        + [column_block(D, 256, place) for place in (4, 5, 6)]
        + [column_block(D, 128, 14)]
        + [whole_block()] * 2,
        16 * length * length * 256 + 2 * length * D * 768,
        8 * 2**20,
        (*chunks, *[first_weights] * 4, freqs, weights),
        [pltpu.VMEM((2, length, 256), LOW)] * 2,
    )


def middle_kernel(
    rank_ref, x0, x1, x2, x3, lower_ref, lower_x_ref, lower_far_ref, upper_ref, upper_y_ref,
    upper_far_ref, wo_ref, gain_ref, heads_ref, own_ref, mixed_ref,
):
    rank = rank_ref[0]
    chunk = x0.shape[0]
    block = chunk // 2
    half_rows = 2 * chunk
    wide = lower_ref.shape[1]
    sources = {
        0: ((lower_ref, 0), (lower_x_ref, 0), (lower_far_ref, 0), (lower_far_ref, wide)),
        1: ((upper_ref, 0), (upper_far_ref, 0), (upper_y_ref, 0), (upper_far_ref, wide)),
    }
    for part, order in enumerate((ORDER_A, ORDER_B)):
        for place, r in enumerate(order):
            for q in range(4):
                ref, column = sources[part][q]
                start = order.index(r ^ q) * block
                heads_ref[
                    part * half_rows + place * block : part * half_rows + (place + 1) * block,
                    q * wide : (q + 1) * wide,
                ] = ref[start : start + block, column : column + wide]
    for place, x_ref in enumerate((x0, x1, x2, x3)):
        rows = slice(place * chunk, (place + 1) * chunk)
        total = x_ref[:, :D].astype(WIDE)
        for q in range(4):
            out_rows = pl.ds(pl.multiple_of((rank ^ q) * wide, wide), wide)
            total = total + dot_plain(
                heads_ref[rows, q * wide : (q + 1) * wide], wo_ref[out_rows, :]
            )
        if place % 2 == 0:
            own_ref[place // 2 * block : (place // 2 + 1) * block, :] = total[:block]
        mixed_ref[rows, :] = (total * unit_rows(total) * gain_ref[1:2, :]).astype(LOW)


def middle(rank, chunks, heads, first_weights, gain):
    chunk = chunks[0].shape[0]
    length = 4 * chunk
    return call(
        middle_kernel,
        "middle",
        [((length, D), LOW), ((chunk, D), WIDE), ((length, D), LOW)],
        [pl.BlockSpec(memory_space=pltpu.SMEM)]
        + [whole_block()] * 10
        + [column_block(D, D, 0), whole_block()],
        2 * length * D * D,
        8 * 2**20,
        (rank, *chunks, *heads, first_weights, gain),
    )


def feed_kernel(mixed_ref, gate_up_ref, both_ref, hidden_ref):
    length, per = hidden_ref.shape
    chunk = length // 4
    for place in range(4):
        rows = slice(place * chunk, (place + 1) * chunk)
        both = dot_plain(mixed_ref[rows, :], gate_up_ref[...])
        both_ref[rows, :] = both
        gate, up = both[:, :per], both[:, per:]
        hidden_ref[rows, :] = (gate / (1.0 + jnp.exp(-gate)) * up).astype(LOW)


def feed(mixed, gate_up):
    length = mixed.shape[0]
    per = gate_up.shape[1] // 2
    return call(
        feed_kernel,
        "feed",
        [((length, 2 * per), WIDE), ((length, per), LOW)],
        [whole_block()] * 2,
        4 * length * D * per,
        16 * 2**20,
        (mixed, gate_up),
    )


def feed_back_kernel(
    both_ref, c0, c1, c2, c3, gate_up_ref, down_ref, grads_ref, back0, back1, back2, back3
):
    chunk = c0.shape[0]
    per = down_ref.shape[0]
    for place, (cot_ref, back_ref) in enumerate(
        zip((c0, c1, c2, c3), (back0, back1, back2, back3))
    ):
        rows = slice(place * chunk, (place + 1) * chunk)
        gate, up = both_ref[rows, :per], both_ref[rows, per:]
        grad_hidden = dot_rows(cot_ref[...], down_ref[...])
        sigmoid = 1.0 / (1.0 + jnp.exp(-gate))
        grads_ref[rows, :per] = (
            grad_hidden * up * (sigmoid * (1.0 + gate * (1.0 - sigmoid)))
        ).astype(LOW)
        grads_ref[rows, per:] = (grad_hidden * (gate * sigmoid)).astype(LOW)
        back_ref[...] = dot_rows(grads_ref[rows, :], gate_up_ref[...]).astype(LOW)


def feed_back(both, cots, gate_up, down):
    length = both.shape[0]
    per = down.shape[0]
    return call(
        feed_back_kernel,
        "feed_back",
        [((length, 2 * per), LOW)] + [((length // 4, D), LOW)] * 4,
        [whole_block()] * 7,
        6 * length * D * per,
        16 * 2**20,
        (both, *cots, gate_up, down),
    )


def own_back_kernel(
    rank_ref, n0, g0, l0, n1, g1, l1, middle_ref, cot_ref, gain_ref, wo_ref,
    grad_ref, p0, p1, p2, p3,
):
    rank = rank_ref[0]
    block = l0.shape[0]
    wide = 256
    for place, (near, got, last) in enumerate(((n0, g0, l0), (n1, g1, l1))):
        rows = slice(place * block, (place + 1) * block)
        arrived = (
            near[:block].astype(WIDE) + got[:block].astype(WIDE) + last[...].astype(WIDE)
        )
        y = middle_ref[rows, :]
        scale = unit_rows(y)
        normed = y * scale
        turned = arrived * gain_ref[1:2, :]
        grad_ref[rows, :] = cot_ref[rows, :].astype(WIDE) + scale * (
            turned - normed * jnp.mean(turned * normed, -1, keepdims=True)
        )
    grad = grad_ref[...].astype(LOW)
    for q, parcel in enumerate((p0, p1, p2, p3)):
        place = pl.ds(pl.multiple_of((rank ^ q) * wide, wide), wide)
        parcel[:, :wide] = dot_rows(grad, wo_ref[place, :]).astype(LOW)
        parcel[:, wide:] = grad_ref[:, place].astype(LOW)


def own_back(rank, sums, middle_own, cot_own, gain, first_weights):
    quarter = cot_own.shape[0]
    return call(
        own_back_kernel,
        "own_back",
        [((quarter, D), WIDE)] + [((quarter, 512), LOW)] * 4,
        [pl.BlockSpec(memory_space=pltpu.SMEM)]
        + [whole_block()] * 9
        + [column_block(D, D, 0)],
        2 * quarter * D * D,
        8 * 2**20,
        (rank, *sums, middle_own, cot_own, gain, first_weights),
    )


def attend_back_kernel(
    pair, p0, p1, p2, p3, q_ref, k_ref, v_ref, wide_ref, log_ref, cos_ref, sin_ref,
    query_side_ref, key_side_ref, weights_ref, out_ref, bias_ref,
    queries_ref, grads_ref, total_ref,
):
    length = q_ref.shape[0]
    chunk = length // 4
    block = chunk // 2
    at = 128 * pair
    parcels = (p0, p1, p2, p3)
    half_lane = lax.broadcasted_iota(jnp.int32, (chunk, 128), 1) // 64
    lane = lax.broadcasted_iota(jnp.int32, (chunk, 128), 1)
    for part, order in enumerate((ORDER_A, ORDER_B)):
        for place in range(4):
            source = parcels[order[place]]
            to = slice((4 * part + place) * block, (4 * part + place + 1) * block)
            rows = slice(part * block, (part + 1) * block)
            for half in range(2):
                grads_ref[half, to, :128] = source[rows, at : at + 128]

    def prepare(index, carry):
        rows = pl.ds(pl.multiple_of(index * chunk, chunk), chunk)
        product = grads_ref[0, rows, :128].astype(WIDE) * wide_ref[rows, :]
        scaled = q_ref[rows, :] * LOW(SCORE_SCALE)
        for half in range(2):
            head = 2 * pair + half
            side = query_side_ref[rows, :] * weights_ref[head : head + 1, :]
            for place, part in enumerate(three_parts(-log_ref[rows, head : head + 1])):
                side = jnp.where(lane == LSE_AT + place, part, side)
            queries_ref[half, rows, :128] = jnp.where(half_lane == half, scaled, LOW(0))
            queries_ref[half, rows, 128:] = side
            delta = jnp.sum(jnp.where(half_lane == half, product, 0.0), 1, keepdims=True)
            extra = jnp.zeros((chunk, 128), LOW)
            for place, part in enumerate(three_parts(-delta)):
                extra = jnp.where(lane == place, part, extra)
            grads_ref[half, rows, 128:] = extra
        total_ref[rows, :] = jnp.zeros((chunk, 128), WIDE)
        return carry

    lax.fori_loop(0, 4, prepare, 0)
    three_ones = jnp.where(lane < 3, 1.0, 0.0).astype(LOW)

    def one_block(index, carry):
        rows = pl.ds(pl.multiple_of(index * chunk, chunk), chunk)
        cosine = cos_ref[rows, :]
        sine = -sin_ref[rows, :]
        key_side = key_side_ref[rows, :]
        first_four = jnp.where(lane < 4, key_side.astype(WIDE), 0.0)
        sums = list(carry)
        keys = k_ref[rows, :]
        values = v_ref[rows, :]
        keys_wide = jnp.concatenate([keys, key_side], 1)
        grad_keys = jnp.zeros((chunk, 128), WIDE)
        grad_values = jnp.zeros((chunk, 128), WIDE)
        for half in range(2):
            mine = half_lane == half
            weights = jnp.exp(dot_rows(keys_wide, queries_ref[half]))
            grad_weights = dot_rows(
                jnp.concatenate([jnp.where(mine, values, LOW(0)), three_ones], 1), grads_ref[half]
            )
            grad_values = jnp.where(
                mine, dot_plain(weights.astype(LOW), grads_ref[half, :, :128]), grad_values
            )
            grad_scores = (weights * grad_weights).astype(LOW)
            both = dot_plain(
                grad_scores,
                jnp.concatenate([queries_ref[half, :, :128], query_side_ref[...]], 1),
            )
            grad_keys = grad_keys + both[:, :128]
            counted = both[:, 128:]
            same = jnp.sum(counted * first_four, 0, keepdims=True)
            every = jnp.sum(jnp.where(lane < 4, counted, 0.0), 0, keepdims=True)
            sums[half] = sums[half] + same
            sums[2 + half] = sums[2 + half] + (every - same)
            total_ref[...] += dot_first(grad_scores, jnp.where(mine, keys, LOW(0)))
        out_ref[rows, 128:256] = turn_pair(grad_keys, cosine, sine).astype(LOW)
        out_ref[rows, 256:] = grad_values.astype(LOW)
        return tuple(sums)

    start = tuple(jnp.zeros((1, 128), WIDE) for _ in range(4))
    sums = lax.fori_loop(0, 4, one_block, start)
    bias_ref[...] = jnp.zeros_like(bias_ref)
    for place in range(4):
        bias_ref[place : place + 1, :] = sums[place]
    for place in range(4):
        rows = slice(place * chunk, (place + 1) * chunk)
        out_ref[rows, :128] = turn_pair(
            total_ref[rows, :] * SCORE_SCALE, cos_ref[rows, :], -sin_ref[rows, :]
        ).astype(LOW)


def attend_back(pair, parcels, kept, weights):
    turned, attended, *others = kept
    length = turned.shape[0]
    specs = [whole_block()] * 4
    specs += [column_block(length, 128, place) for place in (pair, 2 + pair, 4 + pair, pair)]
    specs += [whole_block()] * 6
    return call(
        functools.partial(attend_back_kernel, pair),
        "attend_back",
        [((length, 384), LOW), ((8, 128), WIDE)],
        specs,
        20 * length * length * 256,
        8 * 2**20,
        (*parcels, turned, turned, turned, attended, *others, weights),
        [
            pltpu.VMEM((2, length, 256), LOW),
            pltpu.VMEM((2, length, 256), LOW),
            pltpu.VMEM((length, 128), WIDE),
        ],
    )


def project_back_kernel(proj0_ref, proj1_ref, *refs):
    weight_refs, back_refs = refs[:6], refs[6:]
    chunk = back_refs[0].shape[0]
    for place, back_ref in enumerate(back_refs):
        rows = slice(place * chunk, (place + 1) * chunk)
        total = jnp.zeros((chunk, D), WIDE)
        for part, weight_ref in enumerate(weight_refs):
            source = (proj0_ref, proj1_ref)[part // 3]
            column = 128 * (part % 3)
            total = total + dot_rows(source[rows, column : column + 128], weight_ref[...])
        back_ref[...] = total.astype(LOW)


def project_back(proj0, proj1, first_weights):
    length = proj0.shape[0]
    return call(
        project_back_kernel,
        "project_back",
        [((length // 4, D), LOW)] * 4,
        [whole_block()] * 2 + [column_block(D, 128, place) for place in (8, 10, 12, 9, 11, 13)],
        2 * length * D * 768,
        6 * 2**20,
        (proj0, proj1, *[first_weights] * 6),
    )


def down_grads_kernel(hidden_ref, c0, c1, c2, c3, out_ref):
    chunk = c0.shape[0]
    step = 256
    for at in range(0, hidden_ref.shape[1], step):
        total = jnp.zeros((step, D), WIDE)
        for place, cot_ref in enumerate((c0, c1, c2, c3)):
            rows = slice(place * chunk, (place + 1) * chunk)
            total = total + dot_first(hidden_ref[rows, at : at + step], cot_ref[...])
        out_ref[at : at + step, :] = total.astype(LOW)


def down_grads(hidden, cots):
    length, per = hidden.shape
    return call(
        down_grads_kernel,
        "down_grads",
        [((per, D), LOW)],
        [whole_block()] * 5,
        2 * length * D * per,
        6 * 2**20,
        (hidden, *cots),
    )[0]


def gate_up_grads_kernel(mixed_ref, grads_ref, out_ref):
    step = 256
    for at in range(0, D, step):
        out_ref[at : at + step, :] = dot_first(
            mixed_ref[:, at : at + step], grads_ref[...]
        ).astype(LOW)


def gate_up_grads(mixed, grads):
    length, width = grads.shape
    return call(
        gate_up_grads_kernel,
        "gate_up_grads",
        [((D, width), LOW)],
        [whole_block()] * 2,
        2 * length * D * width,
        10 * 2**20,
        (mixed, grads),
    )[0]


def feed_out_kernel(hidden_ref, down_ref, o0, o1, o2, o3):
    chunk = o0.shape[0]
    for place, out_ref in enumerate((o0, o1, o2, o3)):
        rows = slice(place * chunk, (place + 1) * chunk)
        out_ref[...] = dot_plain(hidden_ref[rows, :], down_ref[...]).astype(LOW)


def feed_out(hidden, down):
    length = hidden.shape[0]
    return call(
        feed_out_kernel,
        "feed_out",
        [((length // 4, D), LOW)] * 4,
        [whole_block()] * 2,
        2 * length * D * D,
        8 * 2**20,
        (hidden, down),
    )


def own_last_kernel(
    n0, g0, l0, n1, g1, l1, m0, h0, k0, m1, h1, k1, x_ref, base_ref, middle_ref, gain_ref, out_ref
):
    block = l0.shape[0]
    piece = out_ref.shape[1] // 2
    each = block // piece

    def total(near, got, last):
        return near[:block].astype(WIDE) + got[:block].astype(WIDE) + last[...].astype(WIDE)

    for part, (back, out) in enumerate(
        (((n0, g0, l0), (m0, h0, k0)), ((n1, g1, l1), (m1, h1, k1)))
    ):
        rows = slice(part * block, (part + 1) * block)
        places = slice(part * each, (part + 1) * each)
        x = x_ref[rows, :D].astype(WIDE)
        scale = unit_rows(x)
        normed = x * scale
        turned = total(*back) * gain_ref[0:1, :]
        grad = base_ref[rows, :] + scale * (
            turned - normed * jnp.mean(turned * normed, -1, keepdims=True)
        )
        out_ref[places, :piece, :] = grad.astype(LOW).reshape(each, piece, D)
        block_rows = middle_ref[rows, :] + total(*out)
        out_ref[places, piece:, :] = block_rows.astype(LOW).reshape(each, piece, D)


def own_last(sums, out_sums, mine, base, middle_own, gain, n_seq):
    quarter = base.shape[0]
    return call(
        own_last_kernel,
        "own_last",
        [((n_seq, 2 * quarter // n_seq, D), LOW)],
        [whole_block()] * 16,
        base.size,
        6 * 2**20,
        (*sums, *out_sums, mine, base, middle_own, gain),
    )[0]


def first_grads_kernel(
    rank_ref, mixed_ref, proj0_ref, proj1_ref, heads_ref, p0, p1, p2, p3, bias_ref, out_ref,
    branch_ref,
):
    rank = rank_ref[0]
    wide = 256
    block = p0.shape[0] // 2
    parcels = (p0, p1, p2, p3)
    for part, order in enumerate((ORDER_A, ORDER_B)):
        for place in range(4):
            to = slice((4 * part + place) * block, (4 * part + place + 1) * block)
            branch_ref[to, :] = parcels[order[place]][part * block : (part + 1) * block, wide:]
    for at in range(0, D, wide):
        here = slice(at, at + wide)
        for pair, proj_ref in enumerate((proj0_ref, proj1_ref)):
            total = dot_first(mixed_ref[:, here], proj_ref[...]).astype(LOW)
            for kind in range(3):
                column = wide * kind + 128 * pair
                out_ref[here, column : column + 128] = total[:, 128 * kind : 128 * (kind + 1)]
        rows = pl.ds(pl.multiple_of((rank ^ (at // wide)) * wide, wide), wide)
        out_ref[rows, 3 * wide : 4 * wide] = dot_first(
            heads_ref[:, here], branch_ref[...]
        ).astype(LOW)
        out_ref[here, 4 * wide :] = bias_ref[...]


def first_grads(rank, mixed, proj0, proj1, heads, parcels, bias_rows):
    length = mixed.shape[0]
    return call(
        first_grads_kernel,
        "first_grads",
        [((D, 768 + 256 + 128), LOW)],
        [pl.BlockSpec(memory_space=pltpu.SMEM)] + [whole_block()] * 9,
        2 * length * D * D,
        8 * 2**20,
        (rank, mixed, proj0, proj1, heads, *parcels, bias_rows),
        [pltpu.VMEM((length, 256), LOW)],
    )[0]


def rank_blocks(lower, lower_far, upper, upper_far):
    half = lower.shape[0] // 2
    return (
        ((lower, 0), (upper, 0)),
        ((lower, half), (upper_far, 0)),
        ((lower_far, 0), (upper, half)),
        ((lower_far, half), (upper_far, half)),
    )


def lay_flat(column, part):
    count = column.shape[0]
    row = lax.broadcasted_iota(jnp.int32, (count, 128), 0) + part * count
    lane = lax.broadcasted_iota(jnp.int32, (count, 128), 1)
    return jnp.sum(jnp.where(row == lane, column, 0.0), 0, keepdims=True)


def spread_feed_kernel(
    rank_ref, lower, lower_far, upper, upper_far, gate_ref, up_ref, gain_ref,
    grad_gate_ref, grad_up_ref, grad_down_ref, grad_gain_ref,
):
    rank = rank_ref[0]
    half = lower.shape[0] // 2
    piece = 128
    ff = gate_ref.shape[1]
    per = ff // 4
    for r, halves in enumerate(rank_blocks(lower, lower_far, upper, upper_far)):
        for part, (ref, start) in enumerate(halves):
            rows = slice(part * half, (part + 1) * half)
            source = slice(start, start + half)
            for s in range(per // piece):
                to = pl.ds(pl.multiple_of((4 * s + (rank ^ r)) * piece, piece), piece)
                grad_gate_ref[rows, to] = ref[source, s * piece : (s + 1) * piece].astype(WIDE)
                grad_up_ref[rows, to] = ref[source, per + s * piece : per + (s + 1) * piece].astype(
                    WIDE
                )
            to = pl.ds(pl.multiple_of((rank ^ r) * 2 * half + part * half, half), half)
            grad_down_ref[to, :] = ref[source, 2 * per :].astype(WIDE)
    flat = jnp.zeros((1, 128), WIDE)
    for part in range(2):
        rows = slice(part * half, (part + 1) * half)
        total = jnp.sum(
            gate_ref[rows, :].astype(WIDE) * grad_gate_ref[rows, :], 1, keepdims=True
        ) + jnp.sum(up_ref[rows, :].astype(WIDE) * grad_up_ref[rows, :], 1, keepdims=True)
        flat = flat + lay_flat(total, part)
    grad_gain_ref[...] = jnp.broadcast_to(flat / gain_ref[...].astype(WIDE), (8, 128))


def spread_feed(rank, pieces, w_gate, w_up, gain):
    shard, ff = w_gate.shape
    return call(
        spread_feed_kernel,
        "spread_feed",
        [((shard, ff), WIDE), ((shard, ff), WIDE), ((ff // 8, D), WIDE), ((8, 128), WIDE)],
        [pl.BlockSpec(memory_space=pltpu.SMEM)] + [whole_block()] * 7,
        4 * shard * ff,
        16 * 2**20,
        (rank, *pieces, w_gate, w_up, gain),
    )


def spread_first_kernel(
    rank_ref, lower, lower_far, upper, upper_far, wq_ref, wk_ref, wv_ref, gain_ref,
    gq_ref, gk_ref, gv_ref, go_ref, grad_gain_ref, bias_ref,
):
    rank = rank_ref[0]
    half = lower.shape[0] // 2
    wide = 256
    bias_ref[...] = jnp.zeros_like(bias_ref)
    for r, halves in enumerate(rank_blocks(lower, lower_far, upper, upper_far)):
        to = pl.ds(pl.multiple_of((rank ^ r) * wide, wide), wide)
        for part, (ref, start) in enumerate(halves):
            rows = slice(part * half, (part + 1) * half)
            source = slice(start, start + half)
            for place, out_ref in enumerate((gq_ref, gk_ref, gv_ref, go_ref)):
                out_ref[rows, to] = ref[source, place * wide : (place + 1) * wide].astype(WIDE)
        ref, start = halves[0]
        bias_ref[pl.ds(rank ^ r, 1), :] = jnp.sum(
            ref[start : start + 16, 4 * wide : 4 * wide + 128].astype(WIDE), 0, keepdims=True
        )
    flat = jnp.zeros((1, 128), WIDE)
    for part in range(2):
        rows = slice(part * half, (part + 1) * half)
        total = jnp.zeros((half, 1), WIDE)
        for weight_ref, grad_ref in ((wq_ref, gq_ref), (wk_ref, gk_ref), (wv_ref, gv_ref)):
            total = total + jnp.sum(
                weight_ref[rows, :].astype(WIDE) * grad_ref[rows, :], 1, keepdims=True
            )
        flat = flat + lay_flat(total, part)
    grad_gain_ref[...] = jnp.broadcast_to(flat / gain_ref[...].astype(WIDE), (8, 128))


def spread_first(rank, pieces, w_query, w_key, w_value, gain):
    shard = w_query.shape[0]
    return call(
        spread_first_kernel,
        "spread_first",
        [((shard, D), WIDE)] * 4 + [((8, 128), WIDE), ((8, 128), WIDE)],
        [pl.BlockSpec(memory_space=pltpu.SMEM)] + [whole_block()] * 8,
        4 * shard * D,
        8 * 2**20,
        (rank, *pieces, w_query, w_key, w_value, gain),
    )


def on_plane(
    inputs,
    w_query,
    w_key,
    w_value,
    w_output,
    gain_attention,
    w_gate,
    w_up,
    w_down,
    gain_feed,
    variate_bias,
    segment_ids,
    variate_ids,
    positions,
    grad_output,
):
    rank = lax.axis_index("batch")
    rank_row = jnp.reshape(rank, (1,)).astype(jnp.int32)
    micro, tokens = inputs.shape[0], inputs.shape[2]
    n_seq = lax.axis_size("seq")
    shard = w_query.shape[0]
    per = D // 4

    packed, first_shard = pack_first(
        rank_row,
        inputs.reshape(micro, tokens, D),
        grad_output.reshape(micro, tokens, D),
        segment_ids.reshape(micro, tokens),
        variate_ids.reshape(micro, tokens),
        positions.reshape(micro, tokens),
        (w_query, w_key, w_value, w_output),
        (gain_attention.reshape(1, shard), gain_feed.reshape(1, shard)),
    )
    first_weights = lax.all_gather(first_shard, "seq", axis=0, tiled=True)
    packed = lax.all_to_all(packed, "batch", 0, 0, tiled=True)
    by_sequence = [
        packed[:, kind].reshape(4 * micro, tokens // 4, D + 128)[:, :, : D + 128 - 128 * kind]
        for kind in range(2)
    ]
    mine, cot_by_sequence = lax.optimization_barrier((over_seq(by_sequence[0]), by_sequence[1]))
    cot_mine = over_seq(cot_by_sequence)
    freqs = jnp.exp((jnp.arange(128) % 32).astype(WIDE) * (-2.0 * math.log(10000.0) / HD))[None, :]
    my_bias = lax.dynamic_slice_in_dim(variate_bias, rank * 4, 4, 1)
    weights = jnp.pad(head_weights(my_bias[0], my_bias[1]), ((0, 4), (0, 0)))

    got = swap_pairs(mine)
    chunks = far_pairs(mine, got)
    gate_up_shard, down_shard = pack_feed(after(rank_row, got), w_gate, w_up, w_down)
    gate_up = lax.all_gather(gate_up_shard, "seq", axis=0, tiled=True)
    down = lax.all_gather(down_shard, "seq", axis=0, tiled=True)
    chunks, cot_mine = lax.optimization_barrier((chunks, cot_mine))
    cot_got = swap_pairs(cot_mine)
    gain, mixed_first, turned, attended, lower, upper, *kept = attend(
        chunks, first_weights, freqs, weights
    )
    lower, upper, cot_got = lax.optimization_barrier((lower, upper, cot_got))
    lower_x, upper_y = swap(lower, 1), swap(upper, 2)
    lower_far = swap(jnp.concatenate([lower, lower_x], 1), 2)
    upper_far = swap(jnp.concatenate([upper, upper_y], 1), 1)
    lower_far, upper_far, cot_got = lax.optimization_barrier((lower_far, upper_far, cot_got))
    cots = far_pairs(cot_mine, cot_got)
    heads, middle_own, mixed_second = middle(
        rank_row,
        chunks,
        (lower, lower_x, lower_far, upper, upper_y, upper_far),
        first_weights,
        gain,
    )

    both, hidden = feed(mixed_second, gate_up)
    down_weight_grads = down_grads(hidden, cots)
    down_grad_shard = lax.psum_scatter(down_weight_grads, "seq", scatter_dimension=0, tiled=True)
    grad_gate_up, *back = feed_back(after(both, down_weight_grads), cots, gate_up, down)
    got = scatter_first(back)
    gate_up_weight_grads = gate_up_grads(after(mixed_second, got), grad_gate_up)
    gate_up_grad_shard = lax.psum_scatter(
        gate_up_weight_grads, "seq", scatter_dimension=0, tiled=True
    )
    sums = scatter_second(back, got)
    sums = lax.optimization_barrier((sums, gate_up_weight_grads))[0]
    grad_middle, *parcels = own_back(rank_row, sums, middle_own, cot_mine, gain, first_weights)
    out_chunks = feed_out(after(hidden, parcels[0]), down)
    parcels = [parcels[0]] + [swap(parcels[r], r) for r in range(1, 4)]
    parcels, out_chunks, down_grad_shard = lax.optimization_barrier(
        (parcels, out_chunks, down_grad_shard)
    )

    out_got = scatter_first(out_chunks)
    kept = (turned, attended, *kept)
    proj0, bias0 = attend_back(0, parcels, kept, weights)
    parcels, proj0, out_got = lax.optimization_barrier((parcels, proj0, out_got))
    out_sums = scatter_second(out_chunks, out_got)
    proj1, bias1 = attend_back(1, parcels, kept, weights)
    proj1, out_sums = lax.optimization_barrier((proj1, out_sums))
    back = project_back(proj0, proj1, first_weights)
    got = scatter_first(back)
    bias_sums = jnp.sum(jnp.concatenate([bias0[:2], bias1[:2], bias0[2:4], bias1[2:4]], 0), 1)
    bias_parts = jnp.pad(jnp.concatenate(three_parts(bias_sums)), (0, 104))[None, :]
    slots = lax.broadcasted_iota(jnp.int32, (per, 1), 0) % shard == lax.axis_index("seq")
    bias_rows = jnp.where(slots, bias_parts, LOW(0))
    first_weight_grads = first_grads(
        rank_row, after(mixed_first, got), proj0, proj1, heads, parcels, bias_rows
    )
    first_grad_shard = lax.psum_scatter(first_weight_grads, "seq", scatter_dimension=0, tiled=True)
    sums = scatter_second(back, got)
    sums, gate_up_grad_shard = lax.optimization_barrier(
        (sums, gate_up_grad_shard, first_weight_grads)
    )[:2]
    last = own_last(sums, out_sums, mine, grad_middle, middle_own, gain, n_seq)
    moved = lax.all_to_all(last, "seq", 0, 0, tiled=True)
    quarter = tokens // 4
    feed_grad_shard = jnp.concatenate([gate_up_grad_shard, down_grad_shard], 1)
    feed_pieces = gather_plane(after(feed_grad_shard, last))
    moved, feed_pieces = lax.optimization_barrier((moved, feed_pieces))
    moved = moved.reshape(4, micro, 2 * quarter, D)
    moved = lax.all_to_all(moved, "batch", 0, 0, tiled=True)
    grad_inputs = jnp.transpose(moved[:, :, :quarter].astype(WIDE), (1, 0, 2, 3))
    block_output = jnp.transpose(moved[:, :, quarter:], (1, 0, 2, 3))

    grad_gate, grad_up, grad_down, grad_gain_second = spread_feed(
        rank_row, feed_pieces, w_gate, w_up, gain_feed.reshape(1, shard)
    )
    first_pieces = gather_plane(after(first_grad_shard, moved))
    grad_query, grad_key, grad_value, grad_output_weights, grad_gain_first, bias_table = (
        spread_first(
            rank_row, first_pieces, w_query, w_key, w_value, gain_attention.reshape(1, shard)
        )
    )
    bias_table = jnp.sum(bias_table[:4, :24].reshape(4, 3, 2, 4), 1)
    grad_bias = jnp.transpose(bias_table, (1, 0, 2)).reshape(2, H)
    return (
        block_output.reshape(inputs.shape),
        grad_inputs.reshape(inputs.shape),
        grad_query,
        grad_key,
        grad_value,
        grad_output_weights,
        grad_gain_first[0],
        grad_gate,
        grad_up,
        grad_down,
        grad_gain_second[0],
        grad_bias,
    )


def solution(mesh):
    n_batch, n_seq = mesh.shape["batch"], mesh.shape["seq"]
    step = on_plane if n_batch == 4 and n_seq == 8 else on_device
    return jax.shard_map(
        step,
        mesh=mesh,
        in_specs=(
            P(None, "batch", "seq", None),
            P("seq", None),
            P("seq", None),
            P("seq", None),
            P("seq", None),
            P("seq"),
            P("seq", None),
            P("seq", None),
            P("seq", None),
            P("seq"),
            P(),
            P(None, "batch", "seq"),
            P(None, "batch", "seq"),
            P(None, "batch", "seq"),
            P(None, "batch", "seq", None),
        ),
        out_specs=(
            P(None, "batch", "seq", None),
            P(None, "batch", "seq", None),
            P("seq", None),
            P("seq", None),
            P("seq", None),
            P("seq", None),
            P("seq"),
            P("seq", None),
            P("seq", None),
            P("seq", None),
            P("seq"),
            P(),
        ),
        check_vma=False,
    )
```

```python
import functools
import math

import jax
import jax.numpy as jnp
from jax import lax
from jax.experimental import pallas as pl
from jax.experimental.pallas import tpu as pltpu
from jax.sharding import PartitionSpec as P

D = 1024
H = 16
HD = 64
REACH = 6


EPSILON = 1e-05
SCORE_SCALE = 0.125
MASKED = -1e30


def from_behind(value, axis, by):
    length = lax.axis_size(axis)
    pairs = [(i, i + by) for i in range(length) if 0 <= i + by < length]
    return lax.ppermute(value, axis, pairs)


def step_offset(step):
    distance = step // 2 + 1
    return distance if step % 2 == 0 else -distance


def rotary(values_in, positions_in, turn):
    row_count = values_in.shape[0]
    halfway = HD // 2
    freqs = jnp.exp(jnp.arange(halfway, dtype=jnp.float32) * (-2.0 * math.log(10000.0) / HD))
    angles = positions_in.astype(jnp.float32)[:, None] * freqs[None, :]
    cosine = jnp.cos(angles)[:, None, :]
    sine = turn * jnp.sin(angles)[:, None, :]
    shaped = values_in.reshape(row_count, H, HD)
    first_half = shaped[..., :halfway]
    second_half = shaped[..., halfway:]
    turned = jnp.concatenate(
        [first_half * cosine - second_half * sine, first_half * sine + second_half * cosine], -1
    )
    return turned.reshape(row_count, H * HD)


def head_scores(query_heads, key_heads, query_variates, key_variates, bias_table):
    raw = jnp.einsum("qhd,khd->hqk", query_heads, key_heads, preferred_element_type=jnp.float32)
    same_variate = (query_variates[:, None] == key_variates[None, :])[None]
    return raw * SCORE_SCALE + jnp.where(
        same_variate, bias_table[0][:, None, None], bias_table[1][:, None, None]
    )


def attend_forward(query_rows, own_keys, own_values, own_segments, own_variates, bias_table):
    tok_count = query_rows.shape[0]
    query_heads = query_rows.reshape(tok_count, H, HD)
    shifted_segments = own_segments + 1

    def fold_keys(carried, piece_rows):
        key_part, value_part, segment_part, variate_part = piece_rows
        part_count = key_part.shape[0]
        live = shifted_segments[:, None] == segment_part[None, :]

        def update(state):
            running_max, running_total, running_sum = state
            logits = head_scores(
                query_heads,
                key_part.reshape(part_count, H, HD),
                own_variates,
                variate_part,
                bias_table,
            )
            logits = jnp.where(live[None], logits, MASKED)
            new_max = jnp.maximum(running_max, jnp.max(logits, -1))
            rescale = jnp.exp(running_max - new_max)
            weights = jnp.where(live[None], jnp.exp(logits - new_max[..., None]), 0.0)
            new_total = running_total * rescale + jnp.sum(weights, -1)
            mixed = jnp.einsum(
                "hqk,khd->qhd",
                weights.astype(jnp.bfloat16),
                value_part.reshape(part_count, H, HD),
                preferred_element_type=jnp.float32,
            )
            new_sum = running_sum * jnp.transpose(rescale)[:, :, None] + mixed
            return (new_max, new_total, new_sum)

        return lax.cond(jnp.any(live), update, lambda state: state, carried)

    near_rows = (own_keys, own_values, shifted_segments, own_variates)
    state = (
        jnp.full((H, tok_count), MASKED, jnp.float32),
        jnp.zeros((H, tok_count), jnp.float32),
        jnp.zeros((tok_count, H, HD), jnp.float32),
    )
    state = fold_keys(state, near_rows)
    for step in range(2 * REACH):
        arrived = from_behind(
            (own_keys, own_values, shifted_segments, own_variates), "seq", step_offset(step)
        )
        state = fold_keys(state, arrived)
    final_max, final_total, final_sum = state
    attended = final_sum / jnp.transpose(final_total)[:, :, None]
    log_rows = jnp.transpose(final_max + jnp.log(final_total))
    return (attended.reshape(tok_count, H * HD), log_rows)


def attend_queries_back(
    query_rows,
    grad_rows,
    log_rows,
    delta_rows,
    own_keys,
    own_values,
    own_segments,
    own_variates,
    bias_table,
):
    tok_count = query_rows.shape[0]
    query_heads = query_rows.reshape(tok_count, H, HD)
    grad_heads = grad_rows.reshape(tok_count, H, HD)
    log_heads = jnp.transpose(log_rows)
    delta_heads = jnp.transpose(delta_rows)
    shifted_segments = own_segments + 1

    def fold_keys_back(carried, piece_rows):
        key_part, value_part, segment_part, variate_part = piece_rows
        part_count = key_part.shape[0]
        live = shifted_segments[:, None] == segment_part[None, :]

        def update(state):
            grad_query, grad_bias = state
            key_heads = key_part.reshape(part_count, H, HD)
            logits = head_scores(query_heads, key_heads, own_variates, variate_part, bias_table)
            weights = jnp.where(live[None], jnp.exp(logits - log_heads[..., None]), 0.0)
            grad_weights = jnp.einsum(
                "qhd,khd->hqk",
                grad_heads,
                value_part.reshape(part_count, H, HD),
                preferred_element_type=jnp.float32,
            )
            grad_logits = (weights * (grad_weights - delta_heads[..., None])).astype(jnp.bfloat16)
            grad_query = grad_query + SCORE_SCALE * jnp.einsum(
                "hqk,khd->qhd", grad_logits, key_heads, preferred_element_type=jnp.float32
            )
            same_variate = (own_variates[:, None] == variate_part[None, :])[None]
            logit_values = grad_logits.astype(jnp.float32)
            same_total = jnp.sum(jnp.where(same_variate, logit_values, 0.0), axis=(1, 2))
            other_total = jnp.sum(jnp.where(same_variate, 0.0, logit_values), axis=(1, 2))
            return (grad_query, grad_bias + jnp.stack([same_total, other_total]))

        return lax.cond(jnp.any(live), update, lambda state: state, carried)

    state = (jnp.zeros((tok_count, H, HD), jnp.float32), jnp.zeros((2, H), jnp.float32))
    state = fold_keys_back(state, (own_keys, own_values, shifted_segments, own_variates))
    for step in range(2 * REACH):
        arrived = from_behind(
            (own_keys, own_values, shifted_segments, own_variates), "seq", step_offset(step)
        )
        state = fold_keys_back(state, arrived)
    grad_query, grad_bias = state
    return (grad_query.reshape(tok_count, H * HD), grad_bias)


def attend_keys_back(
    query_rows,
    grad_rows,
    log_rows,
    delta_rows,
    own_keys,
    own_values,
    own_segments,
    own_variates,
    bias_table,
):
    tok_count = own_keys.shape[0]
    key_heads = own_keys.reshape(tok_count, H, HD)
    value_heads = own_values.reshape(tok_count, H, HD)
    shifted_segments = own_segments + 1

    def fold_queries(carried, piece_rows):
        query_part, grad_part, log_part, delta_part, segment_part, variate_part = piece_rows
        part_count = query_part.shape[0]
        live = segment_part[:, None] == shifted_segments[None, :]

        def update(state):
            grad_key, grad_value = state
            query_heads = query_part.reshape(part_count, H, HD)
            grad_heads = grad_part.reshape(part_count, H, HD)
            logits = head_scores(query_heads, key_heads, variate_part, own_variates, bias_table)
            weights = jnp.where(
                live[None], jnp.exp(logits - jnp.transpose(log_part)[..., None]), 0.0
            )
            grad_value = grad_value + jnp.einsum(
                "hqk,qhd->khd",
                weights.astype(jnp.bfloat16),
                grad_heads,
                preferred_element_type=jnp.float32,
            )
            grad_weights = jnp.einsum(
                "qhd,khd->hqk", grad_heads, value_heads, preferred_element_type=jnp.float32
            )
            grad_logits = (weights * (grad_weights - jnp.transpose(delta_part)[..., None])).astype(
                jnp.bfloat16
            )
            grad_key = grad_key + SCORE_SCALE * jnp.einsum(
                "hqk,qhd->khd", grad_logits, query_heads, preferred_element_type=jnp.float32
            )
            return (grad_key, grad_value)

        return lax.cond(jnp.any(live), update, lambda state: state, carried)

    state = (jnp.zeros((tok_count, H, HD), jnp.float32), jnp.zeros((tok_count, H, HD), jnp.float32))
    state = fold_queries(
        state, (query_rows, grad_rows, log_rows, delta_rows, shifted_segments, own_variates)
    )
    for step in range(2 * REACH):
        arrived = (
            from_behind(query_rows, "seq", step_offset(step)),
            from_behind(grad_rows, "seq", step_offset(step)),
            from_behind(log_rows.astype(jnp.bfloat16), "seq", step_offset(step)).astype(
                log_rows.dtype
            ),
            from_behind(delta_rows.astype(jnp.bfloat16), "seq", step_offset(step)).astype(
                delta_rows.dtype
            ),
            from_behind(shifted_segments, "seq", step_offset(step)),
            from_behind(own_variates, "seq", step_offset(step)),
        )
        state = fold_queries(state, arrived)
    grad_key, grad_value = state
    return (grad_key.reshape(tok_count, H * HD), grad_value.reshape(tok_count, H * HD))


def norm_back(grad_normed, normed, scale_rows):
    return scale_rows * (grad_normed - normed * jnp.mean(grad_normed * normed, -1, keepdims=True))


def on_device(
    inputs,
    w_query,
    w_key,
    w_value,
    w_output,
    gain_attention,
    w_gate,
    w_up,
    w_down,
    gain_feed,
    variate_bias,
    segment_ids,
    variate_ids,
    positions,
    grad_output,
):
    micro_count = inputs.shape[0]
    tok_count = inputs.shape[2]
    row_count = micro_count * tok_count
    residual_in = inputs.reshape(row_count, D).astype(jnp.float32)
    cotangent = grad_output.reshape(row_count, D).astype(jnp.float32)
    segment_rows = segment_ids.reshape(micro_count, tok_count)
    variate_rows = variate_ids.reshape(micro_count, tok_count)
    position_rows = positions.reshape(row_count)
    full_query, full_key, full_value, full_output, full_gain_first = (
        lax.all_gather(w_query, "seq", axis=0, tiled=True),
        lax.all_gather(w_key, "seq", axis=0, tiled=True),
        lax.all_gather(w_value, "seq", axis=0, tiled=True),
        lax.all_gather(w_output, "seq", axis=0, tiled=True),
        lax.all_gather(gain_attention, "seq", axis=0, tiled=True),
    )
    full_gate, full_up, full_down, full_gain_second = (
        lax.all_gather(w_gate, "seq", axis=0, tiled=True),
        lax.all_gather(w_up, "seq", axis=0, tiled=True),
        lax.all_gather(w_down, "seq", axis=0, tiled=True),
        lax.all_gather(gain_feed, "seq", axis=0, tiled=True),
    )
    scale_first = lax.rsqrt(jnp.mean(residual_in * residual_in, -1, keepdims=True) + EPSILON)
    normed_first = residual_in * scale_first
    mixed_first = (normed_first * full_gain_first.astype(jnp.float32)).astype(jnp.bfloat16)
    query_proj = jnp.dot(mixed_first, full_query, preferred_element_type=jnp.float32)
    key_proj = jnp.dot(mixed_first, full_key, preferred_element_type=jnp.float32)
    value_proj = jnp.dot(mixed_first, full_value, preferred_element_type=jnp.float32)
    query_rows = rotary(query_proj, position_rows, 1.0).astype(jnp.bfloat16)
    key_rows = rotary(key_proj, position_rows, 1.0).astype(jnp.bfloat16)
    value_rows = value_proj.astype(jnp.bfloat16)
    attended_parts = []
    log_parts = []
    for micro_index in range(micro_count):
        lower_row = micro_index * tok_count
        upper_row = lower_row + tok_count
        attended_part, log_part = attend_forward(
            query_rows[lower_row:upper_row],
            key_rows[lower_row:upper_row],
            value_rows[lower_row:upper_row],
            segment_rows[micro_index],
            variate_rows[micro_index],
            variate_bias,
        )
        attended_parts.append(attended_part)
        log_parts.append(log_part)
    attended_all = jnp.concatenate(attended_parts, 0)
    attended_low = attended_all.astype(jnp.bfloat16)
    middle = residual_in + jnp.dot(attended_low, full_output, preferred_element_type=jnp.float32)
    scale_second = lax.rsqrt(jnp.mean(middle * middle, -1, keepdims=True) + EPSILON)
    normed_second = middle * scale_second
    mixed_second = (normed_second * full_gain_second.astype(jnp.float32)).astype(jnp.bfloat16)
    gate_proj = jnp.dot(mixed_second, full_gate, preferred_element_type=jnp.float32)
    up_proj = jnp.dot(mixed_second, full_up, preferred_element_type=jnp.float32)
    sigmoid_gate = jax.nn.sigmoid(gate_proj)
    silu_gate = gate_proj * sigmoid_gate
    hidden_rows = (silu_gate * up_proj).astype(jnp.bfloat16)
    block_rows = middle + jnp.dot(hidden_rows, full_down, preferred_element_type=jnp.float32)
    block_output = block_rows.astype(jnp.bfloat16).reshape(inputs.shape)
    full_query, full_key, full_value, full_output, full_gain_first = (
        lax.all_gather(w_query, "seq", axis=0, tiled=True),
        lax.all_gather(w_key, "seq", axis=0, tiled=True),
        lax.all_gather(w_value, "seq", axis=0, tiled=True),
        lax.all_gather(w_output, "seq", axis=0, tiled=True),
        lax.all_gather(gain_attention, "seq", axis=0, tiled=True),
    )
    full_gate, full_up, full_down, full_gain_second = (
        lax.all_gather(w_gate, "seq", axis=0, tiled=True),
        lax.all_gather(w_up, "seq", axis=0, tiled=True),
        lax.all_gather(w_down, "seq", axis=0, tiled=True),
        lax.all_gather(gain_feed, "seq", axis=0, tiled=True),
    )
    grad_branch_second = cotangent.astype(jnp.bfloat16)
    grad_down = jnp.einsum(
        "rf,rd->fd", hidden_rows, grad_branch_second, preferred_element_type=jnp.float32
    )
    grad_hidden = jnp.einsum(
        "rd,fd->rf", grad_branch_second, full_down, preferred_element_type=jnp.float32
    )
    silu_slope = sigmoid_gate * (1.0 + gate_proj * (1.0 - sigmoid_gate))
    grad_gate_rows = (grad_hidden * up_proj * silu_slope).astype(jnp.bfloat16)
    grad_up_rows = (grad_hidden * silu_gate).astype(jnp.bfloat16)
    grad_gate = jnp.einsum(
        "rd,rf->df", mixed_second, grad_gate_rows, preferred_element_type=jnp.float32
    )
    grad_up = jnp.einsum(
        "rd,rf->df", mixed_second, grad_up_rows, preferred_element_type=jnp.float32
    )
    grad_mixed_second = jnp.einsum(
        "rf,df->rd", grad_gate_rows, full_gate, preferred_element_type=jnp.float32
    ) + jnp.einsum("rf,df->rd", grad_up_rows, full_up, preferred_element_type=jnp.float32)
    grad_gain_second = jnp.sum(grad_mixed_second * normed_second, 0)
    grad_middle = cotangent + norm_back(
        grad_mixed_second * full_gain_second.astype(jnp.float32), normed_second, scale_second
    )
    grad_branch_first = grad_middle.astype(jnp.bfloat16)
    grad_out_proj = jnp.einsum(
        "rd,re->de", attended_low, grad_branch_first, preferred_element_type=jnp.float32
    )
    grad_attended = jnp.einsum(
        "re,de->rd", grad_branch_first, full_output, preferred_element_type=jnp.float32
    ).astype(jnp.bfloat16)
    delta_all = jnp.einsum(
        "rhd,rhd->rh",
        grad_attended.astype(jnp.float32).reshape(row_count, H, HD),
        attended_all.reshape(row_count, H, HD),
    )
    grad_bias_local = jnp.zeros((2, H), jnp.float32)
    query_grad_parts = []
    key_grad_parts = []
    value_grad_parts = []
    for micro_index in range(micro_count):
        lower_row = micro_index * tok_count
        upper_row = lower_row + tok_count
        query_grad_part, bias_part = attend_queries_back(
            query_rows[lower_row:upper_row],
            grad_attended[lower_row:upper_row],
            log_parts[micro_index],
            delta_all[lower_row:upper_row],
            key_rows[lower_row:upper_row],
            value_rows[lower_row:upper_row],
            segment_rows[micro_index],
            variate_rows[micro_index],
            variate_bias,
        )
        key_grad_part, value_grad_part = attend_keys_back(
            query_rows[lower_row:upper_row],
            grad_attended[lower_row:upper_row],
            log_parts[micro_index],
            delta_all[lower_row:upper_row],
            key_rows[lower_row:upper_row],
            value_rows[lower_row:upper_row],
            segment_rows[micro_index],
            variate_rows[micro_index],
            variate_bias,
        )
        grad_bias_local = grad_bias_local + bias_part
        query_grad_parts.append(query_grad_part)
        key_grad_parts.append(key_grad_part)
        value_grad_parts.append(value_grad_part)
    grad_query_rows = rotary(jnp.concatenate(query_grad_parts, 0), position_rows, -1.0).astype(
        jnp.bfloat16
    )
    grad_key_rows = rotary(jnp.concatenate(key_grad_parts, 0), position_rows, -1.0).astype(
        jnp.bfloat16
    )
    grad_value_rows = jnp.concatenate(value_grad_parts, 0).astype(jnp.bfloat16)
    grad_query = jnp.einsum(
        "rd,re->de", mixed_first, grad_query_rows, preferred_element_type=jnp.float32
    )
    grad_key = jnp.einsum(
        "rd,re->de", mixed_first, grad_key_rows, preferred_element_type=jnp.float32
    )
    grad_value = jnp.einsum(
        "rd,re->de", mixed_first, grad_value_rows, preferred_element_type=jnp.float32
    )
    grad_mixed_first = (
        jnp.einsum("re,de->rd", grad_query_rows, full_query, preferred_element_type=jnp.float32)
        + jnp.einsum("re,de->rd", grad_key_rows, full_key, preferred_element_type=jnp.float32)
        + jnp.einsum("re,de->rd", grad_value_rows, full_value, preferred_element_type=jnp.float32)
    )
    grad_gain_first = jnp.sum(grad_mixed_first * normed_first, 0)
    grad_input_rows = grad_middle + norm_back(
        grad_mixed_first * full_gain_first.astype(jnp.float32), normed_first, scale_first
    )
    grad_inputs = grad_input_rows.reshape(inputs.shape)
    (
        shard_query,
        shard_key,
        shard_value,
        shard_output,
        shard_gain_first,
        shard_gate,
        shard_up,
        shard_down,
        shard_gain_second,
    ) = (
        lax.psum_scatter(grad_query, "seq", scatter_dimension=0, tiled=True),
        lax.psum_scatter(grad_key, "seq", scatter_dimension=0, tiled=True),
        lax.psum_scatter(grad_value, "seq", scatter_dimension=0, tiled=True),
        lax.psum_scatter(grad_out_proj, "seq", scatter_dimension=0, tiled=True),
        lax.psum_scatter(grad_gain_first, "seq", scatter_dimension=0, tiled=True),
        lax.psum_scatter(grad_gate, "seq", scatter_dimension=0, tiled=True),
        lax.psum_scatter(grad_up, "seq", scatter_dimension=0, tiled=True),
        lax.psum_scatter(grad_down, "seq", scatter_dimension=0, tiled=True),
        lax.psum_scatter(grad_gain_second, "seq", scatter_dimension=0, tiled=True),
    )
    summed = (
        lax.psum(shard_query.astype(jnp.bfloat16), "batch").astype(jnp.float32),
        lax.psum(shard_key.astype(jnp.bfloat16), "batch").astype(jnp.float32),
        lax.psum(shard_value.astype(jnp.bfloat16), "batch").astype(jnp.float32),
        lax.psum(shard_output.astype(jnp.bfloat16), "batch").astype(jnp.float32),
        lax.psum(shard_gain_first.astype(jnp.bfloat16), "batch").astype(jnp.float32),
        lax.psum(shard_gate.astype(jnp.bfloat16), "batch").astype(jnp.float32),
        lax.psum(shard_up.astype(jnp.bfloat16), "batch").astype(jnp.float32),
        lax.psum(shard_down.astype(jnp.bfloat16), "batch").astype(jnp.float32),
        lax.psum(shard_gain_second.astype(jnp.bfloat16), "batch").astype(jnp.float32),
    )
    grad_bias_total = lax.psum(grad_bias_local, ("batch", "seq"))
    return (
        block_output,
        grad_inputs,
        summed[0],
        summed[1],
        summed[2],
        summed[3],
        summed[4],
        summed[5],
        summed[6],
        summed[7],
        summed[8],
        grad_bias_total,
    )


ORDER_A = (0, 1, 2, 3)
ORDER_B = (0, 2, 1, 3)
FEATURES = 128
LSE_AT = 64
LOW = jnp.bfloat16
WIDE = jnp.float32


def swap(value, bit):
    return lax.ppermute(value, "batch", [(i, i ^ bit) for i in range(4)])


def after(value, *others):
    return lax.optimization_barrier((value, *others))[0]


def gather_plane(own):
    half = own.shape[0] // 2
    lower, upper = own[:half], own[half:]
    lower_pair = jnp.concatenate([lower, swap(lower, 1)], 0)
    upper_pair = jnp.concatenate([upper, swap(upper, 2)], 0)
    return lower_pair, swap(lower_pair, 2), upper_pair, swap(upper_pair, 1)


def scatter_first(chunks):
    return swap(chunks[1], 2), swap(chunks[3], 1)


def scatter_second(chunks, got):
    near_lower, _, near_upper, _ = chunks
    got_lower, got_upper = got
    half = near_lower.shape[0] // 2
    last_lower = swap(near_lower[half:] + got_lower[half:], 1)
    last_upper = swap(near_upper[half:] + got_upper[half:], 2)
    return (near_lower, got_lower, last_lower, near_upper, got_upper, last_upper)


def swap_pairs(own):
    half = own.shape[0] // 2
    return swap(own[:half], 1), swap(own[half:], 2)


def far_pairs(own, got):
    half = own.shape[0] // 2
    lower_pair = jnp.concatenate([own[:half], got[0]], 0)
    upper_pair = jnp.concatenate([own[half:], got[1]], 0)
    return lower_pair, swap(lower_pair, 2), upper_pair, swap(upper_pair, 1)


def over_seq(pieces):
    count, quarter, width = pieces.shape
    return lax.all_to_all(pieces, "seq", 0, 0, tiled=True).reshape(count * quarter, width)


def three_parts(value):
    high = value.astype(LOW)
    rest = value - high.astype(WIDE)
    middle = rest.astype(LOW)
    low = (rest - middle.astype(WIDE)).astype(LOW)
    return high, middle, low


def token_features(segments, variates):
    lane = lax.broadcasted_iota(jnp.int32, (segments.shape[0], FEATURES), 1)
    variate_hot = (lane < 12) & (lane % 4 == variates)
    ones = (lane >= 12) & (lane < 15)
    segment_lane = (lane >= 16) & (lane < LSE_AT)
    segment_hot = segment_lane & (lane - 16 == segments)
    segment_cold = segment_lane & (lane - 16 != segments)
    query_side = variate_hot | ones | segment_hot
    key_side = variate_hot | ones | segment_cold | ((lane >= LSE_AT) & (lane < LSE_AT + 3))
    return jnp.where(query_side, 1.0, 0.0).astype(LOW), jnp.where(key_side, 1.0, 0.0).astype(LOW)


def head_weights(same_bias, other_bias):
    gap = [part[:, None] for part in three_parts(same_bias - other_bias)]
    base = [part[:, None] for part in three_parts(other_bias)]
    heads = same_bias.shape[0]
    columns = [jnp.broadcast_to(part, (heads, 4)) for part in gap] + base
    columns.append(jnp.zeros((heads, 1), LOW))
    columns.append(jnp.full((heads, LSE_AT - 16), MASKED, LOW))
    columns.append(jnp.zeros((heads, FEATURES - LSE_AT), LOW))
    return jnp.concatenate(columns, 1)


def turn_pair(pair, cosine, sine):
    lane = lax.broadcasted_iota(jnp.int32, pair.shape, 1)
    crossed = jnp.where(lane % 64 < 32, pltpu.roll(pair, 96, 1), pltpu.roll(pair, 32, 1))
    return pair * cosine + crossed * sine


def dot_plain(left, right):
    return jnp.dot(left, right, preferred_element_type=WIDE)


def dot_rows(left, right):
    return lax.dot_general(left, right, (((1,), (1,)), ((), ())), preferred_element_type=WIDE)


def dot_first(left, right):
    return lax.dot_general(left, right, (((0,), (0,)), ((), ())), preferred_element_type=WIDE)


def whole_block():
    return pl.BlockSpec(memory_space=pltpu.VMEM)


def call(kernel, name, outs, specs, flops, moved, args, scratch=()):
    return pl.pallas_call(
        kernel,
        grid=(1,),
        out_shape=[jax.ShapeDtypeStruct(shape, dtype) for shape, dtype in outs],
        in_specs=specs,
        out_specs=[pl.BlockSpec(memory_space=pltpu.VMEM) for _ in outs],
        scratch_shapes=list(scratch),
        cost_estimate=pl.CostEstimate(flops=flops, bytes_accessed=moved, transcendentals=0),
        compiler_params=pltpu.CompilerParams(vmem_limit_bytes=56 * 2**20),
        name=name,
    )(*args)


class Copies:
    def __init__(self, ref, pairs, sems):
        self.ref = ref
        self.copies = [
            pltpu.make_async_copy(source, target, sems.at[k])
            for k, (source, target) in enumerate(pairs)
        ]
        self.started = self.waited = False

    def start(self, *which):
        self.started = True
        for k in which or range(len(self.copies)):
            self.copies[k].start()

    def wait(self):
        if not self.waited:
            for copy in self.copies:
                copy.wait()
        self.waited = True
        return self.ref

    def _at(self, index, act):
        for k, copy in enumerate(self.copies):
            pl.when(index == k)(functools.partial(act, copy))

    def start_at(self, index):
        self.started = True
        self._at(index, lambda copy: copy.start())

    def wait_at(self, index):
        self.waited = True
        self._at(index, lambda copy: copy.wait())

    def wait_first(self, index):
        if not self.waited:
            self.waited = True

            @pl.when(index == 0)
            def _():
                for copy in self.copies:
                    copy.wait()

        return self.ref


class Plan:
    def __init__(self, arrays, shape, pairs, count):
        self.arrays, self.shape, self.pairs, self.count = arrays, shape, pairs, count


def whole(array, column=None, width=None):
    shape = array.shape if column is None else (array.shape[0], width)

    def pairs(refs, buffer):
        if column is None:
            return [(refs[0], buffer)]
        return [(refs[0].at[:, pl.ds(column, width)], buffer)]

    return Plan([array], shape, pairs, 1)


def top(array):
    half = array.shape[0] // 2
    return Plan(
        [array],
        (half, *array.shape[1:]),
        lambda refs, buffer: [(refs[0].at[pl.ds(0, half)], buffer)],
        1,
    )


def rows_of(array, count=4):
    size = array.shape[0] // count
    return Plan(
        [array],
        (count, size, array.shape[1]),
        lambda refs, buffer: [
            (refs[0].at[pl.ds(k * size, size)], buffer.at[k]) for k in range(count)
        ],
        count,
    )


def columns_of(array, count=4, column=0, width=None):
    size = (width or array.shape[1]) // count
    return Plan(
        [array],
        (count, array.shape[0], size),
        lambda refs, buffer: [
            (refs[0].at[:, pl.ds(column + k * size, size)], buffer.at[k]) for k in range(count)
        ],
        count,
    )


def group(arrays, column=None, width=None):
    rows = arrays[0].shape[0]

    def pairs(refs, buffer):
        if column is None:
            return [(ref, buffer.at[k]) for k, ref in enumerate(refs)]
        return [(ref.at[:, pl.ds(column, width)], buffer.at[k]) for k, ref in enumerate(refs)]

    return Plan(
        list(arrays), (len(arrays), rows, width or arrays[0].shape[1]), pairs, len(arrays)
    )


def out_rows(shape, dtype, count=4):
    size = shape[0] // count

    def pairs(refs, buffer):
        return [(buffer.at[k], refs[0].at[pl.ds(k * size, size)]) for k in range(count)]

    return Plan([(shape, dtype)], (count, size, *shape[1:]), pairs, count)


def out_group(shape, dtype, count=4):
    def pairs(refs, buffer):
        return [(buffer.at[k], ref) for k, ref in enumerate(refs)]

    return Plan([(shape, dtype)] * count, (count, *shape), pairs, count)


def out_whole(shape, dtype):
    return Plan([(shape, dtype)], shape, lambda refs, buffer: [(buffer, refs[0])], 1)


def run(body, name, us, ins, outs, scratch=(), token=None):
    args, in_specs, out_shapes, out_specs, buffers = [], [], [], [], []
    named = len(ins)
    if token is not None:
        ins = [*ins, token]
    for item in ins:
        if isinstance(item, Plan):
            args += item.arrays
            in_specs += [pl.BlockSpec(memory_space=pl.ANY)] * len(item.arrays)
            buffers.append(pltpu.VMEM(item.shape, item.arrays[0].dtype))
            buffers.append(pltpu.SemaphoreType.DMA((item.count,)))
        else:
            args.append(item)
            space = pltpu.SMEM if item.shape == (1,) else pltpu.VMEM
            in_specs.append(pl.BlockSpec(memory_space=space))
    for item in outs:
        if isinstance(item, Plan):
            out_shapes += [jax.ShapeDtypeStruct(*each) for each in item.arrays]
            out_specs += [pl.BlockSpec(memory_space=pl.ANY)] * len(item.arrays)
            buffers.append(pltpu.VMEM(item.shape, item.arrays[0][1]))
            buffers.append(pltpu.SemaphoreType.DMA((item.count,)))
        else:
            out_shapes.append(jax.ShapeDtypeStruct(*item))
            out_specs.append(pl.BlockSpec(memory_space=pltpu.VMEM))
    n_in, n_out = len(args), len(out_shapes)

    def kernel(*refs):
        given, rest = list(refs[: n_in + n_out]), list(refs[n_in + n_out :])
        bound = []
        for item in (*ins, *outs):
            if isinstance(item, Plan):
                near = [given.pop(0) for _ in item.arrays]
                buffer, sems = rest.pop(0), rest.pop(0)
                bound.append(Copies(buffer, item.pairs(near, buffer), sems))
            else:
                bound.append(given.pop(0))
        body(*bound[:named], *bound[len(ins) :], *rest)
        for item in bound[: len(ins)]:
            if isinstance(item, Copies):
                item.wait()
        for item in bound[len(ins) :]:
            if isinstance(item, Copies) and not item.started:
                item.start()
        for item in bound[len(ins) :]:
            if isinstance(item, Copies):
                item.wait()

    return pl.pallas_call(
        kernel,
        out_shape=out_shapes,
        in_specs=in_specs,
        out_specs=out_specs,
        scratch_shapes=buffers + list(scratch),
        cost_estimate=pl.CostEstimate(
            flops=int(us * 1.15e9), bytes_accessed=2**20, transcendentals=0
        ),
        compiler_params=pltpu.CompilerParams(vmem_limit_bytes=60 * 2**20),
        name=name,
    )(*args)


def start_all(*items):
    for item in items:
        item.start()


def unit_rows(rows):
    return lax.rsqrt(jnp.mean(rows * rows, -1, keepdims=True) + EPSILON)


def pack_body(
    rank_ref, x, cot, segment_ref, variate_ref, position_ref, wo, wq, wk, wv, gain_first_ref,
    gain_second_ref, gate, up, down, rows_out, shard_out, gate_up_out, down_out,
):
    start_all(wo, wq, wk, wv, x, cot, gate, up, down)
    micro, _, quarter, _ = x.ref.shape
    tokens = 4 * quarter
    lane = lax.broadcasted_iota(jnp.int32, (tokens, 128), 1)
    on_line = lax.broadcasted_iota(jnp.int32, (tokens, 128), 0) == lane

    def upright(row):
        return jnp.sum(jnp.where(on_line, row, 0.0), 1, keepdims=True)

    gains = jnp.where(
        lane == 0,
        upright(gain_first_ref[...].astype(WIDE)),
        jnp.where(lane == 1, upright(gain_second_ref[...].astype(WIDE)), 0.0),
    )
    shard_out.ref[:, D + 768 :] = gains.astype(LOW)
    shard_out.ref[:, :D] = wo.wait()[...]
    for place, weight in enumerate((wq, wk, wv)):
        shard_out.ref[:, D + 256 * place : D + 256 * (place + 1)] = weight.wait()[...]
    shard_out.start()
    for m in range(micro):
        places = position_ref[m : m + 1, :]
        numbers = jnp.zeros((tokens, 128), WIDE)
        for place, row in enumerate(
            (
                segment_ref[m : m + 1, :],
                variate_ref[m : m + 1, :],
                lax.shift_right_logical(places, 5),
                places & 31,
            )
        ):
            numbers = jnp.where(lane == place, upright(row.astype(WIDE)), numbers)
        numbers = numbers.astype(LOW)
        for r in range(4):
            rows_out.ref[r, 0, m, :, D:] = numbers[r * quarter : (r + 1) * quarter, :]
            rows_out.ref[r, 1, m, :, D:] = jnp.zeros((quarter, 128), LOW)
    x_ref, cot_ref = x.wait(), cot.wait()
    for m in range(micro):
        for r in range(4):
            rows_out.ref[r, 0, m, :, :D] = x_ref[m, r]
            rows_out.ref[r, 1, m, :, :D] = cot_ref[m, r]
    rows_out.start()
    gate_ref, up_ref = gate.wait(), up.wait()
    per = gate_up_out.ref.shape[1] // 2
    piece = gate_ref.shape[2]
    for s in range(per // piece):
        gate_up_out.ref[:, s * piece : (s + 1) * piece] = gate_ref[s]
        gate_up_out.ref[:, per + s * piece : per + (s + 1) * piece] = up_ref[s]
    gate_up_out.start()
    down_out.ref[...] = down.wait()[...]


def pack(rank, x, cot, segments, variates, positions, shards, gains, w_gate, w_up, w_down):
    micro, tokens, _ = x.shape
    quarter = tokens // 4
    shard, ff = w_gate.shape
    piece = w_down.shape[0] // 4
    pieces = ff // 4 // piece

    def quarters(array):
        return array.reshape(micro, 4, quarter, D)

    def mine(array, size, refs_at):
        return Plan([array], size, refs_at, 1)

    def rank_columns(array):
        def pairs(refs, buffer):
            at = pl.multiple_of(lax.axis_index("batch") * 256, 256)
            return [(refs[0].at[:, pl.ds(at, 256)], buffer)]

        return Plan([array], (shard, 256), pairs, 1)

    def feed_columns(array):
        def pairs(refs, buffer):
            rank = lax.axis_index("batch")
            return [
                (refs[0].at[:, pl.ds(pl.multiple_of((4 * s + rank) * piece, piece), piece)], buffer.at[s])
                for s in range(pieces)
            ]

        return Plan([array], (pieces, shard, piece), pairs, pieces)

    def down_rows(array):
        def pairs(refs, buffer):
            at = pl.multiple_of(lax.axis_index("batch") * piece, piece)
            return [(refs[0].at[pl.ds(at, piece)], buffer)]

        return Plan([array], (piece, D), pairs, 1)

    return run(
        pack_body,
        "pack",
        4,
        [rank, whole(quarters(x)), whole(quarters(cot)), segments, variates, positions]
        + [whole(shards[0])]
        + [rank_columns(weight) for weight in shards[1:]]
        + [*gains, feed_columns(w_gate), feed_columns(w_up), down_rows(w_down)],
        [
            out_whole((4, 2, micro, quarter, D + 128), LOW),
            out_whole((shard, D + 896), LOW),
            out_whole((shard, ff // 2), LOW),
            out_whole((piece, D), LOW),
        ],
    )


def attend_body(
    x, qkv, gains, freqs_ref, weights_ref,
    gain_ref, mixed, turned, wide, lower, upper, logs, cos, sin, query_sides, key_sides,
    keys_ref, values_ref, trig_ref,
):
    start_all(x, gains, qkv)
    count, chunk, _ = x.ref.shape
    lane = lax.broadcasted_iota(jnp.int32, (chunk, 128), 1)
    half_lane = lane // 64
    pick = lax.broadcasted_iota(jnp.int32, (16, 128), 0) == lax.broadcasted_iota(
        jnp.int32, (16, 128), 1
    )
    x_ref = x.wait()
    angles = jnp.zeros((chunk, 128), WIDE)
    for k in range(count):
        numbers = x_ref[k, :, D : D + 128].astype(WIDE)
        places = numbers[:, 2:3] * 32.0 + numbers[:, 3:4]
        angles = jnp.where(lane // 32 == k, places * freqs_ref[...], angles)
    trig_ref[0] = jnp.cos(angles)
    trig_ref[1] = jnp.sin(angles)
    gain_ref[...] = dot_rows(jnp.where(pick, 1.0, 0.0).astype(LOW), gains.wait()[...])
    qkv_ref = qkv.wait()

    def one_chunk(index, carry):
        rows = x_ref[index, :, :D].astype(WIDE)
        mixed_rows = (rows * unit_rows(rows) * gain_ref[0:1, :]).astype(LOW)
        mixed.ref[index] = mixed_rows

        def spread(packed):
            own = jnp.where(lane // 32 == index, packed, 0.0)
            own = own + pltpu.roll(own, 64, 1)
            return own + pltpu.roll(own, 32, 1)

        cosine = spread(trig_ref[0])
        sine = spread(trig_ref[1])
        sine = jnp.where(lane % 64 < 32, -sine, sine)
        cos.ref[index] = cosine
        sin.ref[index] = sine
        numbers = x_ref[index, :, D : D + 128].astype(WIDE).astype(jnp.int32)
        query_side, key_side = token_features(numbers[:, 0:1], numbers[:, 1:2])
        query_sides.ref[index] = query_side
        key_sides.ref[index] = key_side
        proj = dot_plain(mixed_rows, qkv_ref[...])
        values = proj[:, 512:].astype(LOW)
        turned.ref[index, :, 512:768] = values
        for pair in range(2):
            at = 128 * pair
            turned.ref[index, :, at : at + 128] = turn_pair(
                proj[:, at : at + 128], cosine, sine
            ).astype(LOW)
            keys = turn_pair(proj[:, 256 + at : 384 + at], cosine, sine).astype(LOW)
            turned.ref[index, :, 256 + at : 384 + at] = keys
            here = pl.ds(pl.multiple_of(index * chunk, chunk), chunk)
            keys_ref[pair, here, :128] = keys
            keys_ref[pair, here, 128:] = key_side
            values_ref[pair, here, :128] = values[:, at : at + 128]
            values_ref[pair, here, 128:] = jnp.where(lane == 0, 1.0, 0.0).astype(LOW)
        return carry

    lax.fori_loop(0, count, one_chunk, 0)
    start_all(mixed, turned, cos, sin, query_sides, key_sides)

    def one_block(index, carry):
        side = query_sides.ref[index]
        log_rows = jnp.zeros((chunk, 128), WIDE)
        here = pl.ds(pl.multiple_of((index % 2) * chunk, chunk), chunk)
        def scores_of(head):
            at = 128 * (head // 2)
            scaled = turned.ref[index, :, at : at + 128] * LOW(SCORE_SCALE)
            query = jnp.concatenate(
                [
                    jnp.where(half_lane == head % 2, scaled, LOW(0)),
                    side * weights_ref[head : head + 1, :],
                ],
                1,
            )
            return dot_rows(query, keys_ref[head // 2])

        scores = scores_of(0)
        parts = []
        for head in range(4):
            high = jnp.max(scores, 1, keepdims=True)
            powers = jnp.exp(scores - high).astype(LOW)
            if head < 3:
                scores = scores_of(head + 1)
            summed = dot_plain(powers, values_ref[head // 2])
            total = summed[:, 128:129]
            parts.append(summed[:, :128] / total)
            log_rows = jnp.where(lane == head, high + jnp.log(total), log_rows)
        for pair in range(2):
            at = 128 * pair
            total_mixed = jnp.where(half_lane == 0, parts[2 * pair], parts[2 * pair + 1])
            wide.ref[index, :, at : at + 128] = total_mixed
            low_rows = total_mixed.astype(LOW)

            @pl.when(index < 2)
            def _(low_rows=low_rows, at=at):
                lower.ref[here, at : at + 128] = low_rows

            @pl.when(index >= 2)
            def _(low_rows=low_rows, at=at):
                upper.ref[here, at : at + 128] = low_rows

        logs.ref[index] = log_rows
        return carry

    lax.fori_loop(0, count, one_block, 0)


def attend(chunks, first_weights, freqs, weights, token):
    chunk = chunks[0].shape[0]
    length = 4 * chunk
    return run(
        attend_body,
        "attend",
        15,
        [
            group(chunks),
            whole(first_weights, D, 768),
            whole(first_weights, D + 768, 128),
            freqs,
            weights,
        ],
        [
            ((16, D), WIDE),
            out_rows((length, D), LOW),
            out_rows((length, 768), LOW),
            out_rows((length, 256), WIDE),
            out_whole((length // 2, 256), LOW),
            out_whole((length // 2, 256), LOW),
            out_rows((length, 128), WIDE),
            out_rows((length, 128), WIDE),
            out_rows((length, 128), WIDE),
            out_rows((length, FEATURES), LOW),
            out_rows((length, FEATURES), LOW),
        ],
        [pltpu.VMEM((2, length, 256), LOW)] * 2 + [pltpu.VMEM((2, chunk, 128), WIDE)],
        token,
    )


def middle_body(rank_ref, x, near, far, wo, gain_ref, heads, own_ref, mixed):
    rank = rank_ref[0]
    start_all(near, far, wo, x)
    count, chunk, _ = x.ref.shape
    block = chunk // 2
    near_ref, far_ref = near.wait(), far.wait()
    width = near_ref.shape[2]
    sources = {
        0: ((near_ref, 0, 0), (near_ref, 2, 0), (far_ref, 0, 0), (far_ref, 0, width)),
        1: ((near_ref, 1, 0), (far_ref, 1, 0), (near_ref, 3, 0), (far_ref, 1, width)),
    }
    for half, order in enumerate((ORDER_A, ORDER_B)):
        for q in range(4):
            ref, which, column = sources[half][q]
            for place, r in enumerate(order):
                start = order.index(r ^ q) * block
                heads.ref[
                    2 * half + place // 2,
                    place % 2 * block : (place % 2 + 1) * block,
                    q * width : (q + 1) * width,
                ] = ref[which, start : start + block, column : column + width]
    heads.start()
    wo_ref = wo.wait()

    def one_chunk(index, carry):
        x.wait_at(index)
        total = x.ref[index, :, :D].astype(WIDE)
        for q in range(4):
            rows = pl.ds(pl.multiple_of((rank ^ q) * width, width), width)
            total = total + dot_plain(
                heads.ref[index, :, q * width : (q + 1) * width], wo_ref[rows, :]
            )

        @pl.when(index % 2 == 0)
        def _():
            own_ref[pl.ds(pl.multiple_of(index // 2 * block, block), block), :] = total[:block]

        mixed.ref[index] = (total * unit_rows(total) * gain_ref[1:2, :]).astype(LOW)
        mixed.start_at(index)
        return carry

    lax.fori_loop(0, count, one_chunk, 0)


def middle(rank, chunks, heads, first_weights, gain):
    chunk = chunks[0].shape[0]
    length = 4 * chunk
    lower, lower_x, lower_far, upper, upper_y, upper_far = heads
    return run(
        middle_body,
        "middle",
        7,
        [
            rank,
            group(chunks),
            group((lower, upper, lower_x, upper_y)),
            group((lower_far, upper_far)),
            whole(first_weights, 0, D),
            gain,
        ],
        [out_rows((length, D), LOW), ((chunk, D), WIDE), out_rows((length, D), LOW)],
    )


def feed_body(mixed, gate_up, both, hidden):
    count, _, per = hidden.ref.shape
    mixed.start(0)
    gate_up.start()
    mixed.start(1, 2, 3)

    def one_chunk(index, carry):
        mixed.wait_at(index)
        gate_up_ref = gate_up.wait_first(index)
        rows = mixed.ref[index]
        for half in range(2):
            here = slice(half * per // 2, (half + 1) * per // 2)
            gate = dot_plain(rows, gate_up_ref[half])
            up = dot_plain(rows, gate_up_ref[2 + half])
            sigmoid = 1.0 / (1.0 + jnp.exp(-gate))
            silu = gate * sigmoid
            both.ref[index, :, here] = (up * (sigmoid + silu * (1.0 - sigmoid))).astype(LOW)
            both.ref[index, :, per + half * per // 2 : per + (half + 1) * per // 2] = silu.astype(LOW)
            hidden.ref[index, :, here] = (silu * up).astype(LOW)
        both.start_at(index)
        hidden.start_at(index)
        return carry

    lax.fori_loop(0, count, one_chunk, 0)


def feed(mixed, gate_up, token):
    length = mixed.shape[0]
    per = gate_up.shape[1] // 2
    return run(
        feed_body,
        "feed",
        8,
        [rows_of(mixed), columns_of(gate_up)],
        [out_rows((length, 2 * per), LOW), out_rows((length, per), LOW)],
        token=token,
    )


def feed_back_body(both, cots, gate_up, down, grads, back):
    start_all(down)
    cots.start(0)
    both.start(0)
    gate_up.start()
    for k in range(1, 4):
        cots.start(k)
        both.start(k)
    count, _, _ = cots.ref.shape
    per = down.ref.shape[0]

    def one_chunk(index, carry):
        cots.wait_at(index)
        both.wait_at(index)
        grad_hidden = dot_rows(cots.ref[index], down.wait_first(index)[...])
        grads.ref[index, :, :per] = (
            grad_hidden * both.ref[index, :, :per].astype(WIDE)
        ).astype(LOW)
        grads.ref[index, :, per:] = (
            grad_hidden * both.ref[index, :, per:].astype(WIDE)
        ).astype(LOW)
        grads.start_at(index)
        back.ref[index] = dot_rows(grads.ref[index], gate_up.wait_first(index)[...]).astype(LOW)
        back.start_at(index)
        return carry

    lax.fori_loop(0, count, one_chunk, 0)


def feed_back(both, cots, gate_up, down, token):
    length = both.shape[0]
    per = down.shape[0]
    return run(
        feed_back_body,
        "feed_back",
        11,
        [rows_of(both), group(cots), whole(gate_up), whole(down)],
        [out_rows((length, 2 * per), LOW), out_group((length // 4, D), LOW)],
        token=token,
    )


def sum_arrived(near, got, last):
    return (
        near.wait()[...].astype(WIDE) + got.wait()[...].astype(WIDE) + last.wait()[...].astype(WIDE)
    )


def arrivals(sums):
    return [whole(x) if place % 3 == 2 else top(x) for place, x in enumerate(sums)]


def own_back_body(
    rank_ref, n0, g0, l0, n1, g1, l1, middle_rows, cot, gain_ref, wo, grad, parcels
):
    rank = rank_ref[0]
    start_all(n0, g0, l0, middle_rows, cot, n1, g1, l1, wo)
    block = l0.ref.shape[0]
    width = parcels.ref.shape[2] // 2
    for place, sums in enumerate(((n0, g0, l0), (n1, g1, l1))):
        rows = slice(place * block, (place + 1) * block)
        arrived = sum_arrived(*sums)
        y = middle_rows.wait()[rows, :]
        scale = unit_rows(y)
        normed = y * scale
        turned = arrived * gain_ref[1:2, :]
        grad.ref[rows, :] = cot.wait()[rows, :].astype(WIDE) + scale * (
            turned - normed * jnp.mean(turned * normed, -1, keepdims=True)
        )
    low_grad = grad.ref[...].astype(LOW)
    wo_ref = wo.wait()
    for q in range(4):
        place = pl.ds(pl.multiple_of((rank ^ q) * width, width), width)
        parcels.ref[q, :, :width] = dot_rows(low_grad, wo_ref[place, :]).astype(LOW)
        parcels.ref[q, :, width:] = grad.ref[:, place].astype(LOW)


def own_back(rank, sums, middle_own, cot_own, gain, first_weights, token):
    quarter = cot_own.shape[0]
    return run(
        own_back_body,
        "own_back",
        4,
        [rank, *arrivals(sums), whole(middle_own), whole(cot_own), gain]
        + [whole(first_weights, 0, D)],
        [out_whole((quarter, D), WIDE), out_group((quarter, 512), LOW)],
        token=token,
    )


def attend_back_body(
    pair, parcels, q, k, v, wide, logs, cos, sin, query_sides, key_sides, weights_ref,
    out, bias_ref, queries_ref, grads_ref, total_ref,
):
    start_all(parcels, q, query_sides, logs, wide, k, v, key_sides, cos, sin)
    length = q.ref.shape[0]
    chunk = length // 4
    block = chunk // 2
    half_lane = lax.broadcasted_iota(jnp.int32, (chunk, 128), 1) // 64
    lane = lax.broadcasted_iota(jnp.int32, (chunk, 128), 1)
    parcels_ref = parcels.wait()
    for half, order in enumerate((ORDER_A, ORDER_B)):
        for place in range(4):
            to = slice((4 * half + place) * block, (4 * half + place + 1) * block)
            rows = slice(half * block, (half + 1) * block)
            for head in range(2):
                grads_ref[head, to, :128] = parcels_ref[order[place], rows, :]
    q_ref, side_ref, log_ref, wide_ref = q.wait(), query_sides.wait(), logs.wait(), wide.wait()

    def prepare(index, carry):
        rows = pl.ds(pl.multiple_of(index * chunk, chunk), chunk)
        product = grads_ref[0, rows, :128].astype(WIDE) * wide_ref[rows, :]
        scaled = q_ref[rows, :] * LOW(SCORE_SCALE)
        for half in range(2):
            head = 2 * pair + half
            side = side_ref[rows, :] * weights_ref[head : head + 1, :]
            for place, piece in enumerate(three_parts(-log_ref[rows, head : head + 1])):
                side = jnp.where(lane == LSE_AT + place, piece, side)
            queries_ref[half, rows, :128] = jnp.where(half_lane == half, scaled, LOW(0))
            queries_ref[half, rows, 128:] = side
            delta = jnp.sum(jnp.where(half_lane == half, product, 0.0), 1, keepdims=True)
            extra = jnp.zeros((chunk, 128), LOW)
            for place, piece in enumerate(three_parts(-delta)):
                extra = jnp.where(lane == place, piece, extra)
            grads_ref[half, rows, 128:] = extra
        total_ref[rows, :] = jnp.zeros((chunk, 128), WIDE)
        return carry

    lax.fori_loop(0, 4, prepare, 0)
    three_ones = jnp.where(lane < 3, 1.0, 0.0).astype(LOW)
    k_ref, v_ref, key_ref, cos_ref, sin_ref = (
        k.wait(), v.wait(), key_sides.wait(), cos.wait(), sin.wait()
    )

    def one_block(index, carry):
        rows = pl.ds(pl.multiple_of(index * chunk, chunk), chunk)
        cosine = cos_ref[rows, :]
        sine = -sin_ref[rows, :]
        key_side = key_ref[rows, :]
        first_four = jnp.where(lane < 4, key_side.astype(WIDE), 0.0)
        sums = list(carry)
        keys = k_ref[rows, :]
        values = v_ref[rows, :]
        keys_wide = jnp.concatenate([keys, key_side], 1)
        grad_keys = jnp.zeros((chunk, 128), WIDE)
        grad_values = jnp.zeros((chunk, 128), WIDE)
        for half in range(2):
            mine = half_lane == half
            weights = jnp.exp(dot_rows(keys_wide, queries_ref[half]))
            grad_weights = dot_rows(
                jnp.concatenate([jnp.where(mine, values, LOW(0)), three_ones], 1), grads_ref[half]
            )
            grad_values = jnp.where(
                mine, dot_plain(weights.astype(LOW), grads_ref[half, :, :128]), grad_values
            )
            grad_scores = (weights * grad_weights).astype(LOW)
            both = dot_plain(
                grad_scores,
                jnp.concatenate([queries_ref[half, :, :128], side_ref[...]], 1),
            )
            grad_keys = grad_keys + both[:, :128]
            counted = both[:, 128:]
            same = jnp.sum(counted * first_four, 0, keepdims=True)
            every = jnp.sum(jnp.where(lane < 4, counted, 0.0), 0, keepdims=True)
            sums[half] = sums[half] + same
            sums[2 + half] = sums[2 + half] + (every - same)
            total_ref[...] += dot_first(grad_scores, jnp.where(mine, keys, LOW(0)))
        out.ref[index, :, 128:256] = turn_pair(grad_keys, cosine, sine).astype(LOW)
        out.ref[index, :, 256:] = grad_values.astype(LOW)
        return tuple(sums)

    start = tuple(jnp.zeros((1, 128), WIDE) for _ in range(4))
    sums = lax.fori_loop(0, 4, one_block, start)
    bias_ref[...] = jnp.zeros_like(bias_ref)
    for place in range(4):
        bias_ref[place : place + 1, :] = sums[place]
    for place in range(4):
        rows = slice(place * chunk, (place + 1) * chunk)
        out.ref[place, :, :128] = turn_pair(
            total_ref[rows, :] * SCORE_SCALE, cos_ref[rows, :], -sin_ref[rows, :]
        ).astype(LOW)


def attend_back(pair, parcels, kept, weights, token):
    turned, attended, *others = kept
    length = turned.shape[0]
    at = 128 * pair
    return run(
        functools.partial(attend_back_body, pair),
        "attend_back",
        40,
        [group(parcels, at, 128)]
        + [whole(turned, column + at, 128) for column in (0, 256, 512)]
        + [whole(attended, at, 128)]
        + [whole(x) for x in others]
        + [weights],
        [out_rows((length, 384), LOW), ((8, 128), WIDE)],
        [
            pltpu.VMEM((2, length, 256), LOW),
            pltpu.VMEM((2, length, 256), LOW),
            pltpu.VMEM((length, 128), WIDE),
        ],
        token,
    )


def project_back_body(proj0, proj1, weights, back, joined_ref):
    start_all(proj0, proj1, weights)
    proj = (proj0.wait(), proj1.wait())
    weights_ref = weights.wait()

    def one_chunk(index, carry):
        for kind in range(3):
            for pair in range(2):
                joined_ref[:, 256 * kind + 128 * pair : 256 * kind + 128 * (pair + 1)] = proj[pair][
                    index, :, 128 * kind : 128 * (kind + 1)
                ]
        back.ref[index] = dot_rows(joined_ref[...], weights_ref[...]).astype(LOW)
        back.start_at(index)
        return carry

    lax.fori_loop(0, back.ref.shape[0], one_chunk, 0)


def project_back(proj0, proj1, first_weights, token):
    length = proj0.shape[0]
    return run(
        project_back_body,
        "project_back",
        5,
        [rows_of(proj0), rows_of(proj1), whole(first_weights, D, 768)],
        [out_group((length // 4, D), LOW)],
        [pltpu.VMEM((length // 4, 768), LOW)],
        token,
    )


def down_grads_body(hidden, cots, out):
    start_all(cots, hidden)
    count, chunk, _ = cots.ref.shape

    def one_part(index, carry):
        cots_ref = cots.wait_first(index)
        hidden.wait_at(index)
        total = dot_first(hidden.ref[index, :chunk, :], cots_ref[0])
        for k in range(1, count):
            total = total + dot_first(
                hidden.ref[index, k * chunk : (k + 1) * chunk, :], cots_ref[k]
            )
        out.ref[index] = total.astype(LOW)
        out.start_at(index)
        return carry

    lax.fori_loop(0, hidden.ref.shape[0], one_part, 0)


def down_grads(hidden, cots):
    per = hidden.shape[1]
    return run(
        down_grads_body,
        "down_grads",
        5,
        [columns_of(hidden), group(cots)],
        [out_rows((per, D), LOW)],
    )[0]


def gate_up_grads_body(mixed, grads, out):
    start_all(grads, mixed)

    def one_part(index, carry):
        grads_ref = grads.wait_first(index)
        mixed.wait_at(index)
        out.ref[index] = dot_first(mixed.ref[index], grads_ref[...]).astype(LOW)
        out.start_at(index)
        return carry

    lax.fori_loop(0, mixed.ref.shape[0], one_part, 0)


def gate_up_grads(mixed, grads, token):
    return run(
        gate_up_grads_body,
        "gate_up_grads",
        8,
        [columns_of(mixed), whole(grads)],
        [out_rows((D, grads.shape[1]), LOW)],
        token=token,
    )[0]


def feed_out_body(hidden, down, out):
    start_all(down, hidden)

    def one_chunk(index, carry):
        down_ref = down.wait_first(index)
        hidden.wait_at(index)
        out.ref[index] = dot_plain(hidden.ref[index], down_ref[...]).astype(LOW)
        out.start_at(index)
        return carry

    lax.fori_loop(0, hidden.ref.shape[0], one_chunk, 0)


def feed_out(hidden, down, token):
    length = hidden.shape[0]
    return run(
        feed_out_body,
        "feed_out",
        5,
        [rows_of(hidden), whole(down)],
        [out_group((length // 4, D), LOW)],
        token=token,
    )


def own_last_body(
    n0, g0, l0, n1, g1, l1, m0, h0, k0, m1, h1, k1, x, base, middle_rows, gain_ref, out
):
    start_all(n0, g0, l0, x, base, m0, h0, k0, middle_rows, n1, g1, l1, m1, h1, k1)
    block = l0.ref.shape[0]
    piece = out.ref.shape[1] // 2
    each = block // piece
    for half, (back, forward) in enumerate(
        (((n0, g0, l0), (m0, h0, k0)), ((n1, g1, l1), (m1, h1, k1)))
    ):
        rows = slice(half * block, (half + 1) * block)
        places = slice(half * each, (half + 1) * each)
        turned = sum_arrived(*back) * gain_ref[0:1, :]
        x_rows = x.wait()[rows, :D].astype(WIDE)
        scale = unit_rows(x_rows)
        normed = x_rows * scale
        grad = base.wait()[rows, :] + scale * (
            turned - normed * jnp.mean(turned * normed, -1, keepdims=True)
        )
        out.ref[places, :piece, :] = grad.astype(LOW).reshape(each, piece, D)
        block_rows = sum_arrived(*forward) + middle_rows.wait()[rows, :]
        out.ref[places, piece:, :] = block_rows.astype(LOW).reshape(each, piece, D)


def own_last(sums, out_sums, mine, base, middle_own, gain, n_seq, token):
    quarter = base.shape[0]
    return run(
        own_last_body,
        "own_last",
        80,
        [*arrivals(sums), *arrivals(out_sums), whole(mine), whole(base), whole(middle_own), gain],
        [out_whole((n_seq, 2 * quarter // n_seq, D), LOW)],
        token=token,
    )[0]


def join_body(left, right, out):
    start_all(left, right)
    width = left.ref.shape[1]
    out.ref[:, :width] = left.wait()[...]
    out.ref[:, width:] = right.wait()[...]


def join(left, right, token):
    rows = left.shape[0]
    return run(
        join_body,
        "join",
        100,
        [whole(left), whole(right)],
        [out_whole((rows, left.shape[1] + right.shape[1]), LOW)],
        token=token,
    )[0]


def first_grads_body(rank_ref, mixed, proj0, proj1, heads, parcels, bias_ref, out, joined_ref):
    rank = rank_ref[0]
    start_all(mixed, proj0, proj1, parcels, heads)
    width = 256
    block = parcels.ref.shape[1] // 2
    for pair, proj in enumerate((proj0, proj1)):
        ref = proj.wait()
        for kind in range(3):
            column = width * kind + 128 * pair
            joined_ref[:, column : column + 128] = ref[:, 128 * kind : 128 * (kind + 1)]
    parcels_ref = parcels.wait()
    for half, order in enumerate((ORDER_A, ORDER_B)):
        for place in range(4):
            to = slice((4 * half + place) * block, (4 * half + place + 1) * block)
            joined_ref[to, 3 * width :] = parcels_ref[
                order[place], half * block : (half + 1) * block, :
            ]
    mixed_ref, heads_ref = mixed.wait(), heads.wait()

    def one_part(index, carry):
        out.ref[index, :, : 3 * width] = dot_first(
            mixed_ref[index], joined_ref[:, : 3 * width]
        ).astype(LOW)
        out.ref[rank ^ index, :, 3 * width : 4 * width] = dot_first(
            heads_ref[index], joined_ref[:, 3 * width :]
        ).astype(LOW)
        out.ref[index, :, 4 * width :] = bias_ref[...]
        return carry

    lax.fori_loop(0, 4, one_part, 0)


def first_grads(rank, mixed, proj0, proj1, heads, parcels, bias_rows, token):
    length = mixed.shape[0]
    return run(
        first_grads_body,
        "first_grads",
        8,
        [rank, columns_of(mixed), whole(proj0), whole(proj1), columns_of(heads)]
        + [group(parcels, 256, 256), bias_rows],
        [out_rows((D, 768 + 256 + 128), LOW)],
        [pltpu.VMEM((length, 1024), LOW)],
        token,
    )[0]


def rank_blocks(lower, lower_far, upper, upper_far):
    half = lower.shape[0] // 2
    return (
        ((lower, 0), (upper, 0)),
        ((lower, half), (upper_far, 0)),
        ((lower_far, 0), (upper, half)),
        ((lower_far, half), (upper_far, half)),
    )


def lay_flat(column, part):
    count = column.shape[0]
    row = lax.broadcasted_iota(jnp.int32, (count, 128), 0) + part * count
    lane = lax.broadcasted_iota(jnp.int32, (count, 128), 1)
    return jnp.sum(jnp.where(row == lane, column, 0.0), 0, keepdims=True)


def spread_feed_kernel(
    rank_ref, lower, lower_far, upper, upper_far, gate_ref, up_ref, gain_ref,
    grad_gate_ref, grad_up_ref, grad_down_ref, grad_gain_ref,
):
    rank = rank_ref[0]
    half = lower.shape[0] // 2
    piece = 128
    ff = gate_ref.shape[1]
    per = ff // 4
    for r, halves in enumerate(rank_blocks(lower, lower_far, upper, upper_far)):
        for part, (ref, start) in enumerate(halves):
            rows = slice(part * half, (part + 1) * half)
            source = slice(start, start + half)
            for s in range(per // piece):
                to = pl.ds(pl.multiple_of((4 * s + (rank ^ r)) * piece, piece), piece)
                grad_gate_ref[rows, to] = ref[source, s * piece : (s + 1) * piece].astype(WIDE)
                grad_up_ref[rows, to] = ref[source, per + s * piece : per + (s + 1) * piece].astype(
                    WIDE
                )
            to = pl.ds(pl.multiple_of((rank ^ r) * 2 * half + part * half, half), half)
            grad_down_ref[to, :] = ref[source, 2 * per :].astype(WIDE)
    flat = jnp.zeros((1, 128), WIDE)
    for part in range(2):
        rows = slice(part * half, (part + 1) * half)
        total = jnp.sum(
            gate_ref[rows, :].astype(WIDE) * grad_gate_ref[rows, :], 1, keepdims=True
        ) + jnp.sum(up_ref[rows, :].astype(WIDE) * grad_up_ref[rows, :], 1, keepdims=True)
        flat = flat + lay_flat(total, part)
    grad_gain_ref[...] = jnp.broadcast_to(flat / gain_ref[...].astype(WIDE), (8, 128))


def spread_feed(rank, pieces, w_gate, w_up, gain):
    shard, ff = w_gate.shape
    return call(
        spread_feed_kernel,
        "spread_feed",
        [((shard, ff), WIDE), ((shard, ff), WIDE), ((ff // 8, D), WIDE), ((8, 128), WIDE)],
        [pl.BlockSpec(memory_space=pltpu.SMEM)] + [whole_block()] * 7,
        4 * shard * ff,
        16 * 2**20,
        (rank, *pieces, w_gate, w_up, gain),
    )


def spread_first_kernel(
    rank_ref, lower, lower_far, upper, upper_far, wq_ref, wk_ref, wv_ref, gain_ref,
    gq_ref, gk_ref, gv_ref, go_ref, grad_gain_ref, bias_ref,
):
    rank = rank_ref[0]
    half = lower.shape[0] // 2
    wide = 256
    bias_ref[...] = jnp.zeros_like(bias_ref)
    for r, halves in enumerate(rank_blocks(lower, lower_far, upper, upper_far)):
        to = pl.ds(pl.multiple_of((rank ^ r) * wide, wide), wide)
        for part, (ref, start) in enumerate(halves):
            rows = slice(part * half, (part + 1) * half)
            source = slice(start, start + half)
            for place, out_ref in enumerate((gq_ref, gk_ref, gv_ref, go_ref)):
                out_ref[rows, to] = ref[source, place * wide : (place + 1) * wide].astype(WIDE)
        ref, start = halves[0]
        bias_ref[pl.ds(rank ^ r, 1), :] = jnp.sum(
            ref[start : start + 16, 4 * wide : 4 * wide + 128].astype(WIDE), 0, keepdims=True
        )
    flat = jnp.zeros((1, 128), WIDE)
    for part in range(2):
        rows = slice(part * half, (part + 1) * half)
        total = jnp.zeros((half, 1), WIDE)
        for weight_ref, grad_ref in ((wq_ref, gq_ref), (wk_ref, gk_ref), (wv_ref, gv_ref)):
            total = total + jnp.sum(
                weight_ref[rows, :].astype(WIDE) * grad_ref[rows, :], 1, keepdims=True
            )
        flat = flat + lay_flat(total, part)
    grad_gain_ref[...] = jnp.broadcast_to(flat / gain_ref[...].astype(WIDE), (8, 128))


def spread_first(rank, pieces, w_query, w_key, w_value, gain):
    shard = w_query.shape[0]
    return call(
        spread_first_kernel,
        "spread_first",
        [((shard, D), WIDE)] * 4 + [((8, 128), WIDE), ((8, 128), WIDE)],
        [pl.BlockSpec(memory_space=pltpu.SMEM)] + [whole_block()] * 8,
        4 * shard * D,
        8 * 2**20,
        (rank, *pieces, w_query, w_key, w_value, gain),
    )


def on_plane(
    inputs,
    w_query,
    w_key,
    w_value,
    w_output,
    gain_attention,
    w_gate,
    w_up,
    w_down,
    gain_feed,
    variate_bias,
    segment_ids,
    variate_ids,
    positions,
    grad_output,
):
    rank = lax.axis_index("batch")
    rank_row = jnp.reshape(rank, (1,)).astype(jnp.int32)
    micro, tokens = inputs.shape[0], inputs.shape[2]
    n_seq = lax.axis_size("seq")
    shard = w_query.shape[0]
    per = D // 4

    packed, first_shard, gate_up_shard, down_shard = pack(
        rank_row,
        inputs.reshape(micro, tokens, D),
        grad_output.reshape(micro, tokens, D),
        segment_ids.reshape(micro, tokens),
        variate_ids.reshape(micro, tokens),
        positions.reshape(micro, tokens),
        (w_output, w_query, w_key, w_value),
        (gain_attention.reshape(1, shard), gain_feed.reshape(1, shard)),
        w_gate,
        w_up,
        w_down,
    )
    first_weights = lax.all_gather(first_shard, "seq", axis=0, tiled=True)
    gate_up = lax.all_gather(gate_up_shard, "seq", axis=0, tiled=True)
    down = lax.all_gather(down_shard, "seq", axis=0, tiled=True)
    packed = lax.all_to_all(packed, "batch", 0, 0, tiled=True)
    by_sequence = [
        packed[:, kind].reshape(4 * micro, tokens // 4, D + 128)[:, :, : D + 128 - 128 * kind]
        for kind in range(2)
    ]
    mine, cot_by_sequence = lax.optimization_barrier((over_seq(by_sequence[0]), by_sequence[1]))
    cot_mine = over_seq(cot_by_sequence)
    freqs = jnp.exp((jnp.arange(128) % 32).astype(WIDE) * (-2.0 * math.log(10000.0) / HD))[None, :]
    my_bias = lax.dynamic_slice_in_dim(variate_bias, rank * 4, 4, 1)
    weights = jnp.pad(head_weights(my_bias[0], my_bias[1]), ((0, 4), (0, 0)))

    chunks = gather_plane(mine)
    gain, mixed_first, turned, attended, lower, upper, *kept = attend(
        chunks, first_weights, freqs, weights, rank_row
    )
    lower_x, upper_y = swap(lower, 1), swap(upper, 2)
    lower_far = swap(jnp.concatenate([lower, lower_x], 1), 2)
    upper_far = swap(jnp.concatenate([upper, upper_y], 1), 1)
    cot_got = swap_pairs(lax.optimization_barrier((cot_mine, lower_far, upper_far))[0])
    heads, middle_own, mixed_second = middle(
        rank_row,
        chunks,
        (lower, lower_x, lower_far, upper, upper_y, upper_far),
        first_weights,
        gain,
    )

    both, hidden = feed(mixed_second, gate_up, after(rank_row, cot_got))
    cots = far_pairs(cot_mine, lax.optimization_barrier((cot_got, mixed_second))[0])
    down_weight_grads = down_grads(hidden, cots)
    down_grad_shard = lax.psum_scatter(down_weight_grads, "seq", scatter_dimension=0, tiled=True)
    grad_gate_up, *back = feed_back(
        both, cots, gate_up, down, after(rank_row, down_weight_grads)
    )
    got = scatter_first(back)
    gate_up_weight_grads = gate_up_grads(mixed_second, grad_gate_up, after(rank_row, got))
    gate_up_grad_shard = lax.psum_scatter(
        gate_up_weight_grads, "seq", scatter_dimension=0, tiled=True
    )
    sums = scatter_second(back, got)
    grad_middle, *parcels = own_back(
        rank_row, sums, middle_own, cot_mine, gain, first_weights,
        after(rank_row, gate_up_weight_grads),
    )
    out_chunks = feed_out(hidden, down, after(rank_row, parcels[0]))
    parcels = [parcels[0]] + [swap(parcels[r], r) for r in range(1, 4)]

    far_chunks = lax.optimization_barrier(((out_chunks[1], out_chunks[3]), parcels))[0]
    out_got = scatter_first((None, far_chunks[0], None, far_chunks[1]))
    kept = (turned, attended, *kept)
    proj0, bias0 = attend_back(
        0, parcels, kept, weights, after(rank_row, far_chunks, down_grad_shard)
    )
    out_got = lax.optimization_barrier((out_got, bias0))[0]
    out_sums = scatter_second(out_chunks, out_got)
    proj1, bias1 = attend_back(1, parcels, kept, weights, after(rank_row, out_got))
    back = project_back(
        proj0, proj1, first_weights, after(rank_row, out_sums[2], out_sums[5])
    )
    got = scatter_first(back)
    bias_sums = jnp.sum(jnp.concatenate([bias0[:2], bias1[:2], bias0[2:4], bias1[2:4]], 0), 1)
    bias_parts = jnp.pad(jnp.concatenate(three_parts(bias_sums)), (0, 104))[None, :]
    slots = lax.broadcasted_iota(jnp.int32, (per, 1), 0) % shard == lax.axis_index("seq")
    bias_rows = jnp.where(slots, bias_parts, LOW(0))
    first_weight_grads = first_grads(
        rank_row, mixed_first, proj0, proj1, heads, parcels, bias_rows, after(rank_row, got)
    )
    first_grad_shard = lax.psum_scatter(first_weight_grads, "seq", scatter_dimension=0, tiled=True)
    sums = scatter_second(back, got)
    last = own_last(
        sums, out_sums, mine, grad_middle, middle_own, gain, n_seq,
        after(rank_row, first_weight_grads),
    )
    moved = lax.all_to_all(last, "seq", 0, 0, tiled=True)
    quarter = tokens // 4
    feed_pieces = gather_plane(
        join(gate_up_grad_shard, down_grad_shard, after(rank_row, last))
    )
    first_pieces = gather_plane(after(first_grad_shard, feed_pieces))
    moved, first_pieces = lax.optimization_barrier((moved, first_pieces))
    moved = moved.reshape(4, micro, 2 * quarter, D)
    moved = lax.all_to_all(moved, "batch", 0, 0, tiled=True)
    grad_inputs = jnp.transpose(moved[:, :, :quarter].astype(WIDE), (1, 0, 2, 3))
    block_output = jnp.transpose(moved[:, :, quarter:], (1, 0, 2, 3))

    grad_gate, grad_up, grad_down, grad_gain_second = spread_feed(
        rank_row, feed_pieces, w_gate, w_up, gain_feed.reshape(1, shard)
    )
    grad_query, grad_key, grad_value, grad_output_weights, grad_gain_first, bias_table = (
        spread_first(
            rank_row, first_pieces, w_query, w_key, w_value, gain_attention.reshape(1, shard)
        )
    )
    bias_table = jnp.sum(bias_table[:4, :24].reshape(4, 3, 2, 4), 1)
    grad_bias = jnp.transpose(bias_table, (1, 0, 2)).reshape(2, H)
    return (
        block_output.reshape(inputs.shape),
        grad_inputs.reshape(inputs.shape),
        grad_query,
        grad_key,
        grad_value,
        grad_output_weights,
        grad_gain_first[0],
        grad_gate,
        grad_up,
        grad_down,
        grad_gain_second[0],
        grad_bias,
    )


def solution(mesh):
    n_batch, n_seq = mesh.shape["batch"], mesh.shape["seq"]
    step = on_plane if n_batch == 4 and n_seq == 8 else on_device
    return jax.shard_map(
        step,
        mesh=mesh,
        in_specs=(
            P(None, "batch", "seq", None),
            P("seq", None),
            P("seq", None),
            P("seq", None),
            P("seq", None),
            P("seq"),
            P("seq", None),
            P("seq", None),
            P("seq", None),
            P("seq"),
            P(),
            P(None, "batch", "seq"),
            P(None, "batch", "seq"),
            P(None, "batch", "seq"),
            P(None, "batch", "seq", None),
        ),
        out_specs=(
            P(None, "batch", "seq", None),
            P(None, "batch", "seq", None),
            P("seq", None),
            P("seq", None),
            P("seq", None),
            P("seq", None),
            P("seq"),
            P("seq", None),
            P("seq", None),
            P("seq", None),
            P("seq"),
            P(),
        ),
        check_vma=False,
    )
```

```python
import functools
import math

import jax
import jax.numpy as jnp
from jax import lax
from jax.experimental import pallas as pl
from jax.experimental.pallas import tpu as pltpu
from jax.sharding import PartitionSpec as P

D = 1024
H = 16
HD = 64
REACH = 6


EPSILON = 1e-05
SCORE_SCALE = 0.125
MASKED = -1e30


def from_behind(value, axis, by):
    length = lax.axis_size(axis)
    pairs = [(i, i + by) for i in range(length) if 0 <= i + by < length]
    return lax.ppermute(value, axis, pairs)


def step_offset(step):
    distance = step // 2 + 1
    return distance if step % 2 == 0 else -distance


def rotary(values_in, positions_in, turn):
    row_count = values_in.shape[0]
    halfway = HD // 2
    freqs = jnp.exp(jnp.arange(halfway, dtype=jnp.float32) * (-2.0 * math.log(10000.0) / HD))
    angles = positions_in.astype(jnp.float32)[:, None] * freqs[None, :]
    cosine = jnp.cos(angles)[:, None, :]
    sine = turn * jnp.sin(angles)[:, None, :]
    shaped = values_in.reshape(row_count, H, HD)
    first_half = shaped[..., :halfway]
    second_half = shaped[..., halfway:]
    turned = jnp.concatenate(
        [first_half * cosine - second_half * sine, first_half * sine + second_half * cosine], -1
    )
    return turned.reshape(row_count, H * HD)


def head_scores(query_heads, key_heads, query_variates, key_variates, bias_table):
    raw = jnp.einsum("qhd,khd->hqk", query_heads, key_heads, preferred_element_type=jnp.float32)
    same_variate = (query_variates[:, None] == key_variates[None, :])[None]
    return raw * SCORE_SCALE + jnp.where(
        same_variate, bias_table[0][:, None, None], bias_table[1][:, None, None]
    )


def attend_forward(query_rows, own_keys, own_values, own_segments, own_variates, bias_table):
    tok_count = query_rows.shape[0]
    query_heads = query_rows.reshape(tok_count, H, HD)
    shifted_segments = own_segments + 1

    def fold_keys(carried, piece_rows):
        key_part, value_part, segment_part, variate_part = piece_rows
        part_count = key_part.shape[0]
        live = shifted_segments[:, None] == segment_part[None, :]

        def update(state):
            running_max, running_total, running_sum = state
            logits = head_scores(
                query_heads,
                key_part.reshape(part_count, H, HD),
                own_variates,
                variate_part,
                bias_table,
            )
            logits = jnp.where(live[None], logits, MASKED)
            new_max = jnp.maximum(running_max, jnp.max(logits, -1))
            rescale = jnp.exp(running_max - new_max)
            weights = jnp.where(live[None], jnp.exp(logits - new_max[..., None]), 0.0)
            new_total = running_total * rescale + jnp.sum(weights, -1)
            mixed = jnp.einsum(
                "hqk,khd->qhd",
                weights.astype(jnp.bfloat16),
                value_part.reshape(part_count, H, HD),
                preferred_element_type=jnp.float32,
            )
            new_sum = running_sum * jnp.transpose(rescale)[:, :, None] + mixed
            return (new_max, new_total, new_sum)

        return lax.cond(jnp.any(live), update, lambda state: state, carried)

    near_rows = (own_keys, own_values, shifted_segments, own_variates)
    state = (
        jnp.full((H, tok_count), MASKED, jnp.float32),
        jnp.zeros((H, tok_count), jnp.float32),
        jnp.zeros((tok_count, H, HD), jnp.float32),
    )
    state = fold_keys(state, near_rows)
    for step in range(2 * REACH):
        arrived = from_behind(
            (own_keys, own_values, shifted_segments, own_variates), "seq", step_offset(step)
        )
        state = fold_keys(state, arrived)
    final_max, final_total, final_sum = state
    attended = final_sum / jnp.transpose(final_total)[:, :, None]
    log_rows = jnp.transpose(final_max + jnp.log(final_total))
    return (attended.reshape(tok_count, H * HD), log_rows)


def attend_queries_back(
    query_rows,
    grad_rows,
    log_rows,
    delta_rows,
    own_keys,
    own_values,
    own_segments,
    own_variates,
    bias_table,
):
    tok_count = query_rows.shape[0]
    query_heads = query_rows.reshape(tok_count, H, HD)
    grad_heads = grad_rows.reshape(tok_count, H, HD)
    log_heads = jnp.transpose(log_rows)
    delta_heads = jnp.transpose(delta_rows)
    shifted_segments = own_segments + 1

    def fold_keys_back(carried, piece_rows):
        key_part, value_part, segment_part, variate_part = piece_rows
        part_count = key_part.shape[0]
        live = shifted_segments[:, None] == segment_part[None, :]

        def update(state):
            grad_query, grad_bias = state
            key_heads = key_part.reshape(part_count, H, HD)
            logits = head_scores(query_heads, key_heads, own_variates, variate_part, bias_table)
            weights = jnp.where(live[None], jnp.exp(logits - log_heads[..., None]), 0.0)
            grad_weights = jnp.einsum(
                "qhd,khd->hqk",
                grad_heads,
                value_part.reshape(part_count, H, HD),
                preferred_element_type=jnp.float32,
            )
            grad_logits = (weights * (grad_weights - delta_heads[..., None])).astype(jnp.bfloat16)
            grad_query = grad_query + SCORE_SCALE * jnp.einsum(
                "hqk,khd->qhd", grad_logits, key_heads, preferred_element_type=jnp.float32
            )
            same_variate = (own_variates[:, None] == variate_part[None, :])[None]
            logit_values = grad_logits.astype(jnp.float32)
            same_total = jnp.sum(jnp.where(same_variate, logit_values, 0.0), axis=(1, 2))
            other_total = jnp.sum(jnp.where(same_variate, 0.0, logit_values), axis=(1, 2))
            return (grad_query, grad_bias + jnp.stack([same_total, other_total]))

        return lax.cond(jnp.any(live), update, lambda state: state, carried)

    state = (jnp.zeros((tok_count, H, HD), jnp.float32), jnp.zeros((2, H), jnp.float32))
    state = fold_keys_back(state, (own_keys, own_values, shifted_segments, own_variates))
    for step in range(2 * REACH):
        arrived = from_behind(
            (own_keys, own_values, shifted_segments, own_variates), "seq", step_offset(step)
        )
        state = fold_keys_back(state, arrived)
    grad_query, grad_bias = state
    return (grad_query.reshape(tok_count, H * HD), grad_bias)


def attend_keys_back(
    query_rows,
    grad_rows,
    log_rows,
    delta_rows,
    own_keys,
    own_values,
    own_segments,
    own_variates,
    bias_table,
):
    tok_count = own_keys.shape[0]
    key_heads = own_keys.reshape(tok_count, H, HD)
    value_heads = own_values.reshape(tok_count, H, HD)
    shifted_segments = own_segments + 1

    def fold_queries(carried, piece_rows):
        query_part, grad_part, log_part, delta_part, segment_part, variate_part = piece_rows
        part_count = query_part.shape[0]
        live = segment_part[:, None] == shifted_segments[None, :]

        def update(state):
            grad_key, grad_value = state
            query_heads = query_part.reshape(part_count, H, HD)
            grad_heads = grad_part.reshape(part_count, H, HD)
            logits = head_scores(query_heads, key_heads, variate_part, own_variates, bias_table)
            weights = jnp.where(
                live[None], jnp.exp(logits - jnp.transpose(log_part)[..., None]), 0.0
            )
            grad_value = grad_value + jnp.einsum(
                "hqk,qhd->khd",
                weights.astype(jnp.bfloat16),
                grad_heads,
                preferred_element_type=jnp.float32,
            )
            grad_weights = jnp.einsum(
                "qhd,khd->hqk", grad_heads, value_heads, preferred_element_type=jnp.float32
            )
            grad_logits = (weights * (grad_weights - jnp.transpose(delta_part)[..., None])).astype(
                jnp.bfloat16
            )
            grad_key = grad_key + SCORE_SCALE * jnp.einsum(
                "hqk,qhd->khd", grad_logits, query_heads, preferred_element_type=jnp.float32
            )
            return (grad_key, grad_value)

        return lax.cond(jnp.any(live), update, lambda state: state, carried)

    state = (jnp.zeros((tok_count, H, HD), jnp.float32), jnp.zeros((tok_count, H, HD), jnp.float32))
    state = fold_queries(
        state, (query_rows, grad_rows, log_rows, delta_rows, shifted_segments, own_variates)
    )
    for step in range(2 * REACH):
        arrived = (
            from_behind(query_rows, "seq", step_offset(step)),
            from_behind(grad_rows, "seq", step_offset(step)),
            from_behind(log_rows.astype(jnp.bfloat16), "seq", step_offset(step)).astype(
                log_rows.dtype
            ),
            from_behind(delta_rows.astype(jnp.bfloat16), "seq", step_offset(step)).astype(
                delta_rows.dtype
            ),
            from_behind(shifted_segments, "seq", step_offset(step)),
            from_behind(own_variates, "seq", step_offset(step)),
        )
        state = fold_queries(state, arrived)
    grad_key, grad_value = state
    return (grad_key.reshape(tok_count, H * HD), grad_value.reshape(tok_count, H * HD))


def norm_back(grad_normed, normed, scale_rows):
    return scale_rows * (grad_normed - normed * jnp.mean(grad_normed * normed, -1, keepdims=True))


def on_device(
    inputs,
    w_query,
    w_key,
    w_value,
    w_output,
    gain_attention,
    w_gate,
    w_up,
    w_down,
    gain_feed,
    variate_bias,
    segment_ids,
    variate_ids,
    positions,
    grad_output,
):
    micro_count = inputs.shape[0]
    tok_count = inputs.shape[2]
    row_count = micro_count * tok_count
    residual_in = inputs.reshape(row_count, D).astype(jnp.float32)
    cotangent = grad_output.reshape(row_count, D).astype(jnp.float32)
    segment_rows = segment_ids.reshape(micro_count, tok_count)
    variate_rows = variate_ids.reshape(micro_count, tok_count)
    position_rows = positions.reshape(row_count)
    full_query, full_key, full_value, full_output, full_gain_first = (
        lax.all_gather(w_query, "seq", axis=0, tiled=True),
        lax.all_gather(w_key, "seq", axis=0, tiled=True),
        lax.all_gather(w_value, "seq", axis=0, tiled=True),
        lax.all_gather(w_output, "seq", axis=0, tiled=True),
        lax.all_gather(gain_attention, "seq", axis=0, tiled=True),
    )
    full_gate, full_up, full_down, full_gain_second = (
        lax.all_gather(w_gate, "seq", axis=0, tiled=True),
        lax.all_gather(w_up, "seq", axis=0, tiled=True),
        lax.all_gather(w_down, "seq", axis=0, tiled=True),
        lax.all_gather(gain_feed, "seq", axis=0, tiled=True),
    )
    scale_first = lax.rsqrt(jnp.mean(residual_in * residual_in, -1, keepdims=True) + EPSILON)
    normed_first = residual_in * scale_first
    mixed_first = (normed_first * full_gain_first.astype(jnp.float32)).astype(jnp.bfloat16)
    query_proj = jnp.dot(mixed_first, full_query, preferred_element_type=jnp.float32)
    key_proj = jnp.dot(mixed_first, full_key, preferred_element_type=jnp.float32)
    value_proj = jnp.dot(mixed_first, full_value, preferred_element_type=jnp.float32)
    query_rows = rotary(query_proj, position_rows, 1.0).astype(jnp.bfloat16)
    key_rows = rotary(key_proj, position_rows, 1.0).astype(jnp.bfloat16)
    value_rows = value_proj.astype(jnp.bfloat16)
    attended_parts = []
    log_parts = []
    for micro_index in range(micro_count):
        lower_row = micro_index * tok_count
        upper_row = lower_row + tok_count
        attended_part, log_part = attend_forward(
            query_rows[lower_row:upper_row],
            key_rows[lower_row:upper_row],
            value_rows[lower_row:upper_row],
            segment_rows[micro_index],
            variate_rows[micro_index],
            variate_bias,
        )
        attended_parts.append(attended_part)
        log_parts.append(log_part)
    attended_all = jnp.concatenate(attended_parts, 0)
    attended_low = attended_all.astype(jnp.bfloat16)
    middle = residual_in + jnp.dot(attended_low, full_output, preferred_element_type=jnp.float32)
    scale_second = lax.rsqrt(jnp.mean(middle * middle, -1, keepdims=True) + EPSILON)
    normed_second = middle * scale_second
    mixed_second = (normed_second * full_gain_second.astype(jnp.float32)).astype(jnp.bfloat16)
    gate_proj = jnp.dot(mixed_second, full_gate, preferred_element_type=jnp.float32)
    up_proj = jnp.dot(mixed_second, full_up, preferred_element_type=jnp.float32)
    sigmoid_gate = jax.nn.sigmoid(gate_proj)
    silu_gate = gate_proj * sigmoid_gate
    hidden_rows = (silu_gate * up_proj).astype(jnp.bfloat16)
    block_rows = middle + jnp.dot(hidden_rows, full_down, preferred_element_type=jnp.float32)
    block_output = block_rows.astype(jnp.bfloat16).reshape(inputs.shape)
    full_query, full_key, full_value, full_output, full_gain_first = (
        lax.all_gather(w_query, "seq", axis=0, tiled=True),
        lax.all_gather(w_key, "seq", axis=0, tiled=True),
        lax.all_gather(w_value, "seq", axis=0, tiled=True),
        lax.all_gather(w_output, "seq", axis=0, tiled=True),
        lax.all_gather(gain_attention, "seq", axis=0, tiled=True),
    )
    full_gate, full_up, full_down, full_gain_second = (
        lax.all_gather(w_gate, "seq", axis=0, tiled=True),
        lax.all_gather(w_up, "seq", axis=0, tiled=True),
        lax.all_gather(w_down, "seq", axis=0, tiled=True),
        lax.all_gather(gain_feed, "seq", axis=0, tiled=True),
    )
    grad_branch_second = cotangent.astype(jnp.bfloat16)
    grad_down = jnp.einsum(
        "rf,rd->fd", hidden_rows, grad_branch_second, preferred_element_type=jnp.float32
    )
    grad_hidden = jnp.einsum(
        "rd,fd->rf", grad_branch_second, full_down, preferred_element_type=jnp.float32
    )
    silu_slope = sigmoid_gate * (1.0 + gate_proj * (1.0 - sigmoid_gate))
    grad_gate_rows = (grad_hidden * up_proj * silu_slope).astype(jnp.bfloat16)
    grad_up_rows = (grad_hidden * silu_gate).astype(jnp.bfloat16)
    grad_gate = jnp.einsum(
        "rd,rf->df", mixed_second, grad_gate_rows, preferred_element_type=jnp.float32
    )
    grad_up = jnp.einsum(
        "rd,rf->df", mixed_second, grad_up_rows, preferred_element_type=jnp.float32
    )
    grad_mixed_second = jnp.einsum(
        "rf,df->rd", grad_gate_rows, full_gate, preferred_element_type=jnp.float32
    ) + jnp.einsum("rf,df->rd", grad_up_rows, full_up, preferred_element_type=jnp.float32)
    grad_gain_second = jnp.sum(grad_mixed_second * normed_second, 0)
    grad_middle = cotangent + norm_back(
        grad_mixed_second * full_gain_second.astype(jnp.float32), normed_second, scale_second
    )
    grad_branch_first = grad_middle.astype(jnp.bfloat16)
    grad_out_proj = jnp.einsum(
        "rd,re->de", attended_low, grad_branch_first, preferred_element_type=jnp.float32
    )
    grad_attended = jnp.einsum(
        "re,de->rd", grad_branch_first, full_output, preferred_element_type=jnp.float32
    ).astype(jnp.bfloat16)
    delta_all = jnp.einsum(
        "rhd,rhd->rh",
        grad_attended.astype(jnp.float32).reshape(row_count, H, HD),
        attended_all.reshape(row_count, H, HD),
    )
    grad_bias_local = jnp.zeros((2, H), jnp.float32)
    query_grad_parts = []
    key_grad_parts = []
    value_grad_parts = []
    for micro_index in range(micro_count):
        lower_row = micro_index * tok_count
        upper_row = lower_row + tok_count
        query_grad_part, bias_part = attend_queries_back(
            query_rows[lower_row:upper_row],
            grad_attended[lower_row:upper_row],
            log_parts[micro_index],
            delta_all[lower_row:upper_row],
            key_rows[lower_row:upper_row],
            value_rows[lower_row:upper_row],
            segment_rows[micro_index],
            variate_rows[micro_index],
            variate_bias,
        )
        key_grad_part, value_grad_part = attend_keys_back(
            query_rows[lower_row:upper_row],
            grad_attended[lower_row:upper_row],
            log_parts[micro_index],
            delta_all[lower_row:upper_row],
            key_rows[lower_row:upper_row],
            value_rows[lower_row:upper_row],
            segment_rows[micro_index],
            variate_rows[micro_index],
            variate_bias,
        )
        grad_bias_local = grad_bias_local + bias_part
        query_grad_parts.append(query_grad_part)
        key_grad_parts.append(key_grad_part)
        value_grad_parts.append(value_grad_part)
    grad_query_rows = rotary(jnp.concatenate(query_grad_parts, 0), position_rows, -1.0).astype(
        jnp.bfloat16
    )
    grad_key_rows = rotary(jnp.concatenate(key_grad_parts, 0), position_rows, -1.0).astype(
        jnp.bfloat16
    )
    grad_value_rows = jnp.concatenate(value_grad_parts, 0).astype(jnp.bfloat16)
    grad_query = jnp.einsum(
        "rd,re->de", mixed_first, grad_query_rows, preferred_element_type=jnp.float32
    )
    grad_key = jnp.einsum(
        "rd,re->de", mixed_first, grad_key_rows, preferred_element_type=jnp.float32
    )
    grad_value = jnp.einsum(
        "rd,re->de", mixed_first, grad_value_rows, preferred_element_type=jnp.float32
    )
    grad_mixed_first = (
        jnp.einsum("re,de->rd", grad_query_rows, full_query, preferred_element_type=jnp.float32)
        + jnp.einsum("re,de->rd", grad_key_rows, full_key, preferred_element_type=jnp.float32)
        + jnp.einsum("re,de->rd", grad_value_rows, full_value, preferred_element_type=jnp.float32)
    )
    grad_gain_first = jnp.sum(grad_mixed_first * normed_first, 0)
    grad_input_rows = grad_middle + norm_back(
        grad_mixed_first * full_gain_first.astype(jnp.float32), normed_first, scale_first
    )
    grad_inputs = grad_input_rows.reshape(inputs.shape)
    (
        shard_query,
        shard_key,
        shard_value,
        shard_output,
        shard_gain_first,
        shard_gate,
        shard_up,
        shard_down,
        shard_gain_second,
    ) = (
        lax.psum_scatter(grad_query, "seq", scatter_dimension=0, tiled=True),
        lax.psum_scatter(grad_key, "seq", scatter_dimension=0, tiled=True),
        lax.psum_scatter(grad_value, "seq", scatter_dimension=0, tiled=True),
        lax.psum_scatter(grad_out_proj, "seq", scatter_dimension=0, tiled=True),
        lax.psum_scatter(grad_gain_first, "seq", scatter_dimension=0, tiled=True),
        lax.psum_scatter(grad_gate, "seq", scatter_dimension=0, tiled=True),
        lax.psum_scatter(grad_up, "seq", scatter_dimension=0, tiled=True),
        lax.psum_scatter(grad_down, "seq", scatter_dimension=0, tiled=True),
        lax.psum_scatter(grad_gain_second, "seq", scatter_dimension=0, tiled=True),
    )
    summed = (
        lax.psum(shard_query.astype(jnp.bfloat16), "batch").astype(jnp.float32),
        lax.psum(shard_key.astype(jnp.bfloat16), "batch").astype(jnp.float32),
        lax.psum(shard_value.astype(jnp.bfloat16), "batch").astype(jnp.float32),
        lax.psum(shard_output.astype(jnp.bfloat16), "batch").astype(jnp.float32),
        lax.psum(shard_gain_first.astype(jnp.bfloat16), "batch").astype(jnp.float32),
        lax.psum(shard_gate.astype(jnp.bfloat16), "batch").astype(jnp.float32),
        lax.psum(shard_up.astype(jnp.bfloat16), "batch").astype(jnp.float32),
        lax.psum(shard_down.astype(jnp.bfloat16), "batch").astype(jnp.float32),
        lax.psum(shard_gain_second.astype(jnp.bfloat16), "batch").astype(jnp.float32),
    )
    grad_bias_total = lax.psum(grad_bias_local, ("batch", "seq"))
    return (
        block_output,
        grad_inputs,
        summed[0],
        summed[1],
        summed[2],
        summed[3],
        summed[4],
        summed[5],
        summed[6],
        summed[7],
        summed[8],
        grad_bias_total,
    )


ORDER_A = (0, 1, 2, 3)
ORDER_B = (0, 2, 1, 3)
FEATURES = 128
LSE_AT = 64
LOW = jnp.bfloat16
WIDE = jnp.float32


def swap(value, bit):
    return lax.ppermute(value, "batch", [(i, i ^ bit) for i in range(4)])


def after(value, *others):
    return lax.optimization_barrier((value, *others))[0]


def gather_plane(own):
    half = own.shape[0] // 2
    lower, upper = own[:half], own[half:]
    lower_pair = jnp.concatenate([lower, swap(lower, 1)], 0)
    upper_pair = jnp.concatenate([upper, swap(upper, 2)], 0)
    return lower_pair, swap(lower_pair, 2), upper_pair, swap(upper_pair, 1)


def scatter_first(chunks):
    return swap(chunks[1], 2), swap(chunks[3], 1)


def scatter_second(chunks, got):
    near_lower, _, near_upper, _ = chunks
    got_lower, got_upper = got
    half = near_lower.shape[0] // 2
    last_lower = swap(near_lower[half:] + got_lower[half:], 1)
    last_upper = swap(near_upper[half:] + got_upper[half:], 2)
    return (near_lower, got_lower, last_lower, near_upper, got_upper, last_upper)


def swap_pairs(own):
    half = own.shape[0] // 2
    return swap(own[:half], 1), swap(own[half:], 2)


def far_pairs(own, got):
    half = own.shape[0] // 2
    lower_pair = jnp.concatenate([own[:half], got[0]], 0)
    upper_pair = jnp.concatenate([own[half:], got[1]], 0)
    return lower_pair, swap(lower_pair, 2), upper_pair, swap(upper_pair, 1)


def over_seq(pieces):
    count, quarter, width = pieces.shape
    return lax.all_to_all(pieces, "seq", 0, 0, tiled=True).reshape(count * quarter, width)


def three_parts(value):
    high = value.astype(LOW)
    rest = value - high.astype(WIDE)
    middle = rest.astype(LOW)
    low = (rest - middle.astype(WIDE)).astype(LOW)
    return high, middle, low


def token_features(segments, variates):
    lane = lax.broadcasted_iota(jnp.int32, (segments.shape[0], FEATURES), 1)
    variate_hot = (lane < 12) & (lane % 4 == variates)
    ones = (lane >= 12) & (lane < 15)
    segment_lane = (lane >= 16) & (lane < LSE_AT)
    segment_hot = segment_lane & (lane - 16 == segments)
    segment_cold = segment_lane & (lane - 16 != segments)
    query_side = variate_hot | ones | segment_hot
    key_side = variate_hot | ones | segment_cold | ((lane >= LSE_AT) & (lane < LSE_AT + 3))
    return jnp.where(query_side, 1.0, 0.0).astype(LOW), jnp.where(key_side, 1.0, 0.0).astype(LOW)


def head_weights(same_bias, other_bias):
    gap = [part[:, None] for part in three_parts(same_bias - other_bias)]
    base = [part[:, None] for part in three_parts(other_bias)]
    heads = same_bias.shape[0]
    columns = [jnp.broadcast_to(part, (heads, 4)) for part in gap] + base
    columns.append(jnp.zeros((heads, 1), LOW))
    columns.append(jnp.full((heads, LSE_AT - 16), MASKED, LOW))
    columns.append(jnp.zeros((heads, FEATURES - LSE_AT), LOW))
    return jnp.concatenate(columns, 1)


def turn_pair(pair, cosine, sine):
    lane = lax.broadcasted_iota(jnp.int32, pair.shape, 1)
    crossed = jnp.where(lane % 64 < 32, pltpu.roll(pair, 96, 1), pltpu.roll(pair, 32, 1))
    return pair * cosine + crossed * sine


def dot_plain(left, right):
    return jnp.dot(left, right, preferred_element_type=WIDE)


def dot_rows(left, right):
    return lax.dot_general(left, right, (((1,), (1,)), ((), ())), preferred_element_type=WIDE)


def dot_first(left, right):
    return lax.dot_general(left, right, (((0,), (0,)), ((), ())), preferred_element_type=WIDE)


def whole_block():
    return pl.BlockSpec(memory_space=pltpu.VMEM)


def call(kernel, name, outs, specs, flops, moved, args, scratch=()):
    return pl.pallas_call(
        kernel,
        grid=(1,),
        out_shape=[jax.ShapeDtypeStruct(shape, dtype) for shape, dtype in outs],
        in_specs=specs,
        out_specs=[pl.BlockSpec(memory_space=pltpu.VMEM) for _ in outs],
        scratch_shapes=list(scratch),
        cost_estimate=pl.CostEstimate(flops=flops, bytes_accessed=moved, transcendentals=0),
        compiler_params=pltpu.CompilerParams(vmem_limit_bytes=56 * 2**20),
        name=name,
    )(*args)


class Copies:
    def __init__(self, ref, pairs, sems):
        self.ref = ref
        self.copies = [
            pltpu.make_async_copy(source, target, sems.at[k])
            for k, (source, target) in enumerate(pairs)
        ]
        self.started = self.waited = False

    def start(self, *which):
        self.started = True
        for k in which or range(len(self.copies)):
            self.copies[k].start()

    def wait(self):
        if not self.waited:
            for copy in self.copies:
                copy.wait()
        self.waited = True
        return self.ref

    def _at(self, index, act):
        for k, copy in enumerate(self.copies):
            pl.when(index == k)(functools.partial(act, copy))

    def start_at(self, index):
        self.started = True
        self._at(index, lambda copy: copy.start())

    def wait_at(self, index):
        self.waited = True
        self._at(index, lambda copy: copy.wait())

    def wait_first(self, index):
        if not self.waited:
            self.waited = True

            @pl.when(index == 0)
            def _():
                for copy in self.copies:
                    copy.wait()

        return self.ref


class Plan:
    def __init__(self, arrays, shape, pairs, count):
        self.arrays, self.shape, self.pairs, self.count = arrays, shape, pairs, count


def whole(array, column=None, width=None):
    shape = array.shape if column is None else (array.shape[0], width)

    def pairs(refs, buffer):
        if column is None:
            return [(refs[0], buffer)]
        return [(refs[0].at[:, pl.ds(column, width)], buffer)]

    return Plan([array], shape, pairs, 1)


def top(array):
    half = array.shape[0] // 2
    return Plan(
        [array],
        (half, *array.shape[1:]),
        lambda refs, buffer: [(refs[0].at[pl.ds(0, half)], buffer)],
        1,
    )


def rows_of(array, count=4):
    size = array.shape[0] // count
    return Plan(
        [array],
        (count, size, array.shape[1]),
        lambda refs, buffer: [
            (refs[0].at[pl.ds(k * size, size)], buffer.at[k]) for k in range(count)
        ],
        count,
    )


def columns_of(array, count=4, column=0, width=None):
    size = (width or array.shape[1]) // count
    return Plan(
        [array],
        (count, array.shape[0], size),
        lambda refs, buffer: [
            (refs[0].at[:, pl.ds(column + k * size, size)], buffer.at[k]) for k in range(count)
        ],
        count,
    )


def group(arrays, column=None, width=None):
    rows = arrays[0].shape[0]

    def pairs(refs, buffer):
        if column is None:
            return [(ref, buffer.at[k]) for k, ref in enumerate(refs)]
        return [(ref.at[:, pl.ds(column, width)], buffer.at[k]) for k, ref in enumerate(refs)]

    return Plan(
        list(arrays), (len(arrays), rows, width or arrays[0].shape[1]), pairs, len(arrays)
    )


def out_rows(shape, dtype, count=4):
    size = shape[0] // count

    def pairs(refs, buffer):
        return [(buffer.at[k], refs[0].at[pl.ds(k * size, size)]) for k in range(count)]

    return Plan([(shape, dtype)], (count, size, *shape[1:]), pairs, count)


def out_group(shape, dtype, count=4):
    def pairs(refs, buffer):
        return [(buffer.at[k], ref) for k, ref in enumerate(refs)]

    return Plan([(shape, dtype)] * count, (count, *shape), pairs, count)


def out_whole(shape, dtype):
    return Plan([(shape, dtype)], shape, lambda refs, buffer: [(buffer, refs[0])], 1)


def run(body, name, us, ins, outs, scratch=(), token=None):
    args, in_specs, out_shapes, out_specs, buffers = [], [], [], [], []
    named = len(ins)
    if token is not None:
        ins = [*ins, token]
    for item in ins:
        if isinstance(item, Plan):
            args += item.arrays
            in_specs += [pl.BlockSpec(memory_space=pl.ANY)] * len(item.arrays)
            buffers.append(pltpu.VMEM(item.shape, item.arrays[0].dtype))
            buffers.append(pltpu.SemaphoreType.DMA((item.count,)))
        else:
            args.append(item)
            space = pltpu.SMEM if item.shape == (1,) else pltpu.VMEM
            in_specs.append(pl.BlockSpec(memory_space=space))
    for item in outs:
        if isinstance(item, Plan):
            out_shapes += [jax.ShapeDtypeStruct(*each) for each in item.arrays]
            out_specs += [pl.BlockSpec(memory_space=pl.ANY)] * len(item.arrays)
            buffers.append(pltpu.VMEM(item.shape, item.arrays[0][1]))
            buffers.append(pltpu.SemaphoreType.DMA((item.count,)))
        else:
            out_shapes.append(jax.ShapeDtypeStruct(*item))
            out_specs.append(pl.BlockSpec(memory_space=pltpu.VMEM))
    n_in, n_out = len(args), len(out_shapes)

    def kernel(*refs):
        given, rest = list(refs[: n_in + n_out]), list(refs[n_in + n_out :])
        bound = []
        for item in (*ins, *outs):
            if isinstance(item, Plan):
                near = [given.pop(0) for _ in item.arrays]
                buffer, sems = rest.pop(0), rest.pop(0)
                bound.append(Copies(buffer, item.pairs(near, buffer), sems))
            else:
                bound.append(given.pop(0))
        body(*bound[:named], *bound[len(ins) :], *rest)
        for item in bound[: len(ins)]:
            if isinstance(item, Copies):
                item.wait()
        for item in bound[len(ins) :]:
            if isinstance(item, Copies) and not item.started:
                item.start()
        for item in bound[len(ins) :]:
            if isinstance(item, Copies):
                item.wait()

    return pl.pallas_call(
        kernel,
        out_shape=out_shapes,
        in_specs=in_specs,
        out_specs=out_specs,
        scratch_shapes=buffers + list(scratch),
        cost_estimate=pl.CostEstimate(
            flops=int(us * 1.15e9), bytes_accessed=2**20, transcendentals=0
        ),
        compiler_params=pltpu.CompilerParams(vmem_limit_bytes=60 * 2**20),
        name=name,
    )(*args)


def output_weights(pieces):
    rows = pieces[0].shape[0] // 2
    places = {
        0: ((0, 0), (0, 1), (1, 0), (1, 1)),
        1: ((2, 0), (3, 0), (2, 1), (3, 1)),
    }

    def pairs(refs, buffer):
        rank = lax.axis_index("batch")
        out = []
        for half in range(2):
            for r, (which, part) in enumerate(places[half]):
                to = pl.ds(pl.multiple_of((rank ^ r) * 256, 256), 256)
                out.append(
                    (
                        refs[which].at[pl.ds(part * rows, rows)],
                        buffer.at[pl.ds(half * rows, rows), to],
                    )
                )
        return out

    return Plan(list(pieces), (2 * rows, D), pairs, 8)


def start_all(*items):
    for item in items:
        item.start()


def unit_rows(rows):
    return lax.rsqrt(jnp.mean(rows * rows, -1, keepdims=True) + EPSILON)


def pack_body(
    rank_ref, x, cot, segment_ref, variate_ref, position_ref, wq, wk, wv, wo, gain_first_ref,
    gain_second_ref, gate, up, down, rows_out, shard_out, gate_up_out, down_out,
):
    start_all(wq, wk, wv, wo, x, cot, gate, up, down)
    micro, _, quarter, _ = x.ref.shape
    tokens = 4 * quarter
    lane = lax.broadcasted_iota(jnp.int32, (tokens, 128), 1)
    on_line = lax.broadcasted_iota(jnp.int32, (tokens, 128), 0) == lane

    def upright(row):
        return jnp.sum(jnp.where(on_line, row, 0.0), 1, keepdims=True)

    gains = jnp.where(
        lane == 0,
        upright(gain_first_ref[...].astype(WIDE)),
        jnp.where(lane == 1, upright(gain_second_ref[...].astype(WIDE)), 0.0),
    )
    shard_out.ref[:, D:] = gains.astype(LOW)
    for place, weight in enumerate((wq, wk, wv, wo)):
        shard_out.ref[:, 256 * place : 256 * (place + 1)] = weight.wait()[...]
    shard_out.start()
    for m in range(micro):
        places = position_ref[m : m + 1, :]
        numbers = jnp.zeros((tokens, 128), WIDE)
        for place, row in enumerate(
            (
                segment_ref[m : m + 1, :],
                variate_ref[m : m + 1, :],
                lax.shift_right_logical(places, 5),
                places & 31,
            )
        ):
            numbers = jnp.where(lane == place, upright(row.astype(WIDE)), numbers)
        numbers = numbers.astype(LOW)
        for r in range(4):
            rows_out.ref[r, 0, m, :, D:] = numbers[r * quarter : (r + 1) * quarter, :]
            rows_out.ref[r, 1, m, :, D:] = jnp.zeros((quarter, 128), LOW)
    x_ref, cot_ref = x.wait(), cot.wait()
    for m in range(micro):
        for r in range(4):
            rows_out.ref[r, 0, m, :, :D] = x_ref[m, r]
            rows_out.ref[r, 1, m, :, :D] = cot_ref[m, r]
    rows_out.start()
    gate_ref, up_ref = gate.wait(), up.wait()
    per = gate_up_out.ref.shape[1] // 2
    piece = gate_ref.shape[2]
    for s in range(per // piece):
        gate_up_out.ref[:, s * piece : (s + 1) * piece] = gate_ref[s]
        gate_up_out.ref[:, per + s * piece : per + (s + 1) * piece] = up_ref[s]
    gate_up_out.start()
    down_out.ref[...] = down.wait()[...]


def pack(rank, x, cot, segments, variates, positions, shards, gains, w_gate, w_up, w_down):
    micro, tokens, _ = x.shape
    quarter = tokens // 4
    shard, ff = w_gate.shape
    piece = w_down.shape[0] // 4
    pieces = ff // 4 // piece

    def quarters(array):
        return array.reshape(micro, 4, quarter, D)

    def mine(array, size, refs_at):
        return Plan([array], size, refs_at, 1)

    def rank_columns(array):
        def pairs(refs, buffer):
            at = pl.multiple_of(lax.axis_index("batch") * 256, 256)
            return [(refs[0].at[:, pl.ds(at, 256)], buffer)]

        return Plan([array], (shard, 256), pairs, 1)

    def feed_columns(array):
        def pairs(refs, buffer):
            rank = lax.axis_index("batch")
            return [
                (refs[0].at[:, pl.ds(pl.multiple_of((4 * s + rank) * piece, piece), piece)], buffer.at[s])
                for s in range(pieces)
            ]

        return Plan([array], (pieces, shard, piece), pairs, pieces)

    def down_rows(array):
        def pairs(refs, buffer):
            at = pl.multiple_of(lax.axis_index("batch") * piece, piece)
            return [(refs[0].at[pl.ds(at, piece)], buffer)]

        return Plan([array], (piece, D), pairs, 1)

    return run(
        pack_body,
        "pack",
        4,
        [rank, whole(quarters(x)), whole(quarters(cot)), segments, variates, positions]
        + [rank_columns(weight) for weight in shards]
        + [*gains, feed_columns(w_gate), feed_columns(w_up), down_rows(w_down)],
        [
            out_whole((4, 2, micro, quarter, D + 128), LOW),
            out_whole((shard, D + 128), LOW),
            out_whole((shard, ff // 2), LOW),
            out_whole((piece, D), LOW),
        ],
    )


def attend_body(
    x, qkv, gains, freqs_ref, weights_ref,
    gain_ref, mixed, turned, wide, lower, upper, logs, cos, sin, query_sides, key_sides,
    keys_ref, values_ref, trig_ref,
):
    start_all(x, gains, qkv)
    count, chunk, _ = x.ref.shape
    lane = lax.broadcasted_iota(jnp.int32, (chunk, 128), 1)
    half_lane = lane // 64
    pick = lax.broadcasted_iota(jnp.int32, (16, 128), 0) == lax.broadcasted_iota(
        jnp.int32, (16, 128), 1
    )
    x_ref = x.wait()
    angles = jnp.zeros((chunk, 128), WIDE)
    for k in range(count):
        numbers = x_ref[k, :, D : D + 128].astype(WIDE)
        places = numbers[:, 2:3] * 32.0 + numbers[:, 3:4]
        angles = jnp.where(lane // 32 == k, places * freqs_ref[...], angles)
    trig_ref[0] = jnp.cos(angles)
    trig_ref[1] = jnp.sin(angles)
    gain_ref[...] = dot_rows(jnp.where(pick, 1.0, 0.0).astype(LOW), gains.wait()[...])
    qkv_ref = qkv.wait()

    def one_chunk(index, carry):
        rows = x_ref[index, :, :D].astype(WIDE)
        mixed_rows = (rows * unit_rows(rows) * gain_ref[0:1, :]).astype(LOW)
        mixed.ref[index] = mixed_rows

        def spread(packed):
            own = jnp.where(lane // 32 == index, packed, 0.0)
            own = own + pltpu.roll(own, 64, 1)
            return own + pltpu.roll(own, 32, 1)

        cosine = spread(trig_ref[0])
        sine = spread(trig_ref[1])
        sine = jnp.where(lane % 64 < 32, -sine, sine)
        cos.ref[index] = cosine
        sin.ref[index] = sine
        numbers = x_ref[index, :, D : D + 128].astype(WIDE).astype(jnp.int32)
        query_side, key_side = token_features(numbers[:, 0:1], numbers[:, 1:2])
        query_sides.ref[index] = query_side
        key_sides.ref[index] = key_side
        proj = dot_plain(mixed_rows, qkv_ref[...])
        values = proj[:, 512:].astype(LOW)
        turned.ref[index, :, 512:768] = values
        for pair in range(2):
            at = 128 * pair
            turned.ref[index, :, at : at + 128] = turn_pair(
                proj[:, at : at + 128], cosine, sine
            ).astype(LOW)
            keys = turn_pair(proj[:, 256 + at : 384 + at], cosine, sine).astype(LOW)
            turned.ref[index, :, 256 + at : 384 + at] = keys
            here = pl.ds(pl.multiple_of(index * chunk, chunk), chunk)
            keys_ref[pair, here, :128] = keys
            keys_ref[pair, here, 128:] = key_side
            values_ref[pair, here, :128] = values[:, at : at + 128]
            values_ref[pair, here, 128:] = jnp.where(lane == 0, 1.0, 0.0).astype(LOW)
        return carry

    lax.fori_loop(0, count, one_chunk, 0)
    start_all(mixed, turned, cos, sin, query_sides, key_sides)

    def one_block(index, carry):
        side = query_sides.ref[index]
        log_rows = jnp.zeros((chunk, 128), WIDE)
        here = pl.ds(pl.multiple_of((index % 2) * chunk, chunk), chunk)
        def scores_of(head):
            at = 128 * (head // 2)
            scaled = turned.ref[index, :, at : at + 128] * LOW(SCORE_SCALE)
            query = jnp.concatenate(
                [
                    jnp.where(half_lane == head % 2, scaled, LOW(0)),
                    side * weights_ref[head : head + 1, :],
                ],
                1,
            )
            return dot_rows(query, keys_ref[head // 2])

        scores = scores_of(0)
        parts = []
        for head in range(4):
            high = jnp.max(scores, 1, keepdims=True)
            powers = jnp.exp(scores - high).astype(LOW)
            if head < 3:
                scores = scores_of(head + 1)
            summed = dot_plain(powers, values_ref[head // 2])
            total = summed[:, 128:129]
            parts.append(summed[:, :128] / total)
            log_rows = jnp.where(lane == head, high + jnp.log(total), log_rows)
        for pair in range(2):
            at = 128 * pair
            total_mixed = jnp.where(half_lane == 0, parts[2 * pair], parts[2 * pair + 1])
            wide.ref[index, :, at : at + 128] = total_mixed
            low_rows = total_mixed.astype(LOW)

            @pl.when(index < 2)
            def _(low_rows=low_rows, at=at):
                lower.ref[here, at : at + 128] = low_rows

            @pl.when(index >= 2)
            def _(low_rows=low_rows, at=at):
                upper.ref[here, at : at + 128] = low_rows

        logs.ref[index] = log_rows
        return carry

    lax.fori_loop(0, count, one_block, 0)


def attend(chunks, first_weights, freqs, weights, token):
    chunk = chunks[0].shape[0]
    length = 4 * chunk
    return run(
        attend_body,
        "attend",
        15,
        [
            group(chunks),
            whole(first_weights, 0, 768),
            whole(first_weights, D, 128),
            freqs,
            weights,
        ],
        [
            ((16, D), WIDE),
            out_rows((length, D), LOW),
            out_rows((length, 768), LOW),
            out_rows((length, 256), WIDE),
            out_whole((length // 2, 256), LOW),
            out_whole((length // 2, 256), LOW),
            out_rows((length, 128), WIDE),
            out_rows((length, 128), WIDE),
            out_rows((length, 128), WIDE),
            out_rows((length, FEATURES), LOW),
            out_rows((length, FEATURES), LOW),
        ],
        [pltpu.VMEM((2, length, 256), LOW)] * 2 + [pltpu.VMEM((2, chunk, 128), WIDE)],
        token,
    )


def middle_body(rank_ref, x, near, far, wo, gain_ref, heads, own, mixed):
    rank = rank_ref[0]
    start_all(near, far, wo, x)
    count, chunk, _ = x.ref.shape
    block = chunk // 2
    near_ref, far_ref = near.wait(), far.wait()
    width = near_ref.shape[2]
    sources = {
        0: ((near_ref, 0, 0), (near_ref, 2, 0), (far_ref, 0, 0), (far_ref, 0, width)),
        1: ((near_ref, 1, 0), (far_ref, 1, 0), (near_ref, 3, 0), (far_ref, 1, width)),
    }
    for half, order in enumerate((ORDER_A, ORDER_B)):
        for q in range(4):
            ref, which, column = sources[half][q]
            for place, r in enumerate(order):
                start = order.index(r ^ q) * block
                heads.ref[
                    2 * half + place // 2,
                    place % 2 * block : (place % 2 + 1) * block,
                    q * width : (q + 1) * width,
                ] = ref[which, start : start + block, column : column + width]
    heads.start()
    wo_ref = wo.wait()

    def one_chunk(index, carry):
        x.wait_at(index)
        total = x.ref[index, :, :D].astype(WIDE)
        for q in range(4):
            rows = pl.ds(pl.multiple_of((rank ^ q) * width, width), width)
            total = total + dot_plain(
                heads.ref[index, :, q * width : (q + 1) * width], wo_ref[rows, :]
            )

        @pl.when(index % 2 == 0)
        def _():
            own.ref[index // 2] = total[:block]
            own.start_at(index // 2)

        mixed.ref[index] = (total * unit_rows(total) * gain_ref[1:2, :]).astype(LOW)
        mixed.start_at(index)
        return carry

    lax.fori_loop(0, count, one_chunk, 0)


def middle(rank, chunks, heads, out_pieces, gain):
    chunk = chunks[0].shape[0]
    length = 4 * chunk
    lower, lower_x, lower_far, upper, upper_y, upper_far = heads
    return run(
        middle_body,
        "middle",
        7,
        [
            rank,
            group(chunks),
            group((lower, upper, lower_x, upper_y)),
            group((lower_far, upper_far)),
            output_weights(out_pieces),
            gain,
        ],
        [out_rows((length, D), LOW), out_rows((chunk, D), WIDE, 2), out_rows((length, D), LOW)],
    )


def feed_body(mixed, gate_up, both, hidden):
    count, _, per = hidden.ref.shape
    mixed.start(0)
    gate_up.start()
    mixed.start(1, 2, 3)

    def one_chunk(index, carry):
        mixed.wait_at(index)
        gate_up_ref = gate_up.wait_first(index)
        rows = mixed.ref[index]
        for half in range(2):
            here = slice(half * per // 2, (half + 1) * per // 2)
            gate = dot_plain(rows, gate_up_ref[half])
            up = dot_plain(rows, gate_up_ref[2 + half])
            sigmoid = 1.0 / (1.0 + jnp.exp(-gate))
            silu = gate * sigmoid
            both.ref[index, :, here] = (up * (sigmoid + silu * (1.0 - sigmoid))).astype(LOW)
            both.ref[index, :, per + half * per // 2 : per + (half + 1) * per // 2] = silu.astype(LOW)
            hidden.ref[index, :, here] = (silu * up).astype(LOW)
        both.start_at(index)
        hidden.start_at(index)
        return carry

    lax.fori_loop(0, count, one_chunk, 0)


def feed(mixed, gate_up, token):
    length = mixed.shape[0]
    per = gate_up.shape[1] // 2
    return run(
        feed_body,
        "feed",
        8,
        [rows_of(mixed), columns_of(gate_up)],
        [out_rows((length, 2 * per), LOW), out_rows((length, per), LOW)],
        token=token,
    )


def feed_back_body(both, cots, gate_up, down, grads, back):
    start_all(down)
    cots.start(0)
    both.start(0)
    gate_up.start()
    cots.start(1)
    both.start(1)
    per = down.ref.shape[0]

    def one_chunk(index, carry):
        cots.wait_at(index)
        both.wait_at(index)
        grad_hidden = dot_rows(cots.ref[index], down.wait_first(index)[...])
        grads.ref[index, :, :per] = (grad_hidden * both.ref[index, :, :per].astype(WIDE)).astype(LOW)
        grads.ref[index, :, per:] = (grad_hidden * both.ref[index, :, per:].astype(WIDE)).astype(LOW)
        grads.start_at(index)
        back.ref[index] = dot_rows(grads.ref[index], gate_up.wait_first(index)[...]).astype(LOW)
        back.start_at(index)
        return carry

    lax.fori_loop(0, 2, one_chunk, 0)


def feed_back(first, both, cots, gate_up, down, token):
    length = both.shape[0]
    chunk = length // 4
    per = down.shape[0]

    def pairs(refs, buffer):
        return [
            (refs[0].at[pl.ds((first + 2 * k) * chunk, chunk)], buffer.at[k]) for k in range(2)
        ]

    return run(
        feed_back_body,
        "feed_back",
        7,
        [Plan([both], (2, chunk, 2 * per), pairs, 2), group((cots[first], cots[first + 2]))]
        + [whole(gate_up), whole(down)],
        [out_rows((length // 2, 2 * per), LOW, 2), out_group((chunk, D), LOW, 2)],
        token=token,
    )


def sum_arrived(near, got, last):
    return (
        near.wait()[...].astype(WIDE) + got.wait()[...].astype(WIDE) + last.wait()[...].astype(WIDE)
    )


def arrivals(sums):
    return [whole(x) if place % 3 == 2 else top(x) for place, x in enumerate(sums)]


def own_back_body(
    rank_ref, n0, g0, l0, n1, g1, l1, middle_rows, cot, gain_ref, wo, grad, parcels
):
    rank = rank_ref[0]
    start_all(n0, g0, l0, middle_rows, cot, n1, g1, l1, wo)
    block = l0.ref.shape[0]
    width = parcels.ref.shape[2] // 2
    for place, sums in enumerate(((n0, g0, l0), (n1, g1, l1))):
        rows = slice(place * block, (place + 1) * block)
        arrived = sum_arrived(*sums)
        y = middle_rows.wait()[rows, :]
        scale = unit_rows(y)
        normed = y * scale
        turned = arrived * gain_ref[1:2, :]
        grad.ref[rows, :] = cot.wait()[rows, :].astype(WIDE) + scale * (
            turned - normed * jnp.mean(turned * normed, -1, keepdims=True)
        )
    low_grad = grad.ref[...].astype(LOW)
    wo_ref = wo.wait()
    for q in range(4):
        place = pl.ds(pl.multiple_of((rank ^ q) * width, width), width)
        parcels.ref[q, :, :width] = dot_rows(low_grad, wo_ref[place, :]).astype(LOW)
        parcels.ref[q, :, width:] = grad.ref[:, place].astype(LOW)


def own_back(rank, sums, middle_own, cot_own, gain, out_pieces, token):
    quarter = cot_own.shape[0]
    return run(
        own_back_body,
        "own_back",
        4,
        [rank, *arrivals(sums), whole(middle_own), whole(cot_own), gain]
        + [output_weights(out_pieces)],
        [out_whole((quarter, D), WIDE), out_group((quarter, 512), LOW)],
        token=token,
    )


def attend_back_body(
    pair, parcels, q, k, v, wide, logs, cos, sin, query_sides, key_sides, weights_ref,
    *rest,
):
    if pair == 1:
        before, projections, out, bias_ref, back, *rest, joined_ref = rest
    else:
        out, bias_ref, *rest = rest
    queries_ref, grads_ref, total_ref = rest
    start_all(parcels, q, query_sides, logs, wide, k, v, key_sides, cos, sin)
    if pair == 1:
        start_all(before, projections)
    length = q.ref.shape[0]
    chunk = length // 4
    block = chunk // 2
    half_lane = lax.broadcasted_iota(jnp.int32, (chunk, 128), 1) // 64
    lane = lax.broadcasted_iota(jnp.int32, (chunk, 128), 1)
    parcels_ref = parcels.wait()
    for half, order in enumerate((ORDER_A, ORDER_B)):
        for place in range(4):
            to = slice((4 * half + place) * block, (4 * half + place + 1) * block)
            rows = slice(half * block, (half + 1) * block)
            for head in range(2):
                grads_ref[head, to, :128] = parcels_ref[order[place], rows, :]
    q_ref, side_ref, log_ref, wide_ref = q.wait(), query_sides.wait(), logs.wait(), wide.wait()

    def prepare(index, carry):
        rows = pl.ds(pl.multiple_of(index * chunk, chunk), chunk)
        product = grads_ref[0, rows, :128].astype(WIDE) * wide_ref[rows, :]
        scaled = q_ref[rows, :] * LOW(SCORE_SCALE)
        for half in range(2):
            head = 2 * pair + half
            side = side_ref[rows, :] * weights_ref[head : head + 1, :]
            for place, piece in enumerate(three_parts(-log_ref[rows, head : head + 1])):
                side = jnp.where(lane == LSE_AT + place, piece, side)
            queries_ref[half, rows, :128] = jnp.where(half_lane == half, scaled, LOW(0))
            queries_ref[half, rows, 128:] = side
            delta = jnp.sum(jnp.where(half_lane == half, product, 0.0), 1, keepdims=True)
            extra = jnp.zeros((chunk, 128), LOW)
            for place, piece in enumerate(three_parts(-delta)):
                extra = jnp.where(lane == place, piece, extra)
            grads_ref[half, rows, 128:] = extra
        total_ref[rows, :] = jnp.zeros((chunk, 128), WIDE)
        return carry

    lax.fori_loop(0, 4, prepare, 0)
    three_ones = jnp.where(lane < 3, 1.0, 0.0).astype(LOW)
    k_ref, v_ref, key_ref, cos_ref, sin_ref = (
        k.wait(), v.wait(), key_sides.wait(), cos.wait(), sin.wait()
    )

    def one_block(index, carry):
        rows = pl.ds(pl.multiple_of(index * chunk, chunk), chunk)
        cosine = cos_ref[rows, :]
        sine = -sin_ref[rows, :]
        key_side = key_ref[rows, :]
        first_four = jnp.where(lane < 4, key_side.astype(WIDE), 0.0)
        sums = list(carry)
        keys = k_ref[rows, :]
        values = v_ref[rows, :]
        keys_wide = jnp.concatenate([keys, key_side], 1)
        grad_keys = jnp.zeros((chunk, 128), WIDE)
        grad_values = jnp.zeros((chunk, 128), WIDE)
        for half in range(2):
            mine = half_lane == half
            weights = jnp.exp(dot_rows(keys_wide, queries_ref[half]))
            grad_weights = dot_rows(
                jnp.concatenate([jnp.where(mine, values, LOW(0)), three_ones], 1), grads_ref[half]
            )
            grad_values = jnp.where(
                mine, dot_plain(weights.astype(LOW), grads_ref[half, :, :128]), grad_values
            )
            grad_scores = (weights * grad_weights).astype(LOW)
            both = dot_plain(
                grad_scores,
                jnp.concatenate([queries_ref[half, :, :128], side_ref[...]], 1),
            )
            grad_keys = grad_keys + both[:, :128]
            counted = both[:, 128:]
            same = jnp.sum(counted * first_four, 0, keepdims=True)
            every = jnp.sum(jnp.where(lane < 4, counted, 0.0), 0, keepdims=True)
            sums[half] = sums[half] + same
            sums[2 + half] = sums[2 + half] + (every - same)
            total_ref[...] += dot_first(grad_scores, jnp.where(mine, keys, LOW(0)))
        out.ref[index, :, 128:256] = turn_pair(grad_keys, cosine, sine).astype(LOW)
        out.ref[index, :, 256:] = grad_values.astype(LOW)
        return tuple(sums)

    start = tuple(jnp.zeros((1, 128), WIDE) for _ in range(4))
    sums = lax.fori_loop(0, 4, one_block, start)
    bias_ref[...] = jnp.zeros_like(bias_ref)
    for place in range(4):
        bias_ref[place : place + 1, :] = sums[place]
    for place in range(4):
        rows = slice(place * chunk, (place + 1) * chunk)
        out.ref[place, :, :128] = turn_pair(
            total_ref[rows, :] * SCORE_SCALE, cos_ref[rows, :], -sin_ref[rows, :]
        ).astype(LOW)
    if pair == 0:
        return
    out.start()
    before_ref, projections_ref = before.wait(), projections.wait()

    def one_chunk(index, carry):
        for kind in range(3):
            here = slice(128 * kind, 128 * (kind + 1))
            joined_ref[:, 256 * kind : 256 * kind + 128] = before_ref[index, :, here]
            joined_ref[:, 256 * kind + 128 : 256 * (kind + 1)] = out.ref[index, :, here]
        back.ref[index] = dot_rows(joined_ref[...], projections_ref[...]).astype(LOW)
        back.start_at(index)
        return carry

    lax.fori_loop(0, 4, one_chunk, 0)


def attend_back(pair, parcels, kept, weights, token, before=None, first_weights=None):
    turned, attended, *others = kept
    length = turned.shape[0]
    at = 128 * pair
    return run(
        functools.partial(attend_back_body, pair),
        "attend_back",
        40,
        [group(parcels, at, 128)]
        + [whole(turned, column + at, 128) for column in (0, 256, 512)]
        + [whole(attended, at, 128)]
        + [whole(x) for x in others]
        + [weights]
        + ([rows_of(before), whole(first_weights, 0, 768)] if pair else []),
        [out_rows((length, 384), LOW), ((8, 128), WIDE)]
        + ([out_group((length // 4, D), LOW)] if pair else []),
        [
            pltpu.VMEM((2, length, 256), LOW),
            pltpu.VMEM((2, length, 256), LOW),
            pltpu.VMEM((length, 128), WIDE),
        ]
        + ([pltpu.VMEM((length // 4, 768), LOW)] if pair else []),
        token,
    )


def down_grads_body(hidden, cots, out):
    start_all(cots, hidden)
    count, chunk, _ = cots.ref.shape

    def one_part(index, carry):
        cots_ref = cots.wait_first(index)
        hidden.wait_at(index)
        total = dot_first(hidden.ref[index, :chunk, :], cots_ref[0])
        for k in range(1, count):
            total = total + dot_first(
                hidden.ref[index, k * chunk : (k + 1) * chunk, :], cots_ref[k]
            )
        out.ref[index] = total.astype(LOW)
        out.start_at(index)
        return carry

    lax.fori_loop(0, hidden.ref.shape[0], one_part, 0)


def down_grads(hidden, cots, token):
    per = hidden.shape[1]
    return run(
        down_grads_body,
        "down_grads",
        5,
        [columns_of(hidden), group(cots)],
        [out_rows((per, D), LOW)],
        token=token,
    )[0]


def gate_up_grads_body(mixed, near, far, out):
    start_all(near, far, mixed)
    chunk = mixed.ref.shape[1] // 4

    def one_part(index, carry):
        near_ref, far_ref = near.wait_first(index), far.wait_first(index)
        mixed.wait_at(index)
        total = None
        for k in range(4):
            more = dot_first(
                mixed.ref[index, k * chunk : (k + 1) * chunk, :], (near_ref, far_ref)[k % 2][k // 2]
            )
            total = more if total is None else total + more
        out.ref[index] = total.astype(LOW)
        out.start_at(index)
        return carry

    lax.fori_loop(0, mixed.ref.shape[0], one_part, 0)


def gate_up_grads(mixed, near, far, token):
    return run(
        gate_up_grads_body,
        "gate_up_grads",
        8,
        [columns_of(mixed), rows_of(near, 2), rows_of(far, 2)],
        [out_rows((D, near.shape[1]), LOW)],
        token=token,
    )[0]


def feed_out_body(hidden, down, out):
    start_all(down, hidden)

    def one_chunk(index, carry):
        down_ref = down.wait_first(index)
        hidden.wait_at(index)
        out.ref[index] = dot_plain(hidden.ref[index], down_ref[...]).astype(LOW)
        out.start_at(index)
        return carry

    lax.fori_loop(0, hidden.ref.shape[0], one_chunk, 0)


def feed_out(hidden, down, token):
    length = hidden.shape[0]
    return run(
        feed_out_body,
        "feed_out",
        5,
        [rows_of(hidden), whole(down)],
        [out_group((length // 4, D), LOW)],
        token=token,
    )


def own_last_body(
    n0, g0, l0, n1, g1, l1, m0, h0, k0, m1, h1, k1, x, base, middle_rows, gain_ref, out
):
    start_all(n0, g0, l0, x, base, m0, h0, k0, middle_rows, n1, g1, l1, m1, h1, k1)
    block = l0.ref.shape[0]
    piece = out.ref.shape[1] // 2
    each = block // piece
    for half, (back, forward) in enumerate(
        (((n0, g0, l0), (m0, h0, k0)), ((n1, g1, l1), (m1, h1, k1)))
    ):
        rows = slice(half * block, (half + 1) * block)
        places = slice(half * each, (half + 1) * each)
        turned = sum_arrived(*back) * gain_ref[0:1, :]
        x_rows = x.wait()[rows, :D].astype(WIDE)
        scale = unit_rows(x_rows)
        normed = x_rows * scale
        grad = base.wait()[rows, :] + scale * (
            turned - normed * jnp.mean(turned * normed, -1, keepdims=True)
        )
        out.ref[places, :piece, :] = grad.astype(LOW).reshape(each, piece, D)
        block_rows = sum_arrived(*forward) + middle_rows.wait()[rows, :]
        out.ref[places, piece:, :] = block_rows.astype(LOW).reshape(each, piece, D)


def own_last(sums, out_sums, mine, base, middle_own, gain, n_seq, token):
    quarter = base.shape[0]
    return run(
        own_last_body,
        "own_last",
        80,
        [*arrivals(sums), *arrivals(out_sums), whole(mine), whole(base), whole(middle_own), gain],
        [out_whole((n_seq, 2 * quarter // n_seq, D), LOW)],
        token=token,
    )[0]


def join_body(left, right, out):
    start_all(left, right)
    width = left.ref.shape[1]
    out.ref[:, :width] = left.wait()[...]
    out.ref[:, width:] = right.wait()[...]


def join(left, right, token):
    rows = left.shape[0]
    return run(
        join_body,
        "join",
        1,
        [whole(left), whole(right)],
        [out_whole((rows, left.shape[1] + right.shape[1]), LOW)],
        token=token,
    )[0]


def first_grads_body(rank_ref, mixed, proj0, proj1, heads, parcels, bias_ref, out, joined_ref):
    rank = rank_ref[0]
    start_all(mixed, proj0, proj1, parcels, heads)
    width = 256
    block = parcels.ref.shape[1] // 2
    for pair, proj in enumerate((proj0, proj1)):
        ref = proj.wait()
        for kind in range(3):
            column = width * kind + 128 * pair
            joined_ref[:, column : column + 128] = ref[:, 128 * kind : 128 * (kind + 1)]
    parcels_ref = parcels.wait()
    for half, order in enumerate((ORDER_A, ORDER_B)):
        for place in range(4):
            to = slice((4 * half + place) * block, (4 * half + place + 1) * block)
            joined_ref[to, 3 * width :] = parcels_ref[
                order[place], half * block : (half + 1) * block, :
            ]
    mixed_ref, heads_ref = mixed.wait(), heads.wait()

    def one_part(index, carry):
        out.ref[index, :, : 3 * width] = dot_first(
            mixed_ref[index], joined_ref[:, : 3 * width]
        ).astype(LOW)
        out.ref[rank ^ index, :, 3 * width : 4 * width] = dot_first(
            heads_ref[index], joined_ref[:, 3 * width :]
        ).astype(LOW)
        out.ref[index, :, 4 * width :] = bias_ref[...]
        return carry

    lax.fori_loop(0, 4, one_part, 0)


def first_grads(rank, mixed, proj0, proj1, heads, parcels, bias_rows, token):
    length = mixed.shape[0]
    return run(
        first_grads_body,
        "first_grads",
        8,
        [rank, columns_of(mixed), whole(proj0), whole(proj1), columns_of(heads)]
        + [group(parcels, 256, 256), bias_rows],
        [out_rows((D, 768 + 256 + 128), LOW)],
        [pltpu.VMEM((length, 1024), LOW)],
        token,
    )[0]


def rank_blocks(lower, lower_far, upper, upper_far):
    half = lower.shape[0] // 2
    return (
        ((lower, 0), (upper, 0)),
        ((lower, half), (upper_far, 0)),
        ((lower_far, 0), (upper, half)),
        ((lower_far, half), (upper_far, half)),
    )


def lay_flat(column, part):
    count = column.shape[0]
    row = lax.broadcasted_iota(jnp.int32, (count, 128), 0) + part * count
    lane = lax.broadcasted_iota(jnp.int32, (count, 128), 1)
    return jnp.sum(jnp.where(row == lane, column, 0.0), 0, keepdims=True)


def spread_feed_kernel(
    rank_ref, lower, lower_far, upper, upper_far, gate_ref, up_ref, gain_ref,
    grad_gate_ref, grad_up_ref, grad_down_ref, grad_gain_ref,
):
    rank = rank_ref[0]
    half = lower.shape[0] // 2
    piece = 128
    ff = gate_ref.shape[1]
    per = ff // 4
    for r, halves in enumerate(rank_blocks(lower, lower_far, upper, upper_far)):
        for part, (ref, start) in enumerate(halves):
            rows = slice(part * half, (part + 1) * half)
            source = slice(start, start + half)
            for s in range(per // piece):
                to = pl.ds(pl.multiple_of((4 * s + (rank ^ r)) * piece, piece), piece)
                grad_gate_ref[rows, to] = ref[source, s * piece : (s + 1) * piece].astype(WIDE)
                grad_up_ref[rows, to] = ref[source, per + s * piece : per + (s + 1) * piece].astype(
                    WIDE
                )
            to = pl.ds(pl.multiple_of((rank ^ r) * 2 * half + part * half, half), half)
            grad_down_ref[to, :] = ref[source, 2 * per :].astype(WIDE)
    flat = jnp.zeros((1, 128), WIDE)
    for part in range(2):
        rows = slice(part * half, (part + 1) * half)
        total = jnp.sum(
            gate_ref[rows, :].astype(WIDE) * grad_gate_ref[rows, :], 1, keepdims=True
        ) + jnp.sum(up_ref[rows, :].astype(WIDE) * grad_up_ref[rows, :], 1, keepdims=True)
        flat = flat + lay_flat(total, part)
    grad_gain_ref[...] = jnp.broadcast_to(flat / gain_ref[...].astype(WIDE), (8, 128))


def spread_feed(rank, pieces, w_gate, w_up, gain):
    shard, ff = w_gate.shape
    return call(
        spread_feed_kernel,
        "spread_feed",
        [((shard, ff), WIDE), ((shard, ff), WIDE), ((ff // 8, D), WIDE), ((8, 128), WIDE)],
        [pl.BlockSpec(memory_space=pltpu.SMEM)] + [whole_block()] * 7,
        4 * shard * ff,
        16 * 2**20,
        (rank, *pieces, w_gate, w_up, gain),
    )


def spread_first_kernel(
    rank_ref, lower, lower_far, upper, upper_far, wq_ref, wk_ref, wv_ref, gain_ref,
    gq_ref, gk_ref, gv_ref, go_ref, grad_gain_ref, bias_ref,
):
    rank = rank_ref[0]
    half = lower.shape[0] // 2
    wide = 256
    bias_ref[...] = jnp.zeros_like(bias_ref)
    for r, halves in enumerate(rank_blocks(lower, lower_far, upper, upper_far)):
        to = pl.ds(pl.multiple_of((rank ^ r) * wide, wide), wide)
        for part, (ref, start) in enumerate(halves):
            rows = slice(part * half, (part + 1) * half)
            source = slice(start, start + half)
            for place, out_ref in enumerate((gq_ref, gk_ref, gv_ref, go_ref)):
                out_ref[rows, to] = ref[source, place * wide : (place + 1) * wide].astype(WIDE)
        ref, start = halves[0]
        bias_ref[pl.ds(rank ^ r, 1), :] = jnp.sum(
            ref[start : start + 16, 4 * wide : 4 * wide + 128].astype(WIDE), 0, keepdims=True
        )
    flat = jnp.zeros((1, 128), WIDE)
    for part in range(2):
        rows = slice(part * half, (part + 1) * half)
        total = jnp.zeros((half, 1), WIDE)
        for weight_ref, grad_ref in ((wq_ref, gq_ref), (wk_ref, gk_ref), (wv_ref, gv_ref)):
            total = total + jnp.sum(
                weight_ref[rows, :].astype(WIDE) * grad_ref[rows, :], 1, keepdims=True
            )
        flat = flat + lay_flat(total, part)
    grad_gain_ref[...] = jnp.broadcast_to(flat / gain_ref[...].astype(WIDE), (8, 128))


def spread_first(rank, pieces, w_query, w_key, w_value, gain):
    shard = w_query.shape[0]
    return call(
        spread_first_kernel,
        "spread_first",
        [((shard, D), WIDE)] * 4 + [((8, 128), WIDE), ((8, 128), WIDE)],
        [pl.BlockSpec(memory_space=pltpu.SMEM)] + [whole_block()] * 8,
        4 * shard * D,
        8 * 2**20,
        (rank, *pieces, w_query, w_key, w_value, gain),
    )


def on_plane(
    inputs,
    w_query,
    w_key,
    w_value,
    w_output,
    gain_attention,
    w_gate,
    w_up,
    w_down,
    gain_feed,
    variate_bias,
    segment_ids,
    variate_ids,
    positions,
    grad_output,
):
    rank = lax.axis_index("batch")
    rank_row = jnp.reshape(rank, (1,)).astype(jnp.int32)
    micro, tokens = inputs.shape[0], inputs.shape[2]
    n_seq = lax.axis_size("seq")
    shard = w_query.shape[0]
    per = D // 4

    packed, first_shard, gate_up_shard, down_shard = pack(
        rank_row,
        inputs.reshape(micro, tokens, D),
        grad_output.reshape(micro, tokens, D),
        segment_ids.reshape(micro, tokens),
        variate_ids.reshape(micro, tokens),
        positions.reshape(micro, tokens),
        (w_query, w_key, w_value, w_output),
        (gain_attention.reshape(1, shard), gain_feed.reshape(1, shard)),
        w_gate,
        w_up,
        w_down,
    )
    first_weights = lax.all_gather(first_shard, "seq", axis=0, tiled=True)
    gate_up = lax.all_gather(gate_up_shard, "seq", axis=0, tiled=True)
    down = lax.all_gather(down_shard, "seq", axis=0, tiled=True)
    packed = lax.all_to_all(packed, "batch", 0, 0, tiled=True)
    by_sequence = [
        packed[:, kind].reshape(4 * micro, tokens // 4, D + 128)[:, :, : D + 128 - 128 * kind]
        for kind in range(2)
    ]
    out_columns = first_weights[:, 768:D]
    out_got = swap_pairs(out_columns)
    mine, cot_by_sequence, out_got = lax.optimization_barrier(
        (over_seq(by_sequence[0]), by_sequence[1], out_got)
    )
    cot_mine = over_seq(cot_by_sequence)
    freqs = jnp.exp((jnp.arange(128) % 32).astype(WIDE) * (-2.0 * math.log(10000.0) / HD))[None, :]
    my_bias = lax.dynamic_slice_in_dim(variate_bias, rank * 4, 4, 1)
    weights = jnp.pad(head_weights(my_bias[0], my_bias[1]), ((0, 4), (0, 0)))

    chunks = gather_plane(mine)
    out_pieces = far_pairs(
        out_columns, lax.optimization_barrier((out_got, chunks[1], chunks[3]))[0]
    )
    gain, mixed_first, turned, attended, lower, upper, *kept = attend(
        chunks, first_weights, freqs, weights, rank_row
    )
    ready = lax.optimization_barrier((lower, upper, out_pieces[1], out_pieces[3]))
    lower_x, upper_y = swap(ready[0], 1), swap(ready[1], 2)
    lower_far = swap(jnp.concatenate([lower, lower_x], 1), 2)
    upper_far = swap(jnp.concatenate([upper, upper_y], 1), 1)
    cot_got = swap_pairs(lax.optimization_barrier((cot_mine, lower_far, upper_far))[0])
    heads, middle_own, mixed_second = middle(
        rank_row,
        chunks,
        (lower, lower_x, lower_far, upper, upper_y, upper_far),
        out_pieces,
        gain,
    )

    both, hidden = feed(mixed_second, gate_up, after(rank_row, cot_got))
    cots = far_pairs(cot_mine, lax.optimization_barrier((cot_got, mixed_second))[0])
    down_weight_grads = down_grads(hidden, cots, rank_row)
    down_grad_shard = lax.psum_scatter(down_weight_grads, "seq", scatter_dimension=0, tiled=True)
    far_grads, far_lower, far_upper = feed_back(
        1, both, cots, gate_up, down, after(rank_row, down_weight_grads)
    )
    got = scatter_first((None, far_lower, None, far_upper))
    near_grads, near_lower, near_upper = feed_back(
        0, both, cots, gate_up, down, after(rank_row, far_lower)
    )
    back = (near_lower, None, near_upper, None)
    gate_up_weight_grads = gate_up_grads(
        mixed_second, near_grads, far_grads, after(rank_row, got)
    )
    gate_up_grad_shard = lax.psum_scatter(
        gate_up_weight_grads, "seq", scatter_dimension=0, tiled=True
    )
    sums = scatter_second(back, got)
    grad_middle, *parcels = own_back(
        rank_row, sums, middle_own, cot_mine, gain, out_pieces,
        after(rank_row, gate_up_weight_grads),
    )
    out_chunks = feed_out(hidden, down, after(rank_row, parcels[0]))
    parcels = [parcels[0]] + [swap(parcels[r], r) for r in range(1, 4)]

    far_chunks = lax.optimization_barrier(((out_chunks[1], out_chunks[3]), parcels))[0]
    out_got = scatter_first((None, far_chunks[0], None, far_chunks[1]))
    kept = (turned, attended, *kept)
    proj0, bias0 = attend_back(
        0, parcels, kept, weights, after(rank_row, far_chunks)
    )
    out_got = lax.optimization_barrier((out_got, bias0))[0]
    out_sums = scatter_second(out_chunks, out_got)
    proj1, bias1, *back = attend_back(
        1, parcels, kept, weights, after(rank_row, out_got), proj0, first_weights
    )
    ready = lax.optimization_barrier((back[1], back[3], out_sums[2], out_sums[5]))
    got = scatter_first((None, ready[0], None, ready[1]))
    bias_sums = jnp.sum(jnp.concatenate([bias0[:2], bias1[:2], bias0[2:4], bias1[2:4]], 0), 1)
    bias_parts = jnp.pad(jnp.concatenate(three_parts(bias_sums)), (0, 104))[None, :]
    slots = lax.broadcasted_iota(jnp.int32, (per, 1), 0) % shard == lax.axis_index("seq")
    bias_rows = jnp.where(slots, bias_parts, LOW(0))
    first_weight_grads = first_grads(
        rank_row, mixed_first, proj0, proj1, heads, parcels, bias_rows, after(rank_row, got)
    )
    first_shard = lax.psum_scatter(first_weight_grads, "seq", scatter_dimension=0, tiled=True)
    sums = scatter_second(back, got)
    last = own_last(
        sums, out_sums, mine, grad_middle, middle_own, gain, n_seq,
        after(rank_row, first_weight_grads),
    )
    moved = lax.all_to_all(last, "seq", 0, 0, tiled=True)
    quarter = tokens // 4
    feed_shard = join(gate_up_grad_shard, down_grad_shard, after(rank_row, first_weight_grads))
    feed_pieces = gather_plane(after(feed_shard, last))
    first_pieces = gather_plane(after(first_shard, feed_pieces))
    moved, first_pieces = lax.optimization_barrier((moved, first_pieces))
    moved = moved.reshape(4, micro, 2 * quarter, D)
    moved = lax.all_to_all(moved, "batch", 0, 0, tiled=True)
    grad_inputs = jnp.transpose(moved[:, :, :quarter].astype(WIDE), (1, 0, 2, 3))
    block_output = jnp.transpose(moved[:, :, quarter:], (1, 0, 2, 3))

    grad_gate, grad_up, grad_down, grad_gain_second = spread_feed(
        rank_row, feed_pieces, w_gate, w_up, gain_feed.reshape(1, shard)
    )
    grad_query, grad_key, grad_value, grad_output_weights, grad_gain_first, bias_table = (
        spread_first(
            rank_row, first_pieces, w_query, w_key, w_value, gain_attention.reshape(1, shard)
        )
    )
    bias_table = jnp.sum(bias_table[:4, :24].reshape(4, 3, 2, 4), 1)
    grad_bias = jnp.transpose(bias_table, (1, 0, 2)).reshape(2, H)
    return (
        block_output.reshape(inputs.shape),
        grad_inputs.reshape(inputs.shape),
        grad_query,
        grad_key,
        grad_value,
        grad_output_weights,
        grad_gain_first[0],
        grad_gate,
        grad_up,
        grad_down,
        grad_gain_second[0],
        grad_bias,
    )


def solution(mesh):
    n_batch, n_seq = mesh.shape["batch"], mesh.shape["seq"]
    step = on_plane if n_batch == 4 and n_seq == 8 else on_device
    return jax.shard_map(
        step,
        mesh=mesh,
        in_specs=(
            P(None, "batch", "seq", None),
            P("seq", None),
            P("seq", None),
            P("seq", None),
            P("seq", None),
            P("seq"),
            P("seq", None),
            P("seq", None),
            P("seq", None),
            P("seq"),
            P(),
            P(None, "batch", "seq"),
            P(None, "batch", "seq"),
            P(None, "batch", "seq"),
            P(None, "batch", "seq", None),
        ),
        out_specs=(
            P(None, "batch", "seq", None),
            P(None, "batch", "seq", None),
            P("seq", None),
            P("seq", None),
            P("seq", None),
            P("seq", None),
            P("seq"),
            P("seq", None),
            P("seq", None),
            P("seq", None),
            P("seq"),
            P(),
        ),
        check_vma=False,
    )
```

```python
import functools
import math

import jax
import jax.numpy as jnp
from jax import lax
from jax.experimental import pallas as pl
from jax.experimental.pallas import tpu as pltpu
from jax.sharding import PartitionSpec as P

D = 1024
H = 16
HD = 64
REACH = 6


EPSILON = 1e-05
SCORE_SCALE = 0.125
MASKED = -1e30


def from_behind(value, axis, by):
    length = lax.axis_size(axis)
    pairs = [(i, i + by) for i in range(length) if 0 <= i + by < length]
    return lax.ppermute(value, axis, pairs)


def step_offset(step):
    distance = step // 2 + 1
    return distance if step % 2 == 0 else -distance


def rotary(values_in, positions_in, turn):
    row_count = values_in.shape[0]
    halfway = HD // 2
    freqs = jnp.exp(jnp.arange(halfway, dtype=jnp.float32) * (-2.0 * math.log(10000.0) / HD))
    angles = positions_in.astype(jnp.float32)[:, None] * freqs[None, :]
    cosine = jnp.cos(angles)[:, None, :]
    sine = turn * jnp.sin(angles)[:, None, :]
    shaped = values_in.reshape(row_count, H, HD)
    first_half = shaped[..., :halfway]
    second_half = shaped[..., halfway:]
    turned = jnp.concatenate(
        [first_half * cosine - second_half * sine, first_half * sine + second_half * cosine], -1
    )
    return turned.reshape(row_count, H * HD)


def head_scores(query_heads, key_heads, query_variates, key_variates, bias_table):
    raw = jnp.einsum("qhd,khd->hqk", query_heads, key_heads, preferred_element_type=jnp.float32)
    same_variate = (query_variates[:, None] == key_variates[None, :])[None]
    return raw * SCORE_SCALE + jnp.where(
        same_variate, bias_table[0][:, None, None], bias_table[1][:, None, None]
    )


def attend_forward(query_rows, own_keys, own_values, own_segments, own_variates, bias_table):
    tok_count = query_rows.shape[0]
    query_heads = query_rows.reshape(tok_count, H, HD)
    shifted_segments = own_segments + 1

    def fold_keys(carried, piece_rows):
        key_part, value_part, segment_part, variate_part = piece_rows
        part_count = key_part.shape[0]
        live = shifted_segments[:, None] == segment_part[None, :]

        def update(state):
            running_max, running_total, running_sum = state
            logits = head_scores(
                query_heads,
                key_part.reshape(part_count, H, HD),
                own_variates,
                variate_part,
                bias_table,
            )
            logits = jnp.where(live[None], logits, MASKED)
            new_max = jnp.maximum(running_max, jnp.max(logits, -1))
            rescale = jnp.exp(running_max - new_max)
            weights = jnp.where(live[None], jnp.exp(logits - new_max[..., None]), 0.0)
            new_total = running_total * rescale + jnp.sum(weights, -1)
            mixed = jnp.einsum(
                "hqk,khd->qhd",
                weights.astype(jnp.bfloat16),
                value_part.reshape(part_count, H, HD),
                preferred_element_type=jnp.float32,
            )
            new_sum = running_sum * jnp.transpose(rescale)[:, :, None] + mixed
            return (new_max, new_total, new_sum)

        return lax.cond(jnp.any(live), update, lambda state: state, carried)

    near_rows = (own_keys, own_values, shifted_segments, own_variates)
    state = (
        jnp.full((H, tok_count), MASKED, jnp.float32),
        jnp.zeros((H, tok_count), jnp.float32),
        jnp.zeros((tok_count, H, HD), jnp.float32),
    )
    state = fold_keys(state, near_rows)
    for step in range(2 * REACH):
        arrived = from_behind(
            (own_keys, own_values, shifted_segments, own_variates), "seq", step_offset(step)
        )
        state = fold_keys(state, arrived)
    final_max, final_total, final_sum = state
    attended = final_sum / jnp.transpose(final_total)[:, :, None]
    log_rows = jnp.transpose(final_max + jnp.log(final_total))
    return (attended.reshape(tok_count, H * HD), log_rows)


def attend_queries_back(
    query_rows,
    grad_rows,
    log_rows,
    delta_rows,
    own_keys,
    own_values,
    own_segments,
    own_variates,
    bias_table,
):
    tok_count = query_rows.shape[0]
    query_heads = query_rows.reshape(tok_count, H, HD)
    grad_heads = grad_rows.reshape(tok_count, H, HD)
    log_heads = jnp.transpose(log_rows)
    delta_heads = jnp.transpose(delta_rows)
    shifted_segments = own_segments + 1

    def fold_keys_back(carried, piece_rows):
        key_part, value_part, segment_part, variate_part = piece_rows
        part_count = key_part.shape[0]
        live = shifted_segments[:, None] == segment_part[None, :]

        def update(state):
            grad_query, grad_bias = state
            key_heads = key_part.reshape(part_count, H, HD)
            logits = head_scores(query_heads, key_heads, own_variates, variate_part, bias_table)
            weights = jnp.where(live[None], jnp.exp(logits - log_heads[..., None]), 0.0)
            grad_weights = jnp.einsum(
                "qhd,khd->hqk",
                grad_heads,
                value_part.reshape(part_count, H, HD),
                preferred_element_type=jnp.float32,
            )
            grad_logits = (weights * (grad_weights - delta_heads[..., None])).astype(jnp.bfloat16)
            grad_query = grad_query + SCORE_SCALE * jnp.einsum(
                "hqk,khd->qhd", grad_logits, key_heads, preferred_element_type=jnp.float32
            )
            same_variate = (own_variates[:, None] == variate_part[None, :])[None]
            logit_values = grad_logits.astype(jnp.float32)
            same_total = jnp.sum(jnp.where(same_variate, logit_values, 0.0), axis=(1, 2))
            other_total = jnp.sum(jnp.where(same_variate, 0.0, logit_values), axis=(1, 2))
            return (grad_query, grad_bias + jnp.stack([same_total, other_total]))

        return lax.cond(jnp.any(live), update, lambda state: state, carried)

    state = (jnp.zeros((tok_count, H, HD), jnp.float32), jnp.zeros((2, H), jnp.float32))
    state = fold_keys_back(state, (own_keys, own_values, shifted_segments, own_variates))
    for step in range(2 * REACH):
        arrived = from_behind(
            (own_keys, own_values, shifted_segments, own_variates), "seq", step_offset(step)
        )
        state = fold_keys_back(state, arrived)
    grad_query, grad_bias = state
    return (grad_query.reshape(tok_count, H * HD), grad_bias)


def attend_keys_back(
    query_rows,
    grad_rows,
    log_rows,
    delta_rows,
    own_keys,
    own_values,
    own_segments,
    own_variates,
    bias_table,
):
    tok_count = own_keys.shape[0]
    key_heads = own_keys.reshape(tok_count, H, HD)
    value_heads = own_values.reshape(tok_count, H, HD)
    shifted_segments = own_segments + 1

    def fold_queries(carried, piece_rows):
        query_part, grad_part, log_part, delta_part, segment_part, variate_part = piece_rows
        part_count = query_part.shape[0]
        live = segment_part[:, None] == shifted_segments[None, :]

        def update(state):
            grad_key, grad_value = state
            query_heads = query_part.reshape(part_count, H, HD)
            grad_heads = grad_part.reshape(part_count, H, HD)
            logits = head_scores(query_heads, key_heads, variate_part, own_variates, bias_table)
            weights = jnp.where(
                live[None], jnp.exp(logits - jnp.transpose(log_part)[..., None]), 0.0
            )
            grad_value = grad_value + jnp.einsum(
                "hqk,qhd->khd",
                weights.astype(jnp.bfloat16),
                grad_heads,
                preferred_element_type=jnp.float32,
            )
            grad_weights = jnp.einsum(
                "qhd,khd->hqk", grad_heads, value_heads, preferred_element_type=jnp.float32
            )
            grad_logits = (weights * (grad_weights - jnp.transpose(delta_part)[..., None])).astype(
                jnp.bfloat16
            )
            grad_key = grad_key + SCORE_SCALE * jnp.einsum(
                "hqk,qhd->khd", grad_logits, query_heads, preferred_element_type=jnp.float32
            )
            return (grad_key, grad_value)

        return lax.cond(jnp.any(live), update, lambda state: state, carried)

    state = (jnp.zeros((tok_count, H, HD), jnp.float32), jnp.zeros((tok_count, H, HD), jnp.float32))
    state = fold_queries(
        state, (query_rows, grad_rows, log_rows, delta_rows, shifted_segments, own_variates)
    )
    for step in range(2 * REACH):
        arrived = (
            from_behind(query_rows, "seq", step_offset(step)),
            from_behind(grad_rows, "seq", step_offset(step)),
            from_behind(log_rows.astype(jnp.bfloat16), "seq", step_offset(step)).astype(
                log_rows.dtype
            ),
            from_behind(delta_rows.astype(jnp.bfloat16), "seq", step_offset(step)).astype(
                delta_rows.dtype
            ),
            from_behind(shifted_segments, "seq", step_offset(step)),
            from_behind(own_variates, "seq", step_offset(step)),
        )
        state = fold_queries(state, arrived)
    grad_key, grad_value = state
    return (grad_key.reshape(tok_count, H * HD), grad_value.reshape(tok_count, H * HD))


def norm_back(grad_normed, normed, scale_rows):
    return scale_rows * (grad_normed - normed * jnp.mean(grad_normed * normed, -1, keepdims=True))


def on_device(
    inputs,
    w_query,
    w_key,
    w_value,
    w_output,
    gain_attention,
    w_gate,
    w_up,
    w_down,
    gain_feed,
    variate_bias,
    segment_ids,
    variate_ids,
    positions,
    grad_output,
):
    micro_count = inputs.shape[0]
    tok_count = inputs.shape[2]
    row_count = micro_count * tok_count
    residual_in = inputs.reshape(row_count, D).astype(jnp.float32)
    cotangent = grad_output.reshape(row_count, D).astype(jnp.float32)
    segment_rows = segment_ids.reshape(micro_count, tok_count)
    variate_rows = variate_ids.reshape(micro_count, tok_count)
    position_rows = positions.reshape(row_count)
    full_query, full_key, full_value, full_output, full_gain_first = (
        lax.all_gather(w_query, "seq", axis=0, tiled=True),
        lax.all_gather(w_key, "seq", axis=0, tiled=True),
        lax.all_gather(w_value, "seq", axis=0, tiled=True),
        lax.all_gather(w_output, "seq", axis=0, tiled=True),
        lax.all_gather(gain_attention, "seq", axis=0, tiled=True),
    )
    full_gate, full_up, full_down, full_gain_second = (
        lax.all_gather(w_gate, "seq", axis=0, tiled=True),
        lax.all_gather(w_up, "seq", axis=0, tiled=True),
        lax.all_gather(w_down, "seq", axis=0, tiled=True),
        lax.all_gather(gain_feed, "seq", axis=0, tiled=True),
    )
    scale_first = lax.rsqrt(jnp.mean(residual_in * residual_in, -1, keepdims=True) + EPSILON)
    normed_first = residual_in * scale_first
    mixed_first = (normed_first * full_gain_first.astype(jnp.float32)).astype(jnp.bfloat16)
    query_proj = jnp.dot(mixed_first, full_query, preferred_element_type=jnp.float32)
    key_proj = jnp.dot(mixed_first, full_key, preferred_element_type=jnp.float32)
    value_proj = jnp.dot(mixed_first, full_value, preferred_element_type=jnp.float32)
    query_rows = rotary(query_proj, position_rows, 1.0).astype(jnp.bfloat16)
    key_rows = rotary(key_proj, position_rows, 1.0).astype(jnp.bfloat16)
    value_rows = value_proj.astype(jnp.bfloat16)
    attended_parts = []
    log_parts = []
    for micro_index in range(micro_count):
        lower_row = micro_index * tok_count
        upper_row = lower_row + tok_count
        attended_part, log_part = attend_forward(
            query_rows[lower_row:upper_row],
            key_rows[lower_row:upper_row],
            value_rows[lower_row:upper_row],
            segment_rows[micro_index],
            variate_rows[micro_index],
            variate_bias,
        )
        attended_parts.append(attended_part)
        log_parts.append(log_part)
    attended_all = jnp.concatenate(attended_parts, 0)
    attended_low = attended_all.astype(jnp.bfloat16)
    middle = residual_in + jnp.dot(attended_low, full_output, preferred_element_type=jnp.float32)
    scale_second = lax.rsqrt(jnp.mean(middle * middle, -1, keepdims=True) + EPSILON)
    normed_second = middle * scale_second
    mixed_second = (normed_second * full_gain_second.astype(jnp.float32)).astype(jnp.bfloat16)
    gate_proj = jnp.dot(mixed_second, full_gate, preferred_element_type=jnp.float32)
    up_proj = jnp.dot(mixed_second, full_up, preferred_element_type=jnp.float32)
    sigmoid_gate = jax.nn.sigmoid(gate_proj)
    silu_gate = gate_proj * sigmoid_gate
    hidden_rows = (silu_gate * up_proj).astype(jnp.bfloat16)
    block_rows = middle + jnp.dot(hidden_rows, full_down, preferred_element_type=jnp.float32)
    block_output = block_rows.astype(jnp.bfloat16).reshape(inputs.shape)
    full_query, full_key, full_value, full_output, full_gain_first = (
        lax.all_gather(w_query, "seq", axis=0, tiled=True),
        lax.all_gather(w_key, "seq", axis=0, tiled=True),
        lax.all_gather(w_value, "seq", axis=0, tiled=True),
        lax.all_gather(w_output, "seq", axis=0, tiled=True),
        lax.all_gather(gain_attention, "seq", axis=0, tiled=True),
    )
    full_gate, full_up, full_down, full_gain_second = (
        lax.all_gather(w_gate, "seq", axis=0, tiled=True),
        lax.all_gather(w_up, "seq", axis=0, tiled=True),
        lax.all_gather(w_down, "seq", axis=0, tiled=True),
        lax.all_gather(gain_feed, "seq", axis=0, tiled=True),
    )
    grad_branch_second = cotangent.astype(jnp.bfloat16)
    grad_down = jnp.einsum(
        "rf,rd->fd", hidden_rows, grad_branch_second, preferred_element_type=jnp.float32
    )
    grad_hidden = jnp.einsum(
        "rd,fd->rf", grad_branch_second, full_down, preferred_element_type=jnp.float32
    )
    silu_slope = sigmoid_gate * (1.0 + gate_proj * (1.0 - sigmoid_gate))
    grad_gate_rows = (grad_hidden * up_proj * silu_slope).astype(jnp.bfloat16)
    grad_up_rows = (grad_hidden * silu_gate).astype(jnp.bfloat16)
    grad_gate = jnp.einsum(
        "rd,rf->df", mixed_second, grad_gate_rows, preferred_element_type=jnp.float32
    )
    grad_up = jnp.einsum(
        "rd,rf->df", mixed_second, grad_up_rows, preferred_element_type=jnp.float32
    )
    grad_mixed_second = jnp.einsum(
        "rf,df->rd", grad_gate_rows, full_gate, preferred_element_type=jnp.float32
    ) + jnp.einsum("rf,df->rd", grad_up_rows, full_up, preferred_element_type=jnp.float32)
    grad_gain_second = jnp.sum(grad_mixed_second * normed_second, 0)
    grad_middle = cotangent + norm_back(
        grad_mixed_second * full_gain_second.astype(jnp.float32), normed_second, scale_second
    )
    grad_branch_first = grad_middle.astype(jnp.bfloat16)
    grad_out_proj = jnp.einsum(
        "rd,re->de", attended_low, grad_branch_first, preferred_element_type=jnp.float32
    )
    grad_attended = jnp.einsum(
        "re,de->rd", grad_branch_first, full_output, preferred_element_type=jnp.float32
    ).astype(jnp.bfloat16)
    delta_all = jnp.einsum(
        "rhd,rhd->rh",
        grad_attended.astype(jnp.float32).reshape(row_count, H, HD),
        attended_all.reshape(row_count, H, HD),
    )
    grad_bias_local = jnp.zeros((2, H), jnp.float32)
    query_grad_parts = []
    key_grad_parts = []
    value_grad_parts = []
    for micro_index in range(micro_count):
        lower_row = micro_index * tok_count
        upper_row = lower_row + tok_count
        query_grad_part, bias_part = attend_queries_back(
            query_rows[lower_row:upper_row],
            grad_attended[lower_row:upper_row],
            log_parts[micro_index],
            delta_all[lower_row:upper_row],
            key_rows[lower_row:upper_row],
            value_rows[lower_row:upper_row],
            segment_rows[micro_index],
            variate_rows[micro_index],
            variate_bias,
        )
        key_grad_part, value_grad_part = attend_keys_back(
            query_rows[lower_row:upper_row],
            grad_attended[lower_row:upper_row],
            log_parts[micro_index],
            delta_all[lower_row:upper_row],
            key_rows[lower_row:upper_row],
            value_rows[lower_row:upper_row],
            segment_rows[micro_index],
            variate_rows[micro_index],
            variate_bias,
        )
        grad_bias_local = grad_bias_local + bias_part
        query_grad_parts.append(query_grad_part)
        key_grad_parts.append(key_grad_part)
        value_grad_parts.append(value_grad_part)
    grad_query_rows = rotary(jnp.concatenate(query_grad_parts, 0), position_rows, -1.0).astype(
        jnp.bfloat16
    )
    grad_key_rows = rotary(jnp.concatenate(key_grad_parts, 0), position_rows, -1.0).astype(
        jnp.bfloat16
    )
    grad_value_rows = jnp.concatenate(value_grad_parts, 0).astype(jnp.bfloat16)
    grad_query = jnp.einsum(
        "rd,re->de", mixed_first, grad_query_rows, preferred_element_type=jnp.float32
    )
    grad_key = jnp.einsum(
        "rd,re->de", mixed_first, grad_key_rows, preferred_element_type=jnp.float32
    )
    grad_value = jnp.einsum(
        "rd,re->de", mixed_first, grad_value_rows, preferred_element_type=jnp.float32
    )
    grad_mixed_first = (
        jnp.einsum("re,de->rd", grad_query_rows, full_query, preferred_element_type=jnp.float32)
        + jnp.einsum("re,de->rd", grad_key_rows, full_key, preferred_element_type=jnp.float32)
        + jnp.einsum("re,de->rd", grad_value_rows, full_value, preferred_element_type=jnp.float32)
    )
    grad_gain_first = jnp.sum(grad_mixed_first * normed_first, 0)
    grad_input_rows = grad_middle + norm_back(
        grad_mixed_first * full_gain_first.astype(jnp.float32), normed_first, scale_first
    )
    grad_inputs = grad_input_rows.reshape(inputs.shape)
    (
        shard_query,
        shard_key,
        shard_value,
        shard_output,
        shard_gain_first,
        shard_gate,
        shard_up,
        shard_down,
        shard_gain_second,
    ) = (
        lax.psum_scatter(grad_query, "seq", scatter_dimension=0, tiled=True),
        lax.psum_scatter(grad_key, "seq", scatter_dimension=0, tiled=True),
        lax.psum_scatter(grad_value, "seq", scatter_dimension=0, tiled=True),
        lax.psum_scatter(grad_out_proj, "seq", scatter_dimension=0, tiled=True),
        lax.psum_scatter(grad_gain_first, "seq", scatter_dimension=0, tiled=True),
        lax.psum_scatter(grad_gate, "seq", scatter_dimension=0, tiled=True),
        lax.psum_scatter(grad_up, "seq", scatter_dimension=0, tiled=True),
        lax.psum_scatter(grad_down, "seq", scatter_dimension=0, tiled=True),
        lax.psum_scatter(grad_gain_second, "seq", scatter_dimension=0, tiled=True),
    )
    summed = (
        lax.psum(shard_query.astype(jnp.bfloat16), "batch").astype(jnp.float32),
        lax.psum(shard_key.astype(jnp.bfloat16), "batch").astype(jnp.float32),
        lax.psum(shard_value.astype(jnp.bfloat16), "batch").astype(jnp.float32),
        lax.psum(shard_output.astype(jnp.bfloat16), "batch").astype(jnp.float32),
        lax.psum(shard_gain_first.astype(jnp.bfloat16), "batch").astype(jnp.float32),
        lax.psum(shard_gate.astype(jnp.bfloat16), "batch").astype(jnp.float32),
        lax.psum(shard_up.astype(jnp.bfloat16), "batch").astype(jnp.float32),
        lax.psum(shard_down.astype(jnp.bfloat16), "batch").astype(jnp.float32),
        lax.psum(shard_gain_second.astype(jnp.bfloat16), "batch").astype(jnp.float32),
    )
    grad_bias_total = lax.psum(grad_bias_local, ("batch", "seq"))
    return (
        block_output,
        grad_inputs,
        summed[0],
        summed[1],
        summed[2],
        summed[3],
        summed[4],
        summed[5],
        summed[6],
        summed[7],
        summed[8],
        grad_bias_total,
    )


ORDER_A = (0, 1, 2, 3)
ORDER_B = (0, 2, 1, 3)
FEATURES = 128
LSE_AT = 64
LOW = jnp.bfloat16
WIDE = jnp.float32


def swap(value, bit):
    return lax.ppermute(value, "batch", [(i, i ^ bit) for i in range(4)])


def after(value, *others):
    return lax.optimization_barrier((value, *others))[0]


def gather_plane(own):
    half = own.shape[0] // 2
    lower, upper = own[:half], own[half:]
    lower_pair = jnp.concatenate([lower, swap(lower, 1)], 0)
    upper_pair = jnp.concatenate([upper, swap(upper, 2)], 0)
    return lower_pair, swap(lower_pair, 2), upper_pair, swap(upper_pair, 1)


def scatter_first(chunks):
    return swap(chunks[1], 2), swap(chunks[3], 1)


def scatter_second(chunks, got):
    near_lower, _, near_upper, _ = chunks
    got_lower, got_upper = got
    half = near_lower.shape[0] // 2
    last_lower = swap(near_lower[half:] + got_lower[half:], 1)
    last_upper = swap(near_upper[half:] + got_upper[half:], 2)
    return (near_lower, got_lower, last_lower, near_upper, got_upper, last_upper)


def swap_pairs(own):
    half = own.shape[0] // 2
    return swap(own[:half], 1), swap(own[half:], 2)


def far_pairs(own, got):
    half = own.shape[0] // 2
    lower_pair = jnp.concatenate([own[:half], got[0]], 0)
    upper_pair = jnp.concatenate([own[half:], got[1]], 0)
    return lower_pair, swap(lower_pair, 2), upper_pair, swap(upper_pair, 1)


def over_seq(pieces):
    count, quarter, width = pieces.shape
    return lax.all_to_all(pieces, "seq", 0, 0, tiled=True).reshape(count * quarter, width)


def three_parts(value):
    high = value.astype(LOW)
    rest = value - high.astype(WIDE)
    middle = rest.astype(LOW)
    low = (rest - middle.astype(WIDE)).astype(LOW)
    return high, middle, low


def token_features(segments, variates):
    lane = lax.broadcasted_iota(jnp.int32, (segments.shape[0], FEATURES), 1)
    variate_hot = (lane < 12) & (lane % 4 == variates)
    ones = (lane >= 12) & (lane < 15)
    segment_lane = (lane >= 16) & (lane < LSE_AT)
    segment_hot = segment_lane & (lane - 16 == segments)
    segment_cold = segment_lane & (lane - 16 != segments)
    query_side = variate_hot | ones | segment_hot
    key_side = variate_hot | ones | segment_cold | ((lane >= LSE_AT) & (lane < LSE_AT + 3))
    return jnp.where(query_side, 1.0, 0.0).astype(LOW), jnp.where(key_side, 1.0, 0.0).astype(LOW)


def head_weights(same_bias, other_bias):
    gap = [part[:, None] for part in three_parts(same_bias - other_bias)]
    base = [part[:, None] for part in three_parts(other_bias)]
    heads = same_bias.shape[0]
    columns = [jnp.broadcast_to(part, (heads, 4)) for part in gap] + base
    columns.append(jnp.zeros((heads, 1), LOW))
    columns.append(jnp.full((heads, LSE_AT - 16), MASKED, LOW))
    columns.append(jnp.zeros((heads, FEATURES - LSE_AT), LOW))
    return jnp.concatenate(columns, 1)


def turn_pair(pair, cosine, sine):
    lane = lax.broadcasted_iota(jnp.int32, pair.shape, 1)
    crossed = jnp.where(lane % 64 < 32, pltpu.roll(pair, 96, 1), pltpu.roll(pair, 32, 1))
    return pair * cosine + crossed * sine


def dot_plain(left, right):
    return jnp.dot(left, right, preferred_element_type=WIDE)


def dot_rows(left, right):
    return lax.dot_general(left, right, (((1,), (1,)), ((), ())), preferred_element_type=WIDE)


def dot_first(left, right):
    return lax.dot_general(left, right, (((0,), (0,)), ((), ())), preferred_element_type=WIDE)


def whole_block():
    return pl.BlockSpec(memory_space=pltpu.VMEM)


def call(kernel, name, outs, specs, flops, moved, args, scratch=()):
    return pl.pallas_call(
        kernel,
        grid=(1,),
        out_shape=[jax.ShapeDtypeStruct(shape, dtype) for shape, dtype in outs],
        in_specs=specs,
        out_specs=[pl.BlockSpec(memory_space=pltpu.VMEM) for _ in outs],
        scratch_shapes=list(scratch),
        cost_estimate=pl.CostEstimate(flops=flops, bytes_accessed=moved, transcendentals=0),
        compiler_params=pltpu.CompilerParams(vmem_limit_bytes=56 * 2**20),
        name=name,
    )(*args)


class Copies:
    def __init__(self, ref, pairs, sems):
        self.ref = ref
        self.copies = [
            pltpu.make_async_copy(source, target, sems.at[k])
            for k, (source, target) in enumerate(pairs)
        ]
        self.started = self.waited = False

    def start(self, *which):
        self.started = True
        for k in which or range(len(self.copies)):
            self.copies[k].start()

    def wait(self):
        if not self.waited:
            for copy in self.copies:
                copy.wait()
        self.waited = True
        return self.ref

    def _at(self, index, act):
        for k, copy in enumerate(self.copies):
            pl.when(index == k)(functools.partial(act, copy))

    def start_at(self, index):
        self.started = True
        self._at(index, lambda copy: copy.start())

    def wait_at(self, index):
        self.waited = True
        self._at(index, lambda copy: copy.wait())

    def wait_first(self, index):
        if not self.waited:
            self.waited = True

            @pl.when(index == 0)
            def _():
                for copy in self.copies:
                    copy.wait()

        return self.ref


class Plan:
    def __init__(self, arrays, shape, pairs, count):
        self.arrays, self.shape, self.pairs, self.count = arrays, shape, pairs, count


def whole(array, column=None, width=None):
    shape = array.shape if column is None else (array.shape[0], width)

    def pairs(refs, buffer):
        if column is None:
            return [(refs[0], buffer)]
        return [(refs[0].at[:, pl.ds(column, width)], buffer)]

    return Plan([array], shape, pairs, 1)


def top(array):
    half = array.shape[0] // 2
    return Plan(
        [array],
        (half, *array.shape[1:]),
        lambda refs, buffer: [(refs[0].at[pl.ds(0, half)], buffer)],
        1,
    )


def rows_of(array, count=4):
    size = array.shape[0] // count
    return Plan(
        [array],
        (count, size, array.shape[1]),
        lambda refs, buffer: [
            (refs[0].at[pl.ds(k * size, size)], buffer.at[k]) for k in range(count)
        ],
        count,
    )


def columns_of(array, count=4, column=0, width=None):
    size = (width or array.shape[1]) // count
    return Plan(
        [array],
        (count, array.shape[0], size),
        lambda refs, buffer: [
            (refs[0].at[:, pl.ds(column + k * size, size)], buffer.at[k]) for k in range(count)
        ],
        count,
    )


def group(arrays, column=None, width=None):
    rows = arrays[0].shape[0]

    def pairs(refs, buffer):
        if column is None:
            return [(ref, buffer.at[k]) for k, ref in enumerate(refs)]
        return [(ref.at[:, pl.ds(column, width)], buffer.at[k]) for k, ref in enumerate(refs)]

    return Plan(
        list(arrays), (len(arrays), rows, width or arrays[0].shape[1]), pairs, len(arrays)
    )


def out_rows(shape, dtype, count=4):
    size = shape[0] // count

    def pairs(refs, buffer):
        return [(buffer.at[k], refs[0].at[pl.ds(k * size, size)]) for k in range(count)]

    return Plan([(shape, dtype)], (count, size, *shape[1:]), pairs, count)


def out_group(shape, dtype, count=4):
    def pairs(refs, buffer):
        return [(buffer.at[k], ref) for k, ref in enumerate(refs)]

    return Plan([(shape, dtype)] * count, (count, *shape), pairs, count)


def out_whole(shape, dtype):
    return Plan([(shape, dtype)], shape, lambda refs, buffer: [(buffer, refs[0])], 1)


def run(body, name, us, ins, outs, scratch=(), token=None):
    args, in_specs, out_shapes, out_specs, buffers = [], [], [], [], []
    named = len(ins)
    if token is not None:
        ins = [*ins, token]
    for item in ins:
        if isinstance(item, Plan):
            args += item.arrays
            in_specs += [pl.BlockSpec(memory_space=pl.ANY)] * len(item.arrays)
            buffers.append(pltpu.VMEM(item.shape, item.arrays[0].dtype))
            buffers.append(pltpu.SemaphoreType.DMA((item.count,)))
        else:
            args.append(item)
            space = pltpu.SMEM if item.shape == (1,) else pltpu.VMEM
            in_specs.append(pl.BlockSpec(memory_space=space))
    for item in outs:
        if isinstance(item, Plan):
            out_shapes += [jax.ShapeDtypeStruct(*each) for each in item.arrays]
            out_specs += [pl.BlockSpec(memory_space=pl.ANY)] * len(item.arrays)
            buffers.append(pltpu.VMEM(item.shape, item.arrays[0][1]))
            buffers.append(pltpu.SemaphoreType.DMA((item.count,)))
        else:
            out_shapes.append(jax.ShapeDtypeStruct(*item))
            out_specs.append(pl.BlockSpec(memory_space=pltpu.VMEM))
    n_in, n_out = len(args), len(out_shapes)

    def kernel(*refs):
        given, rest = list(refs[: n_in + n_out]), list(refs[n_in + n_out :])
        bound = []
        for item in (*ins, *outs):
            if isinstance(item, Plan):
                near = [given.pop(0) for _ in item.arrays]
                buffer, sems = rest.pop(0), rest.pop(0)
                bound.append(Copies(buffer, item.pairs(near, buffer), sems))
            else:
                bound.append(given.pop(0))
        body(*bound[:named], *bound[len(ins) :], *rest)
        for item in bound[: len(ins)]:
            if isinstance(item, Copies):
                item.wait()
        for item in bound[len(ins) :]:
            if isinstance(item, Copies) and not item.started:
                item.start()
        for item in bound[len(ins) :]:
            if isinstance(item, Copies):
                item.wait()

    return pl.pallas_call(
        kernel,
        out_shape=out_shapes,
        in_specs=in_specs,
        out_specs=out_specs,
        scratch_shapes=buffers + list(scratch),
        cost_estimate=pl.CostEstimate(
            flops=int(us * 1.15e9), bytes_accessed=2**20, transcendentals=0
        ),
        compiler_params=pltpu.CompilerParams(vmem_limit_bytes=60 * 2**20),
        name=name,
    )(*args)


def output_weights(pieces):
    rows = pieces[0].shape[0] // 2
    places = {
        0: ((0, 0), (0, 1), (1, 0), (1, 1)),
        1: ((2, 0), (3, 0), (2, 1), (3, 1)),
    }

    def pairs(refs, buffer):
        rank = lax.axis_index("batch")
        out = []
        for half in range(2):
            for r, (which, part) in enumerate(places[half]):
                to = pl.ds(pl.multiple_of((rank ^ r) * 256, 256), 256)
                out.append(
                    (
                        refs[which].at[pl.ds(part * rows, rows)],
                        buffer.at[pl.ds(half * rows, rows), to],
                    )
                )
        return out

    return Plan(list(pieces), (2 * rows, D), pairs, 8)


def start_all(*items):
    for item in items:
        item.start()


def unit_rows(rows):
    return lax.rsqrt(jnp.mean(rows * rows, -1, keepdims=True) + EPSILON)


def pack_body(
    rank_ref, x, cot, segment_ref, variate_ref, position_ref, wq, wk, wv, wo, gain_first_ref,
    gain_second_ref, gate, up, down, rows_out, shard_out, gate_up_out, down_out,
):
    start_all(wq, wk, wv, wo, x, cot, gate, up, down)
    micro, _, quarter, _ = x.ref.shape
    tokens = 4 * quarter
    lane = lax.broadcasted_iota(jnp.int32, (tokens, 128), 1)
    on_line = lax.broadcasted_iota(jnp.int32, (tokens, 128), 0) == lane

    def upright(row):
        return jnp.sum(jnp.where(on_line, row, 0.0), 1, keepdims=True)

    gains = jnp.where(
        lane == 0,
        upright(gain_first_ref[...].astype(WIDE)),
        jnp.where(lane == 1, upright(gain_second_ref[...].astype(WIDE)), 0.0),
    )
    shard_out.ref[:, D:] = gains.astype(LOW)
    for place, weight in enumerate((wq, wk, wv, wo)):
        shard_out.ref[:, 256 * place : 256 * (place + 1)] = weight.wait()[...]
    shard_out.start()
    for m in range(micro):
        places = position_ref[m : m + 1, :]
        numbers = jnp.zeros((tokens, 128), WIDE)
        for place, row in enumerate(
            (
                segment_ref[m : m + 1, :],
                variate_ref[m : m + 1, :],
                lax.shift_right_logical(places, 5),
                places & 31,
            )
        ):
            numbers = jnp.where(lane == place, upright(row.astype(WIDE)), numbers)
        numbers = numbers.astype(LOW)
        for r in range(4):
            rows_out.ref[r, 0, m, :, D:] = numbers[r * quarter : (r + 1) * quarter, :]
            rows_out.ref[r, 1, m, :, D:] = jnp.zeros((quarter, 128), LOW)
    x_ref, cot_ref = x.wait(), cot.wait()
    for m in range(micro):
        for r in range(4):
            rows_out.ref[r, 0, m, :, :D] = x_ref[m, r]
            rows_out.ref[r, 1, m, :, :D] = cot_ref[m, r]
    rows_out.start()
    gate_ref, up_ref = gate.wait(), up.wait()
    per = gate_up_out.ref.shape[1] // 2
    piece = gate_ref.shape[2]
    for s in range(per // piece):
        gate_up_out.ref[:, s * piece : (s + 1) * piece] = gate_ref[s]
        gate_up_out.ref[:, per + s * piece : per + (s + 1) * piece] = up_ref[s]
    gate_up_out.start()
    down_out.ref[...] = down.wait()[...]


def pack(rank, x, cot, segments, variates, positions, shards, gains, w_gate, w_up, w_down):
    micro, tokens, _ = x.shape
    quarter = tokens // 4
    shard, ff = w_gate.shape
    piece = w_down.shape[0] // 4
    pieces = ff // 4 // piece

    def quarters(array):
        return array.reshape(micro, 4, quarter, D)

    def mine(array, size, refs_at):
        return Plan([array], size, refs_at, 1)

    def rank_columns(array):
        def pairs(refs, buffer):
            at = pl.multiple_of(lax.axis_index("batch") * 256, 256)
            return [(refs[0].at[:, pl.ds(at, 256)], buffer)]

        return Plan([array], (shard, 256), pairs, 1)

    def feed_columns(array):
        def pairs(refs, buffer):
            rank = lax.axis_index("batch")
            return [
                (refs[0].at[:, pl.ds(pl.multiple_of((4 * s + rank) * piece, piece), piece)], buffer.at[s])
                for s in range(pieces)
            ]

        return Plan([array], (pieces, shard, piece), pairs, pieces)

    def down_rows(array):
        def pairs(refs, buffer):
            at = pl.multiple_of(lax.axis_index("batch") * piece, piece)
            return [(refs[0].at[pl.ds(at, piece)], buffer)]

        return Plan([array], (piece, D), pairs, 1)

    return run(
        pack_body,
        "pack",
        4,
        [rank, whole(quarters(x)), whole(quarters(cot)), segments, variates, positions]
        + [rank_columns(weight) for weight in shards]
        + [*gains, feed_columns(w_gate), feed_columns(w_up), down_rows(w_down)],
        [
            out_whole((4, 2, micro, quarter, D + 128), LOW),
            out_whole((shard, D + 128), LOW),
            out_whole((shard, ff // 2), LOW),
            out_whole((piece, D), LOW),
        ],
    )


def attend_body(
    x, qkv, gains, freqs_ref, weights_ref,
    gain_ref, mixed, turned, wide, lower, upper, logs, cos, sin, query_sides, key_sides,
    keys_ref, values_ref, trig_ref,
):
    start_all(x, gains, qkv)
    count, chunk, _ = x.ref.shape
    lane = lax.broadcasted_iota(jnp.int32, (chunk, 128), 1)
    half_lane = lane // 64
    pick = lax.broadcasted_iota(jnp.int32, (16, 128), 0) == lax.broadcasted_iota(
        jnp.int32, (16, 128), 1
    )
    x_ref = x.wait()
    angles = jnp.zeros((chunk, 128), WIDE)
    for k in range(count):
        numbers = x_ref[k, :, D : D + 128].astype(WIDE)
        places = numbers[:, 2:3] * 32.0 + numbers[:, 3:4]
        angles = jnp.where(lane // 32 == k, places * freqs_ref[...], angles)
    trig_ref[0] = jnp.cos(angles)
    trig_ref[1] = jnp.sin(angles)
    gain_ref[...] = dot_rows(jnp.where(pick, 1.0, 0.0).astype(LOW), gains.wait()[...])
    qkv_ref = qkv.wait()

    def one_chunk(index, carry):
        rows = x_ref[index, :, :D].astype(WIDE)
        mixed_rows = (rows * unit_rows(rows) * gain_ref[0:1, :]).astype(LOW)
        mixed.ref[index] = mixed_rows

        def spread(packed):
            own = jnp.where(lane // 32 == index, packed, 0.0)
            own = own + pltpu.roll(own, 64, 1)
            return own + pltpu.roll(own, 32, 1)

        cosine = spread(trig_ref[0])
        sine = spread(trig_ref[1])
        sine = jnp.where(lane % 64 < 32, -sine, sine)
        cos.ref[index] = cosine
        sin.ref[index] = sine
        numbers = x_ref[index, :, D : D + 128].astype(WIDE).astype(jnp.int32)
        query_side, key_side = token_features(numbers[:, 0:1], numbers[:, 1:2])
        query_sides.ref[index] = query_side
        key_sides.ref[index] = key_side
        proj = dot_plain(mixed_rows, qkv_ref[...])
        values = proj[:, 512:].astype(LOW)
        turned.ref[index, :, 512:768] = values
        for pair in range(2):
            at = 128 * pair
            turned.ref[index, :, at : at + 128] = turn_pair(
                proj[:, at : at + 128], cosine, sine
            ).astype(LOW)
            keys = turn_pair(proj[:, 256 + at : 384 + at], cosine, sine).astype(LOW)
            turned.ref[index, :, 256 + at : 384 + at] = keys
            here = pl.ds(pl.multiple_of(index * chunk, chunk), chunk)
            keys_ref[pair, here, :128] = keys
            keys_ref[pair, here, 128:] = key_side
            values_ref[pair, here, :128] = values[:, at : at + 128]
            values_ref[pair, here, 128:] = jnp.where(lane == 0, 1.0, 0.0).astype(LOW)
        return carry

    lax.fori_loop(0, count, one_chunk, 0)
    start_all(mixed, turned, cos, sin, query_sides, key_sides)

    def one_block(index, carry):
        side = query_sides.ref[index]
        log_rows = jnp.zeros((chunk, 128), WIDE)
        here = pl.ds(pl.multiple_of((index % 2) * chunk, chunk), chunk)
        def scores_of(head):
            at = 128 * (head // 2)
            scaled = turned.ref[index, :, at : at + 128] * LOW(SCORE_SCALE)
            query = jnp.concatenate(
                [
                    jnp.where(half_lane == head % 2, scaled, LOW(0)),
                    side * weights_ref[head : head + 1, :],
                ],
                1,
            )
            return dot_rows(query, keys_ref[head // 2])

        scores = scores_of(0)
        parts = []
        for head in range(4):
            high = jnp.max(scores, 1, keepdims=True)
            powers = jnp.exp(scores - high).astype(LOW)
            if head < 3:
                scores = scores_of(head + 1)
            summed = dot_plain(powers, values_ref[head // 2])
            total = summed[:, 128:129]
            parts.append(summed[:, :128] / total)
            log_rows = jnp.where(lane == head, high + jnp.log(total), log_rows)
        for pair in range(2):
            at = 128 * pair
            total_mixed = jnp.where(half_lane == 0, parts[2 * pair], parts[2 * pair + 1])
            wide.ref[index, :, at : at + 128] = total_mixed
            low_rows = total_mixed.astype(LOW)

            @pl.when(index < 2)
            def _(low_rows=low_rows, at=at):
                lower.ref[here, at : at + 128] = low_rows

            @pl.when(index >= 2)
            def _(low_rows=low_rows, at=at):
                upper.ref[here, at : at + 128] = low_rows

        logs.ref[index] = log_rows
        return carry

    lax.fori_loop(0, count, one_block, 0)


def attend(chunks, first_weights, freqs, weights, token):
    chunk = chunks[0].shape[0]
    length = 4 * chunk
    return run(
        attend_body,
        "attend",
        15,
        [
            group(chunks),
            whole(first_weights, 0, 768),
            whole(first_weights, D, 128),
            freqs,
            weights,
        ],
        [
            ((16, D), WIDE),
            out_rows((length, D), LOW),
            out_rows((length, 768), LOW),
            out_rows((length, 256), WIDE),
            out_whole((length // 2, 256), LOW),
            out_whole((length // 2, 256), LOW),
            out_rows((length, 128), WIDE),
            out_rows((length, 128), WIDE),
            out_rows((length, 128), WIDE),
            out_rows((length, FEATURES), LOW),
            out_rows((length, FEATURES), LOW),
        ],
        [pltpu.VMEM((2, length, 256), LOW)] * 2 + [pltpu.VMEM((2, chunk, 128), WIDE)],
        token,
    )


def middle_body(rank_ref, x, near, far, wo, gain_ref, heads, own, mixed):
    rank = rank_ref[0]
    start_all(near, far, wo, x)
    count, chunk, _ = x.ref.shape
    block = chunk // 2
    near_ref, far_ref = near.wait(), far.wait()
    width = near_ref.shape[2]
    sources = {
        0: ((near_ref, 0, 0), (near_ref, 2, 0), (far_ref, 0, 0), (far_ref, 0, width)),
        1: ((near_ref, 1, 0), (far_ref, 1, 0), (near_ref, 3, 0), (far_ref, 1, width)),
    }
    for half, order in enumerate((ORDER_A, ORDER_B)):
        for q in range(4):
            ref, which, column = sources[half][q]
            for place, r in enumerate(order):
                start = order.index(r ^ q) * block
                heads.ref[
                    2 * half + place // 2,
                    place % 2 * block : (place % 2 + 1) * block,
                    q * width : (q + 1) * width,
                ] = ref[which, start : start + block, column : column + width]
    heads.start()
    wo_ref = wo.wait()

    def one_chunk(index, carry):
        x.wait_at(index)
        total = x.ref[index, :, :D].astype(WIDE)
        for q in range(4):
            rows = pl.ds(pl.multiple_of((rank ^ q) * width, width), width)
            total = total + dot_plain(
                heads.ref[index, :, q * width : (q + 1) * width], wo_ref[rows, :]
            )

        @pl.when(index % 2 == 0)
        def _():
            own.ref[index // 2] = total[:block]
            own.start_at(index // 2)

        mixed.ref[index] = (total * unit_rows(total) * gain_ref[1:2, :]).astype(LOW)
        mixed.start_at(index)
        return carry

    lax.fori_loop(0, count, one_chunk, 0)


def middle(rank, chunks, heads, out_pieces, gain):
    chunk = chunks[0].shape[0]
    length = 4 * chunk
    lower, lower_x, lower_far, upper, upper_y, upper_far = heads
    return run(
        middle_body,
        "middle",
        7,
        [
            rank,
            group(chunks),
            group((lower, upper, lower_x, upper_y)),
            group((lower_far, upper_far)),
            output_weights(out_pieces),
            gain,
        ],
        [out_rows((length, D), LOW), out_rows((chunk, D), WIDE, 2), out_rows((length, D), LOW)],
    )


def feed_body(mixed, gate_up, both, hidden):
    count, _, per = hidden.ref.shape
    mixed.start(0)
    gate_up.start()
    mixed.start(1, 2, 3)

    def one_chunk(index, carry):
        mixed.wait_at(index)
        gate_up_ref = gate_up.wait_first(index)
        rows = mixed.ref[index]
        for half in range(2):
            here = slice(half * per // 2, (half + 1) * per // 2)
            gate = dot_plain(rows, gate_up_ref[half])
            up = dot_plain(rows, gate_up_ref[2 + half])
            sigmoid = 1.0 / (1.0 + jnp.exp(-gate))
            silu = gate * sigmoid
            both.ref[index, :, here] = (up * (sigmoid + silu * (1.0 - sigmoid))).astype(LOW)
            both.ref[index, :, per + half * per // 2 : per + (half + 1) * per // 2] = silu.astype(LOW)
            hidden.ref[index, :, here] = (silu * up).astype(LOW)
        both.start_at(index)
        hidden.start_at(index)
        return carry

    lax.fori_loop(0, count, one_chunk, 0)


def feed(mixed, gate_up, token):
    length = mixed.shape[0]
    per = gate_up.shape[1] // 2
    return run(
        feed_body,
        "feed",
        8,
        [rows_of(mixed), columns_of(gate_up)],
        [out_rows((length, 2 * per), LOW), out_rows((length, per), LOW)],
        token=token,
    )


def feed_back_body(both, cots, gate_up, down, grads, back, later=()):
    start_all(down)
    cots.start(0)
    both.start(0)
    gate_up.start()
    cots.start(1)
    both.start(1)
    start_all(*later)
    per = down.ref.shape[0]

    def one_chunk(index, carry):
        cots.wait_at(index)
        both.wait_at(index)
        grad_hidden = dot_rows(cots.ref[index], down.wait_first(index)[...])
        grads.ref[index, :, :per] = (grad_hidden * both.ref[index, :, :per].astype(WIDE)).astype(LOW)
        grads.ref[index, :, per:] = (grad_hidden * both.ref[index, :, per:].astype(WIDE)).astype(LOW)
        grads.start_at(index)
        back.ref[index] = dot_rows(grads.ref[index], gate_up.wait_first(index)[...]).astype(LOW)
        back.start_at(index)
        return carry

    lax.fori_loop(0, 2, one_chunk, 0)


def feed_back_far_body(both, cots, gate_up, down, hidden, near_cots, grads, back, out):
    feed_back_body(both, cots, gate_up, down, grads, back, (hidden, near_cots))
    near_ref, far_ref = near_cots.wait(), cots.ref
    chunk = near_ref.shape[1]

    def one_part(index, carry):
        hidden.wait_at(index)
        total = None
        for k in range(4):
            more = dot_first(
                hidden.ref[index, k * chunk : (k + 1) * chunk, :], (near_ref, far_ref)[k % 2][k // 2]
            )
            total = more if total is None else total + more
        out.ref[index] = total.astype(LOW)
        out.start_at(index)
        return carry

    lax.fori_loop(0, hidden.ref.shape[0], one_part, 0)


def feed_back(first, both, cots, gate_up, down, token, hidden=None):
    length = both.shape[0]
    chunk = length // 4
    per = down.shape[0]

    def pairs(refs, buffer):
        return [
            (refs[0].at[pl.ds((first + 2 * k) * chunk, chunk)], buffer.at[k]) for k in range(2)
        ]

    ins = [Plan([both], (2, chunk, 2 * per), pairs, 2), group((cots[first], cots[first + 2]))]
    ins += [whole(gate_up), whole(down)]
    outs = [out_rows((length // 2, 2 * per), LOW, 2), out_group((chunk, D), LOW, 2)]
    if hidden is None:
        return run(feed_back_body, "feed_back", 7, ins, outs, token=token)
    ins += [columns_of(hidden), group((cots[0], cots[2]))]
    outs += [out_rows((per, D), LOW)]
    return run(feed_back_far_body, "feed_back", 12, ins, outs, token=token)


def sum_arrived(near, got, last):
    return (
        near.wait()[...].astype(WIDE) + got.wait()[...].astype(WIDE) + last.wait()[...].astype(WIDE)
    )


def arrivals(sums):
    return [whole(x) if place % 3 == 2 else top(x) for place, x in enumerate(sums)]


def own_back_body(
    rank_ref, n0, g0, l0, n1, g1, l1, middle_rows, cot, gain_ref, wo, grad, parcels
):
    rank = rank_ref[0]
    start_all(n0, g0, l0, middle_rows, cot, n1, g1, l1, wo)
    block = l0.ref.shape[0]
    width = parcels.ref.shape[2] // 2
    for place, sums in enumerate(((n0, g0, l0), (n1, g1, l1))):
        rows = slice(place * block, (place + 1) * block)
        arrived = sum_arrived(*sums)
        y = middle_rows.wait()[rows, :]
        scale = unit_rows(y)
        normed = y * scale
        turned = arrived * gain_ref[1:2, :]
        grad.ref[rows, :] = cot.wait()[rows, :].astype(WIDE) + scale * (
            turned - normed * jnp.mean(turned * normed, -1, keepdims=True)
        )
    low_grad = grad.ref[...].astype(LOW)
    wo_ref = wo.wait()
    for q in range(4):
        place = pl.ds(pl.multiple_of((rank ^ q) * width, width), width)
        parcels.ref[q, :, :width] = dot_rows(low_grad, wo_ref[place, :]).astype(LOW)
        parcels.ref[q, :, width:] = grad.ref[:, place].astype(LOW)


def own_back(rank, sums, middle_own, cot_own, gain, out_pieces, token):
    quarter = cot_own.shape[0]
    return run(
        own_back_body,
        "own_back",
        4,
        [rank, *arrivals(sums), whole(middle_own), whole(cot_own), gain]
        + [output_weights(out_pieces)],
        [out_whole((quarter, D), WIDE), out_group((quarter, 512), LOW)],
        token=token,
    )


def attend_back_body(
    pair, parcels, q, k, v, wide, logs, cos, sin, query_sides, key_sides, weights_ref,
    *rest,
):
    if pair == 1:
        before, projections, out, bias_ref, back, *rest, joined_ref = rest
    else:
        out, bias_ref, *rest = rest
    queries_ref, grads_ref, total_ref = rest
    start_all(parcels, q, query_sides, logs, wide, k, v, key_sides, cos, sin)
    if pair == 1:
        start_all(before, projections)
    length = q.ref.shape[0]
    chunk = length // 4
    block = chunk // 2
    half_lane = lax.broadcasted_iota(jnp.int32, (chunk, 128), 1) // 64
    lane = lax.broadcasted_iota(jnp.int32, (chunk, 128), 1)
    parcels_ref = parcels.wait()
    for half, order in enumerate((ORDER_A, ORDER_B)):
        for place in range(4):
            to = slice((4 * half + place) * block, (4 * half + place + 1) * block)
            rows = slice(half * block, (half + 1) * block)
            for head in range(2):
                grads_ref[head, to, :128] = parcels_ref[order[place], rows, :]
    q_ref, side_ref, log_ref, wide_ref = q.wait(), query_sides.wait(), logs.wait(), wide.wait()

    def prepare(index, carry):
        rows = pl.ds(pl.multiple_of(index * chunk, chunk), chunk)
        product = grads_ref[0, rows, :128].astype(WIDE) * wide_ref[rows, :]
        scaled = q_ref[rows, :] * LOW(SCORE_SCALE)
        for half in range(2):
            head = 2 * pair + half
            side = side_ref[rows, :] * weights_ref[head : head + 1, :]
            for place, piece in enumerate(three_parts(-log_ref[rows, head : head + 1])):
                side = jnp.where(lane == LSE_AT + place, piece, side)
            queries_ref[half, rows, :128] = jnp.where(half_lane == half, scaled, LOW(0))
            queries_ref[half, rows, 128:] = side
            delta = jnp.sum(jnp.where(half_lane == half, product, 0.0), 1, keepdims=True)
            extra = jnp.zeros((chunk, 128), LOW)
            for place, piece in enumerate(three_parts(-delta)):
                extra = jnp.where(lane == place, piece, extra)
            grads_ref[half, rows, 128:] = extra
        total_ref[rows, :] = jnp.zeros((chunk, 128), WIDE)
        return carry

    lax.fori_loop(0, 4, prepare, 0)
    three_ones = jnp.where(lane < 3, 1.0, 0.0).astype(LOW)
    k_ref, v_ref, key_ref, cos_ref, sin_ref = (
        k.wait(), v.wait(), key_sides.wait(), cos.wait(), sin.wait()
    )

    def one_block(index, carry):
        rows = pl.ds(pl.multiple_of(index * chunk, chunk), chunk)
        cosine = cos_ref[rows, :]
        sine = -sin_ref[rows, :]
        key_side = key_ref[rows, :]
        first_four = jnp.where(lane < 4, key_side.astype(WIDE), 0.0)
        sums = list(carry)
        keys = k_ref[rows, :]
        values = v_ref[rows, :]
        keys_wide = jnp.concatenate([keys, key_side], 1)
        grad_keys = jnp.zeros((chunk, 128), WIDE)
        grad_values = jnp.zeros((chunk, 128), WIDE)
        for half in range(2):
            mine = half_lane == half
            weights = jnp.exp(dot_rows(keys_wide, queries_ref[half]))
            grad_weights = dot_rows(
                jnp.concatenate([jnp.where(mine, values, LOW(0)), three_ones], 1), grads_ref[half]
            )
            grad_values = jnp.where(
                mine, dot_plain(weights.astype(LOW), grads_ref[half, :, :128]), grad_values
            )
            grad_scores = (weights * grad_weights).astype(LOW)
            both = dot_plain(
                grad_scores,
                jnp.concatenate([queries_ref[half, :, :128], side_ref[...]], 1),
            )
            grad_keys = grad_keys + both[:, :128]
            counted = both[:, 128:]
            same = jnp.sum(counted * first_four, 0, keepdims=True)
            every = jnp.sum(jnp.where(lane < 4, counted, 0.0), 0, keepdims=True)
            sums[half] = sums[half] + same
            sums[2 + half] = sums[2 + half] + (every - same)
            total_ref[...] += dot_first(grad_scores, jnp.where(mine, keys, LOW(0)))
        out.ref[index, :, 128:256] = turn_pair(grad_keys, cosine, sine).astype(LOW)
        out.ref[index, :, 256:] = grad_values.astype(LOW)
        return tuple(sums)

    start = tuple(jnp.zeros((1, 128), WIDE) for _ in range(4))
    sums = lax.fori_loop(0, 4, one_block, start)
    bias_ref[...] = jnp.zeros_like(bias_ref)
    for place in range(4):
        bias_ref[place : place + 1, :] = sums[place]
    for place in range(4):
        rows = slice(place * chunk, (place + 1) * chunk)
        out.ref[place, :, :128] = turn_pair(
            total_ref[rows, :] * SCORE_SCALE, cos_ref[rows, :], -sin_ref[rows, :]
        ).astype(LOW)
    if pair == 0:
        return
    out.start()
    before_ref, projections_ref = before.wait(), projections.wait()

    def one_chunk(index, carry):
        for kind in range(3):
            here = slice(128 * kind, 128 * (kind + 1))
            joined_ref[:, 256 * kind : 256 * kind + 128] = before_ref[index, :, here]
            joined_ref[:, 256 * kind + 128 : 256 * (kind + 1)] = out.ref[index, :, here]
        back.ref[index] = dot_rows(joined_ref[...], projections_ref[...]).astype(LOW)
        back.start_at(index)
        return carry

    lax.fori_loop(0, 4, one_chunk, 0)


def attend_back(pair, parcels, kept, weights, token, before=None, first_weights=None):
    turned, attended, *others = kept
    length = turned.shape[0]
    at = 128 * pair
    return run(
        functools.partial(attend_back_body, pair),
        "attend_back",
        40,
        [group(parcels, at, 128)]
        + [whole(turned, column + at, 128) for column in (0, 256, 512)]
        + [whole(attended, at, 128)]
        + [whole(x) for x in others]
        + [weights]
        + ([rows_of(before), whole(first_weights, 0, 768)] if pair else []),
        [out_rows((length, 384), LOW), ((8, 128), WIDE)]
        + ([out_group((length // 4, D), LOW)] if pair else []),
        [
            pltpu.VMEM((2, length, 256), LOW),
            pltpu.VMEM((2, length, 256), LOW),
            pltpu.VMEM((length, 128), WIDE),
        ]
        + ([pltpu.VMEM((length // 4, 768), LOW)] if pair else []),
        token,
    )


def gate_up_grads_body(mixed, near, far, out):
    start_all(near, far, mixed)
    chunk = mixed.ref.shape[1] // 4

    def one_part(index, carry):
        near_ref, far_ref = near.wait_first(index), far.wait_first(index)
        mixed.wait_at(index)
        total = None
        for k in range(4):
            more = dot_first(
                mixed.ref[index, k * chunk : (k + 1) * chunk, :], (near_ref, far_ref)[k % 2][k // 2]
            )
            total = more if total is None else total + more
        out.ref[index] = total.astype(LOW)
        out.start_at(index)
        return carry

    lax.fori_loop(0, mixed.ref.shape[0], one_part, 0)


def gate_up_grads(mixed, near, far, token):
    return run(
        gate_up_grads_body,
        "gate_up_grads",
        8,
        [columns_of(mixed), rows_of(near, 2), rows_of(far, 2)],
        [out_rows((D, near.shape[1]), LOW)],
        token=token,
    )[0]


def feed_out_body(hidden, down, out):
    start_all(down, hidden)

    def one_chunk(index, carry):
        down_ref = down.wait_first(index)
        hidden.wait_at(index)
        out.ref[index] = dot_plain(hidden.ref[index], down_ref[...]).astype(LOW)
        out.start_at(index)
        return carry

    lax.fori_loop(0, hidden.ref.shape[0], one_chunk, 0)


def feed_out(hidden, down, token):
    length = hidden.shape[0]
    return run(
        feed_out_body,
        "feed_out",
        5,
        [rows_of(hidden), whole(down)],
        [out_group((length // 4, D), LOW)],
        token=token,
    )


def own_last_body(
    n0, g0, l0, n1, g1, l1, m0, h0, k0, m1, h1, k1, x, base, middle_rows, gain_ref, out
):
    start_all(n0, g0, l0, x, base, m0, h0, k0, middle_rows, n1, g1, l1, m1, h1, k1)
    block = l0.ref.shape[0]
    piece = out.ref.shape[1] // 2
    each = block // piece
    for half, (back, forward) in enumerate(
        (((n0, g0, l0), (m0, h0, k0)), ((n1, g1, l1), (m1, h1, k1)))
    ):
        rows = slice(half * block, (half + 1) * block)
        places = slice(half * each, (half + 1) * each)
        turned = sum_arrived(*back) * gain_ref[0:1, :]
        x_rows = x.wait()[rows, :D].astype(WIDE)
        scale = unit_rows(x_rows)
        normed = x_rows * scale
        grad = base.wait()[rows, :] + scale * (
            turned - normed * jnp.mean(turned * normed, -1, keepdims=True)
        )
        out.ref[places, :piece, :] = grad.astype(LOW).reshape(each, piece, D)
        block_rows = sum_arrived(*forward) + middle_rows.wait()[rows, :]
        out.ref[places, piece:, :] = block_rows.astype(LOW).reshape(each, piece, D)


def own_last(sums, out_sums, mine, base, middle_own, gain, n_seq, token):
    quarter = base.shape[0]
    return run(
        own_last_body,
        "own_last",
        80,
        [*arrivals(sums), *arrivals(out_sums), whole(mine), whole(base), whole(middle_own), gain],
        [out_whole((n_seq, 2 * quarter // n_seq, D), LOW)],
        token=token,
    )[0]


def join_body(left, right, out):
    start_all(left, right)
    width = left.ref.shape[1]
    out.ref[:, :width] = left.wait()[...]
    out.ref[:, width:] = right.wait()[...]


def join(left, right, token):
    rows = left.shape[0]
    return run(
        join_body,
        "join",
        1,
        [whole(left), whole(right)],
        [out_whole((rows, left.shape[1] + right.shape[1]), LOW)],
        token=token,
    )[0]


def first_grads_body(rank_ref, mixed, proj0, proj1, heads, parcels, bias_ref, out, joined_ref):
    rank = rank_ref[0]
    start_all(mixed, proj0, proj1, parcels, heads)
    width = 256
    block = parcels.ref.shape[1] // 2
    for pair, proj in enumerate((proj0, proj1)):
        ref = proj.wait()
        for kind in range(3):
            column = width * kind + 128 * pair
            joined_ref[:, column : column + 128] = ref[:, 128 * kind : 128 * (kind + 1)]
    parcels_ref = parcels.wait()
    for half, order in enumerate((ORDER_A, ORDER_B)):
        for place in range(4):
            to = slice((4 * half + place) * block, (4 * half + place + 1) * block)
            joined_ref[to, 3 * width :] = parcels_ref[
                order[place], half * block : (half + 1) * block, :
            ]
    mixed_ref, heads_ref = mixed.wait(), heads.wait()

    def one_part(index, carry):
        out.ref[index, :, : 3 * width] = dot_first(
            mixed_ref[index], joined_ref[:, : 3 * width]
        ).astype(LOW)
        out.ref[rank ^ index, :, 3 * width : 4 * width] = dot_first(
            heads_ref[index], joined_ref[:, 3 * width :]
        ).astype(LOW)
        out.ref[index, :, 4 * width :] = bias_ref[...]
        return carry

    lax.fori_loop(0, 4, one_part, 0)


def first_grads(rank, mixed, proj0, proj1, heads, parcels, bias_rows, token):
    length = mixed.shape[0]
    return run(
        first_grads_body,
        "first_grads",
        8,
        [rank, columns_of(mixed), whole(proj0), whole(proj1), columns_of(heads)]
        + [group(parcels, 256, 256), bias_rows],
        [out_rows((D, 768 + 256 + 128), LOW)],
        [pltpu.VMEM((length, 1024), LOW)],
        token,
    )[0]


def rank_blocks(lower, lower_far, upper, upper_far):
    half = lower.shape[0] // 2
    return (
        ((lower, 0), (upper, 0)),
        ((lower, half), (upper_far, 0)),
        ((lower_far, 0), (upper, half)),
        ((lower_far, half), (upper_far, half)),
    )


def lay_flat(column, part):
    count = column.shape[0]
    row = lax.broadcasted_iota(jnp.int32, (count, 128), 0) + part * count
    lane = lax.broadcasted_iota(jnp.int32, (count, 128), 1)
    return jnp.sum(jnp.where(row == lane, column, 0.0), 0, keepdims=True)


def spread_feed_kernel(
    rank_ref, lower, lower_far, upper, upper_far, gate_ref, up_ref, gain_ref,
    grad_gate_ref, grad_up_ref, grad_down_ref, grad_gain_ref,
):
    rank = rank_ref[0]
    half = lower.shape[0] // 2
    piece = 128
    ff = gate_ref.shape[1]
    per = ff // 4
    for r, halves in enumerate(rank_blocks(lower, lower_far, upper, upper_far)):
        for part, (ref, start) in enumerate(halves):
            rows = slice(part * half, (part + 1) * half)
            source = slice(start, start + half)
            for s in range(per // piece):
                to = pl.ds(pl.multiple_of((4 * s + (rank ^ r)) * piece, piece), piece)
                grad_gate_ref[rows, to] = ref[source, s * piece : (s + 1) * piece].astype(WIDE)
                grad_up_ref[rows, to] = ref[source, per + s * piece : per + (s + 1) * piece].astype(
                    WIDE
                )
            to = pl.ds(pl.multiple_of((rank ^ r) * 2 * half + part * half, half), half)
            grad_down_ref[to, :] = ref[source, 2 * per :].astype(WIDE)
    flat = jnp.zeros((1, 128), WIDE)
    for part in range(2):
        rows = slice(part * half, (part + 1) * half)
        total = jnp.sum(
            gate_ref[rows, :].astype(WIDE) * grad_gate_ref[rows, :], 1, keepdims=True
        ) + jnp.sum(up_ref[rows, :].astype(WIDE) * grad_up_ref[rows, :], 1, keepdims=True)
        flat = flat + lay_flat(total, part)
    grad_gain_ref[...] = jnp.broadcast_to(flat / gain_ref[...].astype(WIDE), (8, 128))


def spread_feed(rank, pieces, w_gate, w_up, gain):
    shard, ff = w_gate.shape
    return call(
        spread_feed_kernel,
        "spread_feed",
        [((shard, ff), WIDE), ((shard, ff), WIDE), ((ff // 8, D), WIDE), ((8, 128), WIDE)],
        [pl.BlockSpec(memory_space=pltpu.SMEM)] + [whole_block()] * 7,
        4 * shard * ff,
        16 * 2**20,
        (rank, *pieces, w_gate, w_up, gain),
    )


def spread_first_kernel(
    rank_ref, lower, lower_far, upper, upper_far, wq_ref, wk_ref, wv_ref, gain_ref,
    gq_ref, gk_ref, gv_ref, go_ref, grad_gain_ref, bias_ref,
):
    rank = rank_ref[0]
    half = lower.shape[0] // 2
    wide = 256
    bias_ref[...] = jnp.zeros_like(bias_ref)
    for r, halves in enumerate(rank_blocks(lower, lower_far, upper, upper_far)):
        to = pl.ds(pl.multiple_of((rank ^ r) * wide, wide), wide)
        for part, (ref, start) in enumerate(halves):
            rows = slice(part * half, (part + 1) * half)
            source = slice(start, start + half)
            for place, out_ref in enumerate((gq_ref, gk_ref, gv_ref, go_ref)):
                out_ref[rows, to] = ref[source, place * wide : (place + 1) * wide].astype(WIDE)
        ref, start = halves[0]
        bias_ref[pl.ds(rank ^ r, 1), :] = jnp.sum(
            ref[start : start + 16, 4 * wide : 4 * wide + 128].astype(WIDE), 0, keepdims=True
        )
    flat = jnp.zeros((1, 128), WIDE)
    for part in range(2):
        rows = slice(part * half, (part + 1) * half)
        total = jnp.zeros((half, 1), WIDE)
        for weight_ref, grad_ref in ((wq_ref, gq_ref), (wk_ref, gk_ref), (wv_ref, gv_ref)):
            total = total + jnp.sum(
                weight_ref[rows, :].astype(WIDE) * grad_ref[rows, :], 1, keepdims=True
            )
        flat = flat + lay_flat(total, part)
    grad_gain_ref[...] = jnp.broadcast_to(flat / gain_ref[...].astype(WIDE), (8, 128))


def spread_first(rank, pieces, w_query, w_key, w_value, gain):
    shard = w_query.shape[0]
    return call(
        spread_first_kernel,
        "spread_first",
        [((shard, D), WIDE)] * 4 + [((8, 128), WIDE), ((8, 128), WIDE)],
        [pl.BlockSpec(memory_space=pltpu.SMEM)] + [whole_block()] * 8,
        4 * shard * D,
        8 * 2**20,
        (rank, *pieces, w_query, w_key, w_value, gain),
    )


def on_plane(
    inputs,
    w_query,
    w_key,
    w_value,
    w_output,
    gain_attention,
    w_gate,
    w_up,
    w_down,
    gain_feed,
    variate_bias,
    segment_ids,
    variate_ids,
    positions,
    grad_output,
):
    rank = lax.axis_index("batch")
    rank_row = jnp.reshape(rank, (1,)).astype(jnp.int32)
    micro, tokens = inputs.shape[0], inputs.shape[2]
    n_seq = lax.axis_size("seq")
    shard = w_query.shape[0]
    per = D // 4

    packed, first_shard, gate_up_shard, down_shard = pack(
        rank_row,
        inputs.reshape(micro, tokens, D),
        grad_output.reshape(micro, tokens, D),
        segment_ids.reshape(micro, tokens),
        variate_ids.reshape(micro, tokens),
        positions.reshape(micro, tokens),
        (w_query, w_key, w_value, w_output),
        (gain_attention.reshape(1, shard), gain_feed.reshape(1, shard)),
        w_gate,
        w_up,
        w_down,
    )
    first_weights = lax.all_gather(first_shard, "seq", axis=0, tiled=True)
    gate_up = lax.all_gather(gate_up_shard, "seq", axis=0, tiled=True)
    down = lax.all_gather(down_shard, "seq", axis=0, tiled=True)
    packed = lax.all_to_all(packed, "batch", 0, 0, tiled=True)
    by_sequence = [
        packed[:, kind].reshape(4 * micro, tokens // 4, D + 128)[:, :, : D + 128 - 128 * kind]
        for kind in range(2)
    ]
    out_columns = first_weights[:, 768:D]
    out_got = swap_pairs(out_columns)
    mine, cot_by_sequence, out_got = lax.optimization_barrier(
        (over_seq(by_sequence[0]), by_sequence[1], out_got)
    )
    cot_mine = over_seq(cot_by_sequence)
    freqs = jnp.exp((jnp.arange(128) % 32).astype(WIDE) * (-2.0 * math.log(10000.0) / HD))[None, :]
    my_bias = lax.dynamic_slice_in_dim(variate_bias, rank * 4, 4, 1)
    weights = jnp.pad(head_weights(my_bias[0], my_bias[1]), ((0, 4), (0, 0)))

    chunks = gather_plane(mine)
    out_pieces = far_pairs(
        out_columns, lax.optimization_barrier((out_got, chunks[1], chunks[3]))[0]
    )
    gain, mixed_first, turned, attended, lower, upper, *kept = attend(
        chunks, first_weights, freqs, weights, rank_row
    )
    ready = lax.optimization_barrier((lower, upper, out_pieces[1], out_pieces[3]))
    lower_x, upper_y = swap(ready[0], 1), swap(ready[1], 2)
    lower_far = swap(jnp.concatenate([lower, lower_x], 1), 2)
    upper_far = swap(jnp.concatenate([upper, upper_y], 1), 1)
    cot_got = swap_pairs(lax.optimization_barrier((cot_mine, lower_far, upper_far))[0])
    heads, middle_own, mixed_second = middle(
        rank_row,
        chunks,
        (lower, lower_x, lower_far, upper, upper_y, upper_far),
        out_pieces,
        gain,
    )

    both, hidden = feed(mixed_second, gate_up, after(rank_row, cot_got))
    cots = far_pairs(cot_mine, lax.optimization_barrier((cot_got, mixed_second))[0])
    far_grads, far_lower, far_upper, down_weight_grads = feed_back(
        1, both, cots, gate_up, down, rank_row, hidden
    )
    got = scatter_first((None, far_lower, None, far_upper))
    near_grads, near_lower, near_upper = feed_back(
        0, both, cots, gate_up, down, after(rank_row, far_lower)
    )
    down_grad_shard = lax.psum_scatter(down_weight_grads, "seq", scatter_dimension=0, tiled=True)
    back = (near_lower, None, near_upper, None)
    gate_up_weight_grads = gate_up_grads(
        mixed_second, near_grads, far_grads, after(rank_row, got)
    )
    gate_up_grad_shard = lax.psum_scatter(
        gate_up_weight_grads, "seq", scatter_dimension=0, tiled=True
    )
    sums = scatter_second(back, got)
    grad_middle, *parcels = own_back(
        rank_row, sums, middle_own, cot_mine, gain, out_pieces,
        after(rank_row, gate_up_weight_grads),
    )
    out_chunks = feed_out(hidden, down, after(rank_row, parcels[0]))
    parcels = [parcels[0]] + [swap(parcels[r], r) for r in range(1, 4)]

    far_chunks = lax.optimization_barrier(((out_chunks[1], out_chunks[3]), parcels))[0]
    out_got = scatter_first((None, far_chunks[0], None, far_chunks[1]))
    kept = (turned, attended, *kept)
    proj0, bias0 = attend_back(
        0, parcels, kept, weights, after(rank_row, far_chunks)
    )
    out_got = lax.optimization_barrier((out_got, bias0))[0]
    out_sums = scatter_second(out_chunks, out_got)
    proj1, bias1, *back = attend_back(
        1, parcels, kept, weights, after(rank_row, out_got), proj0, first_weights
    )
    ready = lax.optimization_barrier((back[1], back[3], out_sums[2], out_sums[5]))
    got = scatter_first((None, ready[0], None, ready[1]))
    bias_sums = jnp.sum(jnp.concatenate([bias0[:2], bias1[:2], bias0[2:4], bias1[2:4]], 0), 1)
    bias_parts = jnp.pad(jnp.concatenate(three_parts(bias_sums)), (0, 104))[None, :]
    slots = lax.broadcasted_iota(jnp.int32, (per, 1), 0) % shard == lax.axis_index("seq")
    bias_rows = jnp.where(slots, bias_parts, LOW(0))
    first_weight_grads = first_grads(
        rank_row, mixed_first, proj0, proj1, heads, parcels, bias_rows, rank_row
    )
    got, first_weight_grads = lax.optimization_barrier((got, first_weight_grads))
    first_shard = lax.psum_scatter(first_weight_grads, "seq", scatter_dimension=0, tiled=True)
    sums = scatter_second(back, got)
    last = own_last(
        sums, out_sums, mine, grad_middle, middle_own, gain, n_seq,
        after(rank_row, first_weight_grads),
    )
    moved = lax.all_to_all(last, "seq", 0, 0, tiled=True)
    quarter = tokens // 4
    feed_shard = join(gate_up_grad_shard, down_grad_shard, after(rank_row, first_weight_grads))
    feed_pieces = gather_plane(after(feed_shard, last))
    first_pieces = gather_plane(after(first_shard, feed_pieces))
    moved, first_pieces = lax.optimization_barrier((moved, first_pieces))
    moved = moved.reshape(4, micro, 2 * quarter, D)
    moved = lax.all_to_all(moved, "batch", 0, 0, tiled=True)
    grad_inputs = jnp.transpose(moved[:, :, :quarter].astype(WIDE), (1, 0, 2, 3))
    block_output = jnp.transpose(moved[:, :, quarter:], (1, 0, 2, 3))

    grad_gate, grad_up, grad_down, grad_gain_second = spread_feed(
        rank_row, feed_pieces, w_gate, w_up, gain_feed.reshape(1, shard)
    )
    grad_query, grad_key, grad_value, grad_output_weights, grad_gain_first, bias_table = (
        spread_first(
            rank_row, first_pieces, w_query, w_key, w_value, gain_attention.reshape(1, shard)
        )
    )
    bias_table = jnp.sum(bias_table[:4, :24].reshape(4, 3, 2, 4), 1)
    grad_bias = jnp.transpose(bias_table, (1, 0, 2)).reshape(2, H)
    return (
        block_output.reshape(inputs.shape),
        grad_inputs.reshape(inputs.shape),
        grad_query,
        grad_key,
        grad_value,
        grad_output_weights,
        grad_gain_first[0],
        grad_gate,
        grad_up,
        grad_down,
        grad_gain_second[0],
        grad_bias,
    )


def solution(mesh):
    n_batch, n_seq = mesh.shape["batch"], mesh.shape["seq"]
    step = on_plane if n_batch == 4 and n_seq == 8 else on_device
    return jax.shard_map(
        step,
        mesh=mesh,
        in_specs=(
            P(None, "batch", "seq", None),
            P("seq", None),
            P("seq", None),
            P("seq", None),
            P("seq", None),
            P("seq"),
            P("seq", None),
            P("seq", None),
            P("seq", None),
            P("seq"),
            P(),
            P(None, "batch", "seq"),
            P(None, "batch", "seq"),
            P(None, "batch", "seq"),
            P(None, "batch", "seq", None),
        ),
        out_specs=(
            P(None, "batch", "seq", None),
            P(None, "batch", "seq", None),
            P("seq", None),
            P("seq", None),
            P("seq", None),
            P("seq", None),
            P("seq"),
            P("seq", None),
            P("seq", None),
            P("seq", None),
            P("seq"),
            P(),
        ),
        check_vma=False,
    )
```

```python
import functools
import math

import jax
import jax.numpy as jnp
from jax import lax
from jax.experimental import pallas as pl
from jax.experimental.pallas import tpu as pltpu
from jax.sharding import PartitionSpec as P

D = 1024
H = 16
HD = 64
REACH = 6


EPSILON = 1e-05
SCORE_SCALE = 0.125
MASKED = -1e30


def from_behind(value, axis, by):
    length = lax.axis_size(axis)
    pairs = [(i, i + by) for i in range(length) if 0 <= i + by < length]
    return lax.ppermute(value, axis, pairs)


def step_offset(step):
    distance = step // 2 + 1
    return distance if step % 2 == 0 else -distance


def rotary(values_in, positions_in, turn):
    row_count = values_in.shape[0]
    halfway = HD // 2
    freqs = jnp.exp(jnp.arange(halfway, dtype=jnp.float32) * (-2.0 * math.log(10000.0) / HD))
    angles = positions_in.astype(jnp.float32)[:, None] * freqs[None, :]
    cosine = jnp.cos(angles)[:, None, :]
    sine = turn * jnp.sin(angles)[:, None, :]
    shaped = values_in.reshape(row_count, H, HD)
    first_half = shaped[..., :halfway]
    second_half = shaped[..., halfway:]
    turned = jnp.concatenate(
        [first_half * cosine - second_half * sine, first_half * sine + second_half * cosine], -1
    )
    return turned.reshape(row_count, H * HD)


def head_scores(query_heads, key_heads, query_variates, key_variates, bias_table):
    raw = jnp.einsum("qhd,khd->hqk", query_heads, key_heads, preferred_element_type=jnp.float32)
    same_variate = (query_variates[:, None] == key_variates[None, :])[None]
    return raw * SCORE_SCALE + jnp.where(
        same_variate, bias_table[0][:, None, None], bias_table[1][:, None, None]
    )


def attend_forward(query_rows, own_keys, own_values, own_segments, own_variates, bias_table):
    tok_count = query_rows.shape[0]
    query_heads = query_rows.reshape(tok_count, H, HD)
    shifted_segments = own_segments + 1

    def fold_keys(carried, piece_rows):
        key_part, value_part, segment_part, variate_part = piece_rows
        part_count = key_part.shape[0]
        live = shifted_segments[:, None] == segment_part[None, :]

        def update(state):
            running_max, running_total, running_sum = state
            logits = head_scores(
                query_heads,
                key_part.reshape(part_count, H, HD),
                own_variates,
                variate_part,
                bias_table,
            )
            logits = jnp.where(live[None], logits, MASKED)
            new_max = jnp.maximum(running_max, jnp.max(logits, -1))
            rescale = jnp.exp(running_max - new_max)
            weights = jnp.where(live[None], jnp.exp(logits - new_max[..., None]), 0.0)
            new_total = running_total * rescale + jnp.sum(weights, -1)
            mixed = jnp.einsum(
                "hqk,khd->qhd",
                weights.astype(jnp.bfloat16),
                value_part.reshape(part_count, H, HD),
                preferred_element_type=jnp.float32,
            )
            new_sum = running_sum * jnp.transpose(rescale)[:, :, None] + mixed
            return (new_max, new_total, new_sum)

        return lax.cond(jnp.any(live), update, lambda state: state, carried)

    near_rows = (own_keys, own_values, shifted_segments, own_variates)
    state = (
        jnp.full((H, tok_count), MASKED, jnp.float32),
        jnp.zeros((H, tok_count), jnp.float32),
        jnp.zeros((tok_count, H, HD), jnp.float32),
    )
    state = fold_keys(state, near_rows)
    for step in range(2 * REACH):
        arrived = from_behind(
            (own_keys, own_values, shifted_segments, own_variates), "seq", step_offset(step)
        )
        state = fold_keys(state, arrived)
    final_max, final_total, final_sum = state
    attended = final_sum / jnp.transpose(final_total)[:, :, None]
    log_rows = jnp.transpose(final_max + jnp.log(final_total))
    return (attended.reshape(tok_count, H * HD), log_rows)


def attend_queries_back(
    query_rows,
    grad_rows,
    log_rows,
    delta_rows,
    own_keys,
    own_values,
    own_segments,
    own_variates,
    bias_table,
):
    tok_count = query_rows.shape[0]
    query_heads = query_rows.reshape(tok_count, H, HD)
    grad_heads = grad_rows.reshape(tok_count, H, HD)
    log_heads = jnp.transpose(log_rows)
    delta_heads = jnp.transpose(delta_rows)
    shifted_segments = own_segments + 1

    def fold_keys_back(carried, piece_rows):
        key_part, value_part, segment_part, variate_part = piece_rows
        part_count = key_part.shape[0]
        live = shifted_segments[:, None] == segment_part[None, :]

        def update(state):
            grad_query, grad_bias = state
            key_heads = key_part.reshape(part_count, H, HD)
            logits = head_scores(query_heads, key_heads, own_variates, variate_part, bias_table)
            weights = jnp.where(live[None], jnp.exp(logits - log_heads[..., None]), 0.0)
            grad_weights = jnp.einsum(
                "qhd,khd->hqk",
                grad_heads,
                value_part.reshape(part_count, H, HD),
                preferred_element_type=jnp.float32,
            )
            grad_logits = (weights * (grad_weights - delta_heads[..., None])).astype(jnp.bfloat16)
            grad_query = grad_query + SCORE_SCALE * jnp.einsum(
                "hqk,khd->qhd", grad_logits, key_heads, preferred_element_type=jnp.float32
            )
            same_variate = (own_variates[:, None] == variate_part[None, :])[None]
            logit_values = grad_logits.astype(jnp.float32)
            same_total = jnp.sum(jnp.where(same_variate, logit_values, 0.0), axis=(1, 2))
            other_total = jnp.sum(jnp.where(same_variate, 0.0, logit_values), axis=(1, 2))
            return (grad_query, grad_bias + jnp.stack([same_total, other_total]))

        return lax.cond(jnp.any(live), update, lambda state: state, carried)

    state = (jnp.zeros((tok_count, H, HD), jnp.float32), jnp.zeros((2, H), jnp.float32))
    state = fold_keys_back(state, (own_keys, own_values, shifted_segments, own_variates))
    for step in range(2 * REACH):
        arrived = from_behind(
            (own_keys, own_values, shifted_segments, own_variates), "seq", step_offset(step)
        )
        state = fold_keys_back(state, arrived)
    grad_query, grad_bias = state
    return (grad_query.reshape(tok_count, H * HD), grad_bias)


def attend_keys_back(
    query_rows,
    grad_rows,
    log_rows,
    delta_rows,
    own_keys,
    own_values,
    own_segments,
    own_variates,
    bias_table,
):
    tok_count = own_keys.shape[0]
    key_heads = own_keys.reshape(tok_count, H, HD)
    value_heads = own_values.reshape(tok_count, H, HD)
    shifted_segments = own_segments + 1

    def fold_queries(carried, piece_rows):
        query_part, grad_part, log_part, delta_part, segment_part, variate_part = piece_rows
        part_count = query_part.shape[0]
        live = segment_part[:, None] == shifted_segments[None, :]

        def update(state):
            grad_key, grad_value = state
            query_heads = query_part.reshape(part_count, H, HD)
            grad_heads = grad_part.reshape(part_count, H, HD)
            logits = head_scores(query_heads, key_heads, variate_part, own_variates, bias_table)
            weights = jnp.where(
                live[None], jnp.exp(logits - jnp.transpose(log_part)[..., None]), 0.0
            )
            grad_value = grad_value + jnp.einsum(
                "hqk,qhd->khd",
                weights.astype(jnp.bfloat16),
                grad_heads,
                preferred_element_type=jnp.float32,
            )
            grad_weights = jnp.einsum(
                "qhd,khd->hqk", grad_heads, value_heads, preferred_element_type=jnp.float32
            )
            grad_logits = (weights * (grad_weights - jnp.transpose(delta_part)[..., None])).astype(
                jnp.bfloat16
            )
            grad_key = grad_key + SCORE_SCALE * jnp.einsum(
                "hqk,qhd->khd", grad_logits, query_heads, preferred_element_type=jnp.float32
            )
            return (grad_key, grad_value)

        return lax.cond(jnp.any(live), update, lambda state: state, carried)

    state = (jnp.zeros((tok_count, H, HD), jnp.float32), jnp.zeros((tok_count, H, HD), jnp.float32))
    state = fold_queries(
        state, (query_rows, grad_rows, log_rows, delta_rows, shifted_segments, own_variates)
    )
    for step in range(2 * REACH):
        arrived = (
            from_behind(query_rows, "seq", step_offset(step)),
            from_behind(grad_rows, "seq", step_offset(step)),
            from_behind(log_rows.astype(jnp.bfloat16), "seq", step_offset(step)).astype(
                log_rows.dtype
            ),
            from_behind(delta_rows.astype(jnp.bfloat16), "seq", step_offset(step)).astype(
                delta_rows.dtype
            ),
            from_behind(shifted_segments, "seq", step_offset(step)),
            from_behind(own_variates, "seq", step_offset(step)),
        )
        state = fold_queries(state, arrived)
    grad_key, grad_value = state
    return (grad_key.reshape(tok_count, H * HD), grad_value.reshape(tok_count, H * HD))


def norm_back(grad_normed, normed, scale_rows):
    return scale_rows * (grad_normed - normed * jnp.mean(grad_normed * normed, -1, keepdims=True))


def on_device(
    inputs,
    w_query,
    w_key,
    w_value,
    w_output,
    gain_attention,
    w_gate,
    w_up,
    w_down,
    gain_feed,
    variate_bias,
    segment_ids,
    variate_ids,
    positions,
    grad_output,
):
    micro_count = inputs.shape[0]
    tok_count = inputs.shape[2]
    row_count = micro_count * tok_count
    residual_in = inputs.reshape(row_count, D).astype(jnp.float32)
    cotangent = grad_output.reshape(row_count, D).astype(jnp.float32)
    segment_rows = segment_ids.reshape(micro_count, tok_count)
    variate_rows = variate_ids.reshape(micro_count, tok_count)
    position_rows = positions.reshape(row_count)
    full_query, full_key, full_value, full_output, full_gain_first = (
        lax.all_gather(w_query, "seq", axis=0, tiled=True),
        lax.all_gather(w_key, "seq", axis=0, tiled=True),
        lax.all_gather(w_value, "seq", axis=0, tiled=True),
        lax.all_gather(w_output, "seq", axis=0, tiled=True),
        lax.all_gather(gain_attention, "seq", axis=0, tiled=True),
    )
    full_gate, full_up, full_down, full_gain_second = (
        lax.all_gather(w_gate, "seq", axis=0, tiled=True),
        lax.all_gather(w_up, "seq", axis=0, tiled=True),
        lax.all_gather(w_down, "seq", axis=0, tiled=True),
        lax.all_gather(gain_feed, "seq", axis=0, tiled=True),
    )
    scale_first = lax.rsqrt(jnp.mean(residual_in * residual_in, -1, keepdims=True) + EPSILON)
    normed_first = residual_in * scale_first
    mixed_first = (normed_first * full_gain_first.astype(jnp.float32)).astype(jnp.bfloat16)
    query_proj = jnp.dot(mixed_first, full_query, preferred_element_type=jnp.float32)
    key_proj = jnp.dot(mixed_first, full_key, preferred_element_type=jnp.float32)
    value_proj = jnp.dot(mixed_first, full_value, preferred_element_type=jnp.float32)
    query_rows = rotary(query_proj, position_rows, 1.0).astype(jnp.bfloat16)
    key_rows = rotary(key_proj, position_rows, 1.0).astype(jnp.bfloat16)
    value_rows = value_proj.astype(jnp.bfloat16)
    attended_parts = []
    log_parts = []
    for micro_index in range(micro_count):
        lower_row = micro_index * tok_count
        upper_row = lower_row + tok_count
        attended_part, log_part = attend_forward(
            query_rows[lower_row:upper_row],
            key_rows[lower_row:upper_row],
            value_rows[lower_row:upper_row],
            segment_rows[micro_index],
            variate_rows[micro_index],
            variate_bias,
        )
        attended_parts.append(attended_part)
        log_parts.append(log_part)
    attended_all = jnp.concatenate(attended_parts, 0)
    attended_low = attended_all.astype(jnp.bfloat16)
    middle = residual_in + jnp.dot(attended_low, full_output, preferred_element_type=jnp.float32)
    scale_second = lax.rsqrt(jnp.mean(middle * middle, -1, keepdims=True) + EPSILON)
    normed_second = middle * scale_second
    mixed_second = (normed_second * full_gain_second.astype(jnp.float32)).astype(jnp.bfloat16)
    gate_proj = jnp.dot(mixed_second, full_gate, preferred_element_type=jnp.float32)
    up_proj = jnp.dot(mixed_second, full_up, preferred_element_type=jnp.float32)
    sigmoid_gate = jax.nn.sigmoid(gate_proj)
    silu_gate = gate_proj * sigmoid_gate
    hidden_rows = (silu_gate * up_proj).astype(jnp.bfloat16)
    block_rows = middle + jnp.dot(hidden_rows, full_down, preferred_element_type=jnp.float32)
    block_output = block_rows.astype(jnp.bfloat16).reshape(inputs.shape)
    full_query, full_key, full_value, full_output, full_gain_first = (
        lax.all_gather(w_query, "seq", axis=0, tiled=True),
        lax.all_gather(w_key, "seq", axis=0, tiled=True),
        lax.all_gather(w_value, "seq", axis=0, tiled=True),
        lax.all_gather(w_output, "seq", axis=0, tiled=True),
        lax.all_gather(gain_attention, "seq", axis=0, tiled=True),
    )
    full_gate, full_up, full_down, full_gain_second = (
        lax.all_gather(w_gate, "seq", axis=0, tiled=True),
        lax.all_gather(w_up, "seq", axis=0, tiled=True),
        lax.all_gather(w_down, "seq", axis=0, tiled=True),
        lax.all_gather(gain_feed, "seq", axis=0, tiled=True),
    )
    grad_branch_second = cotangent.astype(jnp.bfloat16)
    grad_down = jnp.einsum(
        "rf,rd->fd", hidden_rows, grad_branch_second, preferred_element_type=jnp.float32
    )
    grad_hidden = jnp.einsum(
        "rd,fd->rf", grad_branch_second, full_down, preferred_element_type=jnp.float32
    )
    silu_slope = sigmoid_gate * (1.0 + gate_proj * (1.0 - sigmoid_gate))
    grad_gate_rows = (grad_hidden * up_proj * silu_slope).astype(jnp.bfloat16)
    grad_up_rows = (grad_hidden * silu_gate).astype(jnp.bfloat16)
    grad_gate = jnp.einsum(
        "rd,rf->df", mixed_second, grad_gate_rows, preferred_element_type=jnp.float32
    )
    grad_up = jnp.einsum(
        "rd,rf->df", mixed_second, grad_up_rows, preferred_element_type=jnp.float32
    )
    grad_mixed_second = jnp.einsum(
        "rf,df->rd", grad_gate_rows, full_gate, preferred_element_type=jnp.float32
    ) + jnp.einsum("rf,df->rd", grad_up_rows, full_up, preferred_element_type=jnp.float32)
    grad_gain_second = jnp.sum(grad_mixed_second * normed_second, 0)
    grad_middle = cotangent + norm_back(
        grad_mixed_second * full_gain_second.astype(jnp.float32), normed_second, scale_second
    )
    grad_branch_first = grad_middle.astype(jnp.bfloat16)
    grad_out_proj = jnp.einsum(
        "rd,re->de", attended_low, grad_branch_first, preferred_element_type=jnp.float32
    )
    grad_attended = jnp.einsum(
        "re,de->rd", grad_branch_first, full_output, preferred_element_type=jnp.float32
    ).astype(jnp.bfloat16)
    delta_all = jnp.einsum(
        "rhd,rhd->rh",
        grad_attended.astype(jnp.float32).reshape(row_count, H, HD),
        attended_all.reshape(row_count, H, HD),
    )
    grad_bias_local = jnp.zeros((2, H), jnp.float32)
    query_grad_parts = []
    key_grad_parts = []
    value_grad_parts = []
    for micro_index in range(micro_count):
        lower_row = micro_index * tok_count
        upper_row = lower_row + tok_count
        query_grad_part, bias_part = attend_queries_back(
            query_rows[lower_row:upper_row],
            grad_attended[lower_row:upper_row],
            log_parts[micro_index],
            delta_all[lower_row:upper_row],
            key_rows[lower_row:upper_row],
            value_rows[lower_row:upper_row],
            segment_rows[micro_index],
            variate_rows[micro_index],
            variate_bias,
        )
        key_grad_part, value_grad_part = attend_keys_back(
            query_rows[lower_row:upper_row],
            grad_attended[lower_row:upper_row],
            log_parts[micro_index],
            delta_all[lower_row:upper_row],
            key_rows[lower_row:upper_row],
            value_rows[lower_row:upper_row],
            segment_rows[micro_index],
            variate_rows[micro_index],
            variate_bias,
        )
        grad_bias_local = grad_bias_local + bias_part
        query_grad_parts.append(query_grad_part)
        key_grad_parts.append(key_grad_part)
        value_grad_parts.append(value_grad_part)
    grad_query_rows = rotary(jnp.concatenate(query_grad_parts, 0), position_rows, -1.0).astype(
        jnp.bfloat16
    )
    grad_key_rows = rotary(jnp.concatenate(key_grad_parts, 0), position_rows, -1.0).astype(
        jnp.bfloat16
    )
    grad_value_rows = jnp.concatenate(value_grad_parts, 0).astype(jnp.bfloat16)
    grad_query = jnp.einsum(
        "rd,re->de", mixed_first, grad_query_rows, preferred_element_type=jnp.float32
    )
    grad_key = jnp.einsum(
        "rd,re->de", mixed_first, grad_key_rows, preferred_element_type=jnp.float32
    )
    grad_value = jnp.einsum(
        "rd,re->de", mixed_first, grad_value_rows, preferred_element_type=jnp.float32
    )
    grad_mixed_first = (
        jnp.einsum("re,de->rd", grad_query_rows, full_query, preferred_element_type=jnp.float32)
        + jnp.einsum("re,de->rd", grad_key_rows, full_key, preferred_element_type=jnp.float32)
        + jnp.einsum("re,de->rd", grad_value_rows, full_value, preferred_element_type=jnp.float32)
    )
    grad_gain_first = jnp.sum(grad_mixed_first * normed_first, 0)
    grad_input_rows = grad_middle + norm_back(
        grad_mixed_first * full_gain_first.astype(jnp.float32), normed_first, scale_first
    )
    grad_inputs = grad_input_rows.reshape(inputs.shape)
    (
        shard_query,
        shard_key,
        shard_value,
        shard_output,
        shard_gain_first,
        shard_gate,
        shard_up,
        shard_down,
        shard_gain_second,
    ) = (
        lax.psum_scatter(grad_query, "seq", scatter_dimension=0, tiled=True),
        lax.psum_scatter(grad_key, "seq", scatter_dimension=0, tiled=True),
        lax.psum_scatter(grad_value, "seq", scatter_dimension=0, tiled=True),
        lax.psum_scatter(grad_out_proj, "seq", scatter_dimension=0, tiled=True),
        lax.psum_scatter(grad_gain_first, "seq", scatter_dimension=0, tiled=True),
        lax.psum_scatter(grad_gate, "seq", scatter_dimension=0, tiled=True),
        lax.psum_scatter(grad_up, "seq", scatter_dimension=0, tiled=True),
        lax.psum_scatter(grad_down, "seq", scatter_dimension=0, tiled=True),
        lax.psum_scatter(grad_gain_second, "seq", scatter_dimension=0, tiled=True),
    )
    summed = (
        lax.psum(shard_query.astype(jnp.bfloat16), "batch").astype(jnp.float32),
        lax.psum(shard_key.astype(jnp.bfloat16), "batch").astype(jnp.float32),
        lax.psum(shard_value.astype(jnp.bfloat16), "batch").astype(jnp.float32),
        lax.psum(shard_output.astype(jnp.bfloat16), "batch").astype(jnp.float32),
        lax.psum(shard_gain_first.astype(jnp.bfloat16), "batch").astype(jnp.float32),
        lax.psum(shard_gate.astype(jnp.bfloat16), "batch").astype(jnp.float32),
        lax.psum(shard_up.astype(jnp.bfloat16), "batch").astype(jnp.float32),
        lax.psum(shard_down.astype(jnp.bfloat16), "batch").astype(jnp.float32),
        lax.psum(shard_gain_second.astype(jnp.bfloat16), "batch").astype(jnp.float32),
    )
    grad_bias_total = lax.psum(grad_bias_local, ("batch", "seq"))
    return (
        block_output,
        grad_inputs,
        summed[0],
        summed[1],
        summed[2],
        summed[3],
        summed[4],
        summed[5],
        summed[6],
        summed[7],
        summed[8],
        grad_bias_total,
    )


ORDER_A = (0, 1, 2, 3)
ORDER_B = (0, 2, 1, 3)
FEATURES = 128
LSE_AT = 64
LOW = jnp.bfloat16
WIDE = jnp.float32


def swap(value, bit):
    return lax.ppermute(value, "batch", [(i, i ^ bit) for i in range(4)])


def after(value, *others):
    return lax.optimization_barrier((value, *others))[0]


def gather_plane(own):
    half = own.shape[0] // 2
    lower, upper = own[:half], own[half:]
    lower_pair = jnp.concatenate([lower, swap(lower, 1)], 0)
    upper_pair = jnp.concatenate([upper, swap(upper, 2)], 0)
    return lower_pair, swap(lower_pair, 2), upper_pair, swap(upper_pair, 1)


def scatter_first(chunks):
    return swap(chunks[1], 2), swap(chunks[3], 1)


def scatter_second(chunks, got):
    near_lower, _, near_upper, _ = chunks
    got_lower, got_upper = got
    half = near_lower.shape[0] // 2
    last_lower = swap(near_lower[half:] + got_lower[half:], 1)
    last_upper = swap(near_upper[half:] + got_upper[half:], 2)
    return (near_lower, got_lower, last_lower, near_upper, got_upper, last_upper)


def swap_pairs(own):
    half = own.shape[0] // 2
    return swap(own[:half], 1), swap(own[half:], 2)


def far_pairs(own, got):
    half = own.shape[0] // 2
    lower_pair = jnp.concatenate([own[:half], got[0]], 0)
    upper_pair = jnp.concatenate([own[half:], got[1]], 0)
    return lower_pair, swap(lower_pair, 2), upper_pair, swap(upper_pair, 1)


def over_seq(pieces):
    count, quarter, width = pieces.shape
    return lax.all_to_all(pieces, "seq", 0, 0, tiled=True).reshape(count * quarter, width)


def three_parts(value):
    high = value.astype(LOW)
    rest = value - high.astype(WIDE)
    middle = rest.astype(LOW)
    low = (rest - middle.astype(WIDE)).astype(LOW)
    return high, middle, low


def token_features(segments, variates):
    lane = lax.broadcasted_iota(jnp.int32, (segments.shape[0], FEATURES), 1)
    variate_hot = (lane < 12) & (lane % 4 == variates)
    ones = (lane >= 12) & (lane < 15)
    segment_lane = (lane >= 16) & (lane < LSE_AT)
    segment_hot = segment_lane & (lane - 16 == segments)
    segment_cold = segment_lane & (lane - 16 != segments)
    query_side = variate_hot | ones | segment_hot
    key_side = variate_hot | ones | segment_cold | ((lane >= LSE_AT) & (lane < LSE_AT + 3))
    return jnp.where(query_side, 1.0, 0.0).astype(LOW), jnp.where(key_side, 1.0, 0.0).astype(LOW)


def head_weights(same_bias, other_bias):
    gap = [part[:, None] for part in three_parts(same_bias - other_bias)]
    base = [part[:, None] for part in three_parts(other_bias)]
    heads = same_bias.shape[0]
    columns = [jnp.broadcast_to(part, (heads, 4)) for part in gap] + base
    columns.append(jnp.zeros((heads, 1), LOW))
    columns.append(jnp.full((heads, LSE_AT - 16), MASKED, LOW))
    columns.append(jnp.zeros((heads, FEATURES - LSE_AT), LOW))
    return jnp.concatenate(columns, 1)


def turn_pair(pair, cosine, sine):
    lane = lax.broadcasted_iota(jnp.int32, pair.shape, 1)
    crossed = jnp.where(lane % 64 < 32, pltpu.roll(pair, 96, 1), pltpu.roll(pair, 32, 1))
    return pair * cosine + crossed * sine


def dot_plain(left, right):
    return jnp.dot(left, right, preferred_element_type=WIDE)


def dot_rows(left, right):
    return lax.dot_general(left, right, (((1,), (1,)), ((), ())), preferred_element_type=WIDE)


def dot_first(left, right):
    return lax.dot_general(left, right, (((0,), (0,)), ((), ())), preferred_element_type=WIDE)


def whole_block():
    return pl.BlockSpec(memory_space=pltpu.VMEM)


def call(kernel, name, outs, specs, flops, moved, args, scratch=()):
    return pl.pallas_call(
        kernel,
        grid=(1,),
        out_shape=[jax.ShapeDtypeStruct(shape, dtype) for shape, dtype in outs],
        in_specs=specs,
        out_specs=[pl.BlockSpec(memory_space=pltpu.VMEM) for _ in outs],
        scratch_shapes=list(scratch),
        cost_estimate=pl.CostEstimate(flops=flops, bytes_accessed=moved, transcendentals=0),
        compiler_params=pltpu.CompilerParams(vmem_limit_bytes=56 * 2**20),
        name=name,
    )(*args)


class Copies:
    def __init__(self, ref, pairs, sems):
        self.ref = ref
        self.copies = [
            pltpu.make_async_copy(source, target, sems.at[k])
            for k, (source, target) in enumerate(pairs)
        ]
        self.started = self.waited = False

    def start(self, *which):
        self.started = True
        for k in which or range(len(self.copies)):
            self.copies[k].start()

    def wait(self):
        if not self.waited:
            for copy in self.copies:
                copy.wait()
        self.waited = True
        return self.ref

    def _at(self, index, act):
        for k, copy in enumerate(self.copies):
            pl.when(index == k)(functools.partial(act, copy))

    def start_at(self, index):
        self.started = True
        self._at(index, lambda copy: copy.start())

    def wait_at(self, index):
        self.waited = True
        self._at(index, lambda copy: copy.wait())

    def wait_first(self, index):
        if not self.waited:
            self.waited = True

            @pl.when(index == 0)
            def _():
                for copy in self.copies:
                    copy.wait()

        return self.ref


class Plan:
    def __init__(self, arrays, shape, pairs, count):
        self.arrays, self.shape, self.pairs, self.count = arrays, shape, pairs, count


def whole(array, column=None, width=None):
    shape = array.shape if column is None else (array.shape[0], width)

    def pairs(refs, buffer):
        if column is None:
            return [(refs[0], buffer)]
        return [(refs[0].at[:, pl.ds(column, width)], buffer)]

    return Plan([array], shape, pairs, 1)


def top(array):
    half = array.shape[0] // 2
    return Plan(
        [array],
        (half, *array.shape[1:]),
        lambda refs, buffer: [(refs[0].at[pl.ds(0, half)], buffer)],
        1,
    )


def rows_of(array, count=4):
    size = array.shape[0] // count
    return Plan(
        [array],
        (count, size, array.shape[1]),
        lambda refs, buffer: [
            (refs[0].at[pl.ds(k * size, size)], buffer.at[k]) for k in range(count)
        ],
        count,
    )


def columns_of(array, count=4, column=0, width=None):
    size = (width or array.shape[1]) // count
    return Plan(
        [array],
        (count, array.shape[0], size),
        lambda refs, buffer: [
            (refs[0].at[:, pl.ds(column + k * size, size)], buffer.at[k]) for k in range(count)
        ],
        count,
    )


def group(arrays, column=None, width=None):
    rows = arrays[0].shape[0]

    def pairs(refs, buffer):
        if column is None:
            return [(ref, buffer.at[k]) for k, ref in enumerate(refs)]
        return [(ref.at[:, pl.ds(column, width)], buffer.at[k]) for k, ref in enumerate(refs)]

    return Plan(
        list(arrays), (len(arrays), rows, width or arrays[0].shape[1]), pairs, len(arrays)
    )


def out_rows(shape, dtype, count=4):
    size = shape[0] // count

    def pairs(refs, buffer):
        return [(buffer.at[k], refs[0].at[pl.ds(k * size, size)]) for k in range(count)]

    return Plan([(shape, dtype)], (count, size, *shape[1:]), pairs, count)


def out_group(shape, dtype, count=4):
    def pairs(refs, buffer):
        return [(buffer.at[k], ref) for k, ref in enumerate(refs)]

    return Plan([(shape, dtype)] * count, (count, *shape), pairs, count)


def out_whole(shape, dtype):
    return Plan([(shape, dtype)], shape, lambda refs, buffer: [(buffer, refs[0])], 1)


def run(body, name, us, ins, outs, scratch=(), token=None):
    args, in_specs, out_shapes, out_specs, buffers = [], [], [], [], []
    named = len(ins)
    if token is not None:
        ins = [*ins, token]
    for item in ins:
        if isinstance(item, Plan):
            args += item.arrays
            in_specs += [pl.BlockSpec(memory_space=pl.ANY)] * len(item.arrays)
            buffers.append(pltpu.VMEM(item.shape, item.arrays[0].dtype))
            buffers.append(pltpu.SemaphoreType.DMA((item.count,)))
        else:
            args.append(item)
            space = pltpu.SMEM if item.shape == (1,) else pltpu.VMEM
            in_specs.append(pl.BlockSpec(memory_space=space))
    for item in outs:
        if isinstance(item, Plan):
            out_shapes += [jax.ShapeDtypeStruct(*each) for each in item.arrays]
            out_specs += [pl.BlockSpec(memory_space=pl.ANY)] * len(item.arrays)
            buffers.append(pltpu.VMEM(item.shape, item.arrays[0][1]))
            buffers.append(pltpu.SemaphoreType.DMA((item.count,)))
        else:
            out_shapes.append(jax.ShapeDtypeStruct(*item))
            out_specs.append(pl.BlockSpec(memory_space=pltpu.VMEM))
    n_in, n_out = len(args), len(out_shapes)

    def kernel(*refs):
        given, rest = list(refs[: n_in + n_out]), list(refs[n_in + n_out :])
        bound = []
        for item in (*ins, *outs):
            if isinstance(item, Plan):
                near = [given.pop(0) for _ in item.arrays]
                buffer, sems = rest.pop(0), rest.pop(0)
                bound.append(Copies(buffer, item.pairs(near, buffer), sems))
            else:
                bound.append(given.pop(0))
        body(*bound[:named], *bound[len(ins) :], *rest)
        for item in bound[: len(ins)]:
            if isinstance(item, Copies):
                item.wait()
        for item in bound[len(ins) :]:
            if isinstance(item, Copies) and not item.started:
                item.start()
        for item in bound[len(ins) :]:
            if isinstance(item, Copies):
                item.wait()

    return pl.pallas_call(
        kernel,
        out_shape=out_shapes,
        in_specs=in_specs,
        out_specs=out_specs,
        scratch_shapes=buffers + list(scratch),
        cost_estimate=pl.CostEstimate(
            flops=int(us * 1.15e9), bytes_accessed=2**20, transcendentals=0
        ),
        compiler_params=pltpu.CompilerParams(vmem_limit_bytes=60 * 2**20),
        name=name,
    )(*args)


def output_weights(pieces):
    rows = pieces[0].shape[0] // 2
    places = {
        0: ((0, 0), (0, 1), (1, 0), (1, 1)),
        1: ((2, 0), (3, 0), (2, 1), (3, 1)),
    }

    def pairs(refs, buffer):
        rank = lax.axis_index("batch")
        out = []
        for half in range(2):
            for r, (which, part) in enumerate(places[half]):
                to = pl.ds(pl.multiple_of((rank ^ r) * 256, 256), 256)
                out.append(
                    (
                        refs[which].at[pl.ds(part * rows, rows)],
                        buffer.at[pl.ds(half * rows, rows), to],
                    )
                )
        return out

    return Plan(list(pieces), (2 * rows, D), pairs, 8)


def start_all(*items):
    for item in items:
        item.start()


def unit_rows(rows):
    return lax.rsqrt(jnp.mean(rows * rows, -1, keepdims=True) + EPSILON)


def pack_body(
    rank_ref, x, cot, segment_ref, variate_ref, position_ref, wq, wk, wv, wo, gain_first_ref,
    gain_second_ref, gate, up, down, rows_out, shard_out, gate_up_out, down_out,
):
    start_all(wq, wk, wv, wo, x, cot, gate, up, down)
    micro, _, quarter, _ = x.ref.shape
    tokens = 4 * quarter
    lane = lax.broadcasted_iota(jnp.int32, (tokens, 128), 1)
    on_line = lax.broadcasted_iota(jnp.int32, (tokens, 128), 0) == lane

    def upright(row):
        return jnp.sum(jnp.where(on_line, row, 0.0), 1, keepdims=True)

    gains = jnp.where(
        lane == 0,
        upright(gain_first_ref[...].astype(WIDE)),
        jnp.where(lane == 1, upright(gain_second_ref[...].astype(WIDE)), 0.0),
    )
    shard_out.ref[:, D:] = gains.astype(LOW)
    for place, weight in enumerate((wq, wk, wv, wo)):
        shard_out.ref[:, 256 * place : 256 * (place + 1)] = weight.wait()[...]
    shard_out.start()
    for m in range(micro):
        places = position_ref[m : m + 1, :]
        numbers = jnp.zeros((tokens, 128), WIDE)
        for place, row in enumerate(
            (
                segment_ref[m : m + 1, :],
                variate_ref[m : m + 1, :],
                lax.shift_right_logical(places, 5),
                places & 31,
            )
        ):
            numbers = jnp.where(lane == place, upright(row.astype(WIDE)), numbers)
        numbers = numbers.astype(LOW)
        for r in range(4):
            rows_out.ref[r, 0, m, :, D:] = numbers[r * quarter : (r + 1) * quarter, :]
            rows_out.ref[r, 1, m, :, D:] = jnp.zeros((quarter, 128), LOW)
    x_ref, cot_ref = x.wait(), cot.wait()
    for m in range(micro):
        for r in range(4):
            rows_out.ref[r, 0, m, :, :D] = x_ref[m, r]
            rows_out.ref[r, 1, m, :, :D] = cot_ref[m, r]
    rows_out.start()
    gate_ref, up_ref = gate.wait(), up.wait()
    per = gate_up_out.ref.shape[1] // 2
    piece = gate_ref.shape[2]
    for s in range(per // piece):
        gate_up_out.ref[:, s * piece : (s + 1) * piece] = gate_ref[s]
        gate_up_out.ref[:, per + s * piece : per + (s + 1) * piece] = up_ref[s]
    gate_up_out.start()
    down_out.ref[...] = down.wait()[...]


def pack(rank, x, cot, segments, variates, positions, shards, gains, w_gate, w_up, w_down):
    micro, tokens, _ = x.shape
    quarter = tokens // 4
    shard, ff = w_gate.shape
    piece = w_down.shape[0] // 4
    pieces = ff // 4 // piece

    def quarters(array):
        return array.reshape(micro, 4, quarter, D)

    def mine(array, size, refs_at):
        return Plan([array], size, refs_at, 1)

    def rank_columns(array):
        def pairs(refs, buffer):
            at = pl.multiple_of(lax.axis_index("batch") * 256, 256)
            return [(refs[0].at[:, pl.ds(at, 256)], buffer)]

        return Plan([array], (shard, 256), pairs, 1)

    def feed_columns(array):
        def pairs(refs, buffer):
            rank = lax.axis_index("batch")
            return [
                (refs[0].at[:, pl.ds(pl.multiple_of((4 * s + rank) * piece, piece), piece)], buffer.at[s])
                for s in range(pieces)
            ]

        return Plan([array], (pieces, shard, piece), pairs, pieces)

    def down_rows(array):
        def pairs(refs, buffer):
            at = pl.multiple_of(lax.axis_index("batch") * piece, piece)
            return [(refs[0].at[pl.ds(at, piece)], buffer)]

        return Plan([array], (piece, D), pairs, 1)

    return run(
        pack_body,
        "pack",
        4,
        [rank, whole(quarters(x)), whole(quarters(cot)), segments, variates, positions]
        + [rank_columns(weight) for weight in shards]
        + [*gains, feed_columns(w_gate), feed_columns(w_up), down_rows(w_down)],
        [
            out_whole((4, 2, micro, quarter, D + 128), LOW),
            out_whole((shard, D + 128), LOW),
            out_whole((shard, ff // 2), LOW),
            out_whole((piece, D), LOW),
        ],
    )


def attend_body(
    x, qkv, gains, freqs_ref, weights_ref,
    gain_ref, mixed, turned, wide, lower, upper, logs, cos, sin, query_sides, key_sides,
    keys_ref, values_ref, trig_ref,
):
    start_all(x, gains, qkv)
    count, chunk, _ = x.ref.shape
    lane = lax.broadcasted_iota(jnp.int32, (chunk, 128), 1)
    half_lane = lane // 64
    pick = lax.broadcasted_iota(jnp.int32, (16, 128), 0) == lax.broadcasted_iota(
        jnp.int32, (16, 128), 1
    )
    x_ref = x.wait()
    angles = jnp.zeros((chunk, 128), WIDE)
    for k in range(count):
        numbers = x_ref[k, :, D : D + 128].astype(WIDE)
        places = numbers[:, 2:3] * 32.0 + numbers[:, 3:4]
        angles = jnp.where(lane // 32 == k, places * freqs_ref[...], angles)
    trig_ref[0] = jnp.cos(angles)
    trig_ref[1] = jnp.sin(angles)
    gain_ref[...] = dot_rows(jnp.where(pick, 1.0, 0.0).astype(LOW), gains.wait()[...])
    qkv_ref = qkv.wait()

    def one_chunk(index, carry):
        rows = x_ref[index, :, :D].astype(WIDE)
        mixed_rows = (rows * unit_rows(rows) * gain_ref[0:1, :]).astype(LOW)
        mixed.ref[index] = mixed_rows

        def spread(packed):
            own = jnp.where(lane // 32 == index, packed, 0.0)
            own = own + pltpu.roll(own, 64, 1)
            return own + pltpu.roll(own, 32, 1)

        cosine = spread(trig_ref[0])
        sine = spread(trig_ref[1])
        sine = jnp.where(lane % 64 < 32, -sine, sine)
        cos.ref[index] = cosine
        sin.ref[index] = sine
        numbers = x_ref[index, :, D : D + 128].astype(WIDE).astype(jnp.int32)
        query_side, key_side = token_features(numbers[:, 0:1], numbers[:, 1:2])
        query_sides.ref[index] = query_side
        key_sides.ref[index] = key_side
        proj = dot_plain(mixed_rows, qkv_ref[...])
        values = proj[:, 512:].astype(LOW)
        turned.ref[index, :, 512:768] = values
        for pair in range(2):
            at = 128 * pair
            turned.ref[index, :, at : at + 128] = turn_pair(
                proj[:, at : at + 128], cosine, sine
            ).astype(LOW)
            keys = turn_pair(proj[:, 256 + at : 384 + at], cosine, sine).astype(LOW)
            turned.ref[index, :, 256 + at : 384 + at] = keys
            here = pl.ds(pl.multiple_of(index * chunk, chunk), chunk)
            keys_ref[pair, here, :128] = keys
            keys_ref[pair, here, 128:] = key_side
            values_ref[pair, here, :128] = values[:, at : at + 128]
            values_ref[pair, here, 128:] = jnp.where(lane == 0, 1.0, 0.0).astype(LOW)
        return carry

    lax.fori_loop(0, count, one_chunk, 0)
    start_all(mixed, turned, cos, sin, query_sides, key_sides)

    def one_block(index, carry):
        side = query_sides.ref[index]
        log_rows = jnp.zeros((chunk, 128), WIDE)
        here = pl.ds(pl.multiple_of((index % 2) * chunk, chunk), chunk)
        def scores_of(head):
            at = 128 * (head // 2)
            scaled = turned.ref[index, :, at : at + 128] * LOW(SCORE_SCALE)
            query = jnp.concatenate(
                [
                    jnp.where(half_lane == head % 2, scaled, LOW(0)),
                    side * weights_ref[head : head + 1, :],
                ],
                1,
            )
            return dot_rows(query, keys_ref[head // 2])

        scores = scores_of(0)
        parts = []
        for head in range(4):
            high = jnp.max(scores, 1, keepdims=True)
            powers = jnp.exp(scores - high).astype(LOW)
            if head < 3:
                scores = scores_of(head + 1)
            summed = dot_plain(powers, values_ref[head // 2])
            total = summed[:, 128:129]
            parts.append(summed[:, :128] / total)
            log_rows = jnp.where(lane == head, high + jnp.log(total), log_rows)
        for pair in range(2):
            at = 128 * pair
            total_mixed = jnp.where(half_lane == 0, parts[2 * pair], parts[2 * pair + 1])
            wide.ref[index, :, at : at + 128] = total_mixed
            low_rows = total_mixed.astype(LOW)

            @pl.when(index < 2)
            def _(low_rows=low_rows, at=at):
                lower.ref[here, at : at + 128] = low_rows

            @pl.when(index >= 2)
            def _(low_rows=low_rows, at=at):
                upper.ref[here, at : at + 128] = low_rows

        logs.ref[index] = log_rows
        return carry

    lax.fori_loop(0, count, one_block, 0)


def attend(chunks, first_weights, freqs, weights, token):
    chunk = chunks[0].shape[0]
    length = 4 * chunk
    return run(
        attend_body,
        "attend",
        15,
        [
            group(chunks),
            whole(first_weights, 0, 768),
            whole(first_weights, D, 128),
            freqs,
            weights,
        ],
        [
            ((16, D), WIDE),
            out_rows((length, D), LOW),
            out_rows((length, 768), LOW),
            out_rows((length, 256), WIDE),
            out_whole((length // 2, 256), LOW),
            out_whole((length // 2, 256), LOW),
            out_rows((length, 128), WIDE),
            out_rows((length, 128), WIDE),
            out_rows((length, 128), WIDE),
            out_rows((length, FEATURES), LOW),
            out_rows((length, FEATURES), LOW),
        ],
        [pltpu.VMEM((2, length, 256), LOW)] * 2 + [pltpu.VMEM((2, chunk, 128), WIDE)],
        token,
    )


def middle_body(rank_ref, x, near, far, wo, gain_ref, heads, own, mixed):
    rank = rank_ref[0]
    start_all(near, far, wo, x)
    count, chunk, _ = x.ref.shape
    block = chunk // 2
    near_ref, far_ref = near.wait(), far.wait()
    width = near_ref.shape[2]
    sources = {
        0: ((near_ref, 0, 0), (near_ref, 2, 0), (far_ref, 0, 0), (far_ref, 0, width)),
        1: ((near_ref, 1, 0), (far_ref, 1, 0), (near_ref, 3, 0), (far_ref, 1, width)),
    }
    for half, order in enumerate((ORDER_A, ORDER_B)):
        for q in range(4):
            ref, which, column = sources[half][q]
            for place, r in enumerate(order):
                start = order.index(r ^ q) * block
                heads.ref[
                    2 * half + place // 2,
                    place % 2 * block : (place % 2 + 1) * block,
                    q * width : (q + 1) * width,
                ] = ref[which, start : start + block, column : column + width]
    heads.start()
    wo_ref = wo.wait()

    def one_chunk(index, carry):
        x.wait_at(index)
        total = x.ref[index, :, :D].astype(WIDE)
        for q in range(4):
            rows = pl.ds(pl.multiple_of((rank ^ q) * width, width), width)
            total = total + dot_plain(
                heads.ref[index, :, q * width : (q + 1) * width], wo_ref[rows, :]
            )

        @pl.when(index % 2 == 0)
        def _():
            own.ref[index // 2] = total[:block]
            own.start_at(index // 2)

        mixed.ref[index] = (total * unit_rows(total) * gain_ref[1:2, :]).astype(LOW)
        mixed.start_at(index)
        return carry

    lax.fori_loop(0, count, one_chunk, 0)


def middle(rank, chunks, heads, out_pieces, gain):
    chunk = chunks[0].shape[0]
    length = 4 * chunk
    lower, lower_x, lower_far, upper, upper_y, upper_far = heads
    return run(
        middle_body,
        "middle",
        7,
        [
            rank,
            group(chunks),
            group((lower, upper, lower_x, upper_y)),
            group((lower_far, upper_far)),
            output_weights(out_pieces),
            gain,
        ],
        [out_rows((length, D), LOW), out_rows((chunk, D), WIDE, 2), out_rows((length, D), LOW)],
    )


def feed_body(mixed, gate_up, both, hidden):
    count, _, per = hidden.ref.shape
    mixed.start(0)
    gate_up.start(0, 2)
    mixed.start(1, 2, 3)
    gate_up.start(1, 3)
    for half in range(2):
        here = slice(half * per // 2, (half + 1) * per // 2)
        there = slice(per + half * per // 2, per + (half + 1) * per // 2)

        def one_chunk(index, carry, half=half, here=here, there=there):
            if half == 0:
                mixed.wait_at(index)

            @pl.when(index == 0)
            def _():
                for k in (half, 2 + half):
                    gate_up.copies[k].wait()

            rows = mixed.ref[index]
            gate = dot_plain(rows, gate_up.ref[half])
            up = dot_plain(rows, gate_up.ref[2 + half])
            sigmoid = 1.0 / (1.0 + jnp.exp(-gate))
            silu = gate * sigmoid
            both.ref[index, :, here] = (up * (sigmoid + silu * (1.0 - sigmoid))).astype(LOW)
            both.ref[index, :, there] = silu.astype(LOW)
            hidden.ref[index, :, here] = (silu * up).astype(LOW)
            if half == 1:
                both.start_at(index)
                hidden.start_at(index)
            return carry

        lax.fori_loop(0, count, one_chunk, 0)
    gate_up.waited = True


def feed(mixed, gate_up, token):
    length = mixed.shape[0]
    per = gate_up.shape[1] // 2
    return run(
        feed_body,
        "feed",
        8,
        [rows_of(mixed), columns_of(gate_up)],
        [out_rows((length, 2 * per), LOW), out_rows((length, per), LOW)],
        token=token,
    )


def feed_back_body(both, cots, gate_up, down, grads, back, later=()):
    start_all(down)
    cots.start(0)
    both.start(0)
    gate_up.start()
    cots.start(1)
    both.start(1)
    start_all(*later)
    per = down.ref.shape[0]

    def one_chunk(index, carry):
        cots.wait_at(index)
        both.wait_at(index)
        grad_hidden = dot_rows(cots.ref[index], down.wait_first(index)[...])
        grads.ref[index, :, :per] = (grad_hidden * both.ref[index, :, :per].astype(WIDE)).astype(LOW)
        grads.ref[index, :, per:] = (grad_hidden * both.ref[index, :, per:].astype(WIDE)).astype(LOW)
        grads.start_at(index)
        back.ref[index] = dot_rows(grads.ref[index], gate_up.wait_first(index)[...]).astype(LOW)
        back.start_at(index)
        return carry

    lax.fori_loop(0, 2, one_chunk, 0)


def feed_back_far_body(both, cots, gate_up, down, hidden, near_cots, grads, back, out):
    feed_back_body(both, cots, gate_up, down, grads, back, (hidden, near_cots))
    near_ref, far_ref = near_cots.wait(), cots.ref
    chunk = near_ref.shape[1]

    def one_part(index, carry):
        hidden.wait_at(index)
        total = None
        for k in range(4):
            more = dot_first(
                hidden.ref[index, k * chunk : (k + 1) * chunk, :], (near_ref, far_ref)[k % 2][k // 2]
            )
            total = more if total is None else total + more
        out.ref[index] = total.astype(LOW)
        out.start_at(index)
        return carry

    lax.fori_loop(0, hidden.ref.shape[0], one_part, 0)


def feed_back(first, both, cots, gate_up, down, token, hidden=None):
    length = both.shape[0]
    chunk = length // 4
    per = down.shape[0]

    def pairs(refs, buffer):
        return [
            (refs[0].at[pl.ds((first + 2 * k) * chunk, chunk)], buffer.at[k]) for k in range(2)
        ]

    ins = [Plan([both], (2, chunk, 2 * per), pairs, 2), group((cots[first], cots[first + 2]))]
    ins += [whole(gate_up), whole(down)]
    outs = [out_rows((length // 2, 2 * per), LOW, 2), out_group((chunk, D), LOW, 2)]
    if hidden is None:
        return run(feed_back_body, "feed_back", 7, ins, outs, token=token)
    ins += [columns_of(hidden), group((cots[0], cots[2]))]
    outs += [out_rows((per, D), LOW)]
    return run(feed_back_far_body, "feed_back", 12, ins, outs, token=token)


def sum_arrived(near, got, last):
    return (
        near.wait()[...].astype(WIDE) + got.wait()[...].astype(WIDE) + last.wait()[...].astype(WIDE)
    )


def arrivals(sums):
    return [whole(x) if place % 3 == 2 else top(x) for place, x in enumerate(sums)]


def own_back_body(
    rank_ref, n0, g0, l0, n1, g1, l1, middle_rows, cot, gain_ref, wo, grad, parcels
):
    rank = rank_ref[0]
    start_all(n0, g0, l0, middle_rows, cot, n1, g1, l1, wo)
    block = l0.ref.shape[0]
    width = parcels.ref.shape[2] // 2
    for place, sums in enumerate(((n0, g0, l0), (n1, g1, l1))):
        rows = slice(place * block, (place + 1) * block)
        arrived = sum_arrived(*sums)
        y = middle_rows.wait()[rows, :]
        scale = unit_rows(y)
        normed = y * scale
        turned = arrived * gain_ref[1:2, :]
        grad.ref[rows, :] = cot.wait()[rows, :].astype(WIDE) + scale * (
            turned - normed * jnp.mean(turned * normed, -1, keepdims=True)
        )
    low_grad = grad.ref[...].astype(LOW)
    wo_ref = wo.wait()
    for q in range(4):
        place = pl.ds(pl.multiple_of((rank ^ q) * width, width), width)
        parcels.ref[q, :, :width] = dot_rows(low_grad, wo_ref[place, :]).astype(LOW)
        parcels.ref[q, :, width:] = grad.ref[:, place].astype(LOW)


def own_back(rank, sums, middle_own, cot_own, gain, out_pieces, token):
    quarter = cot_own.shape[0]
    return run(
        own_back_body,
        "own_back",
        4,
        [rank, *arrivals(sums), whole(middle_own), whole(cot_own), gain]
        + [output_weights(out_pieces)],
        [out_whole((quarter, D), WIDE), out_group((quarter, 512), LOW)],
        token=token,
    )


def attend_back_body(
    parcels, turned, wide, logs, cos, sin, query_sides, key_sides, weights_ref, projections,
    out, bias_ref, back, queries_ref, grads_ref, total_ref,
):
    start_all(parcels, turned, query_sides, logs, wide, key_sides, cos, sin, projections)
    length = turned.ref.shape[0]
    chunk = length // 4
    block = chunk // 2
    half_lane = lax.broadcasted_iota(jnp.int32, (chunk, 128), 1) // 64
    lane = lax.broadcasted_iota(jnp.int32, (chunk, 128), 1)
    parcels_ref = parcels.wait()
    for half, order in enumerate((ORDER_A, ORDER_B)):
        for place in range(4):
            to = slice((4 * half + place) * block, (4 * half + place + 1) * block)
            rows = slice(half * block, (half + 1) * block)
            for head in range(4):
                at = 128 * (head // 2)
                grads_ref[head, to, :128] = parcels_ref[order[place], rows, at : at + 128]
    turned_ref, side_ref, log_ref, wide_ref = (
        turned.wait(), query_sides.wait(), logs.wait(), wide.wait()
    )

    def prepare(index, carry):
        rows = pl.ds(pl.multiple_of(index * chunk, chunk), chunk)
        for pair in range(2):
            at = 128 * pair
            product = grads_ref[2 * pair, rows, :128].astype(WIDE) * wide_ref[rows, at : at + 128]
            scaled = turned_ref[rows, at : at + 128] * LOW(SCORE_SCALE)
            for half in range(2):
                head = 2 * pair + half
                side = side_ref[rows, :] * weights_ref[head : head + 1, :]
                for place, piece in enumerate(three_parts(-log_ref[rows, head : head + 1])):
                    side = jnp.where(lane == LSE_AT + place, piece, side)
                queries_ref[head, rows, :128] = jnp.where(half_lane == half, scaled, LOW(0))
                queries_ref[head, rows, 128:] = side
                delta = jnp.sum(jnp.where(half_lane == half, product, 0.0), 1, keepdims=True)
                extra = jnp.zeros((chunk, 128), LOW)
                for place, piece in enumerate(three_parts(-delta)):
                    extra = jnp.where(lane == place, piece, extra)
                grads_ref[head, rows, 128:] = extra
        total_ref[rows, :] = jnp.zeros((chunk, 256), WIDE)
        return carry

    lax.fori_loop(0, 4, prepare, 0)
    three_ones = jnp.where(lane < 3, 1.0, 0.0).astype(LOW)
    key_ref, cos_ref, sin_ref = key_sides.wait(), cos.wait(), sin.wait()

    def one_block(index, carry):
        rows = pl.ds(pl.multiple_of(index * chunk, chunk), chunk)
        cosine = cos_ref[rows, :]
        sine = -sin_ref[rows, :]
        key_side = key_ref[rows, :]
        first_four = jnp.where(lane < 4, key_side.astype(WIDE), 0.0)
        sums = list(carry)
        for pair in range(2):
            at = 128 * pair
            keys = turned_ref[rows, 256 + at : 384 + at]
            values = turned_ref[rows, 512 + at : 640 + at]
            keys_wide = jnp.concatenate([keys, key_side], 1)
            grad_keys = jnp.zeros((chunk, 128), WIDE)
            grad_values = jnp.zeros((chunk, 128), WIDE)
            for half in range(2):
                head = 2 * pair + half
                mine = half_lane == half
                weights = jnp.exp(dot_rows(keys_wide, queries_ref[head]))
                grad_weights = dot_rows(
                    jnp.concatenate([jnp.where(mine, values, LOW(0)), three_ones], 1),
                    grads_ref[head],
                )
                grad_values = jnp.where(
                    mine, dot_plain(weights.astype(LOW), grads_ref[head, :, :128]), grad_values
                )
                grad_scores = (weights * grad_weights).astype(LOW)
                both = dot_plain(
                    grad_scores,
                    jnp.concatenate([queries_ref[head, :, :128], side_ref[...]], 1),
                )
                grad_keys = grad_keys + both[:, :128]
                counted = both[:, 128:]
                same = jnp.sum(counted * first_four, 0, keepdims=True)
                every = jnp.sum(jnp.where(lane < 4, counted, 0.0), 0, keepdims=True)
                sums[head] = sums[head] + same
                sums[4 + head] = sums[4 + head] + (every - same)
                total_ref[:, at : at + 128] += dot_first(
                    grad_scores, jnp.where(mine, keys, LOW(0))
                )
            out.ref[index, :, 256 + at : 384 + at] = turn_pair(grad_keys, cosine, sine).astype(LOW)
            out.ref[index, :, 512 + at : 640 + at] = grad_values.astype(LOW)
        return tuple(sums)

    start = tuple(jnp.zeros((1, 128), WIDE) for _ in range(8))
    sums = lax.fori_loop(0, 4, one_block, start)
    for place in range(8):
        bias_ref[place : place + 1, :] = sums[place]
    projections_ref = projections.wait()

    def one_chunk(index, carry):
        rows = pl.ds(pl.multiple_of(index * chunk, chunk), chunk)
        for pair in range(2):
            at = 128 * pair
            out.ref[index, :, at : at + 128] = turn_pair(
                total_ref[rows, at : at + 128] * SCORE_SCALE, cos_ref[rows, :], -sin_ref[rows, :]
            ).astype(LOW)
        out.start_at(index)
        back.ref[index] = dot_rows(out.ref[index], projections_ref[...]).astype(LOW)
        back.start_at(index)
        return carry

    lax.fori_loop(0, 4, one_chunk, 0)


def attend_back(parcels, kept, weights, first_weights, token):
    turned, attended, *others = kept
    length = turned.shape[0]
    return run(
        attend_back_body,
        "attend_back",
        80,
        [group(parcels, 0, 256), whole(turned), whole(attended)]
        + [whole(x) for x in others]
        + [weights, whole(first_weights, 0, 768)],
        [out_rows((length, 768), LOW), ((8, 128), WIDE), out_group((length // 4, D), LOW)],
        [
            pltpu.VMEM((4, length, 256), LOW),
            pltpu.VMEM((4, length, 256), LOW),
            pltpu.VMEM((length, 256), WIDE),
        ],
        token,
    )


def gate_up_grads_body(mixed, near, far, out):
    mixed.start(0)
    for k in range(2):
        near.start(k)
        far.start(k)
    mixed.start(1, 2, 3)
    near.waited = far.waited = True
    chunk = mixed.ref.shape[1] // 4

    def one_part(index, carry):
        mixed.wait_at(index)
        total = None
        for k in range(4):
            item = (near, far)[k % 2]

            @pl.when(index == 0)
            def _(item=item, k=k):
                item.copies[k // 2].wait()

            more = dot_first(
                mixed.ref[index, k * chunk : (k + 1) * chunk, :], item.ref[k // 2]
            )
            total = more if total is None else total + more
        out.ref[index] = total.astype(LOW)
        out.start_at(index)
        return carry

    lax.fori_loop(0, mixed.ref.shape[0], one_part, 0)


def gate_up_grads(mixed, near, far, token):
    return run(
        gate_up_grads_body,
        "gate_up_grads",
        8,
        [columns_of(mixed), rows_of(near, 2), rows_of(far, 2)],
        [out_rows((D, near.shape[1]), LOW)],
        token=token,
    )[0]


def feed_out_body(hidden, down, out):
    start_all(down, hidden)
    block = out.ref.shape[1]

    def one_chunk(index, carry):
        down_ref = down.wait_first(index)
        hidden.wait_at(index)
        total = dot_plain(hidden.ref[index], down_ref[...]).astype(LOW)
        for p in range(2):
            q = jnp.where(index < 2, 2 * index + p, index - 2 + 2 * p)
            out.ref[2 * q + index // 2] = total[p * block : (p + 1) * block]
        return carry

    lax.fori_loop(0, hidden.ref.shape[0], one_chunk, 0)


def feed_out(hidden, down, token):
    length = hidden.shape[0]
    block = length // 8

    def pairs(refs, buffer):
        return [
            (buffer.at[2 * q + half], ref.at[pl.ds(half * block, block)])
            for q, ref in enumerate(refs)
            for half in range(2)
        ]

    return run(
        feed_out_body,
        "feed_out",
        5,
        [rows_of(hidden), whole(down)],
        [Plan([((2 * block, D), LOW)] * 4, (8, block, D), pairs, 8)],
        token=token,
    )


def own_last_body(n0, g0, l0, n1, g1, l1, forward, x, base, middle_rows, gain_ref, out):
    start_all(n0, g0, l0, x, base, forward, middle_rows, n1, g1, l1)
    block = l0.ref.shape[0]
    piece = out.ref.shape[1] // 2
    each = block // piece
    for half, back in enumerate(((n0, g0, l0), (n1, g1, l1))):
        rows = slice(half * block, (half + 1) * block)
        places = slice(half * each, (half + 1) * each)
        turned = sum_arrived(*back) * gain_ref[0:1, :]
        x_rows = x.wait()[rows, :D].astype(WIDE)
        scale = unit_rows(x_rows)
        normed = x_rows * scale
        grad = base.wait()[rows, :] + scale * (
            turned - normed * jnp.mean(turned * normed, -1, keepdims=True)
        )
        out.ref[places, :piece, :] = grad.astype(LOW).reshape(each, piece, D)
        block_rows = middle_rows.wait()[rows, :]
        forward_ref = forward.wait()
        for q in range(4):
            block_rows = block_rows + forward_ref[q, rows, :].astype(WIDE)
        out.ref[places, piece:, :] = block_rows.astype(LOW).reshape(each, piece, D)


def own_last(sums, outs, mine, base, middle_own, gain, n_seq, token):
    quarter = base.shape[0]
    return run(
        own_last_body,
        "own_last",
        80,
        [*arrivals(sums), group(outs), whole(mine), whole(base), whole(middle_own), gain],
        [out_whole((n_seq, 2 * quarter // n_seq, D), LOW)],
        token=token,
    )[0]


def join_body(left, right, out):
    start_all(left, right)
    width = left.ref.shape[1]
    out.ref[:, :width] = left.wait()[...]
    out.ref[:, width:] = right.wait()[...]


def join(left, right, token):
    rows = left.shape[0]
    return run(
        join_body,
        "join",
        1,
        [whole(left), whole(right)],
        [out_whole((rows, left.shape[1] + right.shape[1]), LOW)],
        token=token,
    )[0]


def first_grads_body(rank_ref, mixed, proj, heads, parcels, bias_ref, out, branch_ref):
    rank = rank_ref[0]
    start_all(mixed, proj, parcels, heads)
    width = proj.ref.shape[1]
    block = parcels.ref.shape[1] // 2
    parcels_ref = parcels.wait()
    for half, order in enumerate((ORDER_A, ORDER_B)):
        for place in range(4):
            to = slice((4 * half + place) * block, (4 * half + place + 1) * block)
            branch_ref[to, :] = parcels_ref[order[place], half * block : (half + 1) * block, :]
    mixed_ref, proj_ref, heads_ref = mixed.wait(), proj.wait(), heads.wait()

    def one_part(index, carry):
        out.ref[index, :, :width] = dot_first(mixed_ref[index], proj_ref[...]).astype(LOW)
        out.ref[rank ^ index, :, width : width + 256] = dot_first(
            heads_ref[index], branch_ref[...]
        ).astype(LOW)
        out.ref[index, :, width + 256 :] = bias_ref[...]
        return carry

    lax.fori_loop(0, 4, one_part, 0)


def first_grads(rank, mixed, proj, heads, parcels, bias_rows, token):
    length = mixed.shape[0]
    return run(
        first_grads_body,
        "first_grads",
        8,
        [rank, columns_of(mixed), whole(proj), columns_of(heads)]
        + [group(parcels, 256, 256), bias_rows],
        [out_rows((D, 768 + 256 + 128), LOW)],
        [pltpu.VMEM((length, 256), LOW)],
        token,
    )[0]


def rank_blocks(lower, lower_far, upper, upper_far):
    half = lower.shape[0] // 2
    return (
        ((lower, 0), (upper, 0)),
        ((lower, half), (upper_far, 0)),
        ((lower_far, 0), (upper, half)),
        ((lower_far, half), (upper_far, half)),
    )


def lay_flat(column, part):
    count = column.shape[0]
    row = lax.broadcasted_iota(jnp.int32, (count, 128), 0) + part * count
    lane = lax.broadcasted_iota(jnp.int32, (count, 128), 1)
    return jnp.sum(jnp.where(row == lane, column, 0.0), 0, keepdims=True)


def spread_feed_kernel(
    rank_ref, lower, lower_far, upper, upper_far, gate_ref, up_ref, gain_ref,
    grad_gate_ref, grad_up_ref, grad_down_ref, grad_gain_ref,
):
    rank = rank_ref[0]
    half = lower.shape[0] // 2
    piece = 128
    ff = gate_ref.shape[1]
    per = ff // 4
    for r, halves in enumerate(rank_blocks(lower, lower_far, upper, upper_far)):
        for part, (ref, start) in enumerate(halves):
            rows = slice(part * half, (part + 1) * half)
            source = slice(start, start + half)
            for s in range(per // piece):
                to = pl.ds(pl.multiple_of((4 * s + (rank ^ r)) * piece, piece), piece)
                grad_gate_ref[rows, to] = ref[source, s * piece : (s + 1) * piece].astype(WIDE)
                grad_up_ref[rows, to] = ref[source, per + s * piece : per + (s + 1) * piece].astype(
                    WIDE
                )
            to = pl.ds(pl.multiple_of((rank ^ r) * 2 * half + part * half, half), half)
            grad_down_ref[to, :] = ref[source, 2 * per :].astype(WIDE)
    flat = jnp.zeros((1, 128), WIDE)
    for part in range(2):
        rows = slice(part * half, (part + 1) * half)
        total = jnp.sum(
            gate_ref[rows, :].astype(WIDE) * grad_gate_ref[rows, :], 1, keepdims=True
        ) + jnp.sum(up_ref[rows, :].astype(WIDE) * grad_up_ref[rows, :], 1, keepdims=True)
        flat = flat + lay_flat(total, part)
    grad_gain_ref[...] = jnp.broadcast_to(flat / gain_ref[...].astype(WIDE), (8, 128))


def spread_feed(rank, pieces, w_gate, w_up, gain):
    shard, ff = w_gate.shape
    return call(
        spread_feed_kernel,
        "spread_feed",
        [((shard, ff), WIDE), ((shard, ff), WIDE), ((ff // 8, D), WIDE), ((8, 128), WIDE)],
        [pl.BlockSpec(memory_space=pltpu.SMEM)] + [whole_block()] * 7,
        4 * shard * ff,
        16 * 2**20,
        (rank, *pieces, w_gate, w_up, gain),
    )


def spread_first_kernel(
    rank_ref, lower, lower_far, upper, upper_far, wq_ref, wk_ref, wv_ref, gain_ref,
    gq_ref, gk_ref, gv_ref, go_ref, grad_gain_ref, bias_ref,
):
    rank = rank_ref[0]
    half = lower.shape[0] // 2
    wide = 256
    bias_ref[...] = jnp.zeros_like(bias_ref)
    for r, halves in enumerate(rank_blocks(lower, lower_far, upper, upper_far)):
        to = pl.ds(pl.multiple_of((rank ^ r) * wide, wide), wide)
        for part, (ref, start) in enumerate(halves):
            rows = slice(part * half, (part + 1) * half)
            source = slice(start, start + half)
            for place, out_ref in enumerate((gq_ref, gk_ref, gv_ref, go_ref)):
                out_ref[rows, to] = ref[source, place * wide : (place + 1) * wide].astype(WIDE)
        ref, start = halves[0]
        bias_ref[pl.ds(rank ^ r, 1), :] = jnp.sum(
            ref[start : start + 16, 4 * wide : 4 * wide + 128].astype(WIDE), 0, keepdims=True
        )
    flat = jnp.zeros((1, 128), WIDE)
    for part in range(2):
        rows = slice(part * half, (part + 1) * half)
        total = jnp.zeros((half, 1), WIDE)
        for weight_ref, grad_ref in ((wq_ref, gq_ref), (wk_ref, gk_ref), (wv_ref, gv_ref)):
            total = total + jnp.sum(
                weight_ref[rows, :].astype(WIDE) * grad_ref[rows, :], 1, keepdims=True
            )
        flat = flat + lay_flat(total, part)
    grad_gain_ref[...] = jnp.broadcast_to(flat / gain_ref[...].astype(WIDE), (8, 128))


def spread_first(rank, pieces, w_query, w_key, w_value, gain):
    shard = w_query.shape[0]
    return call(
        spread_first_kernel,
        "spread_first",
        [((shard, D), WIDE)] * 4 + [((8, 128), WIDE), ((8, 128), WIDE)],
        [pl.BlockSpec(memory_space=pltpu.SMEM)] + [whole_block()] * 8,
        4 * shard * D,
        8 * 2**20,
        (rank, *pieces, w_query, w_key, w_value, gain),
    )


def on_plane(
    inputs,
    w_query,
    w_key,
    w_value,
    w_output,
    gain_attention,
    w_gate,
    w_up,
    w_down,
    gain_feed,
    variate_bias,
    segment_ids,
    variate_ids,
    positions,
    grad_output,
):
    rank = lax.axis_index("batch")
    rank_row = jnp.reshape(rank, (1,)).astype(jnp.int32)
    micro, tokens = inputs.shape[0], inputs.shape[2]
    n_seq = lax.axis_size("seq")
    shard = w_query.shape[0]
    per = D // 4

    packed, first_shard, gate_up_shard, down_shard = pack(
        rank_row,
        inputs.reshape(micro, tokens, D),
        grad_output.reshape(micro, tokens, D),
        segment_ids.reshape(micro, tokens),
        variate_ids.reshape(micro, tokens),
        positions.reshape(micro, tokens),
        (w_query, w_key, w_value, w_output),
        (gain_attention.reshape(1, shard), gain_feed.reshape(1, shard)),
        w_gate,
        w_up,
        w_down,
    )
    first_weights = lax.all_gather(first_shard, "seq", axis=0, tiled=True)
    gate_up = lax.all_gather(gate_up_shard, "seq", axis=0, tiled=True)
    down = lax.all_gather(down_shard, "seq", axis=0, tiled=True)
    packed = lax.all_to_all(packed, "batch", 0, 0, tiled=True)
    by_sequence = [
        packed[:, kind].reshape(4 * micro, tokens // 4, D + 128)[:, :, : D + 128 - 128 * kind]
        for kind in range(2)
    ]
    out_columns = first_weights[:, 768:D]
    out_got = swap_pairs(out_columns)
    mine, cot_by_sequence, out_got = lax.optimization_barrier(
        (over_seq(by_sequence[0]), by_sequence[1], out_got)
    )
    cot_mine = over_seq(cot_by_sequence)
    freqs = jnp.exp((jnp.arange(128) % 32).astype(WIDE) * (-2.0 * math.log(10000.0) / HD))[None, :]
    my_bias = lax.dynamic_slice_in_dim(variate_bias, rank * 4, 4, 1)
    weights = jnp.pad(head_weights(my_bias[0], my_bias[1]), ((0, 4), (0, 0)))

    chunks = gather_plane(mine)
    out_pieces = far_pairs(
        out_columns, lax.optimization_barrier((out_got, chunks[1], chunks[3]))[0]
    )
    gain, mixed_first, turned, attended, lower, upper, *kept = attend(
        chunks, first_weights, freqs, weights, rank_row
    )
    ready = lax.optimization_barrier((lower, upper, out_pieces[1], out_pieces[3]))
    lower_x, upper_y = swap(ready[0], 1), swap(ready[1], 2)
    lower_far = swap(jnp.concatenate([lower, lower_x], 1), 2)
    upper_far = swap(jnp.concatenate([upper, upper_y], 1), 1)
    cot_got = swap_pairs(lax.optimization_barrier((cot_mine, lower_far, upper_far))[0])
    heads, middle_own, mixed_second = middle(
        rank_row,
        chunks,
        (lower, lower_x, lower_far, upper, upper_y, upper_far),
        out_pieces,
        gain,
    )

    both, hidden = feed(mixed_second, gate_up, after(rank_row, cot_got))
    cots = far_pairs(cot_mine, lax.optimization_barrier((cot_got, mixed_second))[0])
    far_grads, far_lower, far_upper, down_weight_grads = feed_back(
        1, both, cots, gate_up, down, rank_row, hidden
    )
    got = scatter_first((None, far_lower, None, far_upper))
    near_grads, near_lower, near_upper = feed_back(
        0, both, cots, gate_up, down, after(rank_row, far_lower)
    )
    down_grad_shard = lax.psum_scatter(down_weight_grads, "seq", scatter_dimension=0, tiled=True)
    back = (near_lower, None, near_upper, None)
    gate_up_weight_grads = gate_up_grads(
        mixed_second, near_grads, far_grads, after(rank_row, got)
    )
    gate_up_grad_shard = lax.psum_scatter(
        gate_up_weight_grads, "seq", scatter_dimension=0, tiled=True
    )
    sums = scatter_second(back, got)
    grad_middle, *parcels = own_back(
        rank_row, sums, middle_own, cot_mine, gain, out_pieces,
        after(rank_row, gate_up_weight_grads),
    )
    outs = feed_out(hidden, down, after(rank_row, parcels[0]))
    parcels = [parcels[0]] + [swap(parcels[r], r) for r in range(1, 4)]

    proj, bias, *back = attend_back(
        parcels, (turned, attended, *kept), weights, first_weights, after(rank_row, outs[0])
    )
    outs = [outs[0]] + [swap(outs[q], q) for q in range(1, 4)]
    ready = lax.optimization_barrier((back[1], back[3], *outs[1:]))
    got = scatter_first((None, ready[0], None, ready[1]))
    bias_sums = jnp.sum(bias, 1)
    bias_parts = jnp.pad(jnp.concatenate(three_parts(bias_sums)), (0, 104))[None, :]
    slots = lax.broadcasted_iota(jnp.int32, (per, 1), 0) % shard == lax.axis_index("seq")
    bias_rows = jnp.where(slots, bias_parts, LOW(0))
    first_weight_grads = first_grads(
        rank_row, mixed_first, proj, heads, parcels, bias_rows, rank_row
    )
    got, first_weight_grads = lax.optimization_barrier((got, first_weight_grads))
    first_shard = lax.psum_scatter(first_weight_grads, "seq", scatter_dimension=0, tiled=True)
    sums = scatter_second(back, got)
    feed_shard = join(gate_up_grad_shard, down_grad_shard, after(rank_row, first_weight_grads))
    last = own_last(
        sums, outs, mine, grad_middle, middle_own, gain, n_seq, after(rank_row, feed_shard)
    )
    moved = lax.all_to_all(last, "seq", 0, 0, tiled=True)
    quarter = tokens // 4
    feed_pieces = gather_plane(after(feed_shard, last))
    first_pieces = gather_plane(after(first_shard, feed_pieces))
    moved, first_pieces = lax.optimization_barrier((moved, first_pieces))
    moved = moved.reshape(4, micro, 2 * quarter, D)
    moved = lax.all_to_all(moved, "batch", 0, 0, tiled=True)
    grad_inputs = jnp.transpose(moved[:, :, :quarter].astype(WIDE), (1, 0, 2, 3))
    block_output = jnp.transpose(moved[:, :, quarter:], (1, 0, 2, 3))

    grad_gate, grad_up, grad_down, grad_gain_second = spread_feed(
        rank_row, feed_pieces, w_gate, w_up, gain_feed.reshape(1, shard)
    )
    grad_query, grad_key, grad_value, grad_output_weights, grad_gain_first, bias_table = (
        spread_first(
            rank_row, first_pieces, w_query, w_key, w_value, gain_attention.reshape(1, shard)
        )
    )
    bias_table = jnp.sum(bias_table[:4, :24].reshape(4, 3, 2, 4), 1)
    grad_bias = jnp.transpose(bias_table, (1, 0, 2)).reshape(2, H)
    return (
        block_output.reshape(inputs.shape),
        grad_inputs.reshape(inputs.shape),
        grad_query,
        grad_key,
        grad_value,
        grad_output_weights,
        grad_gain_first[0],
        grad_gate,
        grad_up,
        grad_down,
        grad_gain_second[0],
        grad_bias,
    )


def solution(mesh):
    n_batch, n_seq = mesh.shape["batch"], mesh.shape["seq"]
    step = on_plane if n_batch == 4 and n_seq == 8 else on_device
    return jax.shard_map(
        step,
        mesh=mesh,
        in_specs=(
            P(None, "batch", "seq", None),
            P("seq", None),
            P("seq", None),
            P("seq", None),
            P("seq", None),
            P("seq"),
            P("seq", None),
            P("seq", None),
            P("seq", None),
            P("seq"),
            P(),
            P(None, "batch", "seq"),
            P(None, "batch", "seq"),
            P(None, "batch", "seq"),
            P(None, "batch", "seq", None),
        ),
        out_specs=(
            P(None, "batch", "seq", None),
            P(None, "batch", "seq", None),
            P("seq", None),
            P("seq", None),
            P("seq", None),
            P("seq", None),
            P("seq"),
            P("seq", None),
            P("seq", None),
            P("seq", None),
            P("seq"),
            P(),
        ),
        check_vma=False,
    )
```

```python
import functools
import math

import jax
import jax.numpy as jnp
from jax import lax
from jax.experimental import pallas as pl
from jax.experimental.pallas import tpu as pltpu
from jax.sharding import PartitionSpec as P

D = 1024
H = 16
HD = 64
REACH = 6


EPSILON = 1e-05
SCORE_SCALE = 0.125
MASKED = -1e30


def from_behind(value, axis, by):
    length = lax.axis_size(axis)
    pairs = [(i, i + by) for i in range(length) if 0 <= i + by < length]
    return lax.ppermute(value, axis, pairs)


def step_offset(step):
    distance = step // 2 + 1
    return distance if step % 2 == 0 else -distance


def rotary(values_in, positions_in, turn):
    row_count = values_in.shape[0]
    halfway = HD // 2
    freqs = jnp.exp(jnp.arange(halfway, dtype=jnp.float32) * (-2.0 * math.log(10000.0) / HD))
    angles = positions_in.astype(jnp.float32)[:, None] * freqs[None, :]
    cosine = jnp.cos(angles)[:, None, :]
    sine = turn * jnp.sin(angles)[:, None, :]
    shaped = values_in.reshape(row_count, H, HD)
    first_half = shaped[..., :halfway]
    second_half = shaped[..., halfway:]
    turned = jnp.concatenate(
        [first_half * cosine - second_half * sine, first_half * sine + second_half * cosine], -1
    )
    return turned.reshape(row_count, H * HD)


def head_scores(query_heads, key_heads, query_variates, key_variates, bias_table):
    raw = jnp.einsum("qhd,khd->hqk", query_heads, key_heads, preferred_element_type=jnp.float32)
    same_variate = (query_variates[:, None] == key_variates[None, :])[None]
    return raw * SCORE_SCALE + jnp.where(
        same_variate, bias_table[0][:, None, None], bias_table[1][:, None, None]
    )


def attend_forward(query_rows, own_keys, own_values, own_segments, own_variates, bias_table):
    tok_count = query_rows.shape[0]
    query_heads = query_rows.reshape(tok_count, H, HD)
    shifted_segments = own_segments + 1

    def fold_keys(carried, piece_rows):
        key_part, value_part, segment_part, variate_part = piece_rows
        part_count = key_part.shape[0]
        live = shifted_segments[:, None] == segment_part[None, :]

        def update(state):
            running_max, running_total, running_sum = state
            logits = head_scores(
                query_heads,
                key_part.reshape(part_count, H, HD),
                own_variates,
                variate_part,
                bias_table,
            )
            logits = jnp.where(live[None], logits, MASKED)
            new_max = jnp.maximum(running_max, jnp.max(logits, -1))
            rescale = jnp.exp(running_max - new_max)
            weights = jnp.where(live[None], jnp.exp(logits - new_max[..., None]), 0.0)
            new_total = running_total * rescale + jnp.sum(weights, -1)
            mixed = jnp.einsum(
                "hqk,khd->qhd",
                weights.astype(jnp.bfloat16),
                value_part.reshape(part_count, H, HD),
                preferred_element_type=jnp.float32,
            )
            new_sum = running_sum * jnp.transpose(rescale)[:, :, None] + mixed
            return (new_max, new_total, new_sum)

        return lax.cond(jnp.any(live), update, lambda state: state, carried)

    near_rows = (own_keys, own_values, shifted_segments, own_variates)
    state = (
        jnp.full((H, tok_count), MASKED, jnp.float32),
        jnp.zeros((H, tok_count), jnp.float32),
        jnp.zeros((tok_count, H, HD), jnp.float32),
    )
    state = fold_keys(state, near_rows)
    for step in range(2 * REACH):
        arrived = from_behind(
            (own_keys, own_values, shifted_segments, own_variates), "seq", step_offset(step)
        )
        state = fold_keys(state, arrived)
    final_max, final_total, final_sum = state
    attended = final_sum / jnp.transpose(final_total)[:, :, None]
    log_rows = jnp.transpose(final_max + jnp.log(final_total))
    return (attended.reshape(tok_count, H * HD), log_rows)


def attend_queries_back(
    query_rows,
    grad_rows,
    log_rows,
    delta_rows,
    own_keys,
    own_values,
    own_segments,
    own_variates,
    bias_table,
):
    tok_count = query_rows.shape[0]
    query_heads = query_rows.reshape(tok_count, H, HD)
    grad_heads = grad_rows.reshape(tok_count, H, HD)
    log_heads = jnp.transpose(log_rows)
    delta_heads = jnp.transpose(delta_rows)
    shifted_segments = own_segments + 1

    def fold_keys_back(carried, piece_rows):
        key_part, value_part, segment_part, variate_part = piece_rows
        part_count = key_part.shape[0]
        live = shifted_segments[:, None] == segment_part[None, :]

        def update(state):
            grad_query, grad_bias = state
            key_heads = key_part.reshape(part_count, H, HD)
            logits = head_scores(query_heads, key_heads, own_variates, variate_part, bias_table)
            weights = jnp.where(live[None], jnp.exp(logits - log_heads[..., None]), 0.0)
            grad_weights = jnp.einsum(
                "qhd,khd->hqk",
                grad_heads,
                value_part.reshape(part_count, H, HD),
                preferred_element_type=jnp.float32,
            )
            grad_logits = (weights * (grad_weights - delta_heads[..., None])).astype(jnp.bfloat16)
            grad_query = grad_query + SCORE_SCALE * jnp.einsum(
                "hqk,khd->qhd", grad_logits, key_heads, preferred_element_type=jnp.float32
            )
            same_variate = (own_variates[:, None] == variate_part[None, :])[None]
            logit_values = grad_logits.astype(jnp.float32)
            same_total = jnp.sum(jnp.where(same_variate, logit_values, 0.0), axis=(1, 2))
            other_total = jnp.sum(jnp.where(same_variate, 0.0, logit_values), axis=(1, 2))
            return (grad_query, grad_bias + jnp.stack([same_total, other_total]))

        return lax.cond(jnp.any(live), update, lambda state: state, carried)

    state = (jnp.zeros((tok_count, H, HD), jnp.float32), jnp.zeros((2, H), jnp.float32))
    state = fold_keys_back(state, (own_keys, own_values, shifted_segments, own_variates))
    for step in range(2 * REACH):
        arrived = from_behind(
            (own_keys, own_values, shifted_segments, own_variates), "seq", step_offset(step)
        )
        state = fold_keys_back(state, arrived)
    grad_query, grad_bias = state
    return (grad_query.reshape(tok_count, H * HD), grad_bias)


def attend_keys_back(
    query_rows,
    grad_rows,
    log_rows,
    delta_rows,
    own_keys,
    own_values,
    own_segments,
    own_variates,
    bias_table,
):
    tok_count = own_keys.shape[0]
    key_heads = own_keys.reshape(tok_count, H, HD)
    value_heads = own_values.reshape(tok_count, H, HD)
    shifted_segments = own_segments + 1

    def fold_queries(carried, piece_rows):
        query_part, grad_part, log_part, delta_part, segment_part, variate_part = piece_rows
        part_count = query_part.shape[0]
        live = segment_part[:, None] == shifted_segments[None, :]

        def update(state):
            grad_key, grad_value = state
            query_heads = query_part.reshape(part_count, H, HD)
            grad_heads = grad_part.reshape(part_count, H, HD)
            logits = head_scores(query_heads, key_heads, variate_part, own_variates, bias_table)
            weights = jnp.where(
                live[None], jnp.exp(logits - jnp.transpose(log_part)[..., None]), 0.0
            )
            grad_value = grad_value + jnp.einsum(
                "hqk,qhd->khd",
                weights.astype(jnp.bfloat16),
                grad_heads,
                preferred_element_type=jnp.float32,
            )
            grad_weights = jnp.einsum(
                "qhd,khd->hqk", grad_heads, value_heads, preferred_element_type=jnp.float32
            )
            grad_logits = (weights * (grad_weights - jnp.transpose(delta_part)[..., None])).astype(
                jnp.bfloat16
            )
            grad_key = grad_key + SCORE_SCALE * jnp.einsum(
                "hqk,qhd->khd", grad_logits, query_heads, preferred_element_type=jnp.float32
            )
            return (grad_key, grad_value)

        return lax.cond(jnp.any(live), update, lambda state: state, carried)

    state = (jnp.zeros((tok_count, H, HD), jnp.float32), jnp.zeros((tok_count, H, HD), jnp.float32))
    state = fold_queries(
        state, (query_rows, grad_rows, log_rows, delta_rows, shifted_segments, own_variates)
    )
    for step in range(2 * REACH):
        arrived = (
            from_behind(query_rows, "seq", step_offset(step)),
            from_behind(grad_rows, "seq", step_offset(step)),
            from_behind(log_rows.astype(jnp.bfloat16), "seq", step_offset(step)).astype(
                log_rows.dtype
            ),
            from_behind(delta_rows.astype(jnp.bfloat16), "seq", step_offset(step)).astype(
                delta_rows.dtype
            ),
            from_behind(shifted_segments, "seq", step_offset(step)),
            from_behind(own_variates, "seq", step_offset(step)),
        )
        state = fold_queries(state, arrived)
    grad_key, grad_value = state
    return (grad_key.reshape(tok_count, H * HD), grad_value.reshape(tok_count, H * HD))


def norm_back(grad_normed, normed, scale_rows):
    return scale_rows * (grad_normed - normed * jnp.mean(grad_normed * normed, -1, keepdims=True))


def on_device(
    inputs,
    w_query,
    w_key,
    w_value,
    w_output,
    gain_attention,
    w_gate,
    w_up,
    w_down,
    gain_feed,
    variate_bias,
    segment_ids,
    variate_ids,
    positions,
    grad_output,
):
    micro_count = inputs.shape[0]
    tok_count = inputs.shape[2]
    row_count = micro_count * tok_count
    residual_in = inputs.reshape(row_count, D).astype(jnp.float32)
    cotangent = grad_output.reshape(row_count, D).astype(jnp.float32)
    segment_rows = segment_ids.reshape(micro_count, tok_count)
    variate_rows = variate_ids.reshape(micro_count, tok_count)
    position_rows = positions.reshape(row_count)
    full_query, full_key, full_value, full_output, full_gain_first = (
        lax.all_gather(w_query, "seq", axis=0, tiled=True),
        lax.all_gather(w_key, "seq", axis=0, tiled=True),
        lax.all_gather(w_value, "seq", axis=0, tiled=True),
        lax.all_gather(w_output, "seq", axis=0, tiled=True),
        lax.all_gather(gain_attention, "seq", axis=0, tiled=True),
    )
    full_gate, full_up, full_down, full_gain_second = (
        lax.all_gather(w_gate, "seq", axis=0, tiled=True),
        lax.all_gather(w_up, "seq", axis=0, tiled=True),
        lax.all_gather(w_down, "seq", axis=0, tiled=True),
        lax.all_gather(gain_feed, "seq", axis=0, tiled=True),
    )
    scale_first = lax.rsqrt(jnp.mean(residual_in * residual_in, -1, keepdims=True) + EPSILON)
    normed_first = residual_in * scale_first
    mixed_first = (normed_first * full_gain_first.astype(jnp.float32)).astype(jnp.bfloat16)
    query_proj = jnp.dot(mixed_first, full_query, preferred_element_type=jnp.float32)
    key_proj = jnp.dot(mixed_first, full_key, preferred_element_type=jnp.float32)
    value_proj = jnp.dot(mixed_first, full_value, preferred_element_type=jnp.float32)
    query_rows = rotary(query_proj, position_rows, 1.0).astype(jnp.bfloat16)
    key_rows = rotary(key_proj, position_rows, 1.0).astype(jnp.bfloat16)
    value_rows = value_proj.astype(jnp.bfloat16)
    attended_parts = []
    log_parts = []
    for micro_index in range(micro_count):
        lower_row = micro_index * tok_count
        upper_row = lower_row + tok_count
        attended_part, log_part = attend_forward(
            query_rows[lower_row:upper_row],
            key_rows[lower_row:upper_row],
            value_rows[lower_row:upper_row],
            segment_rows[micro_index],
            variate_rows[micro_index],
            variate_bias,
        )
        attended_parts.append(attended_part)
        log_parts.append(log_part)
    attended_all = jnp.concatenate(attended_parts, 0)
    attended_low = attended_all.astype(jnp.bfloat16)
    middle = residual_in + jnp.dot(attended_low, full_output, preferred_element_type=jnp.float32)
    scale_second = lax.rsqrt(jnp.mean(middle * middle, -1, keepdims=True) + EPSILON)
    normed_second = middle * scale_second
    mixed_second = (normed_second * full_gain_second.astype(jnp.float32)).astype(jnp.bfloat16)
    gate_proj = jnp.dot(mixed_second, full_gate, preferred_element_type=jnp.float32)
    up_proj = jnp.dot(mixed_second, full_up, preferred_element_type=jnp.float32)
    sigmoid_gate = jax.nn.sigmoid(gate_proj)
    silu_gate = gate_proj * sigmoid_gate
    hidden_rows = (silu_gate * up_proj).astype(jnp.bfloat16)
    block_rows = middle + jnp.dot(hidden_rows, full_down, preferred_element_type=jnp.float32)
    block_output = block_rows.astype(jnp.bfloat16).reshape(inputs.shape)
    full_query, full_key, full_value, full_output, full_gain_first = (
        lax.all_gather(w_query, "seq", axis=0, tiled=True),
        lax.all_gather(w_key, "seq", axis=0, tiled=True),
        lax.all_gather(w_value, "seq", axis=0, tiled=True),
        lax.all_gather(w_output, "seq", axis=0, tiled=True),
        lax.all_gather(gain_attention, "seq", axis=0, tiled=True),
    )
    full_gate, full_up, full_down, full_gain_second = (
        lax.all_gather(w_gate, "seq", axis=0, tiled=True),
        lax.all_gather(w_up, "seq", axis=0, tiled=True),
        lax.all_gather(w_down, "seq", axis=0, tiled=True),
        lax.all_gather(gain_feed, "seq", axis=0, tiled=True),
    )
    grad_branch_second = cotangent.astype(jnp.bfloat16)
    grad_down = jnp.einsum(
        "rf,rd->fd", hidden_rows, grad_branch_second, preferred_element_type=jnp.float32
    )
    grad_hidden = jnp.einsum(
        "rd,fd->rf", grad_branch_second, full_down, preferred_element_type=jnp.float32
    )
    silu_slope = sigmoid_gate * (1.0 + gate_proj * (1.0 - sigmoid_gate))
    grad_gate_rows = (grad_hidden * up_proj * silu_slope).astype(jnp.bfloat16)
    grad_up_rows = (grad_hidden * silu_gate).astype(jnp.bfloat16)
    grad_gate = jnp.einsum(
        "rd,rf->df", mixed_second, grad_gate_rows, preferred_element_type=jnp.float32
    )
    grad_up = jnp.einsum(
        "rd,rf->df", mixed_second, grad_up_rows, preferred_element_type=jnp.float32
    )
    grad_mixed_second = jnp.einsum(
        "rf,df->rd", grad_gate_rows, full_gate, preferred_element_type=jnp.float32
    ) + jnp.einsum("rf,df->rd", grad_up_rows, full_up, preferred_element_type=jnp.float32)
    grad_gain_second = jnp.sum(grad_mixed_second * normed_second, 0)
    grad_middle = cotangent + norm_back(
        grad_mixed_second * full_gain_second.astype(jnp.float32), normed_second, scale_second
    )
    grad_branch_first = grad_middle.astype(jnp.bfloat16)
    grad_out_proj = jnp.einsum(
        "rd,re->de", attended_low, grad_branch_first, preferred_element_type=jnp.float32
    )
    grad_attended = jnp.einsum(
        "re,de->rd", grad_branch_first, full_output, preferred_element_type=jnp.float32
    ).astype(jnp.bfloat16)
    delta_all = jnp.einsum(
        "rhd,rhd->rh",
        grad_attended.astype(jnp.float32).reshape(row_count, H, HD),
        attended_all.reshape(row_count, H, HD),
    )
    grad_bias_local = jnp.zeros((2, H), jnp.float32)
    query_grad_parts = []
    key_grad_parts = []
    value_grad_parts = []
    for micro_index in range(micro_count):
        lower_row = micro_index * tok_count
        upper_row = lower_row + tok_count
        query_grad_part, bias_part = attend_queries_back(
            query_rows[lower_row:upper_row],
            grad_attended[lower_row:upper_row],
            log_parts[micro_index],
            delta_all[lower_row:upper_row],
            key_rows[lower_row:upper_row],
            value_rows[lower_row:upper_row],
            segment_rows[micro_index],
            variate_rows[micro_index],
            variate_bias,
        )
        key_grad_part, value_grad_part = attend_keys_back(
            query_rows[lower_row:upper_row],
            grad_attended[lower_row:upper_row],
            log_parts[micro_index],
            delta_all[lower_row:upper_row],
            key_rows[lower_row:upper_row],
            value_rows[lower_row:upper_row],
            segment_rows[micro_index],
            variate_rows[micro_index],
            variate_bias,
        )
        grad_bias_local = grad_bias_local + bias_part
        query_grad_parts.append(query_grad_part)
        key_grad_parts.append(key_grad_part)
        value_grad_parts.append(value_grad_part)
    grad_query_rows = rotary(jnp.concatenate(query_grad_parts, 0), position_rows, -1.0).astype(
        jnp.bfloat16
    )
    grad_key_rows = rotary(jnp.concatenate(key_grad_parts, 0), position_rows, -1.0).astype(
        jnp.bfloat16
    )
    grad_value_rows = jnp.concatenate(value_grad_parts, 0).astype(jnp.bfloat16)
    grad_query = jnp.einsum(
        "rd,re->de", mixed_first, grad_query_rows, preferred_element_type=jnp.float32
    )
    grad_key = jnp.einsum(
        "rd,re->de", mixed_first, grad_key_rows, preferred_element_type=jnp.float32
    )
    grad_value = jnp.einsum(
        "rd,re->de", mixed_first, grad_value_rows, preferred_element_type=jnp.float32
    )
    grad_mixed_first = (
        jnp.einsum("re,de->rd", grad_query_rows, full_query, preferred_element_type=jnp.float32)
        + jnp.einsum("re,de->rd", grad_key_rows, full_key, preferred_element_type=jnp.float32)
        + jnp.einsum("re,de->rd", grad_value_rows, full_value, preferred_element_type=jnp.float32)
    )
    grad_gain_first = jnp.sum(grad_mixed_first * normed_first, 0)
    grad_input_rows = grad_middle + norm_back(
        grad_mixed_first * full_gain_first.astype(jnp.float32), normed_first, scale_first
    )
    grad_inputs = grad_input_rows.reshape(inputs.shape)
    (
        shard_query,
        shard_key,
        shard_value,
        shard_output,
        shard_gain_first,
        shard_gate,
        shard_up,
        shard_down,
        shard_gain_second,
    ) = (
        lax.psum_scatter(grad_query, "seq", scatter_dimension=0, tiled=True),
        lax.psum_scatter(grad_key, "seq", scatter_dimension=0, tiled=True),
        lax.psum_scatter(grad_value, "seq", scatter_dimension=0, tiled=True),
        lax.psum_scatter(grad_out_proj, "seq", scatter_dimension=0, tiled=True),
        lax.psum_scatter(grad_gain_first, "seq", scatter_dimension=0, tiled=True),
        lax.psum_scatter(grad_gate, "seq", scatter_dimension=0, tiled=True),
        lax.psum_scatter(grad_up, "seq", scatter_dimension=0, tiled=True),
        lax.psum_scatter(grad_down, "seq", scatter_dimension=0, tiled=True),
        lax.psum_scatter(grad_gain_second, "seq", scatter_dimension=0, tiled=True),
    )
    summed = (
        lax.psum(shard_query.astype(jnp.bfloat16), "batch").astype(jnp.float32),
        lax.psum(shard_key.astype(jnp.bfloat16), "batch").astype(jnp.float32),
        lax.psum(shard_value.astype(jnp.bfloat16), "batch").astype(jnp.float32),
        lax.psum(shard_output.astype(jnp.bfloat16), "batch").astype(jnp.float32),
        lax.psum(shard_gain_first.astype(jnp.bfloat16), "batch").astype(jnp.float32),
        lax.psum(shard_gate.astype(jnp.bfloat16), "batch").astype(jnp.float32),
        lax.psum(shard_up.astype(jnp.bfloat16), "batch").astype(jnp.float32),
        lax.psum(shard_down.astype(jnp.bfloat16), "batch").astype(jnp.float32),
        lax.psum(shard_gain_second.astype(jnp.bfloat16), "batch").astype(jnp.float32),
    )
    grad_bias_total = lax.psum(grad_bias_local, ("batch", "seq"))
    return (
        block_output,
        grad_inputs,
        summed[0],
        summed[1],
        summed[2],
        summed[3],
        summed[4],
        summed[5],
        summed[6],
        summed[7],
        summed[8],
        grad_bias_total,
    )


ORDER_A = (0, 1, 2, 3)
ORDER_B = (0, 2, 1, 3)
FEATURES = 128
LSE_AT = 64
LOW = jnp.bfloat16
WIDE = jnp.float32


def swap(value, bit):
    return lax.ppermute(value, "batch", [(i, i ^ bit) for i in range(4)])


def after(value, *others):
    return lax.optimization_barrier((value, *others))[0]


def gather_plane(own):
    half = own.shape[0] // 2
    lower, upper = own[:half], own[half:]
    lower_pair = jnp.concatenate([lower, swap(lower, 1)], 0)
    upper_pair = jnp.concatenate([upper, swap(upper, 2)], 0)
    return lower_pair, swap(lower_pair, 2), upper_pair, swap(upper_pair, 1)


def scatter_first(chunks):
    return swap(chunks[1], 2), swap(chunks[3], 1)


def scatter_second(chunks, got):
    near_lower, _, near_upper, _ = chunks
    got_lower, got_upper = got
    half = near_lower.shape[0] // 2
    last_lower = swap(near_lower[half:] + got_lower[half:], 1)
    last_upper = swap(near_upper[half:] + got_upper[half:], 2)
    return (near_lower, got_lower, last_lower, near_upper, got_upper, last_upper)


def swap_pairs(own):
    half = own.shape[0] // 2
    return swap(own[:half], 1), swap(own[half:], 2)


def far_pairs(own, got):
    half = own.shape[0] // 2
    lower_pair = jnp.concatenate([own[:half], got[0]], 0)
    upper_pair = jnp.concatenate([own[half:], got[1]], 0)
    return lower_pair, swap(lower_pair, 2), upper_pair, swap(upper_pair, 1)


def over_seq(pieces):
    count, quarter, width = pieces.shape
    return lax.all_to_all(pieces, "seq", 0, 0, tiled=True).reshape(count * quarter, width)


def three_parts(value):
    high = value.astype(LOW)
    rest = value - high.astype(WIDE)
    middle = rest.astype(LOW)
    low = (rest - middle.astype(WIDE)).astype(LOW)
    return high, middle, low


def token_features(segments, variates):
    lane = lax.broadcasted_iota(jnp.int32, (segments.shape[0], FEATURES), 1)
    variate_hot = (lane < 12) & (lane % 4 == variates)
    ones = (lane >= 12) & (lane < 15)
    segment_lane = (lane >= 16) & (lane < LSE_AT)
    segment_hot = segment_lane & (lane - 16 == segments)
    segment_cold = segment_lane & (lane - 16 != segments)
    query_side = variate_hot | ones | segment_hot
    key_side = variate_hot | ones | segment_cold | ((lane >= LSE_AT) & (lane < LSE_AT + 3))
    return jnp.where(query_side, 1.0, 0.0).astype(LOW), jnp.where(key_side, 1.0, 0.0).astype(LOW)


def head_weights(same_bias, other_bias):
    gap = [part[:, None] for part in three_parts(same_bias - other_bias)]
    base = [part[:, None] for part in three_parts(other_bias)]
    heads = same_bias.shape[0]
    columns = [jnp.broadcast_to(part, (heads, 4)) for part in gap] + base
    columns.append(jnp.zeros((heads, 1), LOW))
    columns.append(jnp.full((heads, LSE_AT - 16), MASKED, LOW))
    columns.append(jnp.zeros((heads, FEATURES - LSE_AT), LOW))
    return jnp.concatenate(columns, 1)


def turn_pair(pair, cosine, sine):
    lane = lax.broadcasted_iota(jnp.int32, pair.shape, 1)
    crossed = jnp.where(lane % 64 < 32, pltpu.roll(pair, 96, 1), pltpu.roll(pair, 32, 1))
    return pair * cosine + crossed * sine


def dot_plain(left, right):
    return jnp.dot(left, right, preferred_element_type=WIDE)


def dot_rows(left, right):
    return lax.dot_general(left, right, (((1,), (1,)), ((), ())), preferred_element_type=WIDE)


def dot_first(left, right):
    return lax.dot_general(left, right, (((0,), (0,)), ((), ())), preferred_element_type=WIDE)


def whole_block():
    return pl.BlockSpec(memory_space=pltpu.VMEM)


def call(kernel, name, outs, specs, flops, moved, args, scratch=()):
    return pl.pallas_call(
        kernel,
        grid=(1,),
        out_shape=[jax.ShapeDtypeStruct(shape, dtype) for shape, dtype in outs],
        in_specs=specs,
        out_specs=[pl.BlockSpec(memory_space=pltpu.VMEM) for _ in outs],
        scratch_shapes=list(scratch),
        cost_estimate=pl.CostEstimate(flops=flops, bytes_accessed=moved, transcendentals=0),
        compiler_params=pltpu.CompilerParams(vmem_limit_bytes=56 * 2**20),
        name=name,
    )(*args)


class Copies:
    def __init__(self, ref, pairs, sems):
        self.ref = ref
        self.copies = [
            pltpu.make_async_copy(source, target, sems.at[k])
            for k, (source, target) in enumerate(pairs)
        ]
        self.started = self.waited = False

    def start(self, *which):
        self.started = True
        for k in which or range(len(self.copies)):
            self.copies[k].start()

    def wait(self):
        if not self.waited:
            for copy in self.copies:
                copy.wait()
        self.waited = True
        return self.ref

    def _at(self, index, act):
        for k, copy in enumerate(self.copies):
            pl.when(index == k)(functools.partial(act, copy))

    def start_at(self, index):
        self.started = True
        self._at(index, lambda copy: copy.start())

    def wait_at(self, index):
        self.waited = True
        self._at(index, lambda copy: copy.wait())

    def wait_first(self, index):
        if not self.waited:
            self.waited = True

            @pl.when(index == 0)
            def _():
                for copy in self.copies:
                    copy.wait()

        return self.ref


class Plan:
    def __init__(self, arrays, shape, pairs, count):
        self.arrays, self.shape, self.pairs, self.count = arrays, shape, pairs, count


def whole(array, column=None, width=None):
    shape = array.shape if column is None else (array.shape[0], width)

    def pairs(refs, buffer):
        if column is None:
            return [(refs[0], buffer)]
        return [(refs[0].at[:, pl.ds(column, width)], buffer)]

    return Plan([array], shape, pairs, 1)


def top(array):
    half = array.shape[0] // 2
    return Plan(
        [array],
        (half, *array.shape[1:]),
        lambda refs, buffer: [(refs[0].at[pl.ds(0, half)], buffer)],
        1,
    )


def rows_of(array, count=4):
    size = array.shape[0] // count
    return Plan(
        [array],
        (count, size, array.shape[1]),
        lambda refs, buffer: [
            (refs[0].at[pl.ds(k * size, size)], buffer.at[k]) for k in range(count)
        ],
        count,
    )


def columns_of(array, count=4, column=0, width=None):
    size = (width or array.shape[1]) // count
    return Plan(
        [array],
        (count, array.shape[0], size),
        lambda refs, buffer: [
            (refs[0].at[:, pl.ds(column + k * size, size)], buffer.at[k]) for k in range(count)
        ],
        count,
    )


def group(arrays, column=None, width=None):
    rows = arrays[0].shape[0]

    def pairs(refs, buffer):
        if column is None:
            return [(ref, buffer.at[k]) for k, ref in enumerate(refs)]
        return [(ref.at[:, pl.ds(column, width)], buffer.at[k]) for k, ref in enumerate(refs)]

    return Plan(
        list(arrays), (len(arrays), rows, width or arrays[0].shape[1]), pairs, len(arrays)
    )


def out_rows(shape, dtype, count=4):
    size = shape[0] // count

    def pairs(refs, buffer):
        return [(buffer.at[k], refs[0].at[pl.ds(k * size, size)]) for k in range(count)]

    return Plan([(shape, dtype)], (count, size, *shape[1:]), pairs, count)


def out_group(shape, dtype, count=4):
    def pairs(refs, buffer):
        return [(buffer.at[k], ref) for k, ref in enumerate(refs)]

    return Plan([(shape, dtype)] * count, (count, *shape), pairs, count)


def out_whole(shape, dtype):
    return Plan([(shape, dtype)], shape, lambda refs, buffer: [(buffer, refs[0])], 1)


def run(body, name, us, ins, outs, scratch=(), token=None):
    args, in_specs, out_shapes, out_specs, buffers = [], [], [], [], []
    named = len(ins)
    if token is not None:
        ins = [*ins, token]
    for item in ins:
        if isinstance(item, Plan):
            args += item.arrays
            in_specs += [pl.BlockSpec(memory_space=pl.ANY)] * len(item.arrays)
            buffers.append(pltpu.VMEM(item.shape, item.arrays[0].dtype))
            buffers.append(pltpu.SemaphoreType.DMA((item.count,)))
        else:
            args.append(item)
            space = pltpu.SMEM if item.shape == (1,) else pltpu.VMEM
            in_specs.append(pl.BlockSpec(memory_space=space))
    for item in outs:
        if isinstance(item, Plan):
            out_shapes += [jax.ShapeDtypeStruct(*each) for each in item.arrays]
            out_specs += [pl.BlockSpec(memory_space=pl.ANY)] * len(item.arrays)
            buffers.append(pltpu.VMEM(item.shape, item.arrays[0][1]))
            buffers.append(pltpu.SemaphoreType.DMA((item.count,)))
        else:
            out_shapes.append(jax.ShapeDtypeStruct(*item))
            out_specs.append(pl.BlockSpec(memory_space=pltpu.VMEM))
    n_in, n_out = len(args), len(out_shapes)

    def kernel(*refs):
        given, rest = list(refs[: n_in + n_out]), list(refs[n_in + n_out :])
        bound = []
        for item in (*ins, *outs):
            if isinstance(item, Plan):
                near = [given.pop(0) for _ in item.arrays]
                buffer, sems = rest.pop(0), rest.pop(0)
                bound.append(Copies(buffer, item.pairs(near, buffer), sems))
            else:
                bound.append(given.pop(0))
        body(*bound[:named], *bound[len(ins) :], *rest)
        for item in bound[: len(ins)]:
            if isinstance(item, Copies):
                item.wait()
        for item in bound[len(ins) :]:
            if isinstance(item, Copies) and not item.started:
                item.start()
        for item in bound[len(ins) :]:
            if isinstance(item, Copies):
                item.wait()

    return pl.pallas_call(
        kernel,
        out_shape=out_shapes,
        in_specs=in_specs,
        out_specs=out_specs,
        scratch_shapes=buffers + list(scratch),
        cost_estimate=pl.CostEstimate(
            flops=int(us * 1.15e9), bytes_accessed=2**20, transcendentals=0
        ),
        compiler_params=pltpu.CompilerParams(vmem_limit_bytes=60 * 2**20),
        name=name,
    )(*args)


def output_weights(pieces):
    rows = pieces[0].shape[0] // 2
    places = {
        0: ((0, 0), (0, 1), (1, 0), (1, 1)),
        1: ((2, 0), (3, 0), (2, 1), (3, 1)),
    }

    def pairs(refs, buffer):
        rank = lax.axis_index("batch")
        out = []
        for half in range(2):
            for r, (which, part) in enumerate(places[half]):
                to = pl.ds(pl.multiple_of((rank ^ r) * 256, 256), 256)
                out.append(
                    (
                        refs[which].at[pl.ds(part * rows, rows)],
                        buffer.at[pl.ds(half * rows, rows), to],
                    )
                )
        return out

    return Plan(list(pieces), (2 * rows, D), pairs, 8)


def start_all(*items):
    for item in items:
        item.start()


def unit_rows(rows):
    return lax.rsqrt(jnp.mean(rows * rows, -1, keepdims=True) + EPSILON)


def pack_body(
    rank_ref, x, cot, segment_ref, variate_ref, position_ref, wq, wk, wv, wo, gain_first_ref,
    gain_second_ref, gate, up, down, rows_out, shard_out, gate_up_out, down_out,
):
    start_all(wq, wk, wv, wo, x, cot, gate, up, down)
    micro, _, quarter, _ = x.ref.shape
    tokens = 4 * quarter
    lane = lax.broadcasted_iota(jnp.int32, (tokens, 128), 1)
    on_line = lax.broadcasted_iota(jnp.int32, (tokens, 128), 0) == lane

    def upright(row):
        return jnp.sum(jnp.where(on_line, row, 0.0), 1, keepdims=True)

    gains = jnp.where(
        lane == 0,
        upright(gain_first_ref[...].astype(WIDE)),
        jnp.where(lane == 1, upright(gain_second_ref[...].astype(WIDE)), 0.0),
    )
    shard_out.ref[:, D:] = gains.astype(LOW)
    for place, weight in enumerate((wq, wk, wv, wo)):
        shard_out.ref[:, 256 * place : 256 * (place + 1)] = weight.wait()[...]
    shard_out.start()
    for m in range(micro):
        places = position_ref[m : m + 1, :]
        numbers = jnp.zeros((tokens, 128), WIDE)
        for place, row in enumerate(
            (
                segment_ref[m : m + 1, :],
                variate_ref[m : m + 1, :],
                lax.shift_right_logical(places, 5),
                places & 31,
            )
        ):
            numbers = jnp.where(lane == place, upright(row.astype(WIDE)), numbers)
        numbers = numbers.astype(LOW)
        for r in range(4):
            rows_out.ref[r, 0, m, :, D:] = numbers[r * quarter : (r + 1) * quarter, :]
            rows_out.ref[r, 1, m, :, D:] = jnp.zeros((quarter, 128), LOW)
    x_ref, cot_ref = x.wait(), cot.wait()
    for m in range(micro):
        for r in range(4):
            rows_out.ref[r, 0, m, :, :D] = x_ref[m, r]
            rows_out.ref[r, 1, m, :, :D] = cot_ref[m, r]
    rows_out.start()
    gate_ref, up_ref = gate.wait(), up.wait()
    per = gate_up_out.ref.shape[1] // 2
    piece = gate_ref.shape[2]
    for s in range(per // piece):
        gate_up_out.ref[:, s * piece : (s + 1) * piece] = gate_ref[s]
        gate_up_out.ref[:, per + s * piece : per + (s + 1) * piece] = up_ref[s]
    gate_up_out.start()
    down_out.ref[...] = down.wait()[...]


def pack(rank, x, cot, segments, variates, positions, shards, gains, w_gate, w_up, w_down):
    micro, tokens, _ = x.shape
    quarter = tokens // 4
    shard, ff = w_gate.shape
    piece = w_down.shape[0] // 4
    pieces = ff // 4 // piece

    def quarters(array):
        return array.reshape(micro, 4, quarter, D)

    def mine(array, size, refs_at):
        return Plan([array], size, refs_at, 1)

    def rank_columns(array):
        def pairs(refs, buffer):
            at = pl.multiple_of(lax.axis_index("batch") * 256, 256)
            return [(refs[0].at[:, pl.ds(at, 256)], buffer)]

        return Plan([array], (shard, 256), pairs, 1)

    def feed_columns(array):
        def pairs(refs, buffer):
            rank = lax.axis_index("batch")
            return [
                (refs[0].at[:, pl.ds(pl.multiple_of((4 * s + rank) * piece, piece), piece)], buffer.at[s])
                for s in range(pieces)
            ]

        return Plan([array], (pieces, shard, piece), pairs, pieces)

    def down_rows(array):
        def pairs(refs, buffer):
            at = pl.multiple_of(lax.axis_index("batch") * piece, piece)
            return [(refs[0].at[pl.ds(at, piece)], buffer)]

        return Plan([array], (piece, D), pairs, 1)

    return run(
        pack_body,
        "pack",
        4,
        [rank, whole(quarters(x)), whole(quarters(cot)), segments, variates, positions]
        + [rank_columns(weight) for weight in shards]
        + [*gains, feed_columns(w_gate), feed_columns(w_up), down_rows(w_down)],
        [
            out_whole((4, 2, micro, quarter, D + 128), LOW),
            out_whole((shard, D + 128), LOW),
            out_whole((shard, ff // 2), LOW),
            out_whole((piece, D), LOW),
        ],
    )


def attend_body(
    x, qkv, gains, freqs_ref, weights_ref,
    gain_ref, mixed, turned, wide, lower, upper, logs, cos, sin, query_sides, key_sides,
    keys_ref, values_ref, trig_ref,
):
    start_all(x, gains, qkv)
    count, chunk, _ = x.ref.shape
    lane = lax.broadcasted_iota(jnp.int32, (chunk, 128), 1)
    half_lane = lane // 64
    pick = lax.broadcasted_iota(jnp.int32, (16, 128), 0) == lax.broadcasted_iota(
        jnp.int32, (16, 128), 1
    )
    x_ref = x.wait()
    angles = jnp.zeros((chunk, 128), WIDE)
    for k in range(count):
        numbers = x_ref[k, :, D : D + 128].astype(WIDE)
        places = numbers[:, 2:3] * 32.0 + numbers[:, 3:4]
        angles = jnp.where(lane // 32 == k, places * freqs_ref[...], angles)
    trig_ref[0] = jnp.cos(angles)
    trig_ref[1] = jnp.sin(angles)
    gain_ref[...] = dot_rows(jnp.where(pick, 1.0, 0.0).astype(LOW), gains.wait()[...])
    qkv_ref = qkv.wait()

    def one_chunk(index, carry):
        rows = x_ref[index, :, :D].astype(WIDE)
        mixed_rows = (rows * unit_rows(rows) * gain_ref[0:1, :]).astype(LOW)
        mixed.ref[index] = mixed_rows

        def spread(packed):
            own = jnp.where(lane // 32 == index, packed, 0.0)
            own = own + pltpu.roll(own, 64, 1)
            return own + pltpu.roll(own, 32, 1)

        cosine = spread(trig_ref[0])
        sine = spread(trig_ref[1])
        sine = jnp.where(lane % 64 < 32, -sine, sine)
        cos.ref[index] = cosine
        sin.ref[index] = sine
        numbers = x_ref[index, :, D : D + 128].astype(WIDE).astype(jnp.int32)
        query_side, key_side = token_features(numbers[:, 0:1], numbers[:, 1:2])
        query_sides.ref[index] = query_side
        key_sides.ref[index] = key_side
        proj = dot_plain(mixed_rows, qkv_ref[...])
        values = proj[:, 512:].astype(LOW)
        turned.ref[index, :, 512:768] = values
        for pair in range(2):
            at = 128 * pair
            turned.ref[index, :, at : at + 128] = turn_pair(
                proj[:, at : at + 128], cosine, sine
            ).astype(LOW)
            keys = turn_pair(proj[:, 256 + at : 384 + at], cosine, sine).astype(LOW)
            turned.ref[index, :, 256 + at : 384 + at] = keys
            here = pl.ds(pl.multiple_of(index * chunk, chunk), chunk)
            keys_ref[pair, here, :128] = keys
            keys_ref[pair, here, 128:] = key_side
            values_ref[pair, here, :128] = values[:, at : at + 128]
            values_ref[pair, here, 128:] = jnp.where(lane == 0, 1.0, 0.0).astype(LOW)
        return carry

    lax.fori_loop(0, count, one_chunk, 0)
    start_all(mixed, turned, cos, sin, query_sides, key_sides)

    def one_block(index, carry):
        side = query_sides.ref[index]
        log_rows = jnp.zeros((chunk, 128), WIDE)
        here = pl.ds(pl.multiple_of((index % 2) * chunk, chunk), chunk)
        def scores_of(head):
            at = 128 * (head // 2)
            scaled = turned.ref[index, :, at : at + 128] * LOW(SCORE_SCALE)
            query = jnp.concatenate(
                [
                    jnp.where(half_lane == head % 2, scaled, LOW(0)),
                    side * weights_ref[head : head + 1, :],
                ],
                1,
            )
            return dot_rows(query, keys_ref[head // 2])

        scores = scores_of(0)
        parts = []
        for head in range(4):
            high = jnp.max(scores, 1, keepdims=True)
            powers = jnp.exp(scores - high).astype(LOW)
            if head < 3:
                scores = scores_of(head + 1)
            summed = dot_plain(powers, values_ref[head // 2])
            total = summed[:, 128:129]
            parts.append(summed[:, :128] / total)
            log_rows = jnp.where(lane == head, high + jnp.log(total), log_rows)
        for pair in range(2):
            at = 128 * pair
            total_mixed = jnp.where(half_lane == 0, parts[2 * pair], parts[2 * pair + 1])
            wide.ref[index, :, at : at + 128] = total_mixed
            low_rows = total_mixed.astype(LOW)

            @pl.when(index < 2)
            def _(low_rows=low_rows, at=at):
                lower.ref[here, at : at + 128] = low_rows

            @pl.when(index >= 2)
            def _(low_rows=low_rows, at=at):
                upper.ref[here, at : at + 128] = low_rows

        logs.ref[index] = log_rows
        logs.start_at(index)
        wide.start_at(index)
        return carry

    lax.fori_loop(0, count, one_block, 0)


def attend(chunks, first_weights, freqs, weights, token):
    chunk = chunks[0].shape[0]
    length = 4 * chunk
    return run(
        attend_body,
        "attend",
        15,
        [
            group(chunks),
            whole(first_weights, 0, 768),
            whole(first_weights, D, 128),
            freqs,
            weights,
        ],
        [
            ((16, D), WIDE),
            out_rows((length, D), LOW),
            out_rows((length, 768), LOW),
            out_rows((length, 256), WIDE),
            out_whole((length // 2, 256), LOW),
            out_whole((length // 2, 256), LOW),
            out_rows((length, 128), WIDE),
            out_rows((length, 128), WIDE),
            out_rows((length, 128), WIDE),
            out_rows((length, FEATURES), LOW),
            out_rows((length, FEATURES), LOW),
        ],
        [pltpu.VMEM((2, length, 256), LOW)] * 2 + [pltpu.VMEM((2, chunk, 128), WIDE)],
        token,
    )


def middle_body(rank_ref, x, near, far, wo, gain_ref, heads, own, mixed):
    rank = rank_ref[0]
    start_all(near, far, wo, x)
    count, chunk, _ = x.ref.shape
    block = chunk // 2
    near_ref, far_ref = near.wait(), far.wait()
    width = near_ref.shape[2]
    sources = {
        0: ((near_ref, 0, 0), (near_ref, 2, 0), (far_ref, 0, 0), (far_ref, 0, width)),
        1: ((near_ref, 1, 0), (far_ref, 1, 0), (near_ref, 3, 0), (far_ref, 1, width)),
    }
    for half, order in enumerate((ORDER_A, ORDER_B)):
        for q in range(4):
            ref, which, column = sources[half][q]
            for place, r in enumerate(order):
                start = order.index(r ^ q) * block
                heads.ref[
                    2 * half + place // 2,
                    place % 2 * block : (place % 2 + 1) * block,
                    q * width : (q + 1) * width,
                ] = ref[which, start : start + block, column : column + width]
    heads.start()
    wo_ref = wo.wait()

    def one_chunk(index, carry):
        x.wait_at(index)
        total = x.ref[index, :, :D].astype(WIDE)
        for q in range(4):
            rows = pl.ds(pl.multiple_of((rank ^ q) * width, width), width)
            total = total + dot_plain(
                heads.ref[index, :, q * width : (q + 1) * width], wo_ref[rows, :]
            )

        @pl.when(index % 2 == 0)
        def _():
            own.ref[index // 2] = total[:block]
            own.start_at(index // 2)

        mixed.ref[index] = (total * unit_rows(total) * gain_ref[1:2, :]).astype(LOW)
        mixed.start_at(index)
        return carry

    lax.fori_loop(0, count, one_chunk, 0)


def middle(rank, chunks, heads, out_pieces, gain):
    chunk = chunks[0].shape[0]
    length = 4 * chunk
    lower, lower_x, lower_far, upper, upper_y, upper_far = heads
    return run(
        middle_body,
        "middle",
        7,
        [
            rank,
            group(chunks),
            group((lower, upper, lower_x, upper_y)),
            group((lower_far, upper_far)),
            output_weights(out_pieces),
            gain,
        ],
        [out_rows((length, D), LOW), out_rows((chunk, D), WIDE, 2), out_rows((length, D), LOW)],
    )


def feed_body(mixed, gate_up, both, hidden):
    count, _, per = hidden.ref.shape
    mixed.start(0)
    gate_up.start(0, 2)
    mixed.start(1, 2, 3)
    gate_up.start(1, 3)
    for half in range(2):
        here = slice(half * per // 2, (half + 1) * per // 2)
        there = slice(per + half * per // 2, per + (half + 1) * per // 2)

        def one_chunk(index, carry, half=half, here=here, there=there):
            if half == 0:
                mixed.wait_at(index)

            @pl.when(index == 0)
            def _():
                for k in (half, 2 + half):
                    gate_up.copies[k].wait()

            rows = mixed.ref[index]
            gate = dot_plain(rows, gate_up.ref[half])
            up = dot_plain(rows, gate_up.ref[2 + half])
            sigmoid = 1.0 / (1.0 + jnp.exp(-gate))
            silu = gate * sigmoid
            both.ref[index, :, here] = (up * (sigmoid + silu * (1.0 - sigmoid))).astype(LOW)
            both.ref[index, :, there] = silu.astype(LOW)
            hidden.ref[index, :, here] = (silu * up).astype(LOW)
            if half == 1:
                both.start_at(index)
                hidden.start_at(index)
            return carry

        lax.fori_loop(0, count, one_chunk, 0)
    gate_up.waited = True


def feed(mixed, gate_up, token):
    length = mixed.shape[0]
    per = gate_up.shape[1] // 2
    return run(
        feed_body,
        "feed",
        8,
        [rows_of(mixed), columns_of(gate_up)],
        [out_rows((length, 2 * per), LOW), out_rows((length, per), LOW)],
        token=token,
    )


def feed_back_body(both, cots, gate_up, down, grads, back, later=()):
    start_all(down)
    cots.start(0)
    both.start(0)
    gate_up.start()
    cots.start(1)
    both.start(1)
    start_all(*later)
    per = down.ref.shape[0]

    def one_chunk(index, carry):
        cots.wait_at(index)
        both.wait_at(index)
        grad_hidden = dot_rows(cots.ref[index], down.wait_first(index)[...])
        grads.ref[index, :, :per] = (grad_hidden * both.ref[index, :, :per].astype(WIDE)).astype(LOW)
        grads.ref[index, :, per:] = (grad_hidden * both.ref[index, :, per:].astype(WIDE)).astype(LOW)
        grads.start_at(index)
        back.ref[index] = dot_rows(grads.ref[index], gate_up.wait_first(index)[...]).astype(LOW)
        back.start_at(index)
        return carry

    lax.fori_loop(0, 2, one_chunk, 0)


def feed_back_far_body(both, cots, gate_up, down, hidden, near_cots, grads, back, out):
    feed_back_body(both, cots, gate_up, down, grads, back, (hidden, near_cots))
    near_ref, far_ref = near_cots.wait(), cots.ref
    chunk = near_ref.shape[1]

    def one_part(index, carry):
        hidden.wait_at(index)
        total = None
        for k in range(4):
            more = dot_first(
                hidden.ref[index, k * chunk : (k + 1) * chunk, :], (near_ref, far_ref)[k % 2][k // 2]
            )
            total = more if total is None else total + more
        out.ref[index] = total.astype(LOW)
        out.start_at(index)
        return carry

    lax.fori_loop(0, hidden.ref.shape[0], one_part, 0)


def feed_back(first, both, cots, gate_up, down, token, hidden=None):
    length = both.shape[0]
    chunk = length // 4
    per = down.shape[0]

    def pairs(refs, buffer):
        return [
            (refs[0].at[pl.ds((first + 2 * k) * chunk, chunk)], buffer.at[k]) for k in range(2)
        ]

    ins = [Plan([both], (2, chunk, 2 * per), pairs, 2), group((cots[first], cots[first + 2]))]
    ins += [whole(gate_up), whole(down)]
    outs = [out_rows((length // 2, 2 * per), LOW, 2), out_group((chunk, D), LOW, 2)]
    if hidden is None:
        return run(feed_back_body, "feed_back", 7, ins, outs, token=token)
    ins += [columns_of(hidden), group((cots[0], cots[2]))]
    outs += [out_rows((per, D), LOW)]
    return run(feed_back_far_body, "feed_back", 12, ins, outs, token=token)


def sum_arrived(near, got, last):
    return (
        near.wait()[...].astype(WIDE) + got.wait()[...].astype(WIDE) + last.wait()[...].astype(WIDE)
    )


def arrivals(sums):
    return [whole(x) if place % 3 == 2 else top(x) for place, x in enumerate(sums)]


def own_back_body(
    rank_ref, n0, g0, l0, n1, g1, l1, middle_rows, cot, gain_ref, wo, grad, parcels
):
    rank = rank_ref[0]
    start_all(n0, g0, l0, middle_rows, cot, n1, g1, l1, wo)
    block = l0.ref.shape[0]
    width = parcels.ref.shape[2] // 2
    for place, sums in enumerate(((n0, g0, l0), (n1, g1, l1))):
        rows = slice(place * block, (place + 1) * block)
        arrived = sum_arrived(*sums)
        y = middle_rows.wait()[rows, :]
        scale = unit_rows(y)
        normed = y * scale
        turned = arrived * gain_ref[1:2, :]
        grad.ref[rows, :] = cot.wait()[rows, :].astype(WIDE) + scale * (
            turned - normed * jnp.mean(turned * normed, -1, keepdims=True)
        )
    grad.start()
    low_grad = grad.ref[...].astype(LOW)
    wo_ref = wo.wait()
    for q in range(4):
        place = pl.ds(pl.multiple_of((rank ^ q) * width, width), width)
        parcels.ref[q, :, :width] = dot_rows(low_grad, wo_ref[place, :]).astype(LOW)
        parcels.ref[q, :, width:] = grad.ref[:, place].astype(LOW)
        parcels.start(q)


def own_back(rank, sums, middle_own, cot_own, gain, out_pieces, token):
    quarter = cot_own.shape[0]
    return run(
        own_back_body,
        "own_back",
        4,
        [rank, *arrivals(sums), whole(middle_own), whole(cot_own), gain]
        + [output_weights(out_pieces)],
        [out_whole((quarter, D), WIDE), out_group((quarter, 512), LOW)],
        token=token,
    )


def attend_back_body(
    parcels, turned, wide, logs, cos, sin, query_sides, key_sides, weights_ref, projections,
    out, bias_ref, back, queries_ref, grads_ref, total_ref,
):
    start_all(parcels, turned, query_sides, logs, wide, key_sides, cos, sin, projections)
    length = turned.ref.shape[0]
    chunk = length // 4
    block = chunk // 2
    half_lane = lax.broadcasted_iota(jnp.int32, (chunk, 128), 1) // 64
    lane = lax.broadcasted_iota(jnp.int32, (chunk, 128), 1)
    parcels_ref = parcels.wait()
    for half, order in enumerate((ORDER_A, ORDER_B)):
        for place in range(4):
            to = slice((4 * half + place) * block, (4 * half + place + 1) * block)
            rows = slice(half * block, (half + 1) * block)
            for head in range(4):
                at = 128 * (head // 2)
                grads_ref[head, to, :128] = parcels_ref[order[place], rows, at : at + 128]
    turned_ref, side_ref, log_ref, wide_ref = (
        turned.wait(), query_sides.wait(), logs.wait(), wide.wait()
    )

    def prepare(index, carry):
        rows = pl.ds(pl.multiple_of(index * chunk, chunk), chunk)
        for pair in range(2):
            at = 128 * pair
            product = grads_ref[2 * pair, rows, :128].astype(WIDE) * wide_ref[rows, at : at + 128]
            scaled = turned_ref[rows, at : at + 128] * LOW(SCORE_SCALE)
            for half in range(2):
                head = 2 * pair + half
                side = side_ref[rows, :] * weights_ref[head : head + 1, :]
                for place, piece in enumerate(three_parts(-log_ref[rows, head : head + 1])):
                    side = jnp.where(lane == LSE_AT + place, piece, side)
                queries_ref[head, rows, :128] = jnp.where(half_lane == half, scaled, LOW(0))
                queries_ref[head, rows, 128:] = side
                delta = jnp.sum(jnp.where(half_lane == half, product, 0.0), 1, keepdims=True)
                extra = jnp.zeros((chunk, 128), LOW)
                for place, piece in enumerate(three_parts(-delta)):
                    extra = jnp.where(lane == place, piece, extra)
                grads_ref[head, rows, 128:] = extra
        total_ref[rows, :] = jnp.zeros((chunk, 256), WIDE)
        return carry

    lax.fori_loop(0, 4, prepare, 0)
    three_ones = jnp.where(lane < 3, 1.0, 0.0).astype(LOW)
    key_ref, cos_ref, sin_ref = key_sides.wait(), cos.wait(), sin.wait()

    def one_block(index, carry):
        rows = pl.ds(pl.multiple_of(index * chunk, chunk), chunk)
        cosine = cos_ref[rows, :]
        sine = -sin_ref[rows, :]
        key_side = key_ref[rows, :]
        first_four = jnp.where(lane < 4, key_side.astype(WIDE), 0.0)
        sums = list(carry)
        for pair in range(2):
            at = 128 * pair
            keys = turned_ref[rows, 256 + at : 384 + at]
            values = turned_ref[rows, 512 + at : 640 + at]
            keys_wide = jnp.concatenate([keys, key_side], 1)
            grad_keys = jnp.zeros((chunk, 128), WIDE)
            grad_values = jnp.zeros((chunk, 128), WIDE)
            for half in range(2):
                head = 2 * pair + half
                mine = half_lane == half
                weights = jnp.exp(dot_rows(keys_wide, queries_ref[head]))
                grad_weights = dot_rows(
                    jnp.concatenate([jnp.where(mine, values, LOW(0)), three_ones], 1),
                    grads_ref[head],
                )
                grad_values = jnp.where(
                    mine, dot_plain(weights.astype(LOW), grads_ref[head, :, :128]), grad_values
                )
                grad_scores = (weights * grad_weights).astype(LOW)
                both = dot_plain(
                    grad_scores,
                    jnp.concatenate([queries_ref[head, :, :128], side_ref[...]], 1),
                )
                grad_keys = grad_keys + both[:, :128]
                counted = both[:, 128:]
                same = jnp.sum(counted * first_four, 0, keepdims=True)
                every = jnp.sum(jnp.where(lane < 4, counted, 0.0), 0, keepdims=True)
                sums[head] = sums[head] + same
                sums[4 + head] = sums[4 + head] + (every - same)
                total_ref[:, at : at + 128] += dot_first(
                    grad_scores, jnp.where(mine, keys, LOW(0))
                )
            out.ref[index, :, 256 + at : 384 + at] = turn_pair(grad_keys, cosine, sine).astype(LOW)
            out.ref[index, :, 512 + at : 640 + at] = grad_values.astype(LOW)
        return tuple(sums)

    start = tuple(jnp.zeros((1, 128), WIDE) for _ in range(8))
    sums = lax.fori_loop(0, 4, one_block, start)
    for place in range(8):
        bias_ref[place : place + 1, :] = sums[place]
    projections_ref = projections.wait()

    def one_chunk(index, carry):
        rows = pl.ds(pl.multiple_of(index * chunk, chunk), chunk)
        for pair in range(2):
            at = 128 * pair
            out.ref[index, :, at : at + 128] = turn_pair(
                total_ref[rows, at : at + 128] * SCORE_SCALE, cos_ref[rows, :], -sin_ref[rows, :]
            ).astype(LOW)
        out.start_at(index)
        back.ref[index] = dot_rows(out.ref[index], projections_ref[...]).astype(LOW)
        back.start_at(index)
        return carry

    lax.fori_loop(0, 4, one_chunk, 0)


def attend_back(parcels, kept, weights, first_weights, token):
    turned, attended, *others = kept
    length = turned.shape[0]
    return run(
        attend_back_body,
        "attend_back",
        80,
        [group(parcels, 0, 256), whole(turned), whole(attended)]
        + [whole(x) for x in others]
        + [weights, whole(first_weights, 0, 768)],
        [out_rows((length, 768), LOW), ((8, 128), WIDE), out_group((length // 4, D), LOW)],
        [
            pltpu.VMEM((4, length, 256), LOW),
            pltpu.VMEM((4, length, 256), LOW),
            pltpu.VMEM((length, 256), WIDE),
        ],
        token,
    )


def gate_up_grads_body(mixed, near, far, out):
    mixed.start(0)
    for k in range(2):
        near.start(k)
        far.start(k)
    mixed.start(1, 2, 3)
    near.waited = far.waited = True
    chunk = mixed.ref.shape[1] // 4

    def one_part(index, carry):
        mixed.wait_at(index)
        total = None
        for k in range(4):
            item = (near, far)[k % 2]

            @pl.when(index == 0)
            def _(item=item, k=k):
                item.copies[k // 2].wait()

            more = dot_first(
                mixed.ref[index, k * chunk : (k + 1) * chunk, :], item.ref[k // 2]
            )
            total = more if total is None else total + more
        out.ref[index] = total.astype(LOW)
        out.start_at(index)
        return carry

    lax.fori_loop(0, mixed.ref.shape[0], one_part, 0)


def gate_up_grads(mixed, near, far, token):
    return run(
        gate_up_grads_body,
        "gate_up_grads",
        8,
        [columns_of(mixed), rows_of(near, 2), rows_of(far, 2)],
        [out_rows((D, near.shape[1]), LOW)],
        token=token,
    )[0]


def feed_out_body(hidden, down, out):
    start_all(down, hidden)
    block = out.ref.shape[1]

    def one_chunk(index, carry):
        down_ref = down.wait_first(index)
        hidden.wait_at(index)
        total = dot_plain(hidden.ref[index], down_ref[...]).astype(LOW)
        for p in range(2):
            q = jnp.where(index < 2, 2 * index + p, index - 2 + 2 * p)
            out.ref[2 * q + index // 2] = total[p * block : (p + 1) * block]
            out.start_at(2 * q + index // 2)
        return carry

    lax.fori_loop(0, hidden.ref.shape[0], one_chunk, 0)


def feed_out(hidden, down, token):
    length = hidden.shape[0]
    block = length // 8

    def pairs(refs, buffer):
        return [
            (buffer.at[2 * q + half], ref.at[pl.ds(half * block, block)])
            for q, ref in enumerate(refs)
            for half in range(2)
        ]

    return run(
        feed_out_body,
        "feed_out",
        5,
        [rows_of(hidden), whole(down)],
        [Plan([((2 * block, D), LOW)] * 4, (8, block, D), pairs, 8)],
        token=token,
    )


def own_last_body(n0, g0, l0, n1, g1, l1, forward, x, base, middle_rows, gain_ref, out):
    start_all(n0, g0, l0, x, base, forward, middle_rows, n1, g1, l1)
    block = l0.ref.shape[0]
    piece = out.ref.shape[1] // 2
    each = block // piece
    for half, back in enumerate(((n0, g0, l0), (n1, g1, l1))):
        rows = slice(half * block, (half + 1) * block)
        places = slice(half * each, (half + 1) * each)
        turned = sum_arrived(*back) * gain_ref[0:1, :]
        x_rows = x.wait()[rows, :D].astype(WIDE)
        scale = unit_rows(x_rows)
        normed = x_rows * scale
        grad = base.wait()[rows, :] + scale * (
            turned - normed * jnp.mean(turned * normed, -1, keepdims=True)
        )
        out.ref[places, :piece, :] = grad.astype(LOW).reshape(each, piece, D)
        block_rows = middle_rows.wait()[rows, :]
        forward_ref = forward.wait()
        for q in range(4):
            block_rows = block_rows + forward_ref[q, rows, :].astype(WIDE)
        out.ref[places, piece:, :] = block_rows.astype(LOW).reshape(each, piece, D)


def own_last(sums, outs, mine, base, middle_own, gain, n_seq, token):
    quarter = base.shape[0]
    return run(
        own_last_body,
        "own_last",
        80,
        [*arrivals(sums), group(outs), whole(mine), whole(base), whole(middle_own), gain],
        [out_whole((n_seq, 2 * quarter // n_seq, D), LOW)],
        token=token,
    )[0]


def join_body(left, right, out):
    start_all(left, right)
    width = left.ref.shape[1]
    out.ref[:, :width] = left.wait()[...]
    out.ref[:, width:] = right.wait()[...]


def join(left, right, token):
    rows = left.shape[0]
    return run(
        join_body,
        "join",
        1,
        [whole(left), whole(right)],
        [out_whole((rows, left.shape[1] + right.shape[1]), LOW)],
        token=token,
    )[0]


def first_grads_body(rank_ref, mixed, proj, heads, parcels, bias_ref, out, branch_ref):
    rank = rank_ref[0]
    start_all(mixed, proj, parcels, heads)
    width = proj.ref.shape[1]
    block = parcels.ref.shape[1] // 2
    parcels_ref = parcels.wait()
    for half, order in enumerate((ORDER_A, ORDER_B)):
        for place in range(4):
            to = slice((4 * half + place) * block, (4 * half + place + 1) * block)
            branch_ref[to, :] = parcels_ref[order[place], half * block : (half + 1) * block, :]
    mixed_ref, proj_ref, heads_ref = mixed.wait(), proj.wait(), heads.wait()

    def one_part(index, carry):
        out.ref[index, :, :width] = dot_first(mixed_ref[index], proj_ref[...]).astype(LOW)
        out.ref[rank ^ index, :, width : width + 256] = dot_first(
            heads_ref[index], branch_ref[...]
        ).astype(LOW)
        out.ref[index, :, width + 256 :] = bias_ref[...]
        return carry

    lax.fori_loop(0, 4, one_part, 0)


def first_grads(rank, mixed, proj, heads, parcels, bias_rows, token):
    length = mixed.shape[0]
    return run(
        first_grads_body,
        "first_grads",
        8,
        [rank, columns_of(mixed), whole(proj), columns_of(heads)]
        + [group(parcels, 256, 256), bias_rows],
        [out_rows((D, 768 + 256 + 128), LOW)],
        [pltpu.VMEM((length, 256), LOW)],
        token,
    )[0]


def rank_blocks(lower, lower_far, upper, upper_far):
    half = lower.shape[0] // 2
    return (
        ((lower, 0), (upper, 0)),
        ((lower, half), (upper_far, 0)),
        ((lower_far, 0), (upper, half)),
        ((lower_far, half), (upper_far, half)),
    )


def lay_flat(column, part):
    count = column.shape[0]
    row = lax.broadcasted_iota(jnp.int32, (count, 128), 0) + part * count
    lane = lax.broadcasted_iota(jnp.int32, (count, 128), 1)
    return jnp.sum(jnp.where(row == lane, column, 0.0), 0, keepdims=True)


def spread_feed_kernel(
    rank_ref, lower, lower_far, upper, upper_far, gate_ref, up_ref, gain_ref,
    grad_gate_ref, grad_up_ref, grad_down_ref, grad_gain_ref,
):
    rank = rank_ref[0]
    half = lower.shape[0] // 2
    piece = 128
    ff = gate_ref.shape[1]
    per = ff // 4
    for r, halves in enumerate(rank_blocks(lower, lower_far, upper, upper_far)):
        for part, (ref, start) in enumerate(halves):
            rows = slice(part * half, (part + 1) * half)
            source = slice(start, start + half)
            for s in range(per // piece):
                to = pl.ds(pl.multiple_of((4 * s + (rank ^ r)) * piece, piece), piece)
                grad_gate_ref[rows, to] = ref[source, s * piece : (s + 1) * piece].astype(WIDE)
                grad_up_ref[rows, to] = ref[source, per + s * piece : per + (s + 1) * piece].astype(
                    WIDE
                )
            to = pl.ds(pl.multiple_of((rank ^ r) * 2 * half + part * half, half), half)
            grad_down_ref[to, :] = ref[source, 2 * per :].astype(WIDE)
    flat = jnp.zeros((1, 128), WIDE)
    for part in range(2):
        rows = slice(part * half, (part + 1) * half)
        total = jnp.sum(
            gate_ref[rows, :].astype(WIDE) * grad_gate_ref[rows, :], 1, keepdims=True
        ) + jnp.sum(up_ref[rows, :].astype(WIDE) * grad_up_ref[rows, :], 1, keepdims=True)
        flat = flat + lay_flat(total, part)
    grad_gain_ref[...] = jnp.broadcast_to(flat / gain_ref[...].astype(WIDE), (8, 128))


def spread_feed(rank, pieces, w_gate, w_up, gain):
    shard, ff = w_gate.shape
    return call(
        spread_feed_kernel,
        "spread_feed",
        [((shard, ff), WIDE), ((shard, ff), WIDE), ((ff // 8, D), WIDE), ((8, 128), WIDE)],
        [pl.BlockSpec(memory_space=pltpu.SMEM)] + [whole_block()] * 7,
        4 * shard * ff,
        16 * 2**20,
        (rank, *pieces, w_gate, w_up, gain),
    )


def spread_first_kernel(
    rank_ref, lower, lower_far, upper, upper_far, wq_ref, wk_ref, wv_ref, gain_ref,
    gq_ref, gk_ref, gv_ref, go_ref, grad_gain_ref, bias_ref,
):
    rank = rank_ref[0]
    half = lower.shape[0] // 2
    wide = 256
    bias_ref[...] = jnp.zeros_like(bias_ref)
    for r, halves in enumerate(rank_blocks(lower, lower_far, upper, upper_far)):
        to = pl.ds(pl.multiple_of((rank ^ r) * wide, wide), wide)
        for part, (ref, start) in enumerate(halves):
            rows = slice(part * half, (part + 1) * half)
            source = slice(start, start + half)
            for place, out_ref in enumerate((gq_ref, gk_ref, gv_ref, go_ref)):
                out_ref[rows, to] = ref[source, place * wide : (place + 1) * wide].astype(WIDE)
        ref, start = halves[0]
        bias_ref[pl.ds(rank ^ r, 1), :] = jnp.sum(
            ref[start : start + 16, 4 * wide : 4 * wide + 128].astype(WIDE), 0, keepdims=True
        )
    flat = jnp.zeros((1, 128), WIDE)
    for part in range(2):
        rows = slice(part * half, (part + 1) * half)
        total = jnp.zeros((half, 1), WIDE)
        for weight_ref, grad_ref in ((wq_ref, gq_ref), (wk_ref, gk_ref), (wv_ref, gv_ref)):
            total = total + jnp.sum(
                weight_ref[rows, :].astype(WIDE) * grad_ref[rows, :], 1, keepdims=True
            )
        flat = flat + lay_flat(total, part)
    grad_gain_ref[...] = jnp.broadcast_to(flat / gain_ref[...].astype(WIDE), (8, 128))


def spread_first(rank, pieces, w_query, w_key, w_value, gain):
    shard = w_query.shape[0]
    return call(
        spread_first_kernel,
        "spread_first",
        [((shard, D), WIDE)] * 4 + [((8, 128), WIDE), ((8, 128), WIDE)],
        [pl.BlockSpec(memory_space=pltpu.SMEM)] + [whole_block()] * 8,
        4 * shard * D,
        8 * 2**20,
        (rank, *pieces, w_query, w_key, w_value, gain),
    )


def on_plane(
    inputs,
    w_query,
    w_key,
    w_value,
    w_output,
    gain_attention,
    w_gate,
    w_up,
    w_down,
    gain_feed,
    variate_bias,
    segment_ids,
    variate_ids,
    positions,
    grad_output,
):
    rank = lax.axis_index("batch")
    rank_row = jnp.reshape(rank, (1,)).astype(jnp.int32)
    micro, tokens = inputs.shape[0], inputs.shape[2]
    n_seq = lax.axis_size("seq")
    shard = w_query.shape[0]
    per = D // 4

    packed, first_shard, gate_up_shard, down_shard = pack(
        rank_row,
        inputs.reshape(micro, tokens, D),
        grad_output.reshape(micro, tokens, D),
        segment_ids.reshape(micro, tokens),
        variate_ids.reshape(micro, tokens),
        positions.reshape(micro, tokens),
        (w_query, w_key, w_value, w_output),
        (gain_attention.reshape(1, shard), gain_feed.reshape(1, shard)),
        w_gate,
        w_up,
        w_down,
    )
    first_weights = lax.all_gather(first_shard, "seq", axis=0, tiled=True)
    gate_up = lax.all_gather(gate_up_shard, "seq", axis=0, tiled=True)
    down = lax.all_gather(down_shard, "seq", axis=0, tiled=True)
    packed = lax.all_to_all(packed, "batch", 0, 0, tiled=True)
    by_sequence = [
        packed[:, kind].reshape(4 * micro, tokens // 4, D + 128)[:, :, : D + 128 - 128 * kind]
        for kind in range(2)
    ]
    out_columns = first_weights[:, 768:D]
    out_got = swap_pairs(out_columns)
    mine, cot_by_sequence, out_got = lax.optimization_barrier(
        (over_seq(by_sequence[0]), by_sequence[1], out_got)
    )
    cot_mine = over_seq(cot_by_sequence)
    freqs = jnp.exp((jnp.arange(128) % 32).astype(WIDE) * (-2.0 * math.log(10000.0) / HD))[None, :]
    my_bias = lax.dynamic_slice_in_dim(variate_bias, rank * 4, 4, 1)
    weights = jnp.pad(head_weights(my_bias[0], my_bias[1]), ((0, 4), (0, 0)))

    chunks = gather_plane(mine)
    out_pieces = far_pairs(
        out_columns, lax.optimization_barrier((out_got, chunks[1], chunks[3]))[0]
    )
    gain, mixed_first, turned, attended, lower, upper, *kept = attend(
        chunks, first_weights, freqs, weights, rank_row
    )
    ready = lax.optimization_barrier((lower, upper, out_pieces[1], out_pieces[3]))
    lower_x, upper_y = swap(ready[0], 1), swap(ready[1], 2)
    lower_far = swap(jnp.concatenate([lower, lower_x], 1), 2)
    upper_far = swap(jnp.concatenate([upper, upper_y], 1), 1)
    cot_got = swap_pairs(lax.optimization_barrier((cot_mine, lower_far, upper_far))[0])
    heads, middle_own, mixed_second = middle(
        rank_row,
        chunks,
        (lower, lower_x, lower_far, upper, upper_y, upper_far),
        out_pieces,
        gain,
    )

    both, hidden = feed(mixed_second, gate_up, after(rank_row, cot_got))
    cots = far_pairs(cot_mine, lax.optimization_barrier((cot_got, mixed_second))[0])
    far_grads, far_lower, far_upper, down_weight_grads = feed_back(
        1, both, cots, gate_up, down, rank_row, hidden
    )
    got = scatter_first((None, far_lower, None, far_upper))
    near_grads, near_lower, near_upper = feed_back(
        0, both, cots, gate_up, down, after(rank_row, far_lower)
    )
    down_grad_shard = lax.psum_scatter(down_weight_grads, "seq", scatter_dimension=0, tiled=True)
    back = (near_lower, None, near_upper, None)
    gate_up_weight_grads = gate_up_grads(
        mixed_second, near_grads, far_grads, after(rank_row, got)
    )
    gate_up_grad_shard = lax.psum_scatter(
        gate_up_weight_grads, "seq", scatter_dimension=0, tiled=True
    )
    sums = scatter_second(back, got)
    grad_middle, *parcels = own_back(
        rank_row, sums, middle_own, cot_mine, gain, out_pieces,
        after(rank_row, gate_up_weight_grads),
    )
    outs = feed_out(hidden, down, after(rank_row, parcels[0]))
    parcels = [parcels[0]] + [swap(parcels[r], r) for r in range(1, 4)]

    proj, bias, *back = attend_back(
        parcels, (turned, attended, *kept), weights, first_weights, after(rank_row, outs[0])
    )
    outs = [outs[0]] + [swap(outs[q], q) for q in range(1, 4)]
    ready = lax.optimization_barrier((back[1], back[3], *outs[1:]))
    got = scatter_first((None, ready[0], None, ready[1]))
    bias_sums = jnp.sum(bias, 1)
    bias_parts = jnp.pad(jnp.concatenate(three_parts(bias_sums)), (0, 104))[None, :]
    slots = lax.broadcasted_iota(jnp.int32, (per, 1), 0) % shard == lax.axis_index("seq")
    bias_rows = jnp.where(slots, bias_parts, LOW(0))
    first_weight_grads = first_grads(
        rank_row, mixed_first, proj, heads, parcels, bias_rows, rank_row
    )
    got, first_weight_grads = lax.optimization_barrier((got, first_weight_grads))
    first_shard = lax.psum_scatter(first_weight_grads, "seq", scatter_dimension=0, tiled=True)
    sums = scatter_second(back, got)
    feed_shard = join(gate_up_grad_shard, down_grad_shard, after(rank_row, first_weight_grads))
    last = own_last(
        sums, outs, mine, grad_middle, middle_own, gain, n_seq, after(rank_row, feed_shard)
    )
    moved = lax.all_to_all(last, "seq", 0, 0, tiled=True)
    quarter = tokens // 4
    feed_pieces = gather_plane(after(feed_shard, last))
    first_pieces = gather_plane(after(first_shard, feed_pieces))
    moved, first_pieces = lax.optimization_barrier((moved, first_pieces))
    moved = moved.reshape(4, micro, 2 * quarter, D)
    moved = lax.all_to_all(moved, "batch", 0, 0, tiled=True)
    grad_inputs = jnp.transpose(moved[:, :, :quarter].astype(WIDE), (1, 0, 2, 3))
    block_output = jnp.transpose(moved[:, :, quarter:], (1, 0, 2, 3))

    grad_gate, grad_up, grad_down, grad_gain_second = spread_feed(
        rank_row, feed_pieces, w_gate, w_up, gain_feed.reshape(1, shard)
    )
    grad_query, grad_key, grad_value, grad_output_weights, grad_gain_first, bias_table = (
        spread_first(
            rank_row, first_pieces, w_query, w_key, w_value, gain_attention.reshape(1, shard)
        )
    )
    bias_table = jnp.sum(bias_table[:4, :24].reshape(4, 3, 2, 4), 1)
    grad_bias = jnp.transpose(bias_table, (1, 0, 2)).reshape(2, H)
    return (
        block_output.reshape(inputs.shape),
        grad_inputs.reshape(inputs.shape),
        grad_query,
        grad_key,
        grad_value,
        grad_output_weights,
        grad_gain_first[0],
        grad_gate,
        grad_up,
        grad_down,
        grad_gain_second[0],
        grad_bias,
    )


def solution(mesh):
    n_batch, n_seq = mesh.shape["batch"], mesh.shape["seq"]
    step = on_plane if n_batch == 4 and n_seq == 8 else on_device
    return jax.shard_map(
        step,
        mesh=mesh,
        in_specs=(
            P(None, "batch", "seq", None),
            P("seq", None),
            P("seq", None),
            P("seq", None),
            P("seq", None),
            P("seq"),
            P("seq", None),
            P("seq", None),
            P("seq", None),
            P("seq"),
            P(),
            P(None, "batch", "seq"),
            P(None, "batch", "seq"),
            P(None, "batch", "seq"),
            P(None, "batch", "seq", None),
        ),
        out_specs=(
            P(None, "batch", "seq", None),
            P(None, "batch", "seq", None),
            P("seq", None),
            P("seq", None),
            P("seq", None),
            P("seq", None),
            P("seq"),
            P("seq", None),
            P("seq", None),
            P("seq", None),
            P("seq"),
            P(),
        ),
        check_vma=False,
    )
```

```python
import functools
import math

import jax
import jax.numpy as jnp
from jax import lax
from jax.experimental import pallas as pl
from jax.experimental.pallas import tpu as pltpu
from jax.sharding import PartitionSpec as P

D = 1024
H = 16
HD = 64
REACH = 6


EPSILON = 1e-05
SCORE_SCALE = 0.125
MASKED = -1e30


def from_behind(value, axis, by):
    length = lax.axis_size(axis)
    pairs = [(i, i + by) for i in range(length) if 0 <= i + by < length]
    return lax.ppermute(value, axis, pairs)


def step_offset(step):
    distance = step // 2 + 1
    return distance if step % 2 == 0 else -distance


def rotary(values_in, positions_in, turn):
    row_count = values_in.shape[0]
    halfway = HD // 2
    freqs = jnp.exp(jnp.arange(halfway, dtype=jnp.float32) * (-2.0 * math.log(10000.0) / HD))
    angles = positions_in.astype(jnp.float32)[:, None] * freqs[None, :]
    cosine = jnp.cos(angles)[:, None, :]
    sine = turn * jnp.sin(angles)[:, None, :]
    shaped = values_in.reshape(row_count, H, HD)
    first_half = shaped[..., :halfway]
    second_half = shaped[..., halfway:]
    turned = jnp.concatenate(
        [first_half * cosine - second_half * sine, first_half * sine + second_half * cosine], -1
    )
    return turned.reshape(row_count, H * HD)


def head_scores(query_heads, key_heads, query_variates, key_variates, bias_table):
    raw = jnp.einsum("qhd,khd->hqk", query_heads, key_heads, preferred_element_type=jnp.float32)
    same_variate = (query_variates[:, None] == key_variates[None, :])[None]
    return raw * SCORE_SCALE + jnp.where(
        same_variate, bias_table[0][:, None, None], bias_table[1][:, None, None]
    )


def attend_forward(query_rows, own_keys, own_values, own_segments, own_variates, bias_table):
    tok_count = query_rows.shape[0]
    query_heads = query_rows.reshape(tok_count, H, HD)
    shifted_segments = own_segments + 1

    def fold_keys(carried, piece_rows):
        key_part, value_part, segment_part, variate_part = piece_rows
        part_count = key_part.shape[0]
        live = shifted_segments[:, None] == segment_part[None, :]

        def update(state):
            running_max, running_total, running_sum = state
            logits = head_scores(
                query_heads,
                key_part.reshape(part_count, H, HD),
                own_variates,
                variate_part,
                bias_table,
            )
            logits = jnp.where(live[None], logits, MASKED)
            new_max = jnp.maximum(running_max, jnp.max(logits, -1))
            rescale = jnp.exp(running_max - new_max)
            weights = jnp.where(live[None], jnp.exp(logits - new_max[..., None]), 0.0)
            new_total = running_total * rescale + jnp.sum(weights, -1)
            mixed = jnp.einsum(
                "hqk,khd->qhd",
                weights.astype(jnp.bfloat16),
                value_part.reshape(part_count, H, HD),
                preferred_element_type=jnp.float32,
            )
            new_sum = running_sum * jnp.transpose(rescale)[:, :, None] + mixed
            return (new_max, new_total, new_sum)

        return lax.cond(jnp.any(live), update, lambda state: state, carried)

    near_rows = (own_keys, own_values, shifted_segments, own_variates)
    state = (
        jnp.full((H, tok_count), MASKED, jnp.float32),
        jnp.zeros((H, tok_count), jnp.float32),
        jnp.zeros((tok_count, H, HD), jnp.float32),
    )
    state = fold_keys(state, near_rows)
    for step in range(2 * REACH):
        arrived = from_behind(
            (own_keys, own_values, shifted_segments, own_variates), "seq", step_offset(step)
        )
        state = fold_keys(state, arrived)
    final_max, final_total, final_sum = state
    attended = final_sum / jnp.transpose(final_total)[:, :, None]
    log_rows = jnp.transpose(final_max + jnp.log(final_total))
    return (attended.reshape(tok_count, H * HD), log_rows)


def attend_queries_back(
    query_rows,
    grad_rows,
    log_rows,
    delta_rows,
    own_keys,
    own_values,
    own_segments,
    own_variates,
    bias_table,
):
    tok_count = query_rows.shape[0]
    query_heads = query_rows.reshape(tok_count, H, HD)
    grad_heads = grad_rows.reshape(tok_count, H, HD)
    log_heads = jnp.transpose(log_rows)
    delta_heads = jnp.transpose(delta_rows)
    shifted_segments = own_segments + 1

    def fold_keys_back(carried, piece_rows):
        key_part, value_part, segment_part, variate_part = piece_rows
        part_count = key_part.shape[0]
        live = shifted_segments[:, None] == segment_part[None, :]

        def update(state):
            grad_query, grad_bias = state
            key_heads = key_part.reshape(part_count, H, HD)
            logits = head_scores(query_heads, key_heads, own_variates, variate_part, bias_table)
            weights = jnp.where(live[None], jnp.exp(logits - log_heads[..., None]), 0.0)
            grad_weights = jnp.einsum(
                "qhd,khd->hqk",
                grad_heads,
                value_part.reshape(part_count, H, HD),
                preferred_element_type=jnp.float32,
            )
            grad_logits = (weights * (grad_weights - delta_heads[..., None])).astype(jnp.bfloat16)
            grad_query = grad_query + SCORE_SCALE * jnp.einsum(
                "hqk,khd->qhd", grad_logits, key_heads, preferred_element_type=jnp.float32
            )
            same_variate = (own_variates[:, None] == variate_part[None, :])[None]
            logit_values = grad_logits.astype(jnp.float32)
            same_total = jnp.sum(jnp.where(same_variate, logit_values, 0.0), axis=(1, 2))
            other_total = jnp.sum(jnp.where(same_variate, 0.0, logit_values), axis=(1, 2))
            return (grad_query, grad_bias + jnp.stack([same_total, other_total]))

        return lax.cond(jnp.any(live), update, lambda state: state, carried)

    state = (jnp.zeros((tok_count, H, HD), jnp.float32), jnp.zeros((2, H), jnp.float32))
    state = fold_keys_back(state, (own_keys, own_values, shifted_segments, own_variates))
    for step in range(2 * REACH):
        arrived = from_behind(
            (own_keys, own_values, shifted_segments, own_variates), "seq", step_offset(step)
        )
        state = fold_keys_back(state, arrived)
    grad_query, grad_bias = state
    return (grad_query.reshape(tok_count, H * HD), grad_bias)


def attend_keys_back(
    query_rows,
    grad_rows,
    log_rows,
    delta_rows,
    own_keys,
    own_values,
    own_segments,
    own_variates,
    bias_table,
):
    tok_count = own_keys.shape[0]
    key_heads = own_keys.reshape(tok_count, H, HD)
    value_heads = own_values.reshape(tok_count, H, HD)
    shifted_segments = own_segments + 1

    def fold_queries(carried, piece_rows):
        query_part, grad_part, log_part, delta_part, segment_part, variate_part = piece_rows
        part_count = query_part.shape[0]
        live = segment_part[:, None] == shifted_segments[None, :]

        def update(state):
            grad_key, grad_value = state
            query_heads = query_part.reshape(part_count, H, HD)
            grad_heads = grad_part.reshape(part_count, H, HD)
            logits = head_scores(query_heads, key_heads, variate_part, own_variates, bias_table)
            weights = jnp.where(
                live[None], jnp.exp(logits - jnp.transpose(log_part)[..., None]), 0.0
            )
            grad_value = grad_value + jnp.einsum(
                "hqk,qhd->khd",
                weights.astype(jnp.bfloat16),
                grad_heads,
                preferred_element_type=jnp.float32,
            )
            grad_weights = jnp.einsum(
                "qhd,khd->hqk", grad_heads, value_heads, preferred_element_type=jnp.float32
            )
            grad_logits = (weights * (grad_weights - jnp.transpose(delta_part)[..., None])).astype(
                jnp.bfloat16
            )
            grad_key = grad_key + SCORE_SCALE * jnp.einsum(
                "hqk,qhd->khd", grad_logits, query_heads, preferred_element_type=jnp.float32
            )
            return (grad_key, grad_value)

        return lax.cond(jnp.any(live), update, lambda state: state, carried)

    state = (jnp.zeros((tok_count, H, HD), jnp.float32), jnp.zeros((tok_count, H, HD), jnp.float32))
    state = fold_queries(
        state, (query_rows, grad_rows, log_rows, delta_rows, shifted_segments, own_variates)
    )
    for step in range(2 * REACH):
        arrived = (
            from_behind(query_rows, "seq", step_offset(step)),
            from_behind(grad_rows, "seq", step_offset(step)),
            from_behind(log_rows.astype(jnp.bfloat16), "seq", step_offset(step)).astype(
                log_rows.dtype
            ),
            from_behind(delta_rows.astype(jnp.bfloat16), "seq", step_offset(step)).astype(
                delta_rows.dtype
            ),
            from_behind(shifted_segments, "seq", step_offset(step)),
            from_behind(own_variates, "seq", step_offset(step)),
        )
        state = fold_queries(state, arrived)
    grad_key, grad_value = state
    return (grad_key.reshape(tok_count, H * HD), grad_value.reshape(tok_count, H * HD))


def norm_back(grad_normed, normed, scale_rows):
    return scale_rows * (grad_normed - normed * jnp.mean(grad_normed * normed, -1, keepdims=True))


def on_device(
    inputs,
    w_query,
    w_key,
    w_value,
    w_output,
    gain_attention,
    w_gate,
    w_up,
    w_down,
    gain_feed,
    variate_bias,
    segment_ids,
    variate_ids,
    positions,
    grad_output,
):
    micro_count = inputs.shape[0]
    tok_count = inputs.shape[2]
    row_count = micro_count * tok_count
    residual_in = inputs.reshape(row_count, D).astype(jnp.float32)
    cotangent = grad_output.reshape(row_count, D).astype(jnp.float32)
    segment_rows = segment_ids.reshape(micro_count, tok_count)
    variate_rows = variate_ids.reshape(micro_count, tok_count)
    position_rows = positions.reshape(row_count)
    full_query, full_key, full_value, full_output, full_gain_first = (
        lax.all_gather(w_query, "seq", axis=0, tiled=True),
        lax.all_gather(w_key, "seq", axis=0, tiled=True),
        lax.all_gather(w_value, "seq", axis=0, tiled=True),
        lax.all_gather(w_output, "seq", axis=0, tiled=True),
        lax.all_gather(gain_attention, "seq", axis=0, tiled=True),
    )
    full_gate, full_up, full_down, full_gain_second = (
        lax.all_gather(w_gate, "seq", axis=0, tiled=True),
        lax.all_gather(w_up, "seq", axis=0, tiled=True),
        lax.all_gather(w_down, "seq", axis=0, tiled=True),
        lax.all_gather(gain_feed, "seq", axis=0, tiled=True),
    )
    scale_first = lax.rsqrt(jnp.mean(residual_in * residual_in, -1, keepdims=True) + EPSILON)
    normed_first = residual_in * scale_first
    mixed_first = (normed_first * full_gain_first.astype(jnp.float32)).astype(jnp.bfloat16)
    query_proj = jnp.dot(mixed_first, full_query, preferred_element_type=jnp.float32)
    key_proj = jnp.dot(mixed_first, full_key, preferred_element_type=jnp.float32)
    value_proj = jnp.dot(mixed_first, full_value, preferred_element_type=jnp.float32)
    query_rows = rotary(query_proj, position_rows, 1.0).astype(jnp.bfloat16)
    key_rows = rotary(key_proj, position_rows, 1.0).astype(jnp.bfloat16)
    value_rows = value_proj.astype(jnp.bfloat16)
    attended_parts = []
    log_parts = []
    for micro_index in range(micro_count):
        lower_row = micro_index * tok_count
        upper_row = lower_row + tok_count
        attended_part, log_part = attend_forward(
            query_rows[lower_row:upper_row],
            key_rows[lower_row:upper_row],
            value_rows[lower_row:upper_row],
            segment_rows[micro_index],
            variate_rows[micro_index],
            variate_bias,
        )
        attended_parts.append(attended_part)
        log_parts.append(log_part)
    attended_all = jnp.concatenate(attended_parts, 0)
    attended_low = attended_all.astype(jnp.bfloat16)
    middle = residual_in + jnp.dot(attended_low, full_output, preferred_element_type=jnp.float32)
    scale_second = lax.rsqrt(jnp.mean(middle * middle, -1, keepdims=True) + EPSILON)
    normed_second = middle * scale_second
    mixed_second = (normed_second * full_gain_second.astype(jnp.float32)).astype(jnp.bfloat16)
    gate_proj = jnp.dot(mixed_second, full_gate, preferred_element_type=jnp.float32)
    up_proj = jnp.dot(mixed_second, full_up, preferred_element_type=jnp.float32)
    sigmoid_gate = jax.nn.sigmoid(gate_proj)
    silu_gate = gate_proj * sigmoid_gate
    hidden_rows = (silu_gate * up_proj).astype(jnp.bfloat16)
    block_rows = middle + jnp.dot(hidden_rows, full_down, preferred_element_type=jnp.float32)
    block_output = block_rows.astype(jnp.bfloat16).reshape(inputs.shape)
    full_query, full_key, full_value, full_output, full_gain_first = (
        lax.all_gather(w_query, "seq", axis=0, tiled=True),
        lax.all_gather(w_key, "seq", axis=0, tiled=True),
        lax.all_gather(w_value, "seq", axis=0, tiled=True),
        lax.all_gather(w_output, "seq", axis=0, tiled=True),
        lax.all_gather(gain_attention, "seq", axis=0, tiled=True),
    )
    full_gate, full_up, full_down, full_gain_second = (
        lax.all_gather(w_gate, "seq", axis=0, tiled=True),
        lax.all_gather(w_up, "seq", axis=0, tiled=True),
        lax.all_gather(w_down, "seq", axis=0, tiled=True),
        lax.all_gather(gain_feed, "seq", axis=0, tiled=True),
    )
    grad_branch_second = cotangent.astype(jnp.bfloat16)
    grad_down = jnp.einsum(
        "rf,rd->fd", hidden_rows, grad_branch_second, preferred_element_type=jnp.float32
    )
    grad_hidden = jnp.einsum(
        "rd,fd->rf", grad_branch_second, full_down, preferred_element_type=jnp.float32
    )
    silu_slope = sigmoid_gate * (1.0 + gate_proj * (1.0 - sigmoid_gate))
    grad_gate_rows = (grad_hidden * up_proj * silu_slope).astype(jnp.bfloat16)
    grad_up_rows = (grad_hidden * silu_gate).astype(jnp.bfloat16)
    grad_gate = jnp.einsum(
        "rd,rf->df", mixed_second, grad_gate_rows, preferred_element_type=jnp.float32
    )
    grad_up = jnp.einsum(
        "rd,rf->df", mixed_second, grad_up_rows, preferred_element_type=jnp.float32
    )
    grad_mixed_second = jnp.einsum(
        "rf,df->rd", grad_gate_rows, full_gate, preferred_element_type=jnp.float32
    ) + jnp.einsum("rf,df->rd", grad_up_rows, full_up, preferred_element_type=jnp.float32)
    grad_gain_second = jnp.sum(grad_mixed_second * normed_second, 0)
    grad_middle = cotangent + norm_back(
        grad_mixed_second * full_gain_second.astype(jnp.float32), normed_second, scale_second
    )
    grad_branch_first = grad_middle.astype(jnp.bfloat16)
    grad_out_proj = jnp.einsum(
        "rd,re->de", attended_low, grad_branch_first, preferred_element_type=jnp.float32
    )
    grad_attended = jnp.einsum(
        "re,de->rd", grad_branch_first, full_output, preferred_element_type=jnp.float32
    ).astype(jnp.bfloat16)
    delta_all = jnp.einsum(
        "rhd,rhd->rh",
        grad_attended.astype(jnp.float32).reshape(row_count, H, HD),
        attended_all.reshape(row_count, H, HD),
    )
    grad_bias_local = jnp.zeros((2, H), jnp.float32)
    query_grad_parts = []
    key_grad_parts = []
    value_grad_parts = []
    for micro_index in range(micro_count):
        lower_row = micro_index * tok_count
        upper_row = lower_row + tok_count
        query_grad_part, bias_part = attend_queries_back(
            query_rows[lower_row:upper_row],
            grad_attended[lower_row:upper_row],
            log_parts[micro_index],
            delta_all[lower_row:upper_row],
            key_rows[lower_row:upper_row],
            value_rows[lower_row:upper_row],
            segment_rows[micro_index],
            variate_rows[micro_index],
            variate_bias,
        )
        key_grad_part, value_grad_part = attend_keys_back(
            query_rows[lower_row:upper_row],
            grad_attended[lower_row:upper_row],
            log_parts[micro_index],
            delta_all[lower_row:upper_row],
            key_rows[lower_row:upper_row],
            value_rows[lower_row:upper_row],
            segment_rows[micro_index],
            variate_rows[micro_index],
            variate_bias,
        )
        grad_bias_local = grad_bias_local + bias_part
        query_grad_parts.append(query_grad_part)
        key_grad_parts.append(key_grad_part)
        value_grad_parts.append(value_grad_part)
    grad_query_rows = rotary(jnp.concatenate(query_grad_parts, 0), position_rows, -1.0).astype(
        jnp.bfloat16
    )
    grad_key_rows = rotary(jnp.concatenate(key_grad_parts, 0), position_rows, -1.0).astype(
        jnp.bfloat16
    )
    grad_value_rows = jnp.concatenate(value_grad_parts, 0).astype(jnp.bfloat16)
    grad_query = jnp.einsum(
        "rd,re->de", mixed_first, grad_query_rows, preferred_element_type=jnp.float32
    )
    grad_key = jnp.einsum(
        "rd,re->de", mixed_first, grad_key_rows, preferred_element_type=jnp.float32
    )
    grad_value = jnp.einsum(
        "rd,re->de", mixed_first, grad_value_rows, preferred_element_type=jnp.float32
    )
    grad_mixed_first = (
        jnp.einsum("re,de->rd", grad_query_rows, full_query, preferred_element_type=jnp.float32)
        + jnp.einsum("re,de->rd", grad_key_rows, full_key, preferred_element_type=jnp.float32)
        + jnp.einsum("re,de->rd", grad_value_rows, full_value, preferred_element_type=jnp.float32)
    )
    grad_gain_first = jnp.sum(grad_mixed_first * normed_first, 0)
    grad_input_rows = grad_middle + norm_back(
        grad_mixed_first * full_gain_first.astype(jnp.float32), normed_first, scale_first
    )
    grad_inputs = grad_input_rows.reshape(inputs.shape)
    (
        shard_query,
        shard_key,
        shard_value,
        shard_output,
        shard_gain_first,
        shard_gate,
        shard_up,
        shard_down,
        shard_gain_second,
    ) = (
        lax.psum_scatter(grad_query, "seq", scatter_dimension=0, tiled=True),
        lax.psum_scatter(grad_key, "seq", scatter_dimension=0, tiled=True),
        lax.psum_scatter(grad_value, "seq", scatter_dimension=0, tiled=True),
        lax.psum_scatter(grad_out_proj, "seq", scatter_dimension=0, tiled=True),
        lax.psum_scatter(grad_gain_first, "seq", scatter_dimension=0, tiled=True),
        lax.psum_scatter(grad_gate, "seq", scatter_dimension=0, tiled=True),
        lax.psum_scatter(grad_up, "seq", scatter_dimension=0, tiled=True),
        lax.psum_scatter(grad_down, "seq", scatter_dimension=0, tiled=True),
        lax.psum_scatter(grad_gain_second, "seq", scatter_dimension=0, tiled=True),
    )
    summed = (
        lax.psum(shard_query.astype(jnp.bfloat16), "batch").astype(jnp.float32),
        lax.psum(shard_key.astype(jnp.bfloat16), "batch").astype(jnp.float32),
        lax.psum(shard_value.astype(jnp.bfloat16), "batch").astype(jnp.float32),
        lax.psum(shard_output.astype(jnp.bfloat16), "batch").astype(jnp.float32),
        lax.psum(shard_gain_first.astype(jnp.bfloat16), "batch").astype(jnp.float32),
        lax.psum(shard_gate.astype(jnp.bfloat16), "batch").astype(jnp.float32),
        lax.psum(shard_up.astype(jnp.bfloat16), "batch").astype(jnp.float32),
        lax.psum(shard_down.astype(jnp.bfloat16), "batch").astype(jnp.float32),
        lax.psum(shard_gain_second.astype(jnp.bfloat16), "batch").astype(jnp.float32),
    )
    grad_bias_total = lax.psum(grad_bias_local, ("batch", "seq"))
    return (
        block_output,
        grad_inputs,
        summed[0],
        summed[1],
        summed[2],
        summed[3],
        summed[4],
        summed[5],
        summed[6],
        summed[7],
        summed[8],
        grad_bias_total,
    )


ORDER_A = (0, 1, 2, 3)
ORDER_B = (0, 2, 1, 3)
FEATURES = 128
LSE_AT = 64
LOW = jnp.bfloat16
WIDE = jnp.float32


def swap(value, bit):
    return lax.ppermute(value, "batch", [(i, i ^ bit) for i in range(4)])


def after(value, *others):
    return lax.optimization_barrier((value, *others))[0]


def gather_plane(own):
    half = own.shape[0] // 2
    lower, upper = own[:half], own[half:]
    lower_pair = jnp.concatenate([lower, swap(lower, 1)], 0)
    upper_pair = jnp.concatenate([upper, swap(upper, 2)], 0)
    return lower_pair, swap(lower_pair, 2), upper_pair, swap(upper_pair, 1)


def scatter_first(chunks):
    return swap(chunks[1], 2), swap(chunks[3], 1)


def scatter_second(chunks, got):
    near_lower, _, near_upper, _ = chunks
    got_lower, got_upper = got
    half = near_lower.shape[0] // 2
    last_lower = swap(near_lower[half:] + got_lower[half:], 1)
    last_upper = swap(near_upper[half:] + got_upper[half:], 2)
    return (near_lower, got_lower, last_lower, near_upper, got_upper, last_upper)


def swap_pairs(own):
    half = own.shape[0] // 2
    return swap(own[:half], 1), swap(own[half:], 2)


def far_pairs(own, got):
    half = own.shape[0] // 2
    lower_pair = jnp.concatenate([own[:half], got[0]], 0)
    upper_pair = jnp.concatenate([own[half:], got[1]], 0)
    return lower_pair, swap(lower_pair, 2), upper_pair, swap(upper_pair, 1)


def over_seq(pieces):
    count, quarter, width = pieces.shape
    return lax.all_to_all(pieces, "seq", 0, 0, tiled=True).reshape(count * quarter, width)


def three_parts(value):
    high = value.astype(LOW)
    rest = value - high.astype(WIDE)
    middle = rest.astype(LOW)
    low = (rest - middle.astype(WIDE)).astype(LOW)
    return high, middle, low


def token_features(segments, variates):
    lane = lax.broadcasted_iota(jnp.int32, (segments.shape[0], FEATURES), 1)
    variate_hot = (lane < 12) & (lane % 4 == variates)
    ones = (lane >= 12) & (lane < 15)
    segment_lane = (lane >= 16) & (lane < LSE_AT)
    segment_hot = segment_lane & (lane - 16 == segments)
    segment_cold = segment_lane & (lane - 16 != segments)
    query_side = variate_hot | ones | segment_hot
    key_side = variate_hot | ones | segment_cold | ((lane >= LSE_AT) & (lane < LSE_AT + 3))
    return jnp.where(query_side, 1.0, 0.0).astype(LOW), jnp.where(key_side, 1.0, 0.0).astype(LOW)


def head_weights(same_bias, other_bias):
    gap = [part[:, None] for part in three_parts(same_bias - other_bias)]
    base = [part[:, None] for part in three_parts(other_bias)]
    heads = same_bias.shape[0]
    columns = [jnp.broadcast_to(part, (heads, 4)) for part in gap] + base
    columns.append(jnp.zeros((heads, 1), LOW))
    columns.append(jnp.full((heads, LSE_AT - 16), MASKED, LOW))
    columns.append(jnp.zeros((heads, FEATURES - LSE_AT), LOW))
    return jnp.concatenate(columns, 1)


def turn_pair(pair, cosine, sine):
    lane = lax.broadcasted_iota(jnp.int32, pair.shape, 1)
    crossed = jnp.where(lane % 64 < 32, pltpu.roll(pair, 96, 1), pltpu.roll(pair, 32, 1))
    return pair * cosine + crossed * sine


def dot_plain(left, right):
    return jnp.dot(left, right, preferred_element_type=WIDE)


def dot_rows(left, right):
    return lax.dot_general(left, right, (((1,), (1,)), ((), ())), preferred_element_type=WIDE)


def dot_first(left, right):
    return lax.dot_general(left, right, (((0,), (0,)), ((), ())), preferred_element_type=WIDE)


def whole_block():
    return pl.BlockSpec(memory_space=pltpu.VMEM)


def call(kernel, name, outs, specs, flops, moved, args, scratch=()):
    return pl.pallas_call(
        kernel,
        grid=(1,),
        out_shape=[jax.ShapeDtypeStruct(shape, dtype) for shape, dtype in outs],
        in_specs=specs,
        out_specs=[pl.BlockSpec(memory_space=pltpu.VMEM) for _ in outs],
        scratch_shapes=list(scratch),
        cost_estimate=pl.CostEstimate(flops=flops, bytes_accessed=moved, transcendentals=0),
        compiler_params=pltpu.CompilerParams(vmem_limit_bytes=56 * 2**20),
        name=name,
    )(*args)


class Copies:
    def __init__(self, ref, pairs, sems):
        self.ref = ref
        self.copies = [
            pltpu.make_async_copy(source, target, sems.at[k])
            for k, (source, target) in enumerate(pairs)
        ]
        self.started = self.waited = False

    def start(self, *which):
        self.started = True
        for k in which or range(len(self.copies)):
            self.copies[k].start()

    def wait(self):
        if not self.waited:
            for copy in self.copies:
                copy.wait()
        self.waited = True
        return self.ref

    def _at(self, index, act):
        for k, copy in enumerate(self.copies):
            pl.when(index == k)(functools.partial(act, copy))

    def start_at(self, index):
        self.started = True
        self._at(index, lambda copy: copy.start())

    def wait_at(self, index):
        self.waited = True
        self._at(index, lambda copy: copy.wait())

    def wait_first(self, index):
        if not self.waited:
            self.waited = True

            @pl.when(index == 0)
            def _():
                for copy in self.copies:
                    copy.wait()

        return self.ref


class Plan:
    def __init__(self, arrays, shape, pairs, count):
        self.arrays, self.shape, self.pairs, self.count = arrays, shape, pairs, count


def whole(array, column=None, width=None):
    shape = array.shape if column is None else (array.shape[0], width)

    def pairs(refs, buffer):
        if column is None:
            return [(refs[0], buffer)]
        return [(refs[0].at[:, pl.ds(column, width)], buffer)]

    return Plan([array], shape, pairs, 1)


def top(array):
    half = array.shape[0] // 2
    return Plan(
        [array],
        (half, *array.shape[1:]),
        lambda refs, buffer: [(refs[0].at[pl.ds(0, half)], buffer)],
        1,
    )


def rows_of(array, count=4):
    size = array.shape[0] // count
    return Plan(
        [array],
        (count, size, array.shape[1]),
        lambda refs, buffer: [
            (refs[0].at[pl.ds(k * size, size)], buffer.at[k]) for k in range(count)
        ],
        count,
    )


def columns_of(array, count=4, column=0, width=None):
    size = (width or array.shape[1]) // count
    return Plan(
        [array],
        (count, array.shape[0], size),
        lambda refs, buffer: [
            (refs[0].at[:, pl.ds(column + k * size, size)], buffer.at[k]) for k in range(count)
        ],
        count,
    )


def group(arrays, column=None, width=None):
    rows = arrays[0].shape[0]

    def pairs(refs, buffer):
        if column is None:
            return [(ref, buffer.at[k]) for k, ref in enumerate(refs)]
        return [(ref.at[:, pl.ds(column, width)], buffer.at[k]) for k, ref in enumerate(refs)]

    return Plan(
        list(arrays), (len(arrays), rows, width or arrays[0].shape[1]), pairs, len(arrays)
    )


def out_rows(shape, dtype, count=4):
    size = shape[0] // count

    def pairs(refs, buffer):
        return [(buffer.at[k], refs[0].at[pl.ds(k * size, size)]) for k in range(count)]

    return Plan([(shape, dtype)], (count, size, *shape[1:]), pairs, count)


def out_group(shape, dtype, count=4):
    def pairs(refs, buffer):
        return [(buffer.at[k], ref) for k, ref in enumerate(refs)]

    return Plan([(shape, dtype)] * count, (count, *shape), pairs, count)


def out_whole(shape, dtype):
    return Plan([(shape, dtype)], shape, lambda refs, buffer: [(buffer, refs[0])], 1)


def run(body, name, us, ins, outs, scratch=(), token=None):
    args, in_specs, out_shapes, out_specs, buffers = [], [], [], [], []
    named = len(ins)
    if token is not None:
        ins = [*ins, token]
    for item in ins:
        if isinstance(item, Plan):
            args += item.arrays
            in_specs += [pl.BlockSpec(memory_space=pl.ANY)] * len(item.arrays)
            buffers.append(pltpu.VMEM(item.shape, item.arrays[0].dtype))
            buffers.append(pltpu.SemaphoreType.DMA((item.count,)))
        else:
            args.append(item)
            space = pltpu.SMEM if item.shape == (1,) else pltpu.VMEM
            in_specs.append(pl.BlockSpec(memory_space=space))
    for item in outs:
        if isinstance(item, Plan):
            out_shapes += [jax.ShapeDtypeStruct(*each) for each in item.arrays]
            out_specs += [pl.BlockSpec(memory_space=pl.ANY)] * len(item.arrays)
            buffers.append(pltpu.VMEM(item.shape, item.arrays[0][1]))
            buffers.append(pltpu.SemaphoreType.DMA((item.count,)))
        else:
            out_shapes.append(jax.ShapeDtypeStruct(*item))
            out_specs.append(pl.BlockSpec(memory_space=pltpu.VMEM))
    n_in, n_out = len(args), len(out_shapes)

    def kernel(*refs):
        given, rest = list(refs[: n_in + n_out]), list(refs[n_in + n_out :])
        bound = []
        for item in (*ins, *outs):
            if isinstance(item, Plan):
                near = [given.pop(0) for _ in item.arrays]
                buffer, sems = rest.pop(0), rest.pop(0)
                bound.append(Copies(buffer, item.pairs(near, buffer), sems))
            else:
                bound.append(given.pop(0))
        body(*bound[:named], *bound[len(ins) :], *rest)
        for item in bound[: len(ins)]:
            if isinstance(item, Copies):
                item.wait()
        for item in bound[len(ins) :]:
            if isinstance(item, Copies) and not item.started:
                item.start()
        for item in bound[len(ins) :]:
            if isinstance(item, Copies):
                item.wait()

    return pl.pallas_call(
        kernel,
        out_shape=out_shapes,
        in_specs=in_specs,
        out_specs=out_specs,
        scratch_shapes=buffers + list(scratch),
        cost_estimate=pl.CostEstimate(
            flops=int(us * 1.15e9), bytes_accessed=2**20, transcendentals=0
        ),
        compiler_params=pltpu.CompilerParams(vmem_limit_bytes=60 * 2**20),
        name=name,
    )(*args)


def output_weights(pieces):
    rows = pieces[0].shape[0] // 2
    places = {
        0: ((0, 0), (0, 1), (1, 0), (1, 1)),
        1: ((2, 0), (3, 0), (2, 1), (3, 1)),
    }

    def pairs(refs, buffer):
        rank = lax.axis_index("batch")
        out = []
        for half in range(2):
            for r, (which, part) in enumerate(places[half]):
                to = pl.ds(pl.multiple_of((rank ^ r) * 256, 256), 256)
                out.append(
                    (
                        refs[which].at[pl.ds(part * rows, rows)],
                        buffer.at[pl.ds(half * rows, rows), to],
                    )
                )
        return out

    return Plan(list(pieces), (2 * rows, D), pairs, 8)


def start_all(*items):
    for item in items:
        item.start()


def unit_rows(rows):
    return lax.rsqrt(jnp.mean(rows * rows, -1, keepdims=True) + EPSILON)


def pack_body(
    rank_ref, x, cot, segment_ref, variate_ref, position_ref, wq, wk, wv, wo, gain_first_ref,
    gain_second_ref, gate, up, down, rows_out, shard_out, gate_up_out, down_out,
):
    start_all(wq, wk, wv, wo, x, cot, gate, up, down)
    micro, _, quarter, _ = x.ref.shape
    tokens = 4 * quarter
    lane = lax.broadcasted_iota(jnp.int32, (tokens, 128), 1)
    on_line = lax.broadcasted_iota(jnp.int32, (tokens, 128), 0) == lane

    def upright(row):
        return jnp.sum(jnp.where(on_line, row, 0.0), 1, keepdims=True)

    gains = jnp.where(
        lane == 0,
        upright(gain_first_ref[...].astype(WIDE)),
        jnp.where(lane == 1, upright(gain_second_ref[...].astype(WIDE)), 0.0),
    )
    shard_out.ref[:, D:] = gains.astype(LOW)
    for place, weight in enumerate((wq, wk, wv, wo)):
        shard_out.ref[:, 256 * place : 256 * (place + 1)] = weight.wait()[...]
    shard_out.start()
    for m in range(micro):
        places = position_ref[m : m + 1, :]
        numbers = jnp.zeros((tokens, 128), WIDE)
        for place, row in enumerate(
            (
                segment_ref[m : m + 1, :],
                variate_ref[m : m + 1, :],
                lax.shift_right_logical(places, 5),
                places & 31,
            )
        ):
            numbers = jnp.where(lane == place, upright(row.astype(WIDE)), numbers)
        numbers = numbers.astype(LOW)
        for r in range(4):
            rows_out.ref[r, 0, m, :, D:] = numbers[r * quarter : (r + 1) * quarter, :]
            rows_out.ref[r, 1, m, :, D:] = jnp.zeros((quarter, 128), LOW)
    x_ref, cot_ref = x.wait(), cot.wait()
    for m in range(micro):
        for r in range(4):
            rows_out.ref[r, 0, m, :, :D] = x_ref[m, r]
            rows_out.ref[r, 1, m, :, :D] = cot_ref[m, r]
    rows_out.start()
    gate_ref, up_ref = gate.wait(), up.wait()
    per = gate_up_out.ref.shape[1] // 2
    piece = gate_ref.shape[2]
    for s in range(per // piece):
        gate_up_out.ref[:, s * piece : (s + 1) * piece] = gate_ref[s]
        gate_up_out.ref[:, per + s * piece : per + (s + 1) * piece] = up_ref[s]
    gate_up_out.start()
    down_out.ref[...] = down.wait()[...]


def pack(rank, x, cot, segments, variates, positions, shards, gains, w_gate, w_up, w_down):
    micro, tokens, _ = x.shape
    quarter = tokens // 4
    shard, ff = w_gate.shape
    piece = w_down.shape[0] // 4
    pieces = ff // 4 // piece

    def quarters(array):
        return array.reshape(micro, 4, quarter, D)

    def mine(array, size, refs_at):
        return Plan([array], size, refs_at, 1)

    def rank_columns(array):
        def pairs(refs, buffer):
            at = pl.multiple_of(lax.axis_index("batch") * 256, 256)
            return [(refs[0].at[:, pl.ds(at, 256)], buffer)]

        return Plan([array], (shard, 256), pairs, 1)

    def feed_columns(array):
        def pairs(refs, buffer):
            rank = lax.axis_index("batch")
            return [
                (refs[0].at[:, pl.ds(pl.multiple_of((4 * s + rank) * piece, piece), piece)], buffer.at[s])
                for s in range(pieces)
            ]

        return Plan([array], (pieces, shard, piece), pairs, pieces)

    def down_rows(array):
        def pairs(refs, buffer):
            at = pl.multiple_of(lax.axis_index("batch") * piece, piece)
            return [(refs[0].at[pl.ds(at, piece)], buffer)]

        return Plan([array], (piece, D), pairs, 1)

    return run(
        pack_body,
        "pack",
        4,
        [rank, whole(quarters(x)), whole(quarters(cot)), segments, variates, positions]
        + [rank_columns(weight) for weight in shards]
        + [*gains, feed_columns(w_gate), feed_columns(w_up), down_rows(w_down)],
        [
            out_whole((4, 2, micro, quarter, D + 128), LOW),
            out_whole((shard, D + 128), LOW),
            out_whole((shard, ff // 2), LOW),
            out_whole((piece, D), LOW),
        ],
    )


def attend_body(
    x, qkv, gains, freqs_ref, weights_ref,
    gain_ref, mixed, turned, wide, lower, upper, logs, cos, sin, query_sides, key_sides,
    keys_ref, values_ref, trig_ref,
):
    start_all(x, gains, qkv)
    count, chunk, _ = x.ref.shape
    lane = lax.broadcasted_iota(jnp.int32, (chunk, 128), 1)
    half_lane = lane // 64
    pick = lax.broadcasted_iota(jnp.int32, (16, 128), 0) == lax.broadcasted_iota(
        jnp.int32, (16, 128), 1
    )
    x_ref = x.wait()
    angles = jnp.zeros((chunk, 128), WIDE)
    for k in range(count):
        numbers = x_ref[k, :, D : D + 128].astype(WIDE)
        places = numbers[:, 2:3] * 32.0 + numbers[:, 3:4]
        angles = jnp.where(lane // 32 == k, places * freqs_ref[...], angles)
    trig_ref[0] = jnp.cos(angles)
    trig_ref[1] = jnp.sin(angles)
    gain_ref[...] = dot_rows(jnp.where(pick, 1.0, 0.0).astype(LOW), gains.wait()[...])
    qkv_ref = qkv.wait()

    def one_chunk(index, carry):
        rows = x_ref[index, :, :D].astype(WIDE)
        mixed_rows = (rows * unit_rows(rows) * gain_ref[0:1, :]).astype(LOW)
        mixed.ref[index] = mixed_rows

        def spread(packed):
            own = jnp.where(lane // 32 == index, packed, 0.0)
            own = own + pltpu.roll(own, 64, 1)
            return own + pltpu.roll(own, 32, 1)

        cosine = spread(trig_ref[0])
        sine = spread(trig_ref[1])
        sine = jnp.where(lane % 64 < 32, -sine, sine)
        cos.ref[index] = cosine
        sin.ref[index] = sine
        numbers = x_ref[index, :, D : D + 128].astype(WIDE).astype(jnp.int32)
        query_side, key_side = token_features(numbers[:, 0:1], numbers[:, 1:2])
        query_sides.ref[index] = query_side
        key_sides.ref[index] = key_side
        proj = dot_plain(mixed_rows, qkv_ref[...])
        values = proj[:, 512:].astype(LOW)
        turned.ref[index, :, 512:768] = values
        for pair in range(2):
            at = 128 * pair
            turned.ref[index, :, at : at + 128] = turn_pair(
                proj[:, at : at + 128], cosine, sine
            ).astype(LOW)
            keys = turn_pair(proj[:, 256 + at : 384 + at], cosine, sine).astype(LOW)
            turned.ref[index, :, 256 + at : 384 + at] = keys
            here = pl.ds(pl.multiple_of(index * chunk, chunk), chunk)
            keys_ref[pair, here, :128] = keys
            keys_ref[pair, here, 128:] = key_side
            values_ref[pair, here, :128] = values[:, at : at + 128]
            values_ref[pair, here, 128:] = jnp.where(lane == 0, 1.0, 0.0).astype(LOW)
        return carry

    lax.fori_loop(0, count, one_chunk, 0)
    start_all(mixed, turned, cos, sin, query_sides, key_sides)

    def one_block(index, carry):
        side = query_sides.ref[index]
        log_rows = jnp.zeros((chunk, 128), WIDE)
        here = pl.ds(pl.multiple_of((index % 2) * chunk, chunk), chunk)
        def scores_of(head):
            at = 128 * (head // 2)
            scaled = turned.ref[index, :, at : at + 128] * LOW(SCORE_SCALE)
            query = jnp.concatenate(
                [
                    jnp.where(half_lane == head % 2, scaled, LOW(0)),
                    side * weights_ref[head : head + 1, :],
                ],
                1,
            )
            return dot_rows(query, keys_ref[head // 2])

        scores = scores_of(0)
        parts = []
        for head in range(4):
            high = jnp.max(scores, 1, keepdims=True)
            powers = jnp.exp(scores - high).astype(LOW)
            if head < 3:
                scores = scores_of(head + 1)
            summed = dot_plain(powers, values_ref[head // 2])
            total = summed[:, 128:129]
            parts.append(summed[:, :128] / total)
            log_rows = jnp.where(lane == head, high + jnp.log(total), log_rows)
        for pair in range(2):
            at = 128 * pair
            total_mixed = jnp.where(half_lane == 0, parts[2 * pair], parts[2 * pair + 1])
            wide.ref[index, :, at : at + 128] = total_mixed
            low_rows = total_mixed.astype(LOW)

            @pl.when(index < 2)
            def _(low_rows=low_rows, at=at):
                lower.ref[here, at : at + 128] = low_rows

            @pl.when(index >= 2)
            def _(low_rows=low_rows, at=at):
                upper.ref[here, at : at + 128] = low_rows

        logs.ref[index] = log_rows
        logs.start_at(index)
        wide.start_at(index)
        return carry

    lax.fori_loop(0, count, one_block, 0)


def attend(chunks, first_weights, freqs, weights, token):
    chunk = chunks[0].shape[0]
    length = 4 * chunk
    return run(
        attend_body,
        "attend",
        15,
        [
            group(chunks),
            whole(first_weights, 0, 768),
            whole(first_weights, D, 128),
            freqs,
            weights,
        ],
        [
            ((16, D), WIDE),
            out_rows((length, D), LOW),
            out_rows((length, 768), LOW),
            out_rows((length, 256), WIDE),
            out_whole((length // 2, 256), LOW),
            out_whole((length // 2, 256), LOW),
            out_rows((length, 128), WIDE),
            out_rows((length, 128), WIDE),
            out_rows((length, 128), WIDE),
            out_rows((length, FEATURES), LOW),
            out_rows((length, FEATURES), LOW),
        ],
        [pltpu.VMEM((2, length, 256), LOW)] * 2 + [pltpu.VMEM((2, chunk, 128), WIDE)],
        token,
    )


def middle_body(rank_ref, x, near, far, wo, gain_ref, heads, own, mixed):
    rank = rank_ref[0]
    start_all(near, far, wo, x)
    count, chunk, _ = x.ref.shape
    block = chunk // 2
    near_ref, far_ref = near.wait(), far.wait()
    width = near_ref.shape[2]
    sources = {
        0: ((near_ref, 0, 0), (near_ref, 2, 0), (far_ref, 0, 0), (far_ref, 0, width)),
        1: ((near_ref, 1, 0), (far_ref, 1, 0), (near_ref, 3, 0), (far_ref, 1, width)),
    }
    for half, order in enumerate((ORDER_A, ORDER_B)):
        for q in range(4):
            ref, which, column = sources[half][q]
            for place, r in enumerate(order):
                start = order.index(r ^ q) * block
                heads.ref[
                    2 * half + place // 2,
                    place % 2 * block : (place % 2 + 1) * block,
                    q * width : (q + 1) * width,
                ] = ref[which, start : start + block, column : column + width]
    heads.start()
    wo_ref = wo.wait()

    def one_chunk(index, carry):
        x.wait_at(index)
        total = x.ref[index, :, :D].astype(WIDE)
        for q in range(4):
            rows = pl.ds(pl.multiple_of((rank ^ q) * width, width), width)
            total = total + dot_plain(
                heads.ref[index, :, q * width : (q + 1) * width], wo_ref[rows, :]
            )

        @pl.when(index % 2 == 0)
        def _():
            own.ref[index // 2] = total[:block]
            own.start_at(index // 2)

        mixed.ref[index] = (total * unit_rows(total) * gain_ref[1:2, :]).astype(LOW)
        mixed.start_at(index)
        return carry

    lax.fori_loop(0, count, one_chunk, 0)


def middle(rank, chunks, heads, out_pieces, gain):
    chunk = chunks[0].shape[0]
    length = 4 * chunk
    lower, lower_x, lower_far, upper, upper_y, upper_far = heads
    return run(
        middle_body,
        "middle",
        7,
        [
            rank,
            group(chunks),
            group((lower, upper, lower_x, upper_y)),
            group((lower_far, upper_far)),
            output_weights(out_pieces),
            gain,
        ],
        [out_rows((length, D), LOW), out_rows((chunk, D), WIDE, 2), out_rows((length, D), LOW)],
    )


def feed_body(mixed, gate_up, both, hidden):
    count, _, per = hidden.ref.shape
    mixed.start(0)
    gate_up.start(0, 2)
    mixed.start(1, 2, 3)
    gate_up.start(1, 3)
    for half in range(2):
        here = slice(half * per // 2, (half + 1) * per // 2)
        there = slice(per + half * per // 2, per + (half + 1) * per // 2)

        def one_chunk(index, carry, half=half, here=here, there=there):
            if half == 0:
                mixed.wait_at(index)

            @pl.when(index == 0)
            def _():
                for k in (half, 2 + half):
                    gate_up.copies[k].wait()

            rows = mixed.ref[index]
            gate = dot_plain(rows, gate_up.ref[half])
            up = dot_plain(rows, gate_up.ref[2 + half])
            sigmoid = 1.0 / (1.0 + jnp.exp(-gate))
            silu = gate * sigmoid
            both.ref[index, :, here] = (up * (sigmoid + silu * (1.0 - sigmoid))).astype(LOW)
            both.ref[index, :, there] = silu.astype(LOW)
            hidden.ref[index, :, here] = (silu * up).astype(LOW)
            if half == 1:
                both.start_at(index)
                hidden.start_at(index)
            return carry

        lax.fori_loop(0, count, one_chunk, 0)
    gate_up.waited = True


def feed(mixed, gate_up, token):
    length = mixed.shape[0]
    per = gate_up.shape[1] // 2
    return run(
        feed_body,
        "feed",
        8,
        [rows_of(mixed), columns_of(gate_up)],
        [out_rows((length, 2 * per), LOW), out_rows((length, per), LOW)],
        token=token,
    )


def feed_back_body(both, cots, gate_up, down, grads, back, later=()):
    start_all(down)
    cots.start(0)
    both.start(0)
    gate_up.start()
    cots.start(1)
    both.start(1)
    start_all(*later)
    per = down.ref.shape[0]

    def one_chunk(index, carry):
        cots.wait_at(index)
        both.wait_at(index)
        grad_hidden = dot_rows(cots.ref[index], down.wait_first(index)[...])
        grads.ref[index, :, :per] = (grad_hidden * both.ref[index, :, :per].astype(WIDE)).astype(LOW)
        grads.ref[index, :, per:] = (grad_hidden * both.ref[index, :, per:].astype(WIDE)).astype(LOW)
        grads.start_at(index)
        back.ref[index] = dot_rows(grads.ref[index], gate_up.wait_first(index)[...]).astype(LOW)
        back.start_at(index)
        return carry

    lax.fori_loop(0, 2, one_chunk, 0)


def feed_back_far_body(both, cots, gate_up, down, hidden, near_cots, grads, back, out):
    feed_back_body(both, cots, gate_up, down, grads, back, (hidden, near_cots))
    near_ref, far_ref = near_cots.wait(), cots.ref
    chunk = near_ref.shape[1]

    def one_part(index, carry):
        hidden.wait_at(index)
        total = None
        for k in range(4):
            more = dot_first(
                hidden.ref[index, k * chunk : (k + 1) * chunk, :], (near_ref, far_ref)[k % 2][k // 2]
            )
            total = more if total is None else total + more
        out.ref[index] = total.astype(LOW)
        out.start_at(index)
        return carry

    lax.fori_loop(0, hidden.ref.shape[0], one_part, 0)


def feed_back(first, both, cots, gate_up, down, token, hidden=None):
    length = both.shape[0]
    chunk = length // 4
    per = down.shape[0]

    def pairs(refs, buffer):
        return [
            (refs[0].at[pl.ds((first + 2 * k) * chunk, chunk)], buffer.at[k]) for k in range(2)
        ]

    ins = [Plan([both], (2, chunk, 2 * per), pairs, 2), group((cots[first], cots[first + 2]))]
    ins += [whole(gate_up), whole(down)]
    outs = [out_rows((length // 2, 2 * per), LOW, 2), out_group((chunk, D), LOW, 2)]
    if hidden is None:
        return run(feed_back_body, "feed_back", 7, ins, outs, token=token)
    ins += [columns_of(hidden), group((cots[0], cots[2]))]
    outs += [out_rows((per, D), LOW)]
    return run(feed_back_far_body, "feed_back", 12, ins, outs, token=token)


def sum_arrived(near, got, last):
    return (
        near.wait()[...].astype(WIDE) + got.wait()[...].astype(WIDE) + last.wait()[...].astype(WIDE)
    )


def arrivals(sums):
    return [whole(x) if place % 3 == 2 else top(x) for place, x in enumerate(sums)]


def own_back_body(
    rank_ref, n0, g0, l0, n1, g1, l1, middle_rows, cot, gain_ref, wo, grad, parcels
):
    rank = rank_ref[0]
    start_all(n0, g0, l0, middle_rows, cot, n1, g1, l1, wo)
    block = l0.ref.shape[0]
    width = parcels.ref.shape[2] // 2
    for place, sums in enumerate(((n0, g0, l0), (n1, g1, l1))):
        rows = slice(place * block, (place + 1) * block)
        arrived = sum_arrived(*sums)
        y = middle_rows.wait()[rows, :]
        scale = unit_rows(y)
        normed = y * scale
        turned = arrived * gain_ref[1:2, :]
        grad.ref[rows, :] = cot.wait()[rows, :].astype(WIDE) + scale * (
            turned - normed * jnp.mean(turned * normed, -1, keepdims=True)
        )
    grad.start()
    low_grad = grad.ref[...].astype(LOW)
    wo_ref = wo.wait()
    for q in range(4):
        place = pl.ds(pl.multiple_of((rank ^ q) * width, width), width)
        parcels.ref[q, :, :width] = dot_rows(low_grad, wo_ref[place, :]).astype(LOW)
        parcels.ref[q, :, width:] = grad.ref[:, place].astype(LOW)
        parcels.start(q)


def own_back(rank, sums, middle_own, cot_own, gain, out_pieces, token):
    quarter = cot_own.shape[0]
    return run(
        own_back_body,
        "own_back",
        4,
        [rank, *arrivals(sums), whole(middle_own), whole(cot_own), gain]
        + [output_weights(out_pieces)],
        [out_whole((quarter, D), WIDE), out_group((quarter, 512), LOW)],
        token=token,
    )


def attend_back_body(
    parcels, turned, wide, logs, cos, sin, query_sides, key_sides, weights_ref, projections,
    out, bias_ref, back, queries_ref, grads_ref, total_ref,
):
    start_all(parcels, turned, query_sides, logs, wide, key_sides, cos, sin, projections)
    length = turned.ref.shape[0]
    chunk = length // 4
    block = chunk // 2
    half_lane = lax.broadcasted_iota(jnp.int32, (chunk, 128), 1) // 64
    lane = lax.broadcasted_iota(jnp.int32, (chunk, 128), 1)
    parcels_ref = parcels.wait()
    for half, order in enumerate((ORDER_A, ORDER_B)):
        for place in range(4):
            to = slice((4 * half + place) * block, (4 * half + place + 1) * block)
            rows = slice(half * block, (half + 1) * block)
            for head in range(4):
                at = 128 * (head // 2)
                grads_ref[head, to, :128] = parcels_ref[order[place], rows, at : at + 128]
    turned_ref, side_ref, log_ref, wide_ref = (
        turned.wait(), query_sides.wait(), logs.wait(), wide.wait()
    )

    def prepare(index, carry):
        rows = pl.ds(pl.multiple_of(index * chunk, chunk), chunk)
        for pair in range(2):
            at = 128 * pair
            product = grads_ref[2 * pair, rows, :128].astype(WIDE) * wide_ref[rows, at : at + 128]
            scaled = turned_ref[rows, at : at + 128] * LOW(SCORE_SCALE)
            for half in range(2):
                head = 2 * pair + half
                side = side_ref[rows, :] * weights_ref[head : head + 1, :]
                for place, piece in enumerate(three_parts(-log_ref[rows, head : head + 1])):
                    side = jnp.where(lane == LSE_AT + place, piece, side)
                queries_ref[head, rows, :128] = jnp.where(half_lane == half, scaled, LOW(0))
                queries_ref[head, rows, 128:] = side
                delta = jnp.sum(jnp.where(half_lane == half, product, 0.0), 1, keepdims=True)
                extra = jnp.zeros((chunk, 128), LOW)
                for place, piece in enumerate(three_parts(-delta)):
                    extra = jnp.where(lane == place, piece, extra)
                grads_ref[head, rows, 128:] = extra
        total_ref[rows, :] = jnp.zeros((chunk, 256), WIDE)
        return carry

    lax.fori_loop(0, 4, prepare, 0)
    three_ones = jnp.where(lane < 3, 1.0, 0.0).astype(LOW)
    key_ref, cos_ref, sin_ref = key_sides.wait(), cos.wait(), sin.wait()

    def one_block(index, carry):
        rows = pl.ds(pl.multiple_of(index * chunk, chunk), chunk)
        cosine = cos_ref[rows, :]
        sine = -sin_ref[rows, :]
        key_side = key_ref[rows, :]
        first_four = jnp.where(lane < 4, key_side.astype(WIDE), 0.0)
        sums = list(carry)
        for pair in range(2):
            at = 128 * pair
            keys = turned_ref[rows, 256 + at : 384 + at]
            values = turned_ref[rows, 512 + at : 640 + at]
            keys_wide = jnp.concatenate([keys, key_side], 1)
            grad_keys = jnp.zeros((chunk, 128), WIDE)
            grad_values = jnp.zeros((chunk, 128), WIDE)
            for half in range(2):
                head = 2 * pair + half
                mine = half_lane == half
                weights = jnp.exp(dot_rows(keys_wide, queries_ref[head]))
                grad_weights = dot_rows(
                    jnp.concatenate([jnp.where(mine, values, LOW(0)), three_ones], 1),
                    grads_ref[head],
                )
                grad_values = jnp.where(
                    mine, dot_plain(weights.astype(LOW), grads_ref[head, :, :128]), grad_values
                )
                grad_scores = (weights * grad_weights).astype(LOW)
                both = dot_plain(
                    grad_scores,
                    jnp.concatenate([queries_ref[head, :, :128], side_ref[...]], 1),
                )
                grad_keys = grad_keys + both[:, :128]
                counted = both[:, 128:]
                same = jnp.sum(counted * first_four, 0, keepdims=True)
                every = jnp.sum(jnp.where(lane < 4, counted, 0.0), 0, keepdims=True)
                sums[head] = sums[head] + same
                sums[4 + head] = sums[4 + head] + (every - same)
                total_ref[:, at : at + 128] += dot_first(
                    grad_scores, jnp.where(mine, keys, LOW(0))
                )
            out.ref[index, :, 256 + at : 384 + at] = turn_pair(grad_keys, cosine, sine).astype(LOW)
            out.ref[index, :, 512 + at : 640 + at] = grad_values.astype(LOW)
        return tuple(sums)

    start = tuple(jnp.zeros((1, 128), WIDE) for _ in range(8))
    sums = lax.fori_loop(0, 4, one_block, start)
    for place in range(8):
        bias_ref[place : place + 1, :] = sums[place]
    projections_ref = projections.wait()

    def one_chunk(index, carry):
        rows = pl.ds(pl.multiple_of(index * chunk, chunk), chunk)
        for pair in range(2):
            at = 128 * pair
            out.ref[index, :, at : at + 128] = turn_pair(
                total_ref[rows, at : at + 128] * SCORE_SCALE, cos_ref[rows, :], -sin_ref[rows, :]
            ).astype(LOW)
        out.start_at(index)
        back.ref[index] = dot_rows(out.ref[index], projections_ref[...]).astype(LOW)
        back.start_at(index)
        return carry

    lax.fori_loop(0, 4, one_chunk, 0)


def attend_back(parcels, kept, weights, first_weights, token):
    turned, attended, *others = kept
    length = turned.shape[0]
    return run(
        attend_back_body,
        "attend_back",
        80,
        [group(parcels, 0, 256), whole(turned), whole(attended)]
        + [whole(x) for x in others]
        + [weights, whole(first_weights, 0, 768)],
        [out_rows((length, 768), LOW), ((8, 128), WIDE), out_group((length // 4, D), LOW)],
        [
            pltpu.VMEM((4, length, 256), LOW),
            pltpu.VMEM((4, length, 256), LOW),
            pltpu.VMEM((length, 256), WIDE),
        ],
        token,
    )


def gate_up_grads_body(mixed, near, far, out):
    mixed.start(0)
    for k in range(2):
        near.start(k)
        far.start(k)
    mixed.start(1, 2, 3)
    near.waited = far.waited = True
    chunk = mixed.ref.shape[1] // 4

    def one_part(index, carry):
        mixed.wait_at(index)
        total = None
        for k in range(4):
            item = (near, far)[k % 2]

            @pl.when(index == 0)
            def _(item=item, k=k):
                item.copies[k // 2].wait()

            more = dot_first(
                mixed.ref[index, k * chunk : (k + 1) * chunk, :], item.ref[k // 2]
            )
            total = more if total is None else total + more
        out.ref[index] = total.astype(LOW)
        out.start_at(index)
        return carry

    lax.fori_loop(0, mixed.ref.shape[0], one_part, 0)


def gate_up_grads(mixed, near, far, token):
    return run(
        gate_up_grads_body,
        "gate_up_grads",
        8,
        [columns_of(mixed), rows_of(near, 2), rows_of(far, 2)],
        [out_rows((D, near.shape[1]), LOW)],
        token=token,
    )[0]


def feed_out_body(hidden, down, out):
    start_all(down, hidden)
    block = out.ref.shape[1]

    def one_chunk(index, carry):
        down_ref = down.wait_first(index)
        hidden.wait_at(index)
        total = dot_plain(hidden.ref[index], down_ref[...]).astype(LOW)
        for p in range(2):
            q = jnp.where(index < 2, 2 * index + p, index - 2 + 2 * p)
            out.ref[2 * q + index // 2] = total[p * block : (p + 1) * block]
            out.start_at(2 * q + index // 2)
        return carry

    lax.fori_loop(0, hidden.ref.shape[0], one_chunk, 0)


def feed_out(hidden, down, token):
    length = hidden.shape[0]
    block = length // 8

    def pairs(refs, buffer):
        return [
            (buffer.at[2 * q + half], ref.at[pl.ds(half * block, block)])
            for q, ref in enumerate(refs)
            for half in range(2)
        ]

    return run(
        feed_out_body,
        "feed_out",
        5,
        [rows_of(hidden), whole(down)],
        [Plan([((2 * block, D), LOW)] * 4, (8, block, D), pairs, 8)],
        token=token,
    )


def own_last_body(n0, g0, l0, n1, g1, l1, forward, x, base, middle_rows, gain_ref, out):
    start_all(n0, g0, l0, x, base, forward, middle_rows, n1, g1, l1)
    block = l0.ref.shape[0]
    piece = out.ref.shape[1] // 2
    each = block // piece
    for half, back in enumerate(((n0, g0, l0), (n1, g1, l1))):
        rows = slice(half * block, (half + 1) * block)
        places = slice(half * each, (half + 1) * each)
        turned = sum_arrived(*back) * gain_ref[0:1, :]
        x_rows = x.wait()[rows, :D].astype(WIDE)
        scale = unit_rows(x_rows)
        normed = x_rows * scale
        grad = base.wait()[rows, :] + scale * (
            turned - normed * jnp.mean(turned * normed, -1, keepdims=True)
        )
        out.ref[places, :piece, :] = grad.astype(LOW).reshape(each, piece, D)
        block_rows = middle_rows.wait()[rows, :]
        forward_ref = forward.wait()
        for q in range(4):
            block_rows = block_rows + forward_ref[q, rows, :].astype(WIDE)
        out.ref[places, piece:, :] = block_rows.astype(LOW).reshape(each, piece, D)


def own_last(sums, outs, mine, base, middle_own, gain, n_seq, token):
    quarter = base.shape[0]
    return run(
        own_last_body,
        "own_last",
        80,
        [*arrivals(sums), group(outs), whole(mine), whole(base), whole(middle_own), gain],
        [out_whole((n_seq, 2 * quarter // n_seq, D), LOW)],
        token=token,
    )[0]


def join_body(left, right, out):
    start_all(left, right)
    width = left.ref.shape[1]
    out.ref[:, :width] = left.wait()[...]
    out.ref[:, width:] = right.wait()[...]


def join(left, right, token):
    rows = left.shape[0]
    return run(
        join_body,
        "join",
        1,
        [whole(left), whole(right)],
        [out_whole((rows, left.shape[1] + right.shape[1]), LOW)],
        token=token,
    )[0]


def first_grads_body(rank_ref, mixed, proj, heads, parcels, bias_ref, out, branch_ref):
    rank = rank_ref[0]
    start_all(mixed, proj, parcels, heads)
    width = proj.ref.shape[1]
    block = parcels.ref.shape[1] // 2
    parcels_ref = parcels.wait()
    for half, order in enumerate((ORDER_A, ORDER_B)):
        for place in range(4):
            to = slice((4 * half + place) * block, (4 * half + place + 1) * block)
            branch_ref[to, :] = parcels_ref[order[place], half * block : (half + 1) * block, :]
    mixed_ref, proj_ref, heads_ref = mixed.wait(), proj.wait(), heads.wait()

    def one_part(index, carry):
        out.ref[index, :, :width] = dot_first(mixed_ref[index], proj_ref[...]).astype(LOW)
        out.ref[rank ^ index, :, width : width + 256] = dot_first(
            heads_ref[index], branch_ref[...]
        ).astype(LOW)
        out.ref[index, :, width + 256 :] = bias_ref[...]
        return carry

    lax.fori_loop(0, 4, one_part, 0)


def first_grads(rank, mixed, proj, heads, parcels, bias_rows, token):
    length = mixed.shape[0]
    return run(
        first_grads_body,
        "first_grads",
        8,
        [rank, columns_of(mixed), whole(proj), columns_of(heads)]
        + [group(parcels, 256, 256), bias_rows],
        [out_rows((D, 768 + 256 + 128), LOW)],
        [pltpu.VMEM((length, 256), LOW)],
        token,
    )[0]


def rank_blocks(lower, lower_far, upper, upper_far):
    half = lower.shape[0] // 2
    return (
        ((lower, 0), (upper, 0)),
        ((lower, half), (upper_far, 0)),
        ((lower_far, 0), (upper, half)),
        ((lower_far, half), (upper_far, half)),
    )


def lay_flat(column, part):
    count = column.shape[0]
    row = lax.broadcasted_iota(jnp.int32, (count, 128), 0) + part * count
    lane = lax.broadcasted_iota(jnp.int32, (count, 128), 1)
    return jnp.sum(jnp.where(row == lane, column, 0.0), 0, keepdims=True)


def spread_feed_kernel(
    rank_ref, lower, lower_far, upper, upper_far, gate_ref, up_ref, gain_ref,
    grad_gate_ref, grad_up_ref, grad_down_ref, grad_gain_ref,
):
    rank = rank_ref[0]
    half = lower.shape[0] // 2
    piece = 128
    ff = gate_ref.shape[1]
    per = ff // 4
    for r, halves in enumerate(rank_blocks(lower, lower_far, upper, upper_far)):
        for part, (ref, start) in enumerate(halves):
            rows = slice(part * half, (part + 1) * half)
            source = slice(start, start + half)
            for s in range(per // piece):
                to = pl.ds(pl.multiple_of((4 * s + (rank ^ r)) * piece, piece), piece)
                grad_gate_ref[rows, to] = ref[source, s * piece : (s + 1) * piece].astype(WIDE)
                grad_up_ref[rows, to] = ref[source, per + s * piece : per + (s + 1) * piece].astype(
                    WIDE
                )
            to = pl.ds(pl.multiple_of((rank ^ r) * 2 * half + part * half, half), half)
            grad_down_ref[to, :] = ref[source, 2 * per :].astype(WIDE)
    flat = jnp.zeros((1, 128), WIDE)
    for part in range(2):
        rows = slice(part * half, (part + 1) * half)
        total = jnp.sum(
            gate_ref[rows, :].astype(WIDE) * grad_gate_ref[rows, :], 1, keepdims=True
        ) + jnp.sum(up_ref[rows, :].astype(WIDE) * grad_up_ref[rows, :], 1, keepdims=True)
        flat = flat + lay_flat(total, part)
    grad_gain_ref[...] = jnp.broadcast_to(flat / gain_ref[...].astype(WIDE), (8, 128))


def spread_feed(rank, pieces, w_gate, w_up, gain):
    shard, ff = w_gate.shape
    return call(
        spread_feed_kernel,
        "spread_feed",
        [((shard, ff), WIDE), ((shard, ff), WIDE), ((ff // 8, D), WIDE), ((8, 128), WIDE)],
        [pl.BlockSpec(memory_space=pltpu.SMEM)] + [whole_block()] * 7,
        4 * shard * ff,
        16 * 2**20,
        (rank, *pieces, w_gate, w_up, gain),
    )


def spread_first_kernel(
    rank_ref, lower, lower_far, upper, upper_far, wq_ref, wk_ref, wv_ref, gain_ref,
    gq_ref, gk_ref, gv_ref, go_ref, grad_gain_ref, bias_ref,
):
    rank = rank_ref[0]
    half = lower.shape[0] // 2
    wide = 256
    bias_ref[...] = jnp.zeros_like(bias_ref)
    for r, halves in enumerate(rank_blocks(lower, lower_far, upper, upper_far)):
        to = pl.ds(pl.multiple_of((rank ^ r) * wide, wide), wide)
        for part, (ref, start) in enumerate(halves):
            rows = slice(part * half, (part + 1) * half)
            source = slice(start, start + half)
            for place, out_ref in enumerate((gq_ref, gk_ref, gv_ref, go_ref)):
                out_ref[rows, to] = ref[source, place * wide : (place + 1) * wide].astype(WIDE)
        ref, start = halves[0]
        bias_ref[pl.ds(rank ^ r, 1), :] = jnp.sum(
            ref[start : start + 16, 4 * wide : 4 * wide + 128].astype(WIDE), 0, keepdims=True
        )
    flat = jnp.zeros((1, 128), WIDE)
    for part in range(2):
        rows = slice(part * half, (part + 1) * half)
        total = jnp.zeros((half, 1), WIDE)
        for weight_ref, grad_ref in ((wq_ref, gq_ref), (wk_ref, gk_ref), (wv_ref, gv_ref)):
            total = total + jnp.sum(
                weight_ref[rows, :].astype(WIDE) * grad_ref[rows, :], 1, keepdims=True
            )
        flat = flat + lay_flat(total, part)
    grad_gain_ref[...] = jnp.broadcast_to(flat / gain_ref[...].astype(WIDE), (8, 128))


def spread_first(rank, pieces, w_query, w_key, w_value, gain):
    shard = w_query.shape[0]
    return call(
        spread_first_kernel,
        "spread_first",
        [((shard, D), WIDE)] * 4 + [((8, 128), WIDE), ((8, 128), WIDE)],
        [pl.BlockSpec(memory_space=pltpu.SMEM)] + [whole_block()] * 8,
        4 * shard * D,
        8 * 2**20,
        (rank, *pieces, w_query, w_key, w_value, gain),
    )


def on_plane(
    inputs,
    w_query,
    w_key,
    w_value,
    w_output,
    gain_attention,
    w_gate,
    w_up,
    w_down,
    gain_feed,
    variate_bias,
    segment_ids,
    variate_ids,
    positions,
    grad_output,
):
    rank = lax.axis_index("batch")
    rank_row = jnp.reshape(rank, (1,)).astype(jnp.int32)
    micro, tokens = inputs.shape[0], inputs.shape[2]
    n_seq = lax.axis_size("seq")
    shard = w_query.shape[0]
    per = D // 4

    packed, first_shard, gate_up_shard, down_shard = pack(
        rank_row,
        inputs.reshape(micro, tokens, D),
        grad_output.reshape(micro, tokens, D),
        segment_ids.reshape(micro, tokens),
        variate_ids.reshape(micro, tokens),
        positions.reshape(micro, tokens),
        (w_query, w_key, w_value, w_output),
        (gain_attention.reshape(1, shard), gain_feed.reshape(1, shard)),
        w_gate,
        w_up,
        w_down,
    )
    first_weights = lax.all_gather(first_shard, "seq", axis=0, tiled=True)
    gate_up = lax.all_gather(gate_up_shard, "seq", axis=0, tiled=True)
    down = lax.all_gather(down_shard, "seq", axis=0, tiled=True)
    packed = lax.all_to_all(packed, "batch", 0, 0, tiled=True)
    by_sequence = [
        packed[:, kind].reshape(4 * micro, tokens // 4, D + 128)[:, :, : D + 128 - 128 * kind]
        for kind in range(2)
    ]
    out_columns = first_weights[:, 768:D]
    out_got = swap_pairs(out_columns)
    mine, cot_by_sequence, out_got = lax.optimization_barrier(
        (over_seq(by_sequence[0]), by_sequence[1], out_got)
    )
    cot_mine = over_seq(cot_by_sequence)
    freqs = jnp.exp((jnp.arange(128) % 32).astype(WIDE) * (-2.0 * math.log(10000.0) / HD))[None, :]
    my_bias = lax.dynamic_slice_in_dim(variate_bias, rank * 4, 4, 1)
    weights = jnp.pad(head_weights(my_bias[0], my_bias[1]), ((0, 4), (0, 0)))

    chunks = gather_plane(mine)
    out_pieces = far_pairs(
        out_columns, lax.optimization_barrier((out_got, chunks[1], chunks[3]))[0]
    )
    gain, mixed_first, turned, attended, lower, upper, *kept = attend(
        chunks, first_weights, freqs, weights, rank_row
    )
    ready = lax.optimization_barrier((lower, upper, out_pieces[1], out_pieces[3]))
    lower_x, upper_y = swap(ready[0], 1), swap(ready[1], 2)
    lower_far = swap(jnp.concatenate([lower, lower_x], 1), 2)
    upper_far = swap(jnp.concatenate([upper, upper_y], 1), 1)
    cot_got = swap_pairs(lax.optimization_barrier((cot_mine, lower_far, upper_far))[0])
    heads, middle_own, mixed_second = middle(
        rank_row,
        chunks,
        (lower, lower_x, lower_far, upper, upper_y, upper_far),
        out_pieces,
        gain,
    )

    both, hidden = feed(mixed_second, gate_up, after(rank_row, cot_got))
    cots = far_pairs(cot_mine, lax.optimization_barrier((cot_got, mixed_second))[0])
    far_grads, far_lower, far_upper, down_weight_grads = feed_back(
        1, both, cots, gate_up, down, rank_row, hidden
    )
    got = scatter_first((None, far_lower, None, far_upper))
    near_grads, near_lower, near_upper = feed_back(
        0, both, cots, gate_up, down, after(rank_row, far_lower)
    )
    down_grad_shard = lax.psum_scatter(down_weight_grads, "seq", scatter_dimension=0, tiled=True)
    back = (near_lower, None, near_upper, None)
    gate_up_weight_grads = gate_up_grads(
        mixed_second, near_grads, far_grads, after(rank_row, got)
    )
    gate_up_grad_shard = lax.psum_scatter(
        gate_up_weight_grads, "seq", scatter_dimension=0, tiled=True
    )
    sums = scatter_second(back, got)
    grad_middle, *parcels = own_back(
        rank_row, sums, middle_own, cot_mine, gain, out_pieces,
        after(rank_row, gate_up_weight_grads),
    )
    outs = feed_out(hidden, down, after(rank_row, parcels[0]))
    parcels = [parcels[0]] + [swap(parcels[r], r) for r in range(1, 4)]

    proj, bias, *back = attend_back(
        parcels, (turned, attended, *kept), weights, first_weights, after(rank_row, outs[0])
    )
    outs = [outs[0]] + [swap(outs[q], q) for q in range(1, 4)]
    got = scatter_first((None, back[1], None, back[3]))
    bias_sums = jnp.sum(bias, 1)
    bias_parts = jnp.pad(jnp.concatenate(three_parts(bias_sums)), (0, 104))[None, :]
    slots = lax.broadcasted_iota(jnp.int32, (per, 1), 0) % shard == lax.axis_index("seq")
    bias_rows = jnp.where(slots, bias_parts, LOW(0))
    first_weight_grads = first_grads(
        rank_row, mixed_first, proj, heads, parcels, bias_rows, rank_row
    )
    got, first_weight_grads = lax.optimization_barrier((got, first_weight_grads))
    first_shard = lax.psum_scatter(first_weight_grads, "seq", scatter_dimension=0, tiled=True)
    sums = scatter_second(back, got)
    feed_shard = join(gate_up_grad_shard, down_grad_shard, after(rank_row, first_weight_grads))
    last = own_last(
        sums, outs, mine, grad_middle, middle_own, gain, n_seq, after(rank_row, feed_shard)
    )
    moved = lax.all_to_all(last, "seq", 0, 0, tiled=True)
    quarter = tokens // 4
    feed_pieces = gather_plane(after(feed_shard, last))
    first_pieces = gather_plane(after(first_shard, feed_pieces))
    moved, first_pieces = lax.optimization_barrier((moved, first_pieces))
    moved = moved.reshape(4, micro, 2 * quarter, D)
    moved = lax.all_to_all(moved, "batch", 0, 0, tiled=True)
    grad_inputs = jnp.transpose(moved[:, :, :quarter].astype(WIDE), (1, 0, 2, 3))
    block_output = jnp.transpose(moved[:, :, quarter:], (1, 0, 2, 3))

    grad_gate, grad_up, grad_down, grad_gain_second = spread_feed(
        rank_row, feed_pieces, w_gate, w_up, gain_feed.reshape(1, shard)
    )
    grad_query, grad_key, grad_value, grad_output_weights, grad_gain_first, bias_table = (
        spread_first(
            rank_row, first_pieces, w_query, w_key, w_value, gain_attention.reshape(1, shard)
        )
    )
    bias_table = jnp.sum(bias_table[:4, :24].reshape(4, 3, 2, 4), 1)
    grad_bias = jnp.transpose(bias_table, (1, 0, 2)).reshape(2, H)
    return (
        block_output.reshape(inputs.shape),
        grad_inputs.reshape(inputs.shape),
        grad_query,
        grad_key,
        grad_value,
        grad_output_weights,
        grad_gain_first[0],
        grad_gate,
        grad_up,
        grad_down,
        grad_gain_second[0],
        grad_bias,
    )


def solution(mesh):
    n_batch, n_seq = mesh.shape["batch"], mesh.shape["seq"]
    step = on_plane if n_batch == 4 and n_seq == 8 else on_device
    return jax.shard_map(
        step,
        mesh=mesh,
        in_specs=(
            P(None, "batch", "seq", None),
            P("seq", None),
            P("seq", None),
            P("seq", None),
            P("seq", None),
            P("seq"),
            P("seq", None),
            P("seq", None),
            P("seq", None),
            P("seq"),
            P(),
            P(None, "batch", "seq"),
            P(None, "batch", "seq"),
            P(None, "batch", "seq"),
            P(None, "batch", "seq", None),
        ),
        out_specs=(
            P(None, "batch", "seq", None),
            P(None, "batch", "seq", None),
            P("seq", None),
            P("seq", None),
            P("seq", None),
            P("seq", None),
            P("seq"),
            P("seq", None),
            P("seq", None),
            P("seq", None),
            P("seq"),
            P(),
        ),
        check_vma=False,
    )
```
